32 devices in a mesh: task: 8 (over y, x, core), samp: 4 (over z).
Axes of the slice: x: 2, y: 2, z: 4, core: 2. Of those that a mesh axis runs over, the one named last changes fastest.
Arguments:
- cells: bfloat16 [8, 512, 4, 512], P('task', 'samp'), may hold values from -6 to 6
- out_grad: bfloat16 [8, 512, 4, 512], P('task', 'samp'), may hold values from -6 to 6
- sample_counts: int32 [8], P('task'), may hold values from 51 to 512, as said below
- feature_counts: int32 [8], P('task'), may hold values from 2 to 4, as said below
- sample_block: float32 [1049088], P(('task', 'samp'))
- sample_first: float32 [1049088], P(('task', 'samp'))
- sample_second: float32 [1049088], P(('task', 'samp')), as said below
- feature_block: float32 [1049088], P(('task', 'samp'))
- feature_first: float32 [1049088], P(('task', 'samp'))
- feature_second: float32 [1049088], P(('task', 'samp')), as said below
- mlp_block: float32 [2097664], P(('task', 'samp'))
- mlp_first: float32 [2097664], P(('task', 'samp'))
- mlp_second: float32 [2097664], P(('task', 'samp')), as said below
Outputs:
- layer_out: bfloat16 [8, 512, 4, 512], P('task', 'samp')
- cells_grad: float32 [8, 512, 4, 512], P('task', 'samp')
- sample_grad: float32 [1049088], P(('task', 'samp'))
- sample_first_new: float32 [1049088], P(('task', 'samp'))
- sample_second_new: float32 [1049088], P(('task', 'samp'))
- sample_master_new: float32 [1049088], P(('task', 'samp'))
- sample_weights_new: bfloat16 [1049088], P(('task', 'samp'))
- feature_grad: float32 [1049088], P(('task', 'samp'))
- feature_first_new: float32 [1049088], P(('task', 'samp'))
- feature_second_new: float32 [1049088], P(('task', 'samp'))
- feature_master_new: float32 [1049088], P(('task', 'samp'))
- feature_weights_new: bfloat16 [1049088], P(('task', 'samp'))
- mlp_grad: float32 [2097664], P(('task', 'samp'))
- mlp_first_new: float32 [2097664], P(('task', 'samp'))
- mlp_second_new: float32 [2097664], P(('task', 'samp'))
- mlp_master_new: float32 [2097664], P(('task', 'samp'))
- mlp_weights_new: bfloat16 [2097664], P(('task', 'samp'))
- norm_pairs: float32 [9, 2], replicated
The draws below stay inside these ranges and needn't reach their ends.
Inputs may be any that keep to these rules, and one draw needn't show every extreme that they name: `sample_counts`: samples at or beyond a task's count are padding; some task fills all 512 slots. `feature_counts`: features at or beyond a task's count are padding; some task fills all 4 slots. `sample_second`: every entry is positive. `feature_second`: every entry is positive. `mlp_second`: every entry is positive.
All inputs are finite; a program needn't handle non-finite values.
Results may differ from the reference program's by a relative error of at most 0.025.
The reference program's roundings to bfloat16 on the way count: a program that leaves them out, or rounds other values in their place, can miss the bound.
Values may be sent and summed in bfloat16 or wider, within the bound.
A program may use at most 128 MiB of HBM per device.

```python
import math
import jax
import jax.numpy as jnp
from jax import lax

D = 512
HEADS = 8
HEAD_DIM = 64
FF = 2048
SEQ = 512
FMAX = 4
TASKS = 8


def ramp_factor(total):
    return 1.0 + 2.0 * jnp.arange(total, dtype=jnp.float32) / total


def rough_normal(key, entries):
    return jnp.clip(jax.random.normal(key, (entries,), jnp.float32), -4.0, 4.0)


def block_draw(key, width_in, width_mid, value_boost):
    key_gain, key_in, key_out = jax.random.split(key, 3)
    gain_part = 1.0 + 0.1 * rough_normal(key_gain, D)
    in_part = rough_normal(key_in, D * width_in) / (1.5 * math.sqrt(D))
    column = jnp.arange(D * width_in, dtype=jnp.int32) % width_in
    in_part = jnp.where(column >= 2 * D, in_part * value_boost, in_part)
    out_part = rough_normal(key_out, width_mid * D) / math.sqrt(width_mid)
    flat_params = jnp.concatenate([gain_part, in_part, out_part])
    return flat_params * ramp_factor(flat_params.shape[0])


def grad_scale():
    return 0.5 * math.sqrt(0.4 * TASKS * SEQ * FMAX)


def first_draw(key, total):
    return grad_scale() * rough_normal(key, total) * ramp_factor(total)


def second_draw(key, total):
    scale_sq = grad_scale() * grad_scale()
    spread = jnp.exp(jax.random.uniform(key, (total,), jnp.float32, math.log(0.25), math.log(4.0)))
    return scale_sq * spread


def bounded_counts(key, lowest, highest):
    key_draw, key_pick = jax.random.split(key)
    counts = jax.random.randint(key_draw, (TASKS,), lowest, highest + 1, jnp.int32)
    shuffled = jax.random.permutation(key_pick, TASKS)
    counts = counts.at[shuffled[0]].set(highest)
    counts = counts.at[shuffled[1]].set(lowest)
    return counts


def draw_sample_counts(key, part):
    return bounded_counts(jax.random.fold_in(key, 101), max(SEQ // 10, 1), SEQ)


def draw_feature_counts(key, part):
    return bounded_counts(jax.random.fold_in(key, 102), max(FMAX // 2, 1), FMAX)


def draw_sample_block(key, part):
    return block_draw(jax.random.fold_in(key, 201), 3 * D, D, math.sqrt(max(SEQ // 32, 1)))


def draw_feature_block(key, part):
    return block_draw(jax.random.fold_in(key, 202), 3 * D, D, math.sqrt(max(FMAX // 4, 1)))


def draw_mlp_block(key, part):
    return block_draw(jax.random.fold_in(key, 203), FF, FF, 1.0)


def draw_sample_first(key, part):
    return first_draw(jax.random.fold_in(key, 301), D + 4 * D * D)


def draw_feature_first(key, part):
    return first_draw(jax.random.fold_in(key, 302), D + 4 * D * D)


def draw_mlp_first(key, part):
    return first_draw(jax.random.fold_in(key, 303), D + 2 * D * FF)


def draw_sample_second(key, part):
    return second_draw(jax.random.fold_in(key, 401), D + 4 * D * D)


def draw_feature_second(key, part):
    return second_draw(jax.random.fold_in(key, 402), D + 4 * D * D)


def draw_mlp_second(key, part):
    return second_draw(jax.random.fold_in(key, 403), D + 2 * D * FF)


def shard_levels(key, shape, pieces, least, top_value):
    factor_of, own = 1.0, jax.random.fold_in(key, 6)
    for dim, shards_of in pieces:
        draws = jnp.exp(jax.random.uniform(jax.random.fold_in(own, dim), (shards_of,), jnp.float32, least / len(pieces), top_value / len(pieces)))
        factor_of = factor_of * jnp.repeat(draws, shape[dim] // shards_of).reshape([-1 if axis == dim else 1 for axis in range(len(shape))])
    return factor_of


def normal_values(stream_key, shape, scale, reach, cuts=(), held_as=jnp.bfloat16):
    values = scale * jax.random.normal(stream_key, shape, jnp.float32)
    if cuts:
        values = values * shard_levels(stream_key, shape, cuts, -0.22, 0.18)
    return jnp.clip(values, -reach, reach).astype(held_as)


def setup_inputs(seed: int = 0) -> dict:
    seeds = jax.random.split(jax.random.key(seed), 14)
    cells = normal_values(seeds[0], (TASKS, SEQ, FMAX, D), 1.0, 6.0, ((0, 8), (1, 4)))
    out_grad = normal_values(seeds[1], (TASKS, SEQ, FMAX, D), 1.0, 6.0, ((0, 8), (1, 4)))
    sample_counts = draw_sample_counts(jax.random.fold_in(seeds[13], 71), 0)
    feature_counts = draw_feature_counts(jax.random.fold_in(seeds[13], 71), 0)
    sample_block = draw_sample_block(jax.random.fold_in(seeds[13], 71), 0)
    sample_first = draw_sample_first(jax.random.fold_in(seeds[13], 71), 0)
    sample_second = draw_sample_second(jax.random.fold_in(seeds[13], 71), 0)
    feature_block = draw_feature_block(jax.random.fold_in(seeds[13], 71), 0)
    feature_first = draw_feature_first(jax.random.fold_in(seeds[13], 71), 0)
    feature_second = draw_feature_second(jax.random.fold_in(seeds[13], 71), 0)
    mlp_block = draw_mlp_block(jax.random.fold_in(seeds[13], 71), 0)
    mlp_first = draw_mlp_first(jax.random.fold_in(seeds[13], 71), 0)
    mlp_second = draw_mlp_second(jax.random.fold_in(seeds[13], 71), 0)
    return dict(cells=cells, out_grad=out_grad, sample_counts=sample_counts, feature_counts=feature_counts, sample_block=sample_block, sample_first=sample_first, sample_second=sample_second, feature_block=feature_block, feature_first=feature_first, feature_second=feature_second, mlp_block=mlp_block, mlp_first=mlp_first, mlp_second=mlp_second)


@jax.custom_vjp
def low(v):
    return lax.optimization_barrier(v.astype(jnp.bfloat16)).astype(jnp.float32)

@jax.custom_vjp
def low_back(v):
    return v

def low_keep(v):
    return (low(v), None)

def low_pass(kept, grad):
    return (grad,)

def back_keep(v):
    return (v, None)

def back_low(kept, grad):
    return (low(grad),)
low.defvjp(low_keep, low_pass)
low_back.defvjp(back_keep, back_low)
EPS_NORM = 1e-05
EPS_ADAM = 1e-06
STEP_RATE = 0.5
BIG_NEGATIVE = -1e+30

def normalize(hidden, gain_row):
    centre = lax.optimization_barrier(jnp.mean(hidden, -1, keepdims=True))
    shifted = hidden - centre
    spread = lax.optimization_barrier(jnp.mean(shifted * shifted, -1, keepdims=True))
    return shifted * lax.rsqrt(spread + EPS_NORM) * gain_row

def unpack(flat_params, width_in, width_mid):
    gain_row = flat_params[:D]
    w_in = flat_params[D:D + D * width_in].reshape(D, width_in)
    w_out = flat_params[D + D * width_in:].reshape(width_mid, D)
    return (gain_row, w_in, w_out)

def attend(normed, w_in, w_out, key_live):
    batch_count, length = (normed.shape[0], normed.shape[1])
    packed = low_back(low(jnp.einsum('bld,de->ble', normed, w_in, precision=lax.Precision.HIGHEST)))
    shaped = packed.reshape(batch_count, length, 3, HEADS, HEAD_DIM)
    queries, key_rows, values = (shaped[:, :, 0], shaped[:, :, 1], shaped[:, :, 2])
    scores = low_back(jnp.einsum('bqhe,bkhe->bhqk', queries, key_rows, precision=lax.Precision.HIGHEST) * HEAD_DIM ** (-0.5))
    scores = jnp.where(key_live, scores, BIG_NEGATIVE)
    probability = low(jax.nn.softmax(scores, axis=-1))
    attended = jnp.einsum('bhqk,bkhe->bqhe', probability, values, precision=lax.Precision.HIGHEST)
    attended = low_back(low(attended.reshape(batch_count, length, D)))
    return low_back(jnp.einsum('bld,de->ble', attended, w_out, precision=lax.Precision.HIGHEST))

def task_forward(hidden_in, sample_count, feature_count, blocks):
    (gain_one, in_one, out_one), (gain_two, in_two, out_two), (gain_three, up_weight, down_weight) = blocks
    sample_live = jnp.arange(SEQ, dtype=jnp.int32) < sample_count
    feature_live = jnp.arange(FMAX, dtype=jnp.int32) < feature_count
    normed_one = low(normalize(hidden_in, gain_one))
    branch_one = attend(jnp.swapaxes(normed_one, 0, 1), in_one, out_one, sample_live)
    hidden_one = hidden_in + jnp.swapaxes(branch_one, 0, 1)
    normed_two = low(normalize(hidden_one, gain_two))
    hidden_two = hidden_one + attend(normed_two, in_two, out_two, feature_live)
    normed_three = low(normalize(hidden_two, gain_three))
    upward = low_back(jnp.einsum('sfd,de->sfe', normed_three, up_weight, precision=lax.Precision.HIGHEST))
    activated = low_back(low(jax.nn.gelu(upward, approximate=False)))
    branch_three = low_back(jnp.einsum('sfe,ed->sfd', activated, down_weight, precision=lax.Precision.HIGHEST))
    hidden_three = hidden_two + branch_three
    cell_live = sample_live[:, None, None] & feature_live[None, :, None]
    return jnp.where(cell_live, hidden_three, 0.0)

def forward(hidden_all, sample_flat, feature_flat, mlp_flat, sample_counts, feature_counts):
    blocks = (unpack(low(sample_flat), 3 * D, D), unpack(low(feature_flat), 3 * D, D), unpack(low(mlp_flat), FF, FF))

    def one_task(inputs):
        return task_forward(inputs[0], inputs[1], inputs[2], blocks)
    return lax.map(jax.checkpoint(one_task), (hidden_all, sample_counts, feature_counts))

def lamb_update(master, first, second, grad_flat, width_in):
    first_new = 0.5 * first + 0.5 * grad_flat
    second_new = 0.5 * second + 0.5 * grad_flat * grad_flat
    direction = first_new / (jnp.sqrt(second_new) + EPS_ADAM)
    boundaries = (0, D, D + D * width_in, master.shape[0])
    norm_rows = []
    new_pieces = []
    for part_index in range(3):
        piece_master = master[boundaries[part_index]:boundaries[part_index + 1]]
        piece_step = direction[boundaries[part_index]:boundaries[part_index + 1]]
        weight_norm = jnp.sqrt(jnp.sum(piece_master * piece_master))
        update_norm = jnp.sqrt(jnp.sum(piece_step * piece_step))
        norm_rows.append(jnp.stack([weight_norm, update_norm]))
        new_pieces.append(piece_master - STEP_RATE * (weight_norm / (update_norm + EPS_ADAM)) * piece_step)
    master_new = jnp.concatenate(new_pieces)
    return (first_new, second_new, master_new, jnp.stack(norm_rows))

def reference(cells, out_grad, sample_counts, feature_counts, sample_block, sample_first, sample_second, feature_block, feature_first, feature_second, mlp_block, mlp_first, mlp_second):

    def wrapped(hidden_all, sample_flat, feature_flat, mlp_flat):
        return forward(hidden_all, sample_flat, feature_flat, mlp_flat, sample_counts, feature_counts)
    result, pullback = jax.vjp(wrapped, cells.astype(jnp.float32), sample_block, feature_block, mlp_block)
    cells_grad, sample_grad, feature_grad, mlp_grad = pullback(out_grad.astype(jnp.float32))
    sample_out = lamb_update(sample_block, sample_first, sample_second, sample_grad, 3 * D)
    feature_out = lamb_update(feature_block, feature_first, feature_second, feature_grad, 3 * D)
    mlp_out = lamb_update(mlp_block, mlp_first, mlp_second, mlp_grad, FF)
    norm_pairs = jnp.concatenate([sample_out[3], feature_out[3], mlp_out[3]], 0)
    return (result.astype(jnp.bfloat16), cells_grad, sample_grad, sample_out[0], sample_out[1], sample_out[2], sample_out[2].astype(jnp.bfloat16), feature_grad, feature_out[0], feature_out[1], feature_out[2], feature_out[2].astype(jnp.bfloat16), mlp_grad, mlp_out[0], mlp_out[1], mlp_out[2], mlp_out[2].astype(jnp.bfloat16), norm_pairs)
```

```python
import jax
import jax.numpy as jnp
from jax import lax
from jax.experimental import pallas as pl
from jax.experimental.pallas import tpu as pltpu
from jax.sharding import PartitionSpec as P

D = 512
HEADS = 8
HEAD_DIM = 64
FF = 2048


EPS_NORM = 1e-05
EPS_ADAM = 1e-06
STEP_RATE = 0.5
BIG_NEGATIVE = -1e30


def normalize(hidden, gain_row):
    centre = jnp.mean(hidden, -1, keepdims=True)
    shifted = hidden - centre
    spread = jnp.mean(shifted * shifted, -1, keepdims=True)
    return shifted * lax.rsqrt(spread + EPS_NORM) * gain_row


def norm_backward(hidden, gain_row, normed_grad):
    _, pullback = jax.vjp(normalize, hidden, gain_row)
    return pullback(normed_grad)


def gelu_exact(upward):
    return jax.nn.gelu(upward, approximate=False)


def contract_rows(left, right):
    return lax.dot_general(
        left, right, (((0,), (0,)), ((), ())), preferred_element_type=jnp.float32
    )


def times_transpose(left, right):
    return lax.dot_general(
        left, right, (((1,), (1,)), ((), ())), preferred_element_type=jnp.float32
    )


def unpack(flat_params, width_in, width_mid):
    gain_row = flat_params[:D].astype(jnp.float32)
    w_in = flat_params[D : D + D * width_in].reshape(D, width_in)
    w_out = flat_params[D + D * width_in :].reshape(width_mid, D)
    return (gain_row, w_in, w_out)


def fetch_forward(master):
    return lax.all_gather(master.astype(jnp.bfloat16), ("task", "samp"), axis=0, tiled=True)


def fetch_again(master):
    return lax.all_gather(master.astype(jnp.bfloat16), ("task", "samp"), axis=0, tiled=True)


def reduce_grads(gain_grad, in_grad, out_grad_matrix):
    flat_grads = jnp.concatenate([gain_grad, in_grad.reshape(-1), out_grad_matrix.reshape(-1)])
    return lax.psum_scatter(flat_grads, ("task", "samp"), scatter_dimension=0, tiled=True)


def group_size(feature_total, most):
    chosen = 1
    for candidate in range(1, most + 1):
        if feature_total % candidate == 0:
            chosen = candidate
    return chosen


def lamb_prepare(grad_shard, master, first, second, width_in):
    first_new = 0.5 * first + 0.5 * grad_shard
    second_new = 0.5 * second + 0.5 * grad_shard * grad_shard
    direction = first_new / (jnp.sqrt(second_new) + EPS_ADAM)
    entries = master.shape[0]
    position = lax.axis_index(("task", "samp")) * entries + jnp.arange(entries, dtype=jnp.int32)
    segment = (position >= D).astype(jnp.int32) + (position >= D + D * width_in).astype(jnp.int32)
    member = segment[None, :] == jnp.arange(3, dtype=jnp.int32)[:, None]
    weight_sums = jnp.sum(jnp.where(member, (master * master)[None, :], 0.0), 1)
    update_sums = jnp.sum(jnp.where(member, (direction * direction)[None, :], 0.0), 1)
    return (first_new, second_new, direction, member, jnp.stack([weight_sums, update_sums], 1))


def lamb_finish(master, block_state, trust_ratio):
    factor = jnp.sum(jnp.where(block_state[3], trust_ratio[:, None], 0.0), 0)
    return master - STEP_RATE * factor * block_state[2]


def sample_scores(query_part, key_part, key_live, score_scale):
    scores = (
        jnp.einsum("qfhe,kfhe->fhqk", query_part, key_part, preferred_element_type=jnp.float32)
        * score_scale
    )
    return jnp.where(key_live, scores, BIG_NEGATIVE)


def sample_forward(queries, pairs_all, key_live, block_features, score_scale):
    local_rows, features = (queries.shape[0], queries.shape[1])

    def one_block(block_index, results):
        attended, log_totals = results
        offset = block_index * block_features
        query_part = lax.dynamic_slice_in_dim(queries, offset, block_features, 1)
        pair_part = lax.dynamic_slice_in_dim(pairs_all, offset, block_features, 1)
        scores = sample_scores(query_part, pair_part[:, :, 0], key_live, score_scale)
        row_top = jnp.max(scores, -1, keepdims=True)
        exponent = jnp.exp(scores - row_top)
        row_total = jnp.sum(exponent, -1, keepdims=True)
        probability = (exponent / row_total).astype(jnp.bfloat16)
        block_out = jnp.einsum(
            "fhqk,kfhe->qfhe", probability, pair_part[:, :, 1], preferred_element_type=jnp.float32
        )
        attended = lax.dynamic_update_slice_in_dim(
            attended, block_out.astype(jnp.bfloat16), offset, 1
        )
        log_totals = lax.dynamic_update_slice_in_dim(
            log_totals, (row_top + jnp.log(row_total))[..., 0], offset, 0
        )
        return (attended, log_totals)

    start_state = (
        jnp.zeros(queries.shape, jnp.bfloat16),
        jnp.zeros((features, HEADS, local_rows), jnp.float32),
    )
    return lax.fori_loop(0, features // block_features, one_block, start_state)


def query_side(query_part, pair_part, grad_part, log_part, key_live, score_scale):
    key_part = pair_part[:, :, 0]
    value_part = pair_part[:, :, 1]
    scores = sample_scores(query_part, key_part, key_live, score_scale)
    probability = jnp.exp(scores - log_part[..., None])
    prob_grad = jnp.einsum(
        "qfhe,kfhe->fhqk", grad_part, value_part, preferred_element_type=jnp.float32
    )
    row_inner = jnp.sum(probability * prob_grad, -1, keepdims=True)
    score_grad = (probability * (prob_grad - row_inner)).astype(jnp.bfloat16)
    query_block = (
        jnp.einsum("fhqk,kfhe->qfhe", score_grad, key_part, preferred_element_type=jnp.float32)
        * score_scale
    )
    return (probability, score_grad, row_inner, query_block)


def sample_backward(
    queries, pairs_all, key_live, log_totals, attended_grad, block_features, score_scale
):
    local_rows, features = (queries.shape[0], queries.shape[1])

    def one_block(block_index, results):
        query_grads, pair_grads = results
        offset = block_index * block_features
        query_part = lax.dynamic_slice_in_dim(queries, offset, block_features, 1)
        pair_part = lax.dynamic_slice_in_dim(pairs_all, offset, block_features, 1)
        grad_part = lax.dynamic_slice_in_dim(attended_grad, offset, block_features, 1)
        log_part = lax.dynamic_slice_in_dim(log_totals, offset, block_features, 0)
        probability, score_grad, row_inner, query_block = query_side(
            query_part, pair_part, grad_part, log_part, key_live, score_scale
        )
        key_block = (
            jnp.einsum(
                "fhqk,qfhe->kfhe", score_grad, query_part, preferred_element_type=jnp.float32
            )
            * score_scale
        )
        value_block = jnp.einsum(
            "fhqk,qfhe->kfhe",
            probability.astype(jnp.bfloat16),
            grad_part,
            preferred_element_type=jnp.float32,
        )
        pair_terms = jnp.stack([key_block, value_block], 2)
        pair_local = lax.psum_scatter(
            pair_terms.astype(jnp.bfloat16), "samp", scatter_dimension=0, tiled=True
        ).astype(jnp.float32)
        query_grads = lax.dynamic_update_slice_in_dim(query_grads, query_block, offset, 1)
        pair_grads = lax.dynamic_update_slice_in_dim(pair_grads, pair_local, offset, 1)
        return (query_grads, pair_grads)

    start_state = (
        jnp.zeros((local_rows, features, HEADS, HEAD_DIM), jnp.float32),
        jnp.zeros((local_rows, features, 2, HEADS, HEAD_DIM), jnp.float32),
    )
    return lax.fori_loop(0, features // block_features, one_block, start_state)


def on_device(
    cells,
    out_grad,
    sample_counts,
    feature_counts,
    sample_block,
    sample_first,
    sample_second,
    feature_block,
    feature_first,
    feature_second,
    mlp_block,
    mlp_first,
    mlp_second,
):
    local_rows, features = (cells.shape[1], cells.shape[2])
    flat_rows = local_rows * features
    seq_all = local_rows * lax.axis_size("samp")
    score_scale = HEAD_DIM ** (-0.5)
    block_features = group_size(features, max(1, 2048 // (HEADS * local_rows)))
    sample_index = lax.axis_index("samp") * local_rows + jnp.arange(local_rows, dtype=jnp.int32)
    sample_live = sample_index < sample_counts[0]
    key_live = jnp.arange(seq_all, dtype=jnp.int32) < sample_counts[0]
    feature_live = jnp.arange(features, dtype=jnp.int32) < feature_counts[0]
    cell_live = sample_live[:, None, None] & feature_live[None, :, None]
    hidden_in = cells[0].astype(jnp.float32)
    gain_one, in_one, out_one = unpack(fetch_forward(sample_block), 3 * D, D)
    normed_one = normalize(hidden_in, gain_one).astype(jnp.bfloat16)
    packed_one = jnp.dot(
        normed_one.reshape(flat_rows, D), in_one, preferred_element_type=jnp.float32
    )
    packed_one = packed_one.astype(jnp.bfloat16).reshape(local_rows, features, 3, HEADS, HEAD_DIM)
    queries_one = packed_one[:, :, 0]
    pairs_local = packed_one[:, :, 1:]
    pairs_all = lax.all_gather(pairs_local, "samp", axis=0, tiled=True)
    attended_one, log_totals = sample_forward(
        queries_one, pairs_all, key_live, block_features, score_scale
    )
    attended_one_rows = attended_one.reshape(flat_rows, D)
    branch_one = jnp.dot(attended_one_rows, out_one, preferred_element_type=jnp.float32)
    hidden_one = hidden_in + branch_one.reshape(local_rows, features, D)
    gain_two, in_two, out_two = unpack(fetch_forward(feature_block), 3 * D, D)
    normed_two = normalize(hidden_one, gain_two).astype(jnp.bfloat16).reshape(flat_rows, D)
    packed_two = jnp.dot(normed_two, in_two, preferred_element_type=jnp.float32)
    packed_two = packed_two.astype(jnp.bfloat16).reshape(local_rows, features, 3, HEADS, HEAD_DIM)
    queries_two, key_two, value_two = (
        packed_two[:, :, 0],
        packed_two[:, :, 1],
        packed_two[:, :, 2],
    )
    scores_two = (
        jnp.einsum("sqhe,skhe->shqk", queries_two, key_two, preferred_element_type=jnp.float32)
        * score_scale
    )
    scores_two = jnp.where(feature_live, scores_two, BIG_NEGATIVE)
    row_top = jnp.max(scores_two, -1, keepdims=True)
    exponent = jnp.exp(scores_two - row_top)
    probability_two = exponent / jnp.sum(exponent, -1, keepdims=True)
    prob_low_two = probability_two.astype(jnp.bfloat16)
    attended_two = jnp.einsum(
        "shqk,skhe->sqhe", prob_low_two, value_two, preferred_element_type=jnp.float32
    )
    attended_two_rows = attended_two.reshape(flat_rows, D).astype(jnp.bfloat16)
    branch_two = jnp.dot(attended_two_rows, out_two, preferred_element_type=jnp.float32)
    hidden_two = hidden_one + branch_two.reshape(local_rows, features, D)
    gain_three, up_weight, down_weight = unpack(fetch_forward(mlp_block), FF, FF)
    normed_three = normalize(hidden_two, gain_three).astype(jnp.bfloat16).reshape(flat_rows, D)
    upward = jnp.dot(normed_three, up_weight, preferred_element_type=jnp.float32)
    activated = gelu_exact(upward).astype(jnp.bfloat16)
    branch_three = jnp.dot(activated, down_weight, preferred_element_type=jnp.float32)
    hidden_three = hidden_two + branch_three.reshape(local_rows, features, D)
    layer_out = jnp.where(cell_live, hidden_three, 0.0).astype(jnp.bfloat16)[None]
    top_grad = jnp.where(cell_live, out_grad[0], jnp.zeros((), jnp.bfloat16))
    top_rows = top_grad.reshape(flat_rows, D)
    gain_three, up_weight, down_weight = unpack(fetch_again(mlp_block), FF, FF)
    down_grad = contract_rows(activated, top_rows)
    act_grad = times_transpose(top_rows, down_weight).astype(jnp.bfloat16)
    _, gelu_pull = jax.vjp(gelu_exact, upward)
    up_grad = gelu_pull(act_grad.astype(jnp.float32))[0].astype(jnp.bfloat16)
    upw_grad = contract_rows(normed_three, up_grad)
    normed_grad = times_transpose(up_grad, up_weight).reshape(local_rows, features, D)
    hidden_grad, gain_three_grad = norm_backward(hidden_two, gain_three, normed_grad)
    grad_two = top_grad.astype(jnp.float32) + hidden_grad
    mlp_shard = reduce_grads(gain_three_grad, upw_grad, down_grad)
    mlp_state = lamb_prepare(mlp_shard, mlp_block, mlp_first, mlp_second, FF)
    gain_two, in_two, out_two = unpack(fetch_again(feature_block), 3 * D, D)
    branch_grad = grad_two.astype(jnp.bfloat16).reshape(flat_rows, D)
    out_two_grad = contract_rows(attended_two_rows, branch_grad)
    attended_grad = (
        times_transpose(branch_grad, out_two)
        .astype(jnp.bfloat16)
        .reshape(local_rows, features, HEADS, HEAD_DIM)
    )
    prob_grad = jnp.einsum(
        "sqhe,skhe->shqk", attended_grad, value_two, preferred_element_type=jnp.float32
    )
    row_inner = jnp.sum(probability_two * prob_grad, -1, keepdims=True)
    score_grad = (probability_two * (prob_grad - row_inner)).astype(jnp.bfloat16)
    query_grad = (
        jnp.einsum("shqk,skhe->sqhe", score_grad, key_two, preferred_element_type=jnp.float32)
        * score_scale
    )
    key_grad = (
        jnp.einsum("shqk,sqhe->skhe", score_grad, queries_two, preferred_element_type=jnp.float32)
        * score_scale
    )
    value_grad = jnp.einsum(
        "shqk,sqhe->skhe", prob_low_two, attended_grad, preferred_element_type=jnp.float32
    )
    packed_grad = (
        jnp.stack([query_grad, key_grad, value_grad], 2)
        .astype(jnp.bfloat16)
        .reshape(flat_rows, 3 * D)
    )
    in_two_grad = contract_rows(normed_two, packed_grad)
    normed_grad = times_transpose(packed_grad, in_two).reshape(local_rows, features, D)
    hidden_grad, gain_two_grad = norm_backward(hidden_one, gain_two, normed_grad)
    grad_one = grad_two + hidden_grad
    feature_shard = reduce_grads(gain_two_grad, in_two_grad, out_two_grad)
    feature_state = lamb_prepare(feature_shard, feature_block, feature_first, feature_second, 3 * D)
    gain_one, in_one, out_one = unpack(fetch_again(sample_block), 3 * D, D)
    pairs_all = lax.all_gather(pairs_local, "samp", axis=0, tiled=True)
    branch_grad = grad_one.astype(jnp.bfloat16).reshape(flat_rows, D)
    out_one_grad = contract_rows(attended_one_rows, branch_grad)
    attended_grad = (
        times_transpose(branch_grad, out_one)
        .astype(jnp.bfloat16)
        .reshape(local_rows, features, HEADS, HEAD_DIM)
    )
    query_grads, pair_grads = sample_backward(
        queries_one, pairs_all, key_live, log_totals, attended_grad, block_features, score_scale
    )
    packed_grad = (
        jnp.concatenate([query_grads[:, :, None], pair_grads], 2)
        .astype(jnp.bfloat16)
        .reshape(flat_rows, 3 * D)
    )
    in_one_grad = contract_rows(normed_one.reshape(flat_rows, D), packed_grad)
    normed_grad = times_transpose(packed_grad, in_one).reshape(local_rows, features, D)
    hidden_grad, gain_one_grad = norm_backward(hidden_in, gain_one, normed_grad)
    cells_grad = (grad_one + hidden_grad)[None]
    sample_shard = reduce_grads(gain_one_grad, in_one_grad, out_one_grad)
    sample_state = lamb_prepare(sample_shard, sample_block, sample_first, sample_second, 3 * D)
    totals = lax.psum(
        jnp.concatenate([sample_state[4], feature_state[4], mlp_state[4]], 0), ("task", "samp")
    )
    norm_pairs = jnp.sqrt(totals)
    trust_ratio = norm_pairs[:, 0] / (norm_pairs[:, 1] + EPS_ADAM)
    sample_master = lamb_finish(sample_block, sample_state, trust_ratio[0:3])
    feature_master = lamb_finish(feature_block, feature_state, trust_ratio[3:6])
    mlp_master = lamb_finish(mlp_block, mlp_state, trust_ratio[6:9])
    return (
        layer_out,
        cells_grad,
        sample_shard,
        sample_state[0],
        sample_state[1],
        sample_master,
        sample_master.astype(jnp.bfloat16),
        feature_shard,
        feature_state[0],
        feature_state[1],
        feature_master,
        feature_master.astype(jnp.bfloat16),
        mlp_shard,
        mlp_state[0],
        mlp_state[1],
        mlp_master,
        mlp_master.astype(jnp.bfloat16),
        norm_pairs,
    )


D = 512
MESH = pl.DeviceIdType.MESH
BF = jnp.bfloat16
F32 = jnp.float32
NEG = -1e30


def mult(value, factor):
    return pl.multiple_of(value, factor)


def nt(left, right):
    return lax.dot_general(left, right, (((1,), (1,)), ((), ())), preferred_element_type=F32)


def nn(left, right):
    return lax.dot_general(left, right, (((1,), (0,)), ((), ())), preferred_element_type=F32)


def here():
    return lax.axis_index("task"), lax.axis_index("samp")


def peers(t, s):
    return (
        (jnp.bitwise_xor(t, 1), s),
        (jnp.bitwise_xor(t, 2), s),
        (jnp.bitwise_xor(t, 4), s),
        (t, (s + 1) % 4),
        (t, (s + 2) % 4),
        (t, (s + 3) % 4),
    )


def enter(t, s):
    barrier = pltpu.get_barrier_semaphore()
    for peer in peers(t, s):
        pl.semaphore_signal(barrier, inc=1, device_id=peer, device_id_type=MESH)
    return barrier


def send(src, dst, ssem, rsem, peer):
    copy = pltpu.make_async_remote_copy(
        src_ref=src, dst_ref=dst, send_sem=ssem, recv_sem=rsem, device_id=peer, device_id_type=MESH
    )
    copy.start()
    return copy


class Gather:
    def __init__(self, buf, half, ssem, rsem, t, s):
        self.buf, self.t, self.s = buf, t, s
        rows = buf.shape[1]
        self.ha, self.hb = pl.ds(0, half), pl.ds(half, rows - half)
        self.all = pl.ds(0, rows)
        self.ssem, self.rsem = ssem, rsem
        self.count = 0
        self.copies = []
        self.tx, self.ty = jnp.bitwise_xor(t, 2), jnp.bitwise_xor(t, 4)
        self.txy, self.tc = jnp.bitwise_xor(t, 6), jnp.bitwise_xor(t, 1)

    def go(self, slots, rows, peer):
        view = self.buf.at[slots, rows]
        i = self.count
        self.count += 1
        copy = send(view, view, self.ssem.at[i], self.rsem.at[i], peer)
        self.copies.append(copy)
        return copy

    def four(self, t):
        return pl.ds(4 * t, 4)

    def z(self):
        t, s = self.t, self.s
        own = pl.ds(4 * t + s, 1)
        self.zc = [self.go(own, self.all, (t, (s + k) % 4)) for k in (1, 2, 3)]

    def one(self):
        for copy in self.zc:
            copy.wait_recv()
        t, s = self.t, self.s
        self.x1 = self.go(self.four(t), self.ha, (self.tx, s))
        self.y1 = self.go(self.four(t), self.hb, (self.ty, s))
        self.c = [self.go(self.four(t), self.all, (self.tc, s))]

    def two(self):
        s = self.s
        t = self.t
        self.x1.wait_recv()
        self.y2 = [
            self.go(self.four(t), self.ha, (self.ty, s)),
            self.go(self.four(self.tx), self.ha, (self.ty, s)),
        ]
        self.y1.wait_recv()
        self.x2 = [
            self.go(self.four(t), self.hb, (self.tx, s)),
            self.go(self.four(self.ty), self.hb, (self.tx, s)),
        ]
        self.c.append(self.go(self.four(self.tx), self.ha, (self.tc, s)))
        self.c.append(self.go(self.four(self.ty), self.hb, (self.tc, s)))

    def three(self):
        s = self.s
        for copy in self.y2 + self.x2:
            copy.wait_recv()
        self.c.append(self.go(self.four(self.ty), self.ha, (self.tc, s)))
        self.c.append(self.go(self.four(self.txy), self.ha, (self.tc, s)))
        self.c.append(self.go(self.four(self.tx), self.hb, (self.tc, s)))
        self.c.append(self.go(self.four(self.txy), self.hb, (self.tc, s)))

    def end(self):
        for copy in self.c:
            copy.wait_recv()

    def drain(self):
        for copy in self.copies:
            copy.wait_send()


def realign(m_ref, sh_ref, d, rows, out_ref, out_at, roll_to):
    total = m_ref.shape[0]
    q, p = d // 8, d % 8
    lane = lax.broadcasted_iota(jnp.int32, (total, 128), 1)
    roll_to[0:8, :] = jnp.zeros((8, 128), F32)
    rolled = pltpu.roll(m_ref[...], 16 * p, 1)
    roll_to[8 : 8 + total, :] = rolled
    sh_ref[0:8, :] = jnp.zeros((8, 128), F32)
    sh_ref[8 : 8 + total, :] = jnp.where(lane < 16 * p, roll_to[7 : 7 + total, :], rolled)
    firsts = []
    for b in range(4):
        out_ref[out_at, 0:rows, 128 * b : 128 * b + 128] = sh_ref[pl.ds(12 - q + b, rows, stride=4), :].astype(BF)
        firsts.append(sh_ref[pl.ds(8 - q + b, 1), :])
    return jnp.concatenate(firsts, 1)


def spread(buf, firsts, kind, rows, lo, hi, put):
    tail = lax.broadcasted_iota(jnp.int32, (8, D), 0) == 7

    def body(i, _):
        nxt = jnp.minimum(i + 1, 31)
        row = firsts[nxt, 64:80, :].astype(F32)[kind : kind + 1, :]
        block = buf[i, 0:rows, :].astype(F32)
        last = block[rows - 8 : rows, :] + jnp.where(tail & (i < 31), row, 0.0)
        put(i - lo, block[0 : rows - 8, :], last)
        return 0

    lax.fori_loop(lo, hi, body, 0)


def put_f32(dst, rows):
    def put(i, head, last):
        for b in range(4):
            cols = slice(128 * b, 128 * b + 128)
            dst[b, pl.ds(mult(i * rows, rows), rows - 8), :] = head[:, cols]
            dst[b, pl.ds(mult(i * rows + rows - 8, 8), 8), :] = last[:, cols]

    return put


def put_bf(dst, rows):
    def put(i, head, last):
        dst[pl.ds(mult(i * rows, rows), rows), :] = jnp.concatenate([head, last], 0).astype(BF)

    return put


def split_columns(wide, ways, dst):
    def body(i, _):
        for j in range(ways):
            for b in range(4):
                piece = wide[b, pl.ds(64 * ways * i + j, 64, stride=ways), :]
                dst[j, pl.ds(mult(64 * i, 64), 64), 128 * b : 128 * b + 128] = piece.astype(BF)
        return 0

    lax.fori_loop(0, 8, body, 0)


def halves():
    lane = lax.broadcasted_iota(jnp.int32, (128, 128), 1)
    return lane < 64


def attend_chunk(qkv, c, live, out, out_at):
    left = halves()
    one = jnp.where(left, 0.125, 0.0).astype(BF)
    two = jnp.where(left, 0.0, 0.125).astype(BF)

    def body(h, _):
        cols = pl.ds(mult(h * 128, 128), 128)
        q = qkv[0, pl.ds(mult(c * 128, 128), 128), cols]
        qm = jnp.concatenate([q * one, q * two], 0)
        scores = jnp.where(live, nt(qm, qkv[1, :, cols]), NEG)
        top = jnp.max(scores, 1, keepdims=True)
        e = jnp.exp(scores - top)
        prob = (e * (1.0 / jnp.sum(e, 1, keepdims=True))).astype(BF)
        o = nn(prob, qkv[2, :, cols])
        out[out_at, :, cols] = jnp.where(left, o[0:128], o[128:256]).astype(BF)
        return 0

    lax.fori_loop(0, 4, body, 0)


def kernel_a(
    cnt, cells, m1, m2, m3,
    o1rows, w1, wo1, w2, wo2, wup, wdn, gains, qkv, a1, cf,
    g1, g2, g3, wide, sh, ro, o1c, w1v, wo1v, w2v, wo2v, wupv, wdnv, qkvv,
    gs, gr, as_, ar, os_, or_, lsem,
):
    t, s = here()
    d = 4 * t + s
    barrier = enter(t, s)
    ga = Gather(g1, 32, gs.at[0], gr.at[0], t, s)
    gb = Gather(g2, 32, gs.at[1], gr.at[1], t, s)
    gc = Gather(g3, 64, gs.at[2], gr.at[2], t, s)
    f1 = realign(m1, sh, d, 64, g1, d, ro)
    f2 = realign(m2, sh, d, 64, g2, d, ro)
    f3 = realign(m3, sh, d, 128, g3, d, ro)
    row = lax.broadcasted_iota(jnp.int32, (16, D), 0)
    firsts = jnp.where(row == 0, f1, jnp.where(row == 1, f2, jnp.where(row == 2, f3, 0.0)))
    g1[d, 64:80, :] = firsts.astype(BF)
    pl.semaphore_wait(barrier, 6)
    ga.z()
    cf[s] = cells[s]
    moves = [
        send(cells.at[(s + k) % 4], cf.at[s], as_.at[k - 1], ar.at[k - 1], (t, (s + k) % 4)) for k in (1, 2, 3)
    ]
    ga.one()
    ga.two()
    for copy in moves:
        copy.wait_recv()
    gb.z()
    gc.z()
    ga.three()
    ga.end()
    spread(g1, g1, 0, 64, 0, 24, put_f32(wide, 64))
    split_columns(wide, 3, w1v)
    spread(g1, g1, 0, 64, 24, 32, put_bf(wo1v, 64))
    gains[...] = g1[0, 64:80, :].astype(F32)[0:8]
    gain = g1[0, 64:80, :].astype(F32)[0:1]

    def norm(i, _):
        h = cf[i].astype(F32)
        mean = jnp.mean(h, 1, keepdims=True)
        x = h - mean
        var = jnp.mean(x * x, 1, keepdims=True)
        a1[pl.ds(mult(i * 128, 128), 128), :] = (x * lax.rsqrt(var + 1e-5) * gain).astype(BF)
        return 0

    lax.fori_loop(0, 4, norm, 0)

    def project(i, _):
        j, r = i // 4, i % 4
        rows = pl.ds(mult(r * 128, 128), 128)
        qkvv[j, rows, :] = nn(a1[rows, :], w1v[j]).astype(BF)
        return 0

    lax.fori_loop(0, 12, project, 0)
    live = lax.broadcasted_iota(jnp.int32, (1, 512), 1) < cnt[0]
    backs = []
    local = []

    def keep(src, dst):
        copy = pltpu.make_async_copy(src, dst, lsem.at[len(local)])
        copy.start()
        local.append(copy)

    keep(w1v, w1)
    keep(wo1v, wo1)
    keep(qkvv, qkv)
    for k in (2, 1, 3, 0):
        c = (s + k) % 4
        if k:
            attend_chunk(qkvv, c, live, o1c, k - 1)
            backs.append(send(o1c.at[k - 1], o1rows.at[s], os_.at[k - 1], or_.at[k - 1], (t, c)))
        else:
            attend_chunk(qkvv, c, live, o1rows, s)
        if k == 2:
            gb.one()
            gc.one()
        if k == 1:
            gb.two()
            gc.two()
        if k == 3:
            gb.three()
    gb.end()
    spread(g2, g1, 1, 64, 0, 24, put_f32(wide, 64))
    split_columns(wide, 3, w2v)
    spread(g2, g1, 1, 64, 24, 32, put_bf(wo2v, 64))
    keep(w2v, w2)
    keep(wo2v, wo2)
    gc.three()
    gc.end()
    spread(g3, g1, 2, 128, 0, 16, put_f32(wide, 128))
    split_columns(wide, 4, wupv)
    keep(wupv, wup)
    spread(g3, g1, 2, 128, 16, 32, put_bf(wdnv, 128))
    keep(wdnv, wdn)
    for copy in backs:
        copy.wait_recv()
    for copy in moves + backs:
        copy.wait_send()
    ga.drain()
    gb.drain()
    gc.drain()
    for copy in local:
        copy.wait()


def call_a(cnt, cells_fm, m1, m2, m3):
    sds = jax.ShapeDtypeStruct
    vm = pl.BlockSpec(memory_space=pltpu.VMEM)
    hb = pl.BlockSpec(memory_space=pl.ANY)
    return pl.pallas_call(
        kernel_a,
        name="kernel_a",
        out_shape=(
            sds((4, 128, D), BF), sds((3, D, D), BF), sds((D, D), BF), sds((3, D, D), BF), sds((D, D), BF),
            sds((4, D, D), BF), sds((4 * D, D), BF), sds((8, D), F32), sds((3, D, D), BF), sds((D, D), BF),
            sds((4, 128, D), BF),
        ),
        in_specs=[pl.BlockSpec(memory_space=pltpu.SMEM), vm, vm, vm, vm],
        out_specs=(vm, hb, hb, hb, hb, hb, hb, vm, hb, vm, vm),
        scratch_shapes=[
            pltpu.VMEM((32, 80, D), BF), pltpu.VMEM((32, 64, D), BF), pltpu.VMEM((32, 128, D), BF),
            pltpu.VMEM((4, 4 * D, 128), F32), pltpu.VMEM((536, 128), F32), pltpu.VMEM((536, 128), F32),
            pltpu.VMEM((3, 128, D), BF),
            pltpu.VMEM((3, D, D), BF), pltpu.VMEM((D, D), BF), pltpu.VMEM((3, D, D), BF), pltpu.VMEM((D, D), BF),
            pltpu.VMEM((4, D, D), BF), pltpu.VMEM((4 * D, D), BF), pltpu.VMEM((3, D, D), BF),
            pltpu.SemaphoreType.DMA((3, 16)), pltpu.SemaphoreType.DMA((3, 16)),
            pltpu.SemaphoreType.DMA((3,)), pltpu.SemaphoreType.DMA((3,)),
            pltpu.SemaphoreType.DMA((3,)), pltpu.SemaphoreType.DMA((3,)),
            pltpu.SemaphoreType.DMA((7,)),
        ],
        compiler_params=pltpu.CompilerParams(collective_id=1, has_side_effects=True, vmem_limit_bytes=56 << 20),
    )(cnt, cells_fm, m1, m2, m3)


def pad_shard(m):
    rows = m.shape[0] // 1024 + 1
    return jnp.pad(m, (0, rows * 1024 - m.shape[0])).reshape(rows * 8, 128)


class Scatter:
    def __init__(self, part, r1, acc, ry, rx, ry2, rx2, rz, half, ssem, rsem, t, s):
        self.part, self.r1, self.acc = part, r1, acc
        self.ry, self.rx, self.ry2, self.rx2, self.rz = ry, rx, ry2, rx2, rz
        self.rows = part.shape[1]
        self.ha, self.hb = half, self.rows - half
        self.ssem, self.rsem, self.t, self.s = ssem, rsem, t, s
        self.count = 0
        self.copies = []

    def go(self, src, dst, peer):
        i = self.count
        self.count += 1
        copy = send(src, dst, self.ssem.at[i], self.rsem.at[i], peer)
        self.copies.append(copy)
        return copy

    def xor(self, e):
        return jnp.bitwise_xor(self.t, e)

    def core(self):
        tc = self.xor(1)
        self.c = [
            self.go(self.part.at[pl.ds(4 * jnp.bitwise_xor(tc, 2 * e), 4)], self.r1.at[e], (tc, self.s))
            for e in (2, 3, 1, 0)
        ]

    def core_sum(self):
        for n, e in enumerate((2, 3, 1, 0)):
            self.c[n].wait_recv()
            base = 4 * self.xor(2 * e)

            def body(j, _, e=e, base=base):
                own = self.part[base + j, :, :].astype(F32)
                self.acc[e, j, :, :] = (own + self.r1[e, j, :, :].astype(F32)).astype(BF)
                return 0

            lax.fori_loop(0, 4, body, 0)

    def one(self):
        ha, hb = pl.ds(0, self.ha), pl.ds(self.ha, self.hb)
        ty, tx, s = self.xor(4), self.xor(2), self.s
        self.y = [self.go(self.acc.at[2 + e, :, ha], self.ry.at[e], (ty, s)) for e in (0, 1)]
        self.x = [self.go(self.acc.at[1 + 2 * e, :, hb], self.rx.at[e], (tx, s)) for e in (0, 1)]

    def add(self, e, lo, size, got):
        def body(j, _):
            own = self.acc[e, j, lo : lo + size, :].astype(F32)
            self.acc[e, j, lo : lo + size, :] = (own + got(j).astype(F32)).astype(BF)
            return 0

        lax.fori_loop(0, 4, body, 0)

    def two(self):
        ha, hb = pl.ds(0, self.ha), pl.ds(self.ha, self.hb)
        ty, tx, s = self.xor(4), self.xor(2), self.s
        self.y[1].wait_recv()
        self.add(1, 0, self.ha, lambda j: self.ry[1, j, :, :])
        self.x2 = self.go(self.acc.at[1, :, ha], self.rx2, (tx, s))
        self.x[1].wait_recv()
        self.add(2, self.ha, self.hb, lambda j: self.rx[1, j, :, :])
        self.y2 = self.go(self.acc.at[2, :, hb], self.ry2, (ty, s))
        self.y[0].wait_recv()
        self.add(0, 0, self.ha, lambda j: self.ry[0, j, :, :])
        self.x[0].wait_recv()
        self.add(0, self.ha, self.hb, lambda j: self.rx[0, j, :, :])

    def three(self):
        self.x2.wait_recv()
        self.add(0, 0, self.ha, lambda j: self.rx2[j, :, :])
        self.y2.wait_recv()
        self.add(0, self.ha, self.hb, lambda j: self.ry2[j, :, :])
        t, s = self.t, self.s
        self.z = [self.go(self.acc.at[0, (s + k) % 4], self.rz.at[k - 1], (t, (s + k) % 4)) for k in (1, 2, 3)]

    def result(self):
        for copy in self.z:
            copy.wait_recv()
        total = self.acc[0, self.s, :, :].astype(F32)
        for k in range(3):
            total = total + self.rz[k, :, :].astype(F32)
        return total

    def drain(self):
        for copy in self.copies:
            copy.wait_send()


def to_shard(first, main, fl, d, out_ref):
    q, p = d // 8, d % 8
    rows = main.shape[0]
    total = out_ref.shape[0]
    fl[4 + 4 * rows : total + 8, :] = jnp.zeros((total + 4 - 4 * rows, 128), F32)
    for b in range(4):
        fl[b : b + 1, :] = first[:, 128 * b : 128 * b + 128]
        fl[pl.ds(4 + b, rows, stride=4), :] = main[:, 128 * b : 128 * b + 128]
    turn = (128 - 16 * p) % 128
    lane = lax.broadcasted_iota(jnp.int32, (total, 128), 1)
    low = pltpu.roll(fl[pl.ds(q, total), :], turn, 1)
    high = pltpu.roll(fl[pl.ds(q + 1, total), :], turn, 1)
    out_ref[...] = jnp.where(lane < 128 - 16 * p, low, high)


def last_rows(part, bound, kind, gain_row):
    rows = part.shape[1]
    at = lax.broadcasted_iota(jnp.int32, (16, D), 0) == kind

    def body(i, _):
        prev = jnp.maximum(i - 1, 0)
        row = part[prev, rows - 16 : rows, :].astype(F32)[15:16, :]
        row = jnp.where(i > 0, row, gain_row)
        bound[i, :, :] = jnp.where(at, row, bound[i, :, :].astype(F32)).astype(BF)
        return 0

    lax.fori_loop(0, 32, body, 0)


def backward_heads(h, qkv, do, live, dqkv, kt, dkv):
    left = halves()
    one, two = jnp.where(left, 1.0, 0.0).astype(BF), jnp.where(left, 0.0, 1.0).astype(BF)
    cols = pl.ds(mult(h * 128, 128), 128)
    kt[...] = jnp.transpose(qkv[1, :, cols].astype(F32)).astype(BF)
    top_lane = lax.broadcasted_iota(jnp.int32, (128, 128), 0) < 64

    def chunk(c, _):
        rows = pl.ds(mult(c * 128, 128), 128)
        q = qkv[0, rows, cols] * jnp.asarray(0.125, BF)
        qm = jnp.concatenate([q * one, q * two], 0)
        g = do[c, :, cols]
        gm = jnp.concatenate([g * one, g * two], 0)
        scores = jnp.where(live, nt(qkv[1, :, cols], qm), NEG)
        e = jnp.exp(scores - jnp.max(scores, 0, keepdims=True))
        prob = e * (1.0 / jnp.sum(e, 0, keepdims=True))
        pg = nt(qkv[2, :, cols], gm)
        inner = jnp.sum(prob * pg, 0, keepdims=True)
        sg = (prob * (pg - inner)).astype(BF)
        dk = nn(sg, qm)
        dv = nn(prob.astype(BF), gm)
        dqt = nn(kt[...], sg)
        dq = jnp.transpose(jnp.where(top_lane, dqt[:, 0:128], dqt[:, 128:256])) * 0.125
        dqkv[0, rows, cols] = dq.astype(BF)

        @pl.when(c == 0)
        def _():
            dkv[0] = dk
            dkv[1] = dv

        @pl.when(c > 0)
        def _():
            dkv[0] += dk
            dkv[1] += dv

        return 0

    lax.fori_loop(0, 4, chunk, 0)
    dqkv[1, :, cols] = dkv[0].astype(BF)
    dqkv[2, :, cols] = dkv[1].astype(BF)


def kernel_c(
    cnt, do1, qkv, a1, cf, w1, gains, grad1, p1o, p2, p3, dgain,
    cgrad, sh1, sh2, sh3,
    do, dqkv, kt, dkv, at, wide, p1, pb, dhs, dhr, fl,
    r1a, aa, rya, rxa, rya2, rxa2, rza,
    r1b, ab, ryb, rxb, ryb2, rxb2, rzb,
    r1c, ac, ryc, rxc, ryc2, rxc2, rzc,
    r1d, ad, ryd, rxd, ryd2, rxd2, rzd,
    ssem, rsem, dss, dsr, hss, hsr,
):
    t, s = here()
    d = 4 * t + s
    barrier = enter(t, s)
    do[s] = do1[s]
    pb[...] = jnp.zeros((32, 16, D), BF)
    sa = Scatter(p1, r1a, aa, rya, rxa, rya2, rxa2, rza, 32, ssem.at[0], rsem.at[0], t, s)
    sb = Scatter(p2, r1b, ab, ryb, rxb, ryb2, rxb2, rzb, 32, ssem.at[1], rsem.at[1], t, s)
    sc = Scatter(p3, r1c, ac, ryc, rxc, ryc2, rxc2, rzc, 64, ssem.at[2], rsem.at[2], t, s)
    pl.semaphore_wait(barrier, 6)
    moves = [
        send(do1.at[(s + k) % 4], do.at[s], dss.at[k - 1], dsr.at[k - 1], (t, (s + k) % 4)) for k in (1, 2, 3)
    ]
    sc.core()
    sb.core()
    sc.core_sum()
    sc.one()
    at[...] = jnp.transpose(a1[...].astype(F32)).astype(BF)
    sb.core_sum()
    for copy in moves:
        copy.wait_recv()
    live = lax.broadcasted_iota(jnp.int32, (512, 1), 0) < cnt[0]

    def heads(lo, hi):
        def body(h, _):
            backward_heads(h, qkv, do, live, dqkv, kt, dkv)
            return 0

        lax.fori_loop(lo, hi, body, 0)

    heads(0, 2)
    sc.two()
    sb.one()
    heads(2, 3)
    sc.three()
    heads(3, 4)
    sb.two()
    gain = gains[0:1, :]
    dg = jnp.zeros((1, D), F32)

    def norm_back(i, dg):
        rows = pl.ds(mult(i * 128, 128), 128)
        da = nt(dqkv[0, rows, :], w1[0]) + nt(dqkv[1, rows, :], w1[1]) + nt(dqkv[2, rows, :], w1[2])
        h = cf[i].astype(F32)
        x = h - jnp.mean(h, 1, keepdims=True)
        rstd = lax.rsqrt(jnp.mean(x * x, 1, keepdims=True) + 1e-5)
        x = x * rstd
        dg = dg + jnp.sum(da * x, 0, keepdims=True)
        dx = da * gain
        dh = rstd * (dx - jnp.mean(dx, 1, keepdims=True) - x * jnp.mean(dx * x, 1, keepdims=True))
        dhs[i] = dh.astype(BF)
        return dg

    dg = lax.fori_loop(0, 4, norm_back, dg)

    def weights(i, _):
        j, r = i // 4, i % 4
        part = nn(at[pl.ds(mult(r * 128, 128), 128), :], dqkv[j])
        for b in range(4):
            wide[b, pl.ds(384 * r + j, 128, stride=3), :] = part[:, 128 * b : 128 * b + 128]
        return 0

    lax.fori_loop(0, 12, weights, 0)

    def narrow(i, _):
        rows = pl.ds(mult(i * 64, 64), 64)
        for b in range(4):
            p1[i, :, 128 * b : 128 * b + 128] = wide[b, rows, :].astype(BF)
        return 0

    lax.fori_loop(0, 24, narrow, 0)

    def copy_out(i, _):
        p1[24 + i] = p1o[pl.ds(mult(i * 64, 64), 64), :]
        return 0

    lax.fori_loop(0, 8, copy_out, 0)
    last_rows(p1, pb, 0, dg)
    last_rows(p2, pb, 1, dgain[1:2, :])
    last_rows(p3, pb, 2, dgain[2:3, :])
    sd = Scatter(pb, r1d, ad, ryd, rxd, ryd2, rxd2, rzd, 0, ssem.at[3], rsem.at[3], t, s)
    sd.ha, sd.hb = 16, 16
    sa.core()
    sd.core()
    homes = [
        send(dhs.at[(s + k) % 4], dhr.at[s], hss.at[k - 1], hsr.at[k - 1], (t, (s + k) % 4)) for k in (1, 2, 3)
    ]
    sb.three()
    sa.core_sum()
    sa.one()
    sd.core_sum()
    bound_one(sd)
    main3 = sc.result()
    main2 = sb.result()
    sa.two()
    bound_two(sd)
    sa.three()
    bound_three(sd)
    cgrad[s] = grad1[s] + dhs[s].astype(F32)
    for k in (1, 2, 3):
        homes[k - 1].wait_recv()
        f = (s + 4 - k) % 4
        cgrad[f] = grad1[f] + dhr[f].astype(F32)
    main1 = sa.result()
    first = sd.result()
    to_shard(first[0:1, :], main1, fl, d, sh1)
    to_shard(first[1:2, :], main2, fl, d, sh2)
    to_shard(first[2:3, :], main3, fl, d, sh3)
    for one in (sa, sb, sc, sd):
        one.drain()
    for copy in moves + homes:
        copy.wait_send()


def bound_one(sd):
    sd.y = [sd.go(sd.acc.at[2 + e], sd.ry.at[e], (sd.xor(4), sd.s)) for e in (0, 1)]


def bound_two(sd):
    for e in (1, 0):
        sd.y[e].wait_recv()
        sd.add(e, 0, 16, lambda j, e=e: sd.ry[e, j, :, :])
        if e:
            sd.x2 = sd.go(sd.acc.at[1], sd.rx2, (sd.xor(2), sd.s))


def bound_three(sd):
    sd.x2.wait_recv()
    sd.add(0, 0, 16, lambda j: sd.rx2[j, :, :])
    t, s = sd.t, sd.s
    sd.z = [sd.go(sd.acc.at[0, (s + k) % 4], sd.rz.at[k - 1], (t, (s + k) % 4)) for k in (1, 2, 3)]


def scatter_scratch(rows, ha, hb):
    return [
        pltpu.VMEM((4, 4, rows, D), BF), pltpu.VMEM((4, 4, rows, D), BF),
        pltpu.VMEM((2, 4, ha, D), BF), pltpu.VMEM((2, 4, hb, D), BF),
        pltpu.VMEM((4, hb, D), BF), pltpu.VMEM((4, ha, D), BF), pltpu.VMEM((3, rows, D), BF),
    ]


def call_c(cnt, do1, qkv, a1, cf, w1, gains, grad1, p1o, p2, p3, dgain):
    sds = jax.ShapeDtypeStruct
    vm = pl.BlockSpec(memory_space=pltpu.VMEM)
    return pl.pallas_call(
        kernel_c,
        name="kernel_c",
        out_shape=(sds((4, 128, D), F32), sds((264, 128), F32), sds((264, 128), F32), sds((520, 128), F32)),
        in_specs=[pl.BlockSpec(memory_space=pltpu.SMEM)] + [vm] * 11,
        out_specs=(vm,) * 4,
        scratch_shapes=[
            pltpu.VMEM((4, 128, D), BF), pltpu.VMEM((3, D, D), BF), pltpu.VMEM((128, D), BF),
            pltpu.VMEM((2, D, 128), F32), pltpu.VMEM((D, D), BF), pltpu.VMEM((4, 3 * D, 128), F32),
            pltpu.VMEM((32, 64, D), BF), pltpu.VMEM((32, 16, D), BF),
            pltpu.VMEM((4, 128, D), BF), pltpu.VMEM((4, 128, D), BF), pltpu.VMEM((528, 128), F32),
            *scatter_scratch(64, 32, 32), *scatter_scratch(64, 32, 32), *scatter_scratch(128, 64, 64),
            *scatter_scratch(16, 16, 16),
            pltpu.SemaphoreType.DMA((4, 14)), pltpu.SemaphoreType.DMA((4, 14)),
            pltpu.SemaphoreType.DMA((3,)), pltpu.SemaphoreType.DMA((3,)),
            pltpu.SemaphoreType.DMA((3,)), pltpu.SemaphoreType.DMA((3,)),
        ],
        compiler_params=pltpu.CompilerParams(collective_id=2, has_side_effects=True, vmem_limit_bytes=60 << 20),
    )(cnt, do1, qkv, a1, cf, w1, gains, grad1, p1o, p2.reshape(32, 64, D), p3.reshape(32, 128, D), dgain)


def kernel_d(x, out, buf, got, zs, ssem, rsem):
    t, s = here()
    barrier = enter(t, s)
    pl.semaphore_wait(barrier, 6)
    buf[0] = x[...]
    copies = []
    for i, e in enumerate((1, 2, 4)):
        copy = send(buf.at[i], got.at[i], ssem.at[i], rsem.at[i], (jnp.bitwise_xor(t, e), s))
        copies.append(copy)
        copy.wait_recv()
        if i < 2:
            buf[i + 1] = buf[i] + got[i]
        else:
            zs[s] = buf[i] + got[i]
    last = [
        send(zs.at[s], zs.at[s], ssem.at[2 + k], rsem.at[2 + k], (t, (s + k) % 4)) for k in (1, 2, 3)
    ]
    for copy in last:
        copy.wait_recv()
    out[...] = zs[0] + zs[1] + zs[2] + zs[3]
    for copy in copies + last:
        copy.wait_send()


def call_d(x):
    vm = pl.BlockSpec(memory_space=pltpu.VMEM)
    return pl.pallas_call(
        kernel_d,
        name="kernel_d",
        out_shape=jax.ShapeDtypeStruct((8, 128), F32),
        in_specs=[vm],
        out_specs=vm,
        scratch_shapes=[
            pltpu.VMEM((3, 8, 128), F32), pltpu.VMEM((3, 8, 128), F32), pltpu.VMEM((4, 8, 128), F32),
            pltpu.SemaphoreType.DMA((6,)), pltpu.SemaphoreType.DMA((6,)),
        ],
        compiler_params=pltpu.CompilerParams(collective_id=3, has_side_effects=True),
    )(x)


def plain_norm(hidden, gain_row):
    centre = jnp.mean(hidden, -1, keepdims=True)
    shifted = hidden - centre
    spread = jnp.mean(shifted * shifted, -1, keepdims=True)
    return shifted * lax.rsqrt(spread + 1e-5) * gain_row


def plain_norm_back(hidden, gain_row, grad):
    _, pull = jax.vjp(plain_norm, hidden, gain_row)
    return pull(grad)


def tn(left, right):
    return lax.dot_general(left, right, (((0,), (0,)), ((), ())), preferred_element_type=F32)


def middle(cells, top, o1rows, wo1, w2, wo2, wup, wdn, gains, scnt, fcnt):
    s = lax.axis_index("samp")
    sample_live = (s * 128 + jnp.arange(128)) < scnt
    feature_live = jnp.arange(4) < fcnt
    live = (feature_live[:, None] & sample_live[None, :]).reshape(512, 1)
    h0 = cells.reshape(512, D).astype(F32)
    o1 = o1rows.reshape(512, D)
    h1 = h0 + nn(o1, wo1)
    g2, g3 = gains[1:2], gains[2:3]
    a2 = plain_norm(h1, g2).astype(BF)
    qkv = [nn(a2, w2[j]).astype(BF).reshape(4, 128, 8, 64) for j in range(3)]
    sc = jnp.einsum("fshe,gshe->shfg", qkv[0], qkv[1], preferred_element_type=F32) * 0.125
    sc = jnp.where(feature_live, sc, NEG)
    pr = jax.nn.softmax(sc, -1)
    prl = pr.astype(BF)
    o2 = jnp.einsum("shfg,gshe->fshe", prl, qkv[2], preferred_element_type=F32).astype(BF).reshape(512, D)
    h2 = h1 + nn(o2, wo2)
    a3 = plain_norm(h2, g3).astype(BF)
    up = jnp.concatenate([nn(a3, wup[j]) for j in range(4)], 1)
    z, pull = jax.vjp(lambda u: jax.nn.gelu(u, approximate=False), up)
    z = z.astype(BF)
    h3 = h2 + nn(z, wdn)
    out = jnp.where(live, h3, 0.0).astype(BF).reshape(4, 128, D)
    g = jnp.where(live, top.reshape(512, D), jnp.zeros((), BF))
    ddown = tn(z, g)
    dz = nt(g, wdn).astype(BF)
    du = pull(dz.astype(F32))[0].astype(BF)
    dup = tn(a3, du)
    da3 = sum(nt(du[:, 512 * j : 512 * j + 512], wup[j]) for j in range(4))
    dh, dg3 = plain_norm_back(h2, g3, da3)
    gr2 = g.astype(F32) + dh
    b2 = gr2.astype(BF)
    dwo2 = tn(o2, b2)
    do2 = nt(b2, wo2).astype(BF).reshape(4, 128, 8, 64)
    dp = jnp.einsum("fshe,gshe->shfg", do2, qkv[2], preferred_element_type=F32)
    ds = (pr * (dp - jnp.sum(pr * dp, -1, keepdims=True))).astype(BF)
    dq = jnp.einsum("shfg,gshe->fshe", ds, qkv[1], preferred_element_type=F32) * 0.125
    dk = jnp.einsum("shfg,fshe->gshe", ds, qkv[0], preferred_element_type=F32) * 0.125
    dv = jnp.einsum("shfg,fshe->gshe", prl, do2, preferred_element_type=F32)
    dqkv = [x.astype(BF).reshape(512, D) for x in (dq, dk, dv)]
    dw2 = jnp.concatenate([tn(a2, x) for x in dqkv], 1).reshape(1536, D)
    da2 = sum(nt(x, w2[j]) for j, x in enumerate(dqkv))
    dh, dg2 = plain_norm_back(h1, g2, da2)
    gr1 = gr2 + dh
    b1 = gr1.astype(BF)
    dwo1 = tn(o1, b1).astype(BF)
    do1 = nt(b1, wo1).astype(BF).reshape(4, 128, D)
    p2 = jnp.concatenate([dw2, dwo2], 0).astype(BF)
    p3 = jnp.concatenate([dup.reshape(2048, D), ddown], 0).astype(BF)
    dgain = jnp.concatenate([jnp.zeros((1, D), F32), dg2, dg3, jnp.zeros((5, D), F32)], 0)
    return out, gr1.reshape(4, 128, D), do1, dwo1, p2, p3, dgain


def lamb_start(grad, master, first, second, width_in):
    first_new = 0.5 * first + 0.5 * grad
    second_new = 0.5 * second + 0.5 * grad * grad
    direction = first_new / (jnp.sqrt(second_new) + 1e-6)
    entries = master.shape[0]
    position = lax.axis_index(("task", "samp")) * entries + jnp.arange(entries, dtype=jnp.int32)
    segment = (position >= D).astype(jnp.int32) + (position >= D + D * width_in).astype(jnp.int32)
    sums = []
    for value in (master * master, direction * direction):
        for k in range(3):
            sums.append(jnp.sum(jnp.where(segment == k, value, 0.0)))
    return first_new, second_new, direction, segment, jnp.stack(sums).reshape(2, 3).T


def fast_device(cells, out_grad, scnt, fcnt, b1, f1, s1, b2, f2, s2, b3, f3, s3):
    cfm = jnp.transpose(cells[0], (1, 0, 2))
    top = jnp.transpose(out_grad[0], (1, 0, 2))
    o1rows, w1, wo1, w2, wo2, wup, wdn, gains, qkv, a1, cf = call_a(
        scnt, cfm, pad_shard(b1), pad_shard(b2), pad_shard(b3)
    )
    out, gr1, do1, dwo1, p2, p3, dgain = middle(cfm, top, o1rows, wo1, w2, wo2, wup, wdn, gains, scnt[0], fcnt[0])
    cgrad, sh1, sh2, sh3 = call_c(scnt, do1, qkv, a1, cf, w1, gains, gr1, dwo1, p2, p3, dgain)
    grads = [sh.reshape(-1)[: b.shape[0]] for sh, b in ((sh1, b1), (sh2, b2), (sh3, b3))]
    states = [
        lamb_start(g, b, f, s, w)
        for g, b, f, s, w in zip(grads, (b1, b2, b3), (f1, f2, f3), (s1, s2, s3), (3 * D, 3 * D, 4 * D))
    ]
    sums = jnp.concatenate([st[4] for st in states], 0)
    flat = jnp.pad(sums.reshape(-1), (0, 1024 - 18)).reshape(8, 128)
    total = call_d(flat).reshape(-1)[:18].reshape(9, 2)
    pairs = jnp.sqrt(total)
    ratio = pairs[:, 0] / (pairs[:, 1] + 1e-6)
    outs = []
    for i, (g, st, b) in enumerate(zip(grads, states, (b1, b2, b3))):
        k = st[3]
        factor = jnp.where(k == 0, ratio[3 * i], jnp.where(k == 1, ratio[3 * i + 1], ratio[3 * i + 2]))
        new = b - 0.5 * factor * st[2]
        outs += [g, st[0], st[1], new, new.astype(BF)]
    return (
        jnp.transpose(out, (1, 0, 2))[None],
        jnp.transpose(cgrad, (1, 0, 2))[None],
        *outs,
        pairs,
    )


def step(*args):
    cells = args[0]
    fits = lax.axis_size("task") == 8 and lax.axis_size("samp") == 4 and cells.shape == (1, 128, 4, D)
    return fast_device(*args) if fits else on_device(*args)


def solution(mesh):
    placed = (
        P("task", "samp", None, None),
        P("task", "samp", None, None),
        P("task"),
        P("task"),
        P(("task", "samp")),
        P(("task", "samp")),
        P(("task", "samp")),
        P(("task", "samp")),
        P(("task", "samp")),
        P(("task", "samp")),
        P(("task", "samp")),
        P(("task", "samp")),
        P(("task", "samp")),
    )
    return jax.shard_map(
        step,
        mesh=mesh,
        in_specs=placed,
        out_specs=(
            P("task", "samp", None, None),
            P("task", "samp", None, None),
            P(("task", "samp")),
            P(("task", "samp")),
            P(("task", "samp")),
            P(("task", "samp")),
            P(("task", "samp")),
            P(("task", "samp")),
            P(("task", "samp")),
            P(("task", "samp")),
            P(("task", "samp")),
            P(("task", "samp")),
            P(("task", "samp")),
            P(("task", "samp")),
            P(("task", "samp")),
            P(("task", "samp")),
            P(("task", "samp")),
            P(),
        ),
        check_vma=False,
    )
```

```python
import jax
import jax.numpy as jnp
from jax import lax
from jax.experimental import pallas as pl
from jax.experimental.pallas import tpu as pltpu
from jax.sharding import PartitionSpec as P

D = 512
HEADS = 8
HEAD_DIM = 64
FF = 2048


EPS_NORM = 1e-05
EPS_ADAM = 1e-06
STEP_RATE = 0.5
BIG_NEGATIVE = -1e30


def normalize(hidden, gain_row):
    centre = jnp.mean(hidden, -1, keepdims=True)
    shifted = hidden - centre
    spread = jnp.mean(shifted * shifted, -1, keepdims=True)
    return shifted * lax.rsqrt(spread + EPS_NORM) * gain_row


def norm_backward(hidden, gain_row, normed_grad):
    _, pullback = jax.vjp(normalize, hidden, gain_row)
    return pullback(normed_grad)


def gelu_exact(upward):
    return jax.nn.gelu(upward, approximate=False)


def contract_rows(left, right):
    return lax.dot_general(
        left, right, (((0,), (0,)), ((), ())), preferred_element_type=jnp.float32
    )


def times_transpose(left, right):
    return lax.dot_general(
        left, right, (((1,), (1,)), ((), ())), preferred_element_type=jnp.float32
    )


def unpack(flat_params, width_in, width_mid):
    gain_row = flat_params[:D].astype(jnp.float32)
    w_in = flat_params[D : D + D * width_in].reshape(D, width_in)
    w_out = flat_params[D + D * width_in :].reshape(width_mid, D)
    return (gain_row, w_in, w_out)


def fetch_forward(master):
    return lax.all_gather(master.astype(jnp.bfloat16), ("task", "samp"), axis=0, tiled=True)


def fetch_again(master):
    return lax.all_gather(master.astype(jnp.bfloat16), ("task", "samp"), axis=0, tiled=True)


def reduce_grads(gain_grad, in_grad, out_grad_matrix):
    flat_grads = jnp.concatenate([gain_grad, in_grad.reshape(-1), out_grad_matrix.reshape(-1)])
    return lax.psum_scatter(flat_grads, ("task", "samp"), scatter_dimension=0, tiled=True)


def group_size(feature_total, most):
    chosen = 1
    for candidate in range(1, most + 1):
        if feature_total % candidate == 0:
            chosen = candidate
    return chosen


def lamb_prepare(grad_shard, master, first, second, width_in):
    first_new = 0.5 * first + 0.5 * grad_shard
    second_new = 0.5 * second + 0.5 * grad_shard * grad_shard
    direction = first_new / (jnp.sqrt(second_new) + EPS_ADAM)
    entries = master.shape[0]
    position = lax.axis_index(("task", "samp")) * entries + jnp.arange(entries, dtype=jnp.int32)
    segment = (position >= D).astype(jnp.int32) + (position >= D + D * width_in).astype(jnp.int32)
    member = segment[None, :] == jnp.arange(3, dtype=jnp.int32)[:, None]
    weight_sums = jnp.sum(jnp.where(member, (master * master)[None, :], 0.0), 1)
    update_sums = jnp.sum(jnp.where(member, (direction * direction)[None, :], 0.0), 1)
    return (first_new, second_new, direction, member, jnp.stack([weight_sums, update_sums], 1))


def lamb_finish(master, block_state, trust_ratio):
    factor = jnp.sum(jnp.where(block_state[3], trust_ratio[:, None], 0.0), 0)
    return master - STEP_RATE * factor * block_state[2]


def sample_scores(query_part, key_part, key_live, score_scale):
    scores = (
        jnp.einsum("qfhe,kfhe->fhqk", query_part, key_part, preferred_element_type=jnp.float32)
        * score_scale
    )
    return jnp.where(key_live, scores, BIG_NEGATIVE)


def sample_forward(queries, pairs_all, key_live, block_features, score_scale):
    local_rows, features = (queries.shape[0], queries.shape[1])

    def one_block(block_index, results):
        attended, log_totals = results
        offset = block_index * block_features
        query_part = lax.dynamic_slice_in_dim(queries, offset, block_features, 1)
        pair_part = lax.dynamic_slice_in_dim(pairs_all, offset, block_features, 1)
        scores = sample_scores(query_part, pair_part[:, :, 0], key_live, score_scale)
        row_top = jnp.max(scores, -1, keepdims=True)
        exponent = jnp.exp(scores - row_top)
        row_total = jnp.sum(exponent, -1, keepdims=True)
        probability = (exponent / row_total).astype(jnp.bfloat16)
        block_out = jnp.einsum(
            "fhqk,kfhe->qfhe", probability, pair_part[:, :, 1], preferred_element_type=jnp.float32
        )
        attended = lax.dynamic_update_slice_in_dim(
            attended, block_out.astype(jnp.bfloat16), offset, 1
        )
        log_totals = lax.dynamic_update_slice_in_dim(
            log_totals, (row_top + jnp.log(row_total))[..., 0], offset, 0
        )
        return (attended, log_totals)

    start_state = (
        jnp.zeros(queries.shape, jnp.bfloat16),
        jnp.zeros((features, HEADS, local_rows), jnp.float32),
    )
    return lax.fori_loop(0, features // block_features, one_block, start_state)


def query_side(query_part, pair_part, grad_part, log_part, key_live, score_scale):
    key_part = pair_part[:, :, 0]
    value_part = pair_part[:, :, 1]
    scores = sample_scores(query_part, key_part, key_live, score_scale)
    probability = jnp.exp(scores - log_part[..., None])
    prob_grad = jnp.einsum(
        "qfhe,kfhe->fhqk", grad_part, value_part, preferred_element_type=jnp.float32
    )
    row_inner = jnp.sum(probability * prob_grad, -1, keepdims=True)
    score_grad = (probability * (prob_grad - row_inner)).astype(jnp.bfloat16)
    query_block = (
        jnp.einsum("fhqk,kfhe->qfhe", score_grad, key_part, preferred_element_type=jnp.float32)
        * score_scale
    )
    return (probability, score_grad, row_inner, query_block)


def sample_backward(
    queries, pairs_all, key_live, log_totals, attended_grad, block_features, score_scale
):
    local_rows, features = (queries.shape[0], queries.shape[1])

    def one_block(block_index, results):
        query_grads, pair_grads = results
        offset = block_index * block_features
        query_part = lax.dynamic_slice_in_dim(queries, offset, block_features, 1)
        pair_part = lax.dynamic_slice_in_dim(pairs_all, offset, block_features, 1)
        grad_part = lax.dynamic_slice_in_dim(attended_grad, offset, block_features, 1)
        log_part = lax.dynamic_slice_in_dim(log_totals, offset, block_features, 0)
        probability, score_grad, row_inner, query_block = query_side(
            query_part, pair_part, grad_part, log_part, key_live, score_scale
        )
        key_block = (
            jnp.einsum(
                "fhqk,qfhe->kfhe", score_grad, query_part, preferred_element_type=jnp.float32
            )
            * score_scale
        )
        value_block = jnp.einsum(
            "fhqk,qfhe->kfhe",
            probability.astype(jnp.bfloat16),
            grad_part,
            preferred_element_type=jnp.float32,
        )
        pair_terms = jnp.stack([key_block, value_block], 2)
        pair_local = lax.psum_scatter(
            pair_terms.astype(jnp.bfloat16), "samp", scatter_dimension=0, tiled=True
        ).astype(jnp.float32)
        query_grads = lax.dynamic_update_slice_in_dim(query_grads, query_block, offset, 1)
        pair_grads = lax.dynamic_update_slice_in_dim(pair_grads, pair_local, offset, 1)
        return (query_grads, pair_grads)

    start_state = (
        jnp.zeros((local_rows, features, HEADS, HEAD_DIM), jnp.float32),
        jnp.zeros((local_rows, features, 2, HEADS, HEAD_DIM), jnp.float32),
    )
    return lax.fori_loop(0, features // block_features, one_block, start_state)


def on_device(
    cells,
    out_grad,
    sample_counts,
    feature_counts,
    sample_block,
    sample_first,
    sample_second,
    feature_block,
    feature_first,
    feature_second,
    mlp_block,
    mlp_first,
    mlp_second,
):
    local_rows, features = (cells.shape[1], cells.shape[2])
    flat_rows = local_rows * features
    seq_all = local_rows * lax.axis_size("samp")
    score_scale = HEAD_DIM ** (-0.5)
    block_features = group_size(features, max(1, 2048 // (HEADS * local_rows)))
    sample_index = lax.axis_index("samp") * local_rows + jnp.arange(local_rows, dtype=jnp.int32)
    sample_live = sample_index < sample_counts[0]
    key_live = jnp.arange(seq_all, dtype=jnp.int32) < sample_counts[0]
    feature_live = jnp.arange(features, dtype=jnp.int32) < feature_counts[0]
    cell_live = sample_live[:, None, None] & feature_live[None, :, None]
    hidden_in = cells[0].astype(jnp.float32)
    gain_one, in_one, out_one = unpack(fetch_forward(sample_block), 3 * D, D)
    normed_one = normalize(hidden_in, gain_one).astype(jnp.bfloat16)
    packed_one = jnp.dot(
        normed_one.reshape(flat_rows, D), in_one, preferred_element_type=jnp.float32
    )
    packed_one = packed_one.astype(jnp.bfloat16).reshape(local_rows, features, 3, HEADS, HEAD_DIM)
    queries_one = packed_one[:, :, 0]
    pairs_local = packed_one[:, :, 1:]
    pairs_all = lax.all_gather(pairs_local, "samp", axis=0, tiled=True)
    attended_one, log_totals = sample_forward(
        queries_one, pairs_all, key_live, block_features, score_scale
    )
    attended_one_rows = attended_one.reshape(flat_rows, D)
    branch_one = jnp.dot(attended_one_rows, out_one, preferred_element_type=jnp.float32)
    hidden_one = hidden_in + branch_one.reshape(local_rows, features, D)
    gain_two, in_two, out_two = unpack(fetch_forward(feature_block), 3 * D, D)
    normed_two = normalize(hidden_one, gain_two).astype(jnp.bfloat16).reshape(flat_rows, D)
    packed_two = jnp.dot(normed_two, in_two, preferred_element_type=jnp.float32)
    packed_two = packed_two.astype(jnp.bfloat16).reshape(local_rows, features, 3, HEADS, HEAD_DIM)
    queries_two, key_two, value_two = (
        packed_two[:, :, 0],
        packed_two[:, :, 1],
        packed_two[:, :, 2],
    )
    scores_two = (
        jnp.einsum("sqhe,skhe->shqk", queries_two, key_two, preferred_element_type=jnp.float32)
        * score_scale
    )
    scores_two = jnp.where(feature_live, scores_two, BIG_NEGATIVE)
    row_top = jnp.max(scores_two, -1, keepdims=True)
    exponent = jnp.exp(scores_two - row_top)
    probability_two = exponent / jnp.sum(exponent, -1, keepdims=True)
    prob_low_two = probability_two.astype(jnp.bfloat16)
    attended_two = jnp.einsum(
        "shqk,skhe->sqhe", prob_low_two, value_two, preferred_element_type=jnp.float32
    )
    attended_two_rows = attended_two.reshape(flat_rows, D).astype(jnp.bfloat16)
    branch_two = jnp.dot(attended_two_rows, out_two, preferred_element_type=jnp.float32)
    hidden_two = hidden_one + branch_two.reshape(local_rows, features, D)
    gain_three, up_weight, down_weight = unpack(fetch_forward(mlp_block), FF, FF)
    normed_three = normalize(hidden_two, gain_three).astype(jnp.bfloat16).reshape(flat_rows, D)
    upward = jnp.dot(normed_three, up_weight, preferred_element_type=jnp.float32)
    activated = gelu_exact(upward).astype(jnp.bfloat16)
    branch_three = jnp.dot(activated, down_weight, preferred_element_type=jnp.float32)
    hidden_three = hidden_two + branch_three.reshape(local_rows, features, D)
    layer_out = jnp.where(cell_live, hidden_three, 0.0).astype(jnp.bfloat16)[None]
    top_grad = jnp.where(cell_live, out_grad[0], jnp.zeros((), jnp.bfloat16))
    top_rows = top_grad.reshape(flat_rows, D)
    gain_three, up_weight, down_weight = unpack(fetch_again(mlp_block), FF, FF)
    down_grad = contract_rows(activated, top_rows)
    act_grad = times_transpose(top_rows, down_weight).astype(jnp.bfloat16)
    _, gelu_pull = jax.vjp(gelu_exact, upward)
    up_grad = gelu_pull(act_grad.astype(jnp.float32))[0].astype(jnp.bfloat16)
    upw_grad = contract_rows(normed_three, up_grad)
    normed_grad = times_transpose(up_grad, up_weight).reshape(local_rows, features, D)
    hidden_grad, gain_three_grad = norm_backward(hidden_two, gain_three, normed_grad)
    grad_two = top_grad.astype(jnp.float32) + hidden_grad
    mlp_shard = reduce_grads(gain_three_grad, upw_grad, down_grad)
    mlp_state = lamb_prepare(mlp_shard, mlp_block, mlp_first, mlp_second, FF)
    gain_two, in_two, out_two = unpack(fetch_again(feature_block), 3 * D, D)
    branch_grad = grad_two.astype(jnp.bfloat16).reshape(flat_rows, D)
    out_two_grad = contract_rows(attended_two_rows, branch_grad)
    attended_grad = (
        times_transpose(branch_grad, out_two)
        .astype(jnp.bfloat16)
        .reshape(local_rows, features, HEADS, HEAD_DIM)
    )
    prob_grad = jnp.einsum(
        "sqhe,skhe->shqk", attended_grad, value_two, preferred_element_type=jnp.float32
    )
    row_inner = jnp.sum(probability_two * prob_grad, -1, keepdims=True)
    score_grad = (probability_two * (prob_grad - row_inner)).astype(jnp.bfloat16)
    query_grad = (
        jnp.einsum("shqk,skhe->sqhe", score_grad, key_two, preferred_element_type=jnp.float32)
        * score_scale
    )
    key_grad = (
        jnp.einsum("shqk,sqhe->skhe", score_grad, queries_two, preferred_element_type=jnp.float32)
        * score_scale
    )
    value_grad = jnp.einsum(
        "shqk,sqhe->skhe", prob_low_two, attended_grad, preferred_element_type=jnp.float32
    )
    packed_grad = (
        jnp.stack([query_grad, key_grad, value_grad], 2)
        .astype(jnp.bfloat16)
        .reshape(flat_rows, 3 * D)
    )
    in_two_grad = contract_rows(normed_two, packed_grad)
    normed_grad = times_transpose(packed_grad, in_two).reshape(local_rows, features, D)
    hidden_grad, gain_two_grad = norm_backward(hidden_one, gain_two, normed_grad)
    grad_one = grad_two + hidden_grad
    feature_shard = reduce_grads(gain_two_grad, in_two_grad, out_two_grad)
    feature_state = lamb_prepare(feature_shard, feature_block, feature_first, feature_second, 3 * D)
    gain_one, in_one, out_one = unpack(fetch_again(sample_block), 3 * D, D)
    pairs_all = lax.all_gather(pairs_local, "samp", axis=0, tiled=True)
    branch_grad = grad_one.astype(jnp.bfloat16).reshape(flat_rows, D)
    out_one_grad = contract_rows(attended_one_rows, branch_grad)
    attended_grad = (
        times_transpose(branch_grad, out_one)
        .astype(jnp.bfloat16)
        .reshape(local_rows, features, HEADS, HEAD_DIM)
    )
    query_grads, pair_grads = sample_backward(
        queries_one, pairs_all, key_live, log_totals, attended_grad, block_features, score_scale
    )
    packed_grad = (
        jnp.concatenate([query_grads[:, :, None], pair_grads], 2)
        .astype(jnp.bfloat16)
        .reshape(flat_rows, 3 * D)
    )
    in_one_grad = contract_rows(normed_one.reshape(flat_rows, D), packed_grad)
    normed_grad = times_transpose(packed_grad, in_one).reshape(local_rows, features, D)
    hidden_grad, gain_one_grad = norm_backward(hidden_in, gain_one, normed_grad)
    cells_grad = (grad_one + hidden_grad)[None]
    sample_shard = reduce_grads(gain_one_grad, in_one_grad, out_one_grad)
    sample_state = lamb_prepare(sample_shard, sample_block, sample_first, sample_second, 3 * D)
    totals = lax.psum(
        jnp.concatenate([sample_state[4], feature_state[4], mlp_state[4]], 0), ("task", "samp")
    )
    norm_pairs = jnp.sqrt(totals)
    trust_ratio = norm_pairs[:, 0] / (norm_pairs[:, 1] + EPS_ADAM)
    sample_master = lamb_finish(sample_block, sample_state, trust_ratio[0:3])
    feature_master = lamb_finish(feature_block, feature_state, trust_ratio[3:6])
    mlp_master = lamb_finish(mlp_block, mlp_state, trust_ratio[6:9])
    return (
        layer_out,
        cells_grad,
        sample_shard,
        sample_state[0],
        sample_state[1],
        sample_master,
        sample_master.astype(jnp.bfloat16),
        feature_shard,
        feature_state[0],
        feature_state[1],
        feature_master,
        feature_master.astype(jnp.bfloat16),
        mlp_shard,
        mlp_state[0],
        mlp_state[1],
        mlp_master,
        mlp_master.astype(jnp.bfloat16),
        norm_pairs,
    )


D = 512
MESH = pl.DeviceIdType.MESH
BF = jnp.bfloat16
F32 = jnp.float32
NEG = -1e30


def mult(value, factor):
    return pl.multiple_of(value, factor)


def nt(left, right):
    return lax.dot_general(left, right, (((1,), (1,)), ((), ())), preferred_element_type=F32)


def nn(left, right):
    return lax.dot_general(left, right, (((1,), (0,)), ((), ())), preferred_element_type=F32)


def here():
    return lax.axis_index("task"), lax.axis_index("samp")


def peers(t, s):
    return (
        (jnp.bitwise_xor(t, 1), s),
        (jnp.bitwise_xor(t, 2), s),
        (jnp.bitwise_xor(t, 4), s),
        (t, (s + 1) % 4),
        (t, (s + 2) % 4),
        (t, (s + 3) % 4),
    )


def enter(t, s):
    barrier = pltpu.get_barrier_semaphore()
    for peer in peers(t, s):
        pl.semaphore_signal(barrier, inc=1, device_id=peer, device_id_type=MESH)
    return barrier


def send(src, dst, ssem, rsem, peer):
    copy = pltpu.make_async_remote_copy(
        src_ref=src, dst_ref=dst, send_sem=ssem, recv_sem=rsem, device_id=peer, device_id_type=MESH
    )
    copy.start()
    return copy


class Gather:
    def __init__(self, buf, half, ssem, rsem, t, s):
        self.buf, self.t, self.s = buf, t, s
        rows = buf.shape[1]
        self.ha, self.hb = pl.ds(0, half), pl.ds(half, rows - half)
        self.all = pl.ds(0, rows)
        self.ssem, self.rsem = ssem, rsem
        self.count = 0
        self.copies = []
        self.tx, self.ty = jnp.bitwise_xor(t, 2), jnp.bitwise_xor(t, 4)
        self.txy, self.tc = jnp.bitwise_xor(t, 6), jnp.bitwise_xor(t, 1)

    def go(self, slots, rows, peer):
        view = self.buf.at[slots, rows]
        i = self.count
        self.count += 1
        copy = send(view, view, self.ssem.at[i], self.rsem.at[i], peer)
        self.copies.append(copy)
        return copy

    def four(self, t):
        return pl.ds(4 * t, 4)

    def z(self):
        t, s = self.t, self.s
        own = pl.ds(4 * t + s, 1)
        self.zc = [self.go(own, self.all, (t, (s + k) % 4)) for k in (1, 2, 3)]

    def one(self):
        for copy in self.zc:
            copy.wait_recv()
        t, s = self.t, self.s
        self.x1 = self.go(self.four(t), self.ha, (self.tx, s))
        self.y1 = self.go(self.four(t), self.hb, (self.ty, s))
        self.c = [self.go(self.four(t), self.all, (self.tc, s))]

    def two(self):
        s = self.s
        t = self.t
        self.x1.wait_recv()
        self.y2 = [
            self.go(self.four(t), self.ha, (self.ty, s)),
            self.go(self.four(self.tx), self.ha, (self.ty, s)),
        ]
        self.y1.wait_recv()
        self.x2 = [
            self.go(self.four(t), self.hb, (self.tx, s)),
            self.go(self.four(self.ty), self.hb, (self.tx, s)),
        ]
        self.c.append(self.go(self.four(self.tx), self.ha, (self.tc, s)))
        self.c.append(self.go(self.four(self.ty), self.hb, (self.tc, s)))

    def three(self):
        s = self.s
        for copy in self.y2 + self.x2:
            copy.wait_recv()
        self.c.append(self.go(self.four(self.ty), self.ha, (self.tc, s)))
        self.c.append(self.go(self.four(self.txy), self.ha, (self.tc, s)))
        self.c.append(self.go(self.four(self.tx), self.hb, (self.tc, s)))
        self.c.append(self.go(self.four(self.txy), self.hb, (self.tc, s)))

    def end(self):
        for copy in self.c:
            copy.wait_recv()

    def drain(self):
        for copy in self.copies:
            copy.wait_send()


def realign(m_ref, sh_ref, d, rows, out_ref, out_at, roll_to):
    whole = 4 * rows
    total = whole + 8
    q, p = d // 8, d % 8
    lane = lax.broadcasted_iota(jnp.int32, (total, 128), 1)
    roll_to[0:8, :] = jnp.zeros((8, 128), F32)
    for i in range(whole // 8):
        sh_ref[8 * i : 8 * i + 8, :] = m_ref[pl.ds(1024 * i, 1024)].reshape(8, 128)
    sh_ref[whole:total, :] = jnp.zeros((8, 128), F32)
    sh_ref[whole : whole + 1, 0:16] = m_ref[pl.ds(128 * whole, 16)].reshape(1, 16)
    rolled = pltpu.roll(sh_ref[0:total, :], 16 * p, 1)
    roll_to[8 : 8 + total, :] = rolled
    sh_ref[0:8, :] = jnp.zeros((8, 128), F32)
    sh_ref[8 : 8 + total, :] = jnp.where(lane < 16 * p, roll_to[7 : 7 + total, :], rolled)
    firsts = []
    for b in range(4):
        out_ref[out_at, 0:rows, 128 * b : 128 * b + 128] = sh_ref[pl.ds(12 - q + b, rows, stride=4), :].astype(BF)
        firsts.append(sh_ref[pl.ds(8 - q + b, 1), :])
    return jnp.concatenate(firsts, 1)


def spread(buf, firsts, kind, rows, lo, hi, put):
    tail = lax.broadcasted_iota(jnp.int32, (8, D), 0) == 7

    def body(i, _):
        nxt = jnp.minimum(i + 1, 31)
        row = firsts[nxt, 64:80, :].astype(F32)[kind : kind + 1, :]
        block = buf[i, 0:rows, :].astype(F32)
        last = block[rows - 8 : rows, :] + jnp.where(tail & (i < 31), row, 0.0)
        put(i - lo, block[0 : rows - 8, :], last)
        return 0

    lax.fori_loop(lo, hi, body, 0)


def put_f32(dst, rows):
    def put(i, head, last):
        for b in range(4):
            cols = slice(128 * b, 128 * b + 128)
            dst[b, pl.ds(mult(i * rows, rows), rows - 8), :] = head[:, cols]
            dst[b, pl.ds(mult(i * rows + rows - 8, 8), 8), :] = last[:, cols]

    return put


def put_bf(dst, rows):
    def put(i, head, last):
        dst[pl.ds(mult(i * rows, rows), rows), :] = jnp.concatenate([head, last], 0).astype(BF)

    return put


def split_columns(wide, ways, dst):
    def body(i, _):
        for j in range(ways):
            for b in range(4):
                piece = wide[b, pl.ds(64 * ways * i + j, 64, stride=ways), :]
                dst[j, pl.ds(mult(64 * i, 64), 64), 128 * b : 128 * b + 128] = piece.astype(BF)
        return 0

    lax.fori_loop(0, 8, body, 0)


def halves():
    lane = lax.broadcasted_iota(jnp.int32, (128, 128), 1)
    return lane < 64


def attend_chunk(qkv, c, live, out):
    left = halves()
    one = jnp.where(left, 0.125, 0.0).astype(BF)
    two = jnp.where(left, 0.0, 0.125).astype(BF)

    def body(h, _):
        cols = pl.ds(mult(h * 128, 128), 128)
        q = qkv[0, pl.ds(mult(c * 128, 128), 128), cols]
        qm = jnp.concatenate([q * one, q * two], 0)
        scores = jnp.where(live, nt(qm, qkv[1, :, cols]), NEG)
        top = jnp.max(scores, 1, keepdims=True)
        e = jnp.exp(scores - top)
        prob = (e * (1.0 / jnp.sum(e, 1, keepdims=True))).astype(BF)
        o = nn(prob, qkv[2, :, cols])
        o = jnp.where(left, o[0:128], o[128:256]).astype(BF)
        for g in range(4):
            out[g, :, cols] = o[32 * g : 32 * g + 32]
        return 0

    lax.fori_loop(0, 4, body, 0)


def kernel_a(
    cnt, cells, m1, m2, m3,
    o1rows, w1, wo1, w2, wo2, wup, wdn, gains, qkv, a1, cf,
    g1, g2, g3, wide, sh, ro, o1c, w1v, wo1v, w2v, wo2v, wupv, wdnv, qkvv,
    gs, gr, as_, ar, os_, or_, lsem,
):
    t, s = here()
    d = 4 * t + s
    barrier = enter(t, s)
    ga = Gather(g1, 32, gs.at[0], gr.at[0], t, s)
    gb = Gather(g2, 32, gs.at[1], gr.at[1], t, s)
    gc = Gather(g3, 64, gs.at[2], gr.at[2], t, s)
    f1 = realign(m1, sh, d, 64, g1, d, ro)
    f2 = realign(m2, sh, d, 64, g2, d, ro)
    f3 = realign(m3, sh, d, 128, g3, d, ro)
    row = lax.broadcasted_iota(jnp.int32, (16, D), 0)
    firsts = jnp.where(row == 0, f1, jnp.where(row == 1, f2, jnp.where(row == 2, f3, 0.0)))
    g1[d, 64:80, :] = firsts.astype(BF)
    pl.semaphore_wait(barrier, 6)
    ga.z()
    cf[s] = cells[:, s, :, :]
    moves = [
        send(cells.at[:, (s + k) % 4], cf.at[s], as_.at[k - 1], ar.at[k - 1], (t, (s + k) % 4)) for k in (1, 2, 3)
    ]
    ga.one()
    ga.two()
    for copy in moves:
        copy.wait_recv()
    gb.z()
    gc.z()
    ga.three()
    ga.end()
    spread(g1, g1, 0, 64, 0, 24, put_f32(wide, 64))
    split_columns(wide, 3, w1v)
    spread(g1, g1, 0, 64, 24, 32, put_bf(wo1v, 64))
    gains[...] = g1[0, 64:80, :].astype(F32)[0:8]
    gain = g1[0, 64:80, :].astype(F32)[0:1]

    def norm(i, _):
        h = cf[i].astype(F32).reshape(128, D)
        mean = jnp.mean(h, 1, keepdims=True)
        x = h - mean
        var = jnp.mean(x * x, 1, keepdims=True)
        a1[pl.ds(mult(i * 128, 128), 128), :] = (x * lax.rsqrt(var + 1e-5) * gain).astype(BF)
        return 0

    lax.fori_loop(0, 4, norm, 0)

    def project(i, _):
        j, r = i // 4, i % 4
        rows = pl.ds(mult(r * 128, 128), 128)
        qkvv[j, rows, :] = nn(a1[rows, :], w1v[j]).astype(BF)
        return 0

    lax.fori_loop(0, 12, project, 0)
    live = lax.broadcasted_iota(jnp.int32, (1, 512), 1) < cnt[0]
    backs = []
    local = []

    def keep(src, dst):
        copy = pltpu.make_async_copy(src, dst, lsem.at[len(local)])
        copy.start()
        local.append(copy)

    keep(w1v, w1)
    keep(wo1v, wo1)
    keep(qkvv, qkv)
    for k in (2, 1, 3, 0):
        c = (s + k) % 4
        if k:
            attend_chunk(qkvv, c, live, o1c.at[k - 1])
            backs.append(send(o1c.at[k - 1], o1rows.at[:, s], os_.at[k - 1], or_.at[k - 1], (t, c)))
        else:
            attend_chunk(qkvv, c, live, o1rows.at[:, s])
        if k == 2:
            gb.one()
            gc.one()
        if k == 1:
            gb.two()
            gc.two()
        if k == 3:
            gb.three()
    gb.end()
    spread(g2, g1, 1, 64, 0, 24, put_f32(wide, 64))
    split_columns(wide, 3, w2v)
    spread(g2, g1, 1, 64, 24, 32, put_bf(wo2v, 64))
    keep(w2v, w2)
    keep(wo2v, wo2)
    gc.three()
    gc.end()
    spread(g3, g1, 2, 128, 0, 16, put_f32(wide, 128))
    split_columns(wide, 4, wupv)
    keep(wupv, wup)
    spread(g3, g1, 2, 128, 16, 32, put_bf(wdnv, 128))
    keep(wdnv, wdn)
    for copy in backs:
        copy.wait_recv()
    for copy in moves + backs:
        copy.wait_send()
    ga.drain()
    gb.drain()
    gc.drain()
    for copy in local:
        copy.wait()


def call_a(cnt, cells_fm, m1, m2, m3):
    sds = jax.ShapeDtypeStruct
    vm = pl.BlockSpec(memory_space=pltpu.VMEM)
    hb = pl.BlockSpec(memory_space=pl.ANY)
    return pl.pallas_call(
        kernel_a,
        name="kernel_a",
        out_shape=(
            sds((4, 4, 32, D), BF), sds((3, D, D), BF), sds((D, D), BF), sds((3, D, D), BF), sds((D, D), BF),
            sds((4, D, D), BF), sds((4 * D, D), BF), sds((8, D), F32), sds((3, D, D), BF), sds((D, D), BF),
            sds((4, 4, 32, D), BF),
        ),
        in_specs=[pl.BlockSpec(memory_space=pltpu.SMEM), vm, vm, vm, vm],
        out_specs=(vm, hb, hb, hb, hb, hb, hb, vm, hb, vm, vm),
        scratch_shapes=[
            pltpu.VMEM((32, 80, D), BF), pltpu.VMEM((32, 64, D), BF), pltpu.VMEM((32, 128, D), BF),
            pltpu.VMEM((4, 4 * D, 128), F32), pltpu.VMEM((536, 128), F32), pltpu.VMEM((536, 128), F32),
            pltpu.VMEM((3, 4, 32, D), BF),
            pltpu.VMEM((3, D, D), BF), pltpu.VMEM((D, D), BF), pltpu.VMEM((3, D, D), BF), pltpu.VMEM((D, D), BF),
            pltpu.VMEM((4, D, D), BF), pltpu.VMEM((4 * D, D), BF), pltpu.VMEM((3, D, D), BF),
            pltpu.SemaphoreType.DMA((3, 16)), pltpu.SemaphoreType.DMA((3, 16)),
            pltpu.SemaphoreType.DMA((3,)), pltpu.SemaphoreType.DMA((3,)),
            pltpu.SemaphoreType.DMA((3,)), pltpu.SemaphoreType.DMA((3,)),
            pltpu.SemaphoreType.DMA((7,)),
        ],
        compiler_params=pltpu.CompilerParams(collective_id=1, has_side_effects=True, vmem_limit_bytes=56 << 20),
    )(cnt, cells_fm, m1, m2, m3)


def edges(d, entries, width):
    begin = d * entries
    return D - begin, D + D * width - begin


def segment(k, ends):
    return (k >= ends[0]).astype(jnp.int32) + (k >= ends[1]).astype(jnp.int32)


def lamb_step(g, m, f, s):
    fn = 0.5 * f + 0.5 * g
    sn = 0.5 * s + 0.5 * g * g
    return fn, sn, fn / (jnp.sqrt(sn) + 1e-6)


def squares(sh, m, f, s, sums, d, width, b):
    entries = m.shape[0]
    whole = entries // 1024
    ends = edges(d, entries, width)
    lane = lax.broadcasted_iota(jnp.int32, (8, 128), 0) * 128 + lax.broadcasted_iota(jnp.int32, (8, 128), 1)
    zero = jnp.zeros((8, 128), F32)

    def body(i, acc):
        at = pl.ds(mult(i * 1024, 1024), 1024)
        old = m[at].reshape(8, 128)
        _, _, r = lamb_step(
            sh[pl.ds(mult(i * 8, 8), 8), :], old, f[at].reshape(8, 128), s[at].reshape(8, 128)
        )
        part = segment(lane + i * 1024, ends)
        out = []
        for n, value in enumerate((old * old, r * r)):
            for k in range(3):
                out.append(acc[3 * n + k] + jnp.where(part == k, value, 0.0))
        return tuple(out)

    acc = lax.fori_loop(0, whole, body, (zero,) * 6)
    at = pl.ds(whole * 1024, 16)
    old = m[at].reshape(1, 16)
    _, _, r = lamb_step(
        sh[8 * whole : 8 * whole + 1, 0:16], old, f[at].reshape(1, 16), s[at].reshape(1, 16)
    )
    part = segment(lax.broadcasted_iota(jnp.int32, (1, 16), 1) + whole * 1024, ends)
    first = lax.broadcasted_iota(jnp.int32, (1, 128), 1) == 0
    for n, value in enumerate((old * old, r * r)):
        for k in range(3):
            row = 16 * n + 3 * b + k
            tail = jnp.sum(jnp.where(part == k, value, 0.0), 1, keepdims=True)
            sums[row : row + 1, :] = jnp.sum(acc[3 * n + k], 0, keepdims=True) + jnp.where(first, tail, 0.0)


def update(sh, m, f, s, grad, fout, sout, mout, wout, ratio, d, width, b):
    entries = m.shape[0]
    whole = entries // 1024
    ends = edges(d, entries, width)
    half = [0.5 * ratio[3 * b + k : 3 * b + k + 1, :] for k in range(3)]

    def put(at, g, part, shape):
        old = m[at].reshape(shape)
        fn, sn, r = lamb_step(g, old, f[at].reshape(shape), s[at].reshape(shape))
        factor = jnp.where(part == 0, half[0], jnp.where(part == 1, half[1], half[2]))
        new = (old - factor * r).reshape(-1)
        grad[at] = g.reshape(-1)
        fout[at] = fn.reshape(-1)
        sout[at] = sn.reshape(-1)
        mout[at] = new
        wout[at] = new.astype(BF)

    lane = lax.broadcasted_iota(jnp.int32, (8, 128), 0) * 128 + lax.broadcasted_iota(jnp.int32, (8, 128), 1)

    def body(i, _):
        at = pl.ds(mult(i * 1024, 1024), 1024)
        put(at, sh[pl.ds(mult(i * 8, 8), 8), :], segment(lane + i * 1024, ends), (8, 128))
        return 0

    lax.fori_loop(0, whole, body, 0)
    part = segment(lax.broadcasted_iota(jnp.int32, (1, 16), 1) + whole * 1024, ends)
    put(pl.ds(whole * 1024, 16), sh[8 * whole : 8 * whole + 1, 0:16], part, (1, 16))


def sum_all(sums, got, zs, ssem, rsem, t, s):
    copies = []
    for i, e in enumerate((1, 2, 4)):
        copy = send(sums.at[i], got.at[i], ssem.at[i], rsem.at[i], (jnp.bitwise_xor(t, e), s))
        copies.append(copy)
        copy.wait_recv()
        if i < 2:
            sums[i + 1] = sums[i] + got[i]
        else:
            zs[s] = sums[i] + got[i]
    last = [
        send(zs.at[s], zs.at[s], ssem.at[2 + k], rsem.at[2 + k], (t, (s + k) % 4)) for k in (1, 2, 3)
    ]
    for copy in last:
        copy.wait_recv()
    return zs[0] + zs[1] + zs[2] + zs[3], copies + last


def kernel_e(
    total, sh1, sh2, sh3, m1, f1, s1, m2, f2, s2, m3, f3, s3,
    g1, fo1, so1, mo1, wo1, g2, fo2, so2, mo2, wo2, g3, fo3, so3, mo3, wo3, pairs,
):
    t, s = here()
    d = 4 * t + s
    norm = jnp.sqrt(jnp.sum(total[...], 1, keepdims=True))
    pairs[...] = jnp.concatenate([norm[0:9], norm[16:25]], 1)
    ratio = norm[0:9] / (norm[16:25] + 1e-6)
    update(sh1, m1, f1, s1, g1, fo1, so1, mo1, wo1, ratio, d, 3 * D, 0)
    update(sh2, m2, f2, s2, g2, fo2, so2, mo2, wo2, ratio, d, 3 * D, 1)
    update(sh3, m3, f3, s3, g3, fo3, so3, mo3, wo3, ratio, d, 4 * D, 2)


def call_e(total, shards, args):
    sds = jax.ShapeDtypeStruct
    vm = pl.BlockSpec(memory_space=pltpu.VMEM)
    shapes = []
    for m in args[0::3]:
        n = m.shape
        shapes += [sds(n, F32)] * 4 + [sds(n, BF)]
    return pl.pallas_call(
        kernel_e,
        name="kernel_e",
        out_shape=(*shapes, sds((9, 2), F32)),
        in_specs=[vm] * 13,
        out_specs=(vm,) * 16,
        compiler_params=pltpu.CompilerParams(vmem_limit_bytes=40 << 20),
    )(total, *shards, *args)


class Scatter:
    def __init__(self, part, r1, acc, ry, rx, ry2, rx2, rz, half, ssem, rsem, t, s):
        self.part, self.r1, self.acc = part, r1, acc
        self.ry, self.rx, self.ry2, self.rx2, self.rz = ry, rx, ry2, rx2, rz
        self.rows = part.shape[1]
        self.ha, self.hb = half, self.rows - half
        self.ssem, self.rsem, self.t, self.s = ssem, rsem, t, s
        self.count = 0
        self.copies = []

    def go(self, src, dst, peer):
        i = self.count
        self.count += 1
        copy = send(src, dst, self.ssem.at[i], self.rsem.at[i], peer)
        self.copies.append(copy)
        return copy

    def xor(self, e):
        return jnp.bitwise_xor(self.t, e)

    def core(self):
        tc = self.xor(1)
        self.c = [
            self.go(self.part.at[pl.ds(4 * jnp.bitwise_xor(tc, 2 * e), 4)], self.r1.at[e], (tc, self.s))
            for e in (2, 3, 1, 0)
        ]

    def core_sum(self):
        for n, e in enumerate((2, 3, 1, 0)):
            self.c[n].wait_recv()
            base = 4 * self.xor(2 * e)

            def body(j, _, e=e, base=base):
                own = self.part[base + j, :, :].astype(F32)
                self.acc[e, j, :, :] = (own + self.r1[e, j, :, :].astype(F32)).astype(BF)
                return 0

            lax.fori_loop(0, 4, body, 0)

    def one(self):
        ha, hb = pl.ds(0, self.ha), pl.ds(self.ha, self.hb)
        ty, tx, s = self.xor(4), self.xor(2), self.s
        self.y = [self.go(self.acc.at[2 + e, :, ha], self.ry.at[e], (ty, s)) for e in (0, 1)]
        self.x = [self.go(self.acc.at[1 + 2 * e, :, hb], self.rx.at[e], (tx, s)) for e in (0, 1)]

    def add(self, e, lo, size, got):
        def body(j, _):
            own = self.acc[e, j, lo : lo + size, :].astype(F32)
            self.acc[e, j, lo : lo + size, :] = (own + got(j).astype(F32)).astype(BF)
            return 0

        lax.fori_loop(0, 4, body, 0)

    def two(self):
        ha, hb = pl.ds(0, self.ha), pl.ds(self.ha, self.hb)
        ty, tx, s = self.xor(4), self.xor(2), self.s
        self.y[1].wait_recv()
        self.add(1, 0, self.ha, lambda j: self.ry[1, j, :, :])
        self.x2 = self.go(self.acc.at[1, :, ha], self.rx2, (tx, s))
        self.x[1].wait_recv()
        self.add(2, self.ha, self.hb, lambda j: self.rx[1, j, :, :])
        self.y2 = self.go(self.acc.at[2, :, hb], self.ry2, (ty, s))
        self.y[0].wait_recv()
        self.add(0, 0, self.ha, lambda j: self.ry[0, j, :, :])
        self.x[0].wait_recv()
        self.add(0, self.ha, self.hb, lambda j: self.rx[0, j, :, :])

    def three(self):
        self.x2.wait_recv()
        self.add(0, 0, self.ha, lambda j: self.rx2[j, :, :])
        self.y2.wait_recv()
        self.add(0, self.ha, self.hb, lambda j: self.ry2[j, :, :])
        t, s = self.t, self.s
        self.z = [self.go(self.acc.at[0, (s + k) % 4], self.rz.at[k - 1], (t, (s + k) % 4)) for k in (1, 2, 3)]

    def result(self):
        for copy in self.z:
            copy.wait_recv()
        total = self.acc[0, self.s, :, :].astype(F32)
        for k in range(3):
            total = total + self.rz[k, :, :].astype(F32)
        return total

    def drain(self):
        for copy in self.copies:
            copy.wait_send()


def to_shard(first, main, fl, d, out_ref):
    q, p = d // 8, d % 8
    rows = main.shape[0]
    total = out_ref.shape[0]
    fl[4 + 4 * rows : total + 8, :] = jnp.zeros((total + 4 - 4 * rows, 128), F32)
    for b in range(4):
        fl[b : b + 1, :] = first[:, 128 * b : 128 * b + 128]
        fl[pl.ds(4 + b, rows, stride=4), :] = main[:, 128 * b : 128 * b + 128]
    turn = (128 - 16 * p) % 128
    lane = lax.broadcasted_iota(jnp.int32, (total, 128), 1)
    low = pltpu.roll(fl[pl.ds(q, total), :], turn, 1)
    high = pltpu.roll(fl[pl.ds(q + 1, total), :], turn, 1)
    out_ref[...] = jnp.where(lane < 128 - 16 * p, low, high)


def last_rows(part, bound, kind, gain_row):
    rows = part.shape[1]
    at = lax.broadcasted_iota(jnp.int32, (16, D), 0) == kind

    def body(i, _):
        prev = jnp.maximum(i - 1, 0)
        row = part[prev, rows - 16 : rows, :].astype(F32)[15:16, :]
        row = jnp.where(i > 0, row, gain_row)
        bound[i, :, :] = jnp.where(at, row, bound[i, :, :].astype(F32)).astype(BF)
        return 0

    lax.fori_loop(0, 32, body, 0)


def backward_heads(h, qkv, do, live, dqkv, kt, dkv):
    left = halves()
    one, two = jnp.where(left, 1.0, 0.0).astype(BF), jnp.where(left, 0.0, 1.0).astype(BF)
    cols = pl.ds(mult(h * 128, 128), 128)
    kt[...] = jnp.transpose(qkv[1, :, cols].astype(F32)).astype(BF)
    top_lane = lax.broadcasted_iota(jnp.int32, (128, 128), 0) < 64

    def chunk(c, _):
        rows = pl.ds(mult(c * 128, 128), 128)
        q = qkv[0, rows, cols] * jnp.asarray(0.125, BF)
        qm = jnp.concatenate([q * one, q * two], 0)
        g = do[c, :, :, cols].reshape(128, 128)
        gm = jnp.concatenate([g * one, g * two], 0)
        scores = jnp.where(live, nt(qkv[1, :, cols], qm), NEG)
        e = jnp.exp(scores - jnp.max(scores, 0, keepdims=True))
        prob = e * (1.0 / jnp.sum(e, 0, keepdims=True))
        pg = nt(qkv[2, :, cols], gm)
        inner = jnp.sum(prob * pg, 0, keepdims=True)
        sg = (prob * (pg - inner)).astype(BF)
        dk = nn(sg, qm)
        dv = nn(prob.astype(BF), gm)
        dqt = nn(kt[...], sg)
        dq = jnp.transpose(jnp.where(top_lane, dqt[:, 0:128], dqt[:, 128:256])) * 0.125
        dqkv[0, rows, cols] = dq.astype(BF)

        @pl.when(c == 0)
        def _():
            dkv[0] = dk
            dkv[1] = dv

        @pl.when(c > 0)
        def _():
            dkv[0] += dk
            dkv[1] += dv

        return 0

    lax.fori_loop(0, 4, chunk, 0)
    dqkv[1, :, cols] = dkv[0].astype(BF)
    dqkv[2, :, cols] = dkv[1].astype(BF)


def kernel_c(
    cnt, do1, qkv, a1, cf, w1, gains, grad1, p1o, p2, p3, dgain,
    m1, f1, s1, m2, f2, s2, m3, f3, s3,
    cgrad, sh1, sh2, sh3, total,
    do, dqkv, kt, dkv, at, wide, p1, pb, dhs, dhr, fl,
    r1a, aa, rya, rxa, rya2, rxa2, rza,
    r1b, ab, ryb, rxb, ryb2, rxb2, rzb,
    r1c, ac, ryc, rxc, ryc2, rxc2, rzc,
    r1d, ad, ryd, rxd, ryd2, rxd2, rzd,
    ssem, rsem, dss, dsr, hss, hsr, sums, got, zs, nss, nsr,
):
    t, s = here()
    d = 4 * t + s
    barrier = enter(t, s)
    do[s] = do1[:, s, :, :]
    pb[...] = jnp.zeros((32, 16, D), BF)
    sa = Scatter(p1, r1a, aa, rya, rxa, rya2, rxa2, rza, 32, ssem.at[0], rsem.at[0], t, s)
    sb = Scatter(p2, r1b, ab, ryb, rxb, ryb2, rxb2, rzb, 32, ssem.at[1], rsem.at[1], t, s)
    sc = Scatter(p3, r1c, ac, ryc, rxc, ryc2, rxc2, rzc, 64, ssem.at[2], rsem.at[2], t, s)
    pl.semaphore_wait(barrier, 6)
    moves = [
        send(do1.at[:, (s + k) % 4], do.at[s], dss.at[k - 1], dsr.at[k - 1], (t, (s + k) % 4)) for k in (1, 2, 3)
    ]
    sc.core()
    sb.core()
    sc.core_sum()
    sc.one()
    at[...] = jnp.transpose(a1[...].astype(F32)).astype(BF)
    sb.core_sum()
    for copy in moves:
        copy.wait_recv()
    live = lax.broadcasted_iota(jnp.int32, (512, 1), 0) < cnt[0]

    def heads(lo, hi):
        def body(h, _):
            backward_heads(h, qkv, do, live, dqkv, kt, dkv)
            return 0

        lax.fori_loop(lo, hi, body, 0)

    heads(0, 2)
    sc.two()
    sb.one()
    heads(2, 3)
    sc.three()
    heads(3, 4)
    sb.two()
    gain = gains[0:1, :]
    dg = jnp.zeros((1, D), F32)

    def norm_back(i, dg):
        rows = pl.ds(mult(i * 128, 128), 128)
        da = nt(dqkv[0, rows, :], w1[0]) + nt(dqkv[1, rows, :], w1[1]) + nt(dqkv[2, rows, :], w1[2])
        h = cf[i].astype(F32).reshape(128, D)
        x = h - jnp.mean(h, 1, keepdims=True)
        rstd = lax.rsqrt(jnp.mean(x * x, 1, keepdims=True) + 1e-5)
        x = x * rstd
        dg = dg + jnp.sum(da * x, 0, keepdims=True)
        dx = da * gain
        dh = rstd * (dx - jnp.mean(dx, 1, keepdims=True) - x * jnp.mean(dx * x, 1, keepdims=True))
        dhs[i] = dh.astype(BF).reshape(4, 32, D)
        return dg

    dg = lax.fori_loop(0, 4, norm_back, dg)

    def weights(i, _):
        j, r = i // 4, i % 4
        part = nn(at[pl.ds(mult(r * 128, 128), 128), :], dqkv[j])
        for b in range(4):
            wide[b, pl.ds(384 * r + j, 128, stride=3), :] = part[:, 128 * b : 128 * b + 128]
        return 0

    lax.fori_loop(0, 12, weights, 0)

    def narrow(i, _):
        rows = pl.ds(mult(i * 64, 64), 64)
        for b in range(4):
            p1[i, :, 128 * b : 128 * b + 128] = wide[b, rows, :].astype(BF)
        return 0

    lax.fori_loop(0, 24, narrow, 0)

    def copy_out(i, _):
        p1[24 + i] = p1o[pl.ds(mult(i * 64, 64), 64), :]
        return 0

    lax.fori_loop(0, 8, copy_out, 0)
    last_rows(p1, pb, 0, dg)
    last_rows(p2, pb, 1, dgain[1:2, :])
    last_rows(p3, pb, 2, dgain[2:3, :])
    sd = Scatter(pb, r1d, ad, ryd, rxd, ryd2, rxd2, rzd, 0, ssem.at[3], rsem.at[3], t, s)
    sd.ha, sd.hb = 16, 16
    sa.core()
    sd.core()
    homes = [
        send(dhs.at[(s + k) % 4], dhr.at[:, s], hss.at[k - 1], hsr.at[k - 1], (t, (s + k) % 4)) for k in (1, 2, 3)
    ]
    sb.three()
    sa.core_sum()
    sa.one()
    sd.core_sum()
    bound_one(sd)
    main3 = sc.result()
    main2 = sb.result()
    sa.two()
    bound_two(sd)
    sa.three()
    bound_three(sd)
    cgrad[:, s, :, :] = grad1[:, s, :, :] + dhs[s].astype(F32)
    for k in (1, 2, 3):
        homes[k - 1].wait_recv()
        f = (s + 4 - k) % 4
        cgrad[:, f, :, :] = grad1[:, f, :, :] + dhr[:, f, :, :].astype(F32)
    main1 = sa.result()
    first = sd.result()
    to_shard(first[0:1, :], main1, fl, d, sh1)
    to_shard(first[1:2, :], main2, fl, d, sh2)
    to_shard(first[2:3, :], main3, fl, d, sh3)
    sums[0] = jnp.zeros((32, 128), F32)
    squares(sh1, m1, f1, s1, sums.at[0], d, 3 * D, 0)
    squares(sh2, m2, f2, s2, sums.at[0], d, 3 * D, 1)
    squares(sh3, m3, f3, s3, sums.at[0], d, 4 * D, 2)
    total[...], adds = sum_all(sums, got, zs, nss, nsr, t, s)
    for one in (sa, sb, sc, sd):
        one.drain()
    for copy in moves + homes + adds:
        copy.wait_send()


def bound_one(sd):
    sd.y = [sd.go(sd.acc.at[2 + e], sd.ry.at[e], (sd.xor(4), sd.s)) for e in (0, 1)]


def bound_two(sd):
    for e in (1, 0):
        sd.y[e].wait_recv()
        sd.add(e, 0, 16, lambda j, e=e: sd.ry[e, j, :, :])
        if e:
            sd.x2 = sd.go(sd.acc.at[1], sd.rx2, (sd.xor(2), sd.s))


def bound_three(sd):
    sd.x2.wait_recv()
    sd.add(0, 0, 16, lambda j: sd.rx2[j, :, :])
    t, s = sd.t, sd.s
    sd.z = [sd.go(sd.acc.at[0, (s + k) % 4], sd.rz.at[k - 1], (t, (s + k) % 4)) for k in (1, 2, 3)]


def scatter_scratch(rows, ha, hb):
    return [
        pltpu.VMEM((4, 4, rows, D), BF), pltpu.VMEM((4, 4, rows, D), BF),
        pltpu.VMEM((2, 4, ha, D), BF), pltpu.VMEM((2, 4, hb, D), BF),
        pltpu.VMEM((4, hb, D), BF), pltpu.VMEM((4, ha, D), BF), pltpu.VMEM((3, rows, D), BF),
    ]


def call_c(cnt, do1, qkv, a1, cf, w1, gains, grad1, p1o, p2, p3, dgain, params):
    sds = jax.ShapeDtypeStruct
    vm = pl.BlockSpec(memory_space=pltpu.VMEM)
    return pl.pallas_call(
        kernel_c,
        name="kernel_c",
        out_shape=(sds((4, 4, 32, D), F32), sds((264, 128), F32), sds((264, 128), F32), sds((520, 128), F32), sds((32, 128), F32)),
        in_specs=[pl.BlockSpec(memory_space=pltpu.SMEM)] + [vm] * 20,
        out_specs=(vm,) * 5,
        scratch_shapes=[
            pltpu.VMEM((4, 4, 32, D), BF), pltpu.VMEM((3, D, D), BF), pltpu.VMEM((128, D), BF),
            pltpu.VMEM((2, D, 128), F32), pltpu.VMEM((D, D), BF), pltpu.VMEM((4, 3 * D, 128), F32),
            pltpu.VMEM((32, 64, D), BF), pltpu.VMEM((32, 16, D), BF),
            pltpu.VMEM((4, 4, 32, D), BF), pltpu.VMEM((4, 4, 32, D), BF), pltpu.VMEM((528, 128), F32),
            *scatter_scratch(64, 32, 32), *scatter_scratch(64, 32, 32), *scatter_scratch(128, 64, 64),
            *scatter_scratch(16, 16, 16),
            pltpu.SemaphoreType.DMA((4, 14)), pltpu.SemaphoreType.DMA((4, 14)),
            pltpu.SemaphoreType.DMA((3,)), pltpu.SemaphoreType.DMA((3,)),
            pltpu.SemaphoreType.DMA((3,)), pltpu.SemaphoreType.DMA((3,)),
            pltpu.VMEM((3, 32, 128), F32), pltpu.VMEM((3, 32, 128), F32), pltpu.VMEM((4, 32, 128), F32),
            pltpu.SemaphoreType.DMA((6,)), pltpu.SemaphoreType.DMA((6,)),
        ],
        compiler_params=pltpu.CompilerParams(collective_id=2, has_side_effects=True, vmem_limit_bytes=60 << 20),
    )(cnt, do1, qkv, a1, cf, w1, gains, grad1, p1o, p2, p3, dgain, *params)


def turn(x):
    return jnp.transpose(x)


def stats(h):
    x = h - jnp.mean(h, 1, keepdims=True)
    rstd = lax.rsqrt(jnp.mean(x * x, 1, keepdims=True) + 1e-5)
    return x * rstd, rstd


def norm_grad(h, da, gain):
    x, rstd = stats(h)
    dgain = jnp.sum(da * x, 0, keepdims=True)
    dx = da * gain
    dh = rstd * (dx - jnp.mean(dx, 1, keepdims=True) - x * jnp.mean(dx * x, 1, keepdims=True))
    return dh, dgain


def block(g):
    return pl.ds(mult(g * 128, 128), 128)


def feature_mask(fcnt, axis):
    shape = (256, 128) if axis else (128, 256)
    query = lax.broadcasted_iota(jnp.int32, shape, 1 - axis)
    key = lax.broadcasted_iota(jnp.int32, shape, axis)
    return (query % 32 == key % 32) & (key // 32 < fcnt)


def feature_forward(qkv, o2, fcnt):
    left = halves()
    one = jnp.where(left, 0.125, 0.0).astype(BF)
    two = jnp.where(left, 0.0, 0.125).astype(BF)
    ok = feature_mask(fcnt, 1)

    def body(n, _):
        rows, cols = block(n // 4), block(n % 4)
        q = qkv[0, rows, cols]
        qm = jnp.concatenate([q * one, q * two], 0)
        scores = jnp.where(ok, nt(qm, qkv[1, rows, cols]), NEG)
        e = jnp.exp(scores - jnp.max(scores, 1, keepdims=True))
        prob = (e * (1.0 / jnp.sum(e, 1, keepdims=True))).astype(BF)
        o = nn(prob, qkv[2, rows, cols])
        o2[rows, cols] = jnp.where(left, o[0:128], o[128:256]).astype(BF)
        return 0

    lax.fori_loop(0, 16, body, 0)


def feature_backward(qkv, do, dqkv, fcnt):
    left = halves()
    one, two = jnp.where(left, 1.0, 0.0).astype(BF), jnp.where(left, 0.0, 1.0).astype(BF)
    ok = feature_mask(fcnt, 0)
    top_lane = lax.broadcasted_iota(jnp.int32, (128, 128), 0) < 64

    def body(n, _):
        rows, cols = block(n // 4), block(n % 4)
        q = qkv[0, rows, cols] * jnp.asarray(0.125, BF)
        qm = jnp.concatenate([q * one, q * two], 0)
        g = do[rows, cols]
        gm = jnp.concatenate([g * one, g * two], 0)
        k = qkv[1, rows, cols]
        scores = jnp.where(ok, nt(k, qm), NEG)
        e = jnp.exp(scores - jnp.max(scores, 0, keepdims=True))
        prob = e * (1.0 / jnp.sum(e, 0, keepdims=True))
        pg = nt(qkv[2, rows, cols], gm)
        sg = (prob * (pg - jnp.sum(prob * pg, 0, keepdims=True))).astype(BF)
        dqt = nn(turn(k), sg)
        dq = turn(jnp.where(top_lane, dqt[:, 0:128], dqt[:, 128:256])) * 0.125
        dqkv[0, rows, cols] = dq.astype(BF)
        dqkv[1, rows, cols] = nn(sg, qm).astype(BF)
        dqkv[2, rows, cols] = nn(prob.astype(BF), gm).astype(BF)
        return 0

    lax.fori_loop(0, 16, body, 0)


def four_blocks(body, init=0):
    return lax.fori_loop(0, 4, body, init)


def flat(x):
    return x.reshape(128, D)


def cube(x):
    return x.reshape(4, 32, D)


def narrow_to(wide, part, slots, rows):
    def body(i, _):
        at = pl.ds(mult(i * rows, rows), rows)
        for b in range(4):
            part[i, :, 128 * b : 128 * b + 128] = wide[b, at, :].astype(BF)
        return 0

    lax.fori_loop(0, slots, body, 0)


def store_wide(wide, j, ways, value):
    for b in range(4):
        wide[b, pl.ds(j, value.shape[0], stride=ways), :] = value[:, 128 * b : 128 * b + 128]


def mlp(a3, a3t, g, h2, wup, wdn, h3, da, zb, dub, u, dz, wide, p3):
    h3[...] = h2[...]
    da[...] = jnp.zeros((512, D), F32)

    def body(j, _):
        u[...] = nn(a3[...], wup[j])
        dz[...] = nt(g[...], wdn[j]).astype(BF)

        def act(r, _):
            rows = pl.ds(mult(r * 64, 64), 64)
            x = u[rows, :]
            cdf = 0.5 * (1.0 + lax.erf(x * 0.7071067811865476))
            zb[rows, :] = (x * cdf).astype(BF)
            slope = cdf + x * (0.3989422804014327 * jnp.exp(-0.5 * x * x))
            dub[rows, :] = (slope * dz[rows, :].astype(F32)).astype(BF)
            return 0

        lax.fori_loop(0, 8, act, 0)
        h3[...] += nn(zb[...], wdn[j])
        da[...] += nt(dub[...], wup[j])
        store_wide(wide, j, 4, nn(a3t[...], dub[...]))
        dw = nn(turn(zb[...]), g[...]).astype(BF)
        for i in range(4):
            p3[16 + 4 * j + i] = dw[128 * i : 128 * i + 128]
        return 0

    lax.fori_loop(0, 4, body, 0)
    narrow_to(wide, p3, 16, 128)


def middle_forward(s, cells, top, o1, wo1, w2, wo2, gains, scnt, fcnt, h1, h2, a2, qkv, o2, a3, g):
    gain2, gain3 = gains[1:2, :], gains[2:3, :]
    h1[...] = nn(o1[...].reshape(512, D), wo1[...])

    def first(r, _):
        rows = block(r)
        h = h1[rows, :] + flat(cells[r].astype(F32))
        h1[rows, :] = h
        x, _ = stats(h)
        a2[rows, :] = (x * gain2).astype(BF)
        n = lax.broadcasted_iota(jnp.int32, (128, 1), 0)
        live = (n // 32 < fcnt) & (128 * s + 32 * r + n % 32 < scnt)
        g[rows, :] = jnp.where(live, flat(top[r].astype(F32)), 0.0).astype(BF)
        return 0

    four_blocks(first)

    def project(j, _):
        qkv[j] = nn(a2[...], w2[j]).astype(BF)
        return 0

    lax.fori_loop(0, 3, project, 0)
    feature_forward(qkv, o2, fcnt)
    h2[...] = h1[...] + nn(o2[...], wo2[...])

    def second(r, _):
        rows = block(r)
        x, _ = stats(h2[rows, :])
        a3[rows, :] = (x * gain3).astype(BF)
        return 0

    four_blocks(second)


def layer_output(s, h3, lout, scnt, fcnt):
    def last(r, _):
        n = lax.broadcasted_iota(jnp.int32, (128, 1), 0)
        live = (n // 32 < fcnt) & (128 * s + 32 * r + n % 32 < scnt)
        lout[r] = cube(jnp.where(live, h3[block(r), :], 0.0).astype(BF))
        return 0

    four_blocks(last)


def feature_grads(o1, wo1, w2, wo2, gains, fcnt, h1, h2, a2, qkv, o2, g, da, b, do, dqkv, wide, p2, dwo1, do1, gr, dgain):
    gain2, gain3 = gains[1:2, :], gains[2:3, :]

    def third(r, dg):
        rows = block(r)
        dh, part = norm_grad(h2[rows, :], da[rows, :], gain3)
        total = g[rows, :].astype(F32) + dh
        gr[r] = cube(total)
        b[rows, :] = total.astype(BF)
        return dg + part

    dg3 = four_blocks(third, jnp.zeros((1, D), F32))
    do[...] = nt(b[...], wo2[...]).astype(BF)
    dw = nn(turn(o2[...]), b[...]).astype(BF)
    for i in range(8):
        p2[24 + i] = dw[64 * i : 64 * i + 64]
    feature_backward(qkv, do, dqkv, fcnt)

    def weights(j, _):
        store_wide(wide, j, 3, nn(turn(a2[...]), dqkv[j]))
        return 0

    lax.fori_loop(0, 3, weights, 0)
    narrow_to(wide, p2, 24, 64)
    da[...] = nt(dqkv[0], w2[0]) + nt(dqkv[1], w2[1]) + nt(dqkv[2], w2[2])

    def fourth(r, dg):
        rows = block(r)
        dh, part = norm_grad(h1[rows, :], da[rows, :], gain2)
        total = flat(gr[r]) + dh
        gr[r] = cube(total)
        b[rows, :] = total.astype(BF)
        return dg + part

    dg2 = four_blocks(fourth, jnp.zeros((1, D), F32))
    do1[...] = nt(b[...], wo1[...]).astype(BF).reshape(4, 4, 32, D)
    dwo1[...] = nn(turn(o1[...].reshape(512, D)), b[...]).astype(BF)
    n = lax.broadcasted_iota(jnp.int32, (8, D), 0)
    dgain[...] = jnp.where(n == 1, dg2, jnp.where(n == 2, dg3, 0.0))


def kernel_b(
    scnt, fcnt, cells, top, o1, wo1, w2, wo2, wup, wdn, gains,
    lout, gr, do1, dwo1, p2, p3, dgain,
    h1, h2, a2, qkv, o2, a3, a3t, g, h3, da, zb, dub, u, dz, wide, b, do, dqkv,
):
    s = lax.axis_index("samp")
    middle_forward(s, cells, top, o1, wo1, w2, wo2, gains, scnt[0], fcnt[0], h1, h2, a2, qkv, o2, a3, g)
    a3t[...] = turn(a3[...])
    mlp(a3, a3t, g, h2, wup, wdn, h3, da, zb, dub, u, dz, wide, p3)
    layer_output(s, h3, lout, scnt[0], fcnt[0])
    feature_grads(
        o1, wo1, w2, wo2, gains, fcnt[0], h1, h2, a2, qkv, o2, g, da, b, do, dqkv, wide, p2, dwo1, do1, gr, dgain
    )


def middle_scratch():
    w = pltpu.VMEM((D, D), F32)
    n = pltpu.VMEM((D, D), BF)
    three = pltpu.VMEM((3, D, D), BF)
    return [w, w, n, three, n, n, n, n, w, w, n, n, w, n, pltpu.VMEM((4, 4 * D, 128), F32), n, n, three]


def call_b(scnt, fcnt, cells, top, o1, wo1, w2, wo2, wup, wdn, gains):
    sds = jax.ShapeDtypeStruct
    vm = pl.BlockSpec(memory_space=pltpu.VMEM)
    sm = pl.BlockSpec(memory_space=pltpu.SMEM)
    return pl.pallas_call(
        kernel_b,
        name="kernel_b",
        out_shape=(
            sds((4, 4, 32, D), BF), sds((4, 4, 32, D), F32), sds((4, 4, 32, D), BF), sds((D, D), BF),
            sds((32, 64, D), BF), sds((32, 128, D), BF), sds((8, D), F32),
        ),
        in_specs=[sm, sm] + [vm] * 9,
        out_specs=(vm,) * 7,
        scratch_shapes=middle_scratch(),
        compiler_params=pltpu.CompilerParams(vmem_limit_bytes=60 << 20),
    )(scnt, fcnt, cells, top, o1, wo1, w2, wo2, wup, wdn.reshape(4, D, D), gains)


def local(x):
    return jnp.transpose(x.reshape(4, 32, 4, D), (0, 2, 1, 3))


def globe(x):
    return jnp.transpose(x, (0, 2, 1, 3)).reshape(1, 128, 4, D)


def fast_device(cells, out_grad, scnt, fcnt, b1, f1, s1, b2, f2, s2, b3, f3, s3):
    here_cells, top = local(cells), local(out_grad)
    o1, w1, wo1, w2, wo2, wup, wdn, gains, qkv, a1, cf = call_a(scnt, here_cells, b1, b2, b3)
    out, gr, do1, dwo1, p2, p3, dgain = call_b(scnt, fcnt, here_cells, top, o1, wo1, w2, wo2, wup, wdn, gains)
    params = (b1, f1, s1, b2, f2, s2, b3, f3, s3)
    cgrad, sh1, sh2, sh3, total = call_c(scnt, do1, qkv, a1, cf, w1, gains, gr, dwo1, p2, p3, dgain, params)
    outs = call_e(total, (sh1, sh2, sh3), params)
    return (globe(out), globe(cgrad), *outs)


def step(*args):
    cells = args[0]
    fits = lax.axis_size("task") == 8 and lax.axis_size("samp") == 4 and cells.shape == (1, 128, 4, D)
    return fast_device(*args) if fits else on_device(*args)


def solution(mesh):
    placed = (
        P("task", "samp", None, None),
        P("task", "samp", None, None),
        P("task"),
        P("task"),
        P(("task", "samp")),
        P(("task", "samp")),
        P(("task", "samp")),
        P(("task", "samp")),
        P(("task", "samp")),
        P(("task", "samp")),
        P(("task", "samp")),
        P(("task", "samp")),
        P(("task", "samp")),
    )
    return jax.shard_map(
        step,
        mesh=mesh,
        in_specs=placed,
        out_specs=(
            P("task", "samp", None, None),
            P("task", "samp", None, None),
            P(("task", "samp")),
            P(("task", "samp")),
            P(("task", "samp")),
            P(("task", "samp")),
            P(("task", "samp")),
            P(("task", "samp")),
            P(("task", "samp")),
            P(("task", "samp")),
            P(("task", "samp")),
            P(("task", "samp")),
            P(("task", "samp")),
            P(("task", "samp")),
            P(("task", "samp")),
            P(("task", "samp")),
            P(("task", "samp")),
            P(),
        ),
        check_vma=False,
    )
```

```python
import jax
import jax.numpy as jnp
from jax import lax
from jax.experimental import pallas as pl
from jax.experimental.pallas import tpu as pltpu
from jax.sharding import PartitionSpec as P

D = 512
HEADS = 8
HEAD_DIM = 64
FF = 2048


EPS_NORM = 1e-05
EPS_ADAM = 1e-06
STEP_RATE = 0.5
BIG_NEGATIVE = -1e30


def normalize(hidden, gain_row):
    centre = jnp.mean(hidden, -1, keepdims=True)
    shifted = hidden - centre
    spread = jnp.mean(shifted * shifted, -1, keepdims=True)
    return shifted * lax.rsqrt(spread + EPS_NORM) * gain_row


def norm_backward(hidden, gain_row, normed_grad):
    _, pullback = jax.vjp(normalize, hidden, gain_row)
    return pullback(normed_grad)


def gelu_exact(upward):
    return jax.nn.gelu(upward, approximate=False)


def contract_rows(left, right):
    return lax.dot_general(
        left, right, (((0,), (0,)), ((), ())), preferred_element_type=jnp.float32
    )


def times_transpose(left, right):
    return lax.dot_general(
        left, right, (((1,), (1,)), ((), ())), preferred_element_type=jnp.float32
    )


def unpack(flat_params, width_in, width_mid):
    gain_row = flat_params[:D].astype(jnp.float32)
    w_in = flat_params[D : D + D * width_in].reshape(D, width_in)
    w_out = flat_params[D + D * width_in :].reshape(width_mid, D)
    return (gain_row, w_in, w_out)


def fetch_forward(master):
    return lax.all_gather(master.astype(jnp.bfloat16), ("task", "samp"), axis=0, tiled=True)


def fetch_again(master):
    return lax.all_gather(master.astype(jnp.bfloat16), ("task", "samp"), axis=0, tiled=True)


def reduce_grads(gain_grad, in_grad, out_grad_matrix):
    flat_grads = jnp.concatenate([gain_grad, in_grad.reshape(-1), out_grad_matrix.reshape(-1)])
    return lax.psum_scatter(flat_grads, ("task", "samp"), scatter_dimension=0, tiled=True)


def group_size(feature_total, most):
    chosen = 1
    for candidate in range(1, most + 1):
        if feature_total % candidate == 0:
            chosen = candidate
    return chosen


def lamb_prepare(grad_shard, master, first, second, width_in):
    first_new = 0.5 * first + 0.5 * grad_shard
    second_new = 0.5 * second + 0.5 * grad_shard * grad_shard
    direction = first_new / (jnp.sqrt(second_new) + EPS_ADAM)
    entries = master.shape[0]
    position = lax.axis_index(("task", "samp")) * entries + jnp.arange(entries, dtype=jnp.int32)
    segment = (position >= D).astype(jnp.int32) + (position >= D + D * width_in).astype(jnp.int32)
    member = segment[None, :] == jnp.arange(3, dtype=jnp.int32)[:, None]
    weight_sums = jnp.sum(jnp.where(member, (master * master)[None, :], 0.0), 1)
    update_sums = jnp.sum(jnp.where(member, (direction * direction)[None, :], 0.0), 1)
    return (first_new, second_new, direction, member, jnp.stack([weight_sums, update_sums], 1))


def lamb_finish(master, block_state, trust_ratio):
    factor = jnp.sum(jnp.where(block_state[3], trust_ratio[:, None], 0.0), 0)
    return master - STEP_RATE * factor * block_state[2]


def sample_scores(query_part, key_part, key_live, score_scale):
    scores = (
        jnp.einsum("qfhe,kfhe->fhqk", query_part, key_part, preferred_element_type=jnp.float32)
        * score_scale
    )
    return jnp.where(key_live, scores, BIG_NEGATIVE)


def sample_forward(queries, pairs_all, key_live, block_features, score_scale):
    local_rows, features = (queries.shape[0], queries.shape[1])

    def one_block(block_index, results):
        attended, log_totals = results
        offset = block_index * block_features
        query_part = lax.dynamic_slice_in_dim(queries, offset, block_features, 1)
        pair_part = lax.dynamic_slice_in_dim(pairs_all, offset, block_features, 1)
        scores = sample_scores(query_part, pair_part[:, :, 0], key_live, score_scale)
        row_top = jnp.max(scores, -1, keepdims=True)
        exponent = jnp.exp(scores - row_top)
        row_total = jnp.sum(exponent, -1, keepdims=True)
        probability = (exponent / row_total).astype(jnp.bfloat16)
        block_out = jnp.einsum(
            "fhqk,kfhe->qfhe", probability, pair_part[:, :, 1], preferred_element_type=jnp.float32
        )
        attended = lax.dynamic_update_slice_in_dim(
            attended, block_out.astype(jnp.bfloat16), offset, 1
        )
        log_totals = lax.dynamic_update_slice_in_dim(
            log_totals, (row_top + jnp.log(row_total))[..., 0], offset, 0
        )
        return (attended, log_totals)

    start_state = (
        jnp.zeros(queries.shape, jnp.bfloat16),
        jnp.zeros((features, HEADS, local_rows), jnp.float32),
    )
    return lax.fori_loop(0, features // block_features, one_block, start_state)


def query_side(query_part, pair_part, grad_part, log_part, key_live, score_scale):
    key_part = pair_part[:, :, 0]
    value_part = pair_part[:, :, 1]
    scores = sample_scores(query_part, key_part, key_live, score_scale)
    probability = jnp.exp(scores - log_part[..., None])
    prob_grad = jnp.einsum(
        "qfhe,kfhe->fhqk", grad_part, value_part, preferred_element_type=jnp.float32
    )
    row_inner = jnp.sum(probability * prob_grad, -1, keepdims=True)
    score_grad = (probability * (prob_grad - row_inner)).astype(jnp.bfloat16)
    query_block = (
        jnp.einsum("fhqk,kfhe->qfhe", score_grad, key_part, preferred_element_type=jnp.float32)
        * score_scale
    )
    return (probability, score_grad, row_inner, query_block)


def sample_backward(
    queries, pairs_all, key_live, log_totals, attended_grad, block_features, score_scale
):
    local_rows, features = (queries.shape[0], queries.shape[1])

    def one_block(block_index, results):
        query_grads, pair_grads = results
        offset = block_index * block_features
        query_part = lax.dynamic_slice_in_dim(queries, offset, block_features, 1)
        pair_part = lax.dynamic_slice_in_dim(pairs_all, offset, block_features, 1)
        grad_part = lax.dynamic_slice_in_dim(attended_grad, offset, block_features, 1)
        log_part = lax.dynamic_slice_in_dim(log_totals, offset, block_features, 0)
        probability, score_grad, row_inner, query_block = query_side(
            query_part, pair_part, grad_part, log_part, key_live, score_scale
        )
        key_block = (
            jnp.einsum(
                "fhqk,qfhe->kfhe", score_grad, query_part, preferred_element_type=jnp.float32
            )
            * score_scale
        )
        value_block = jnp.einsum(
            "fhqk,qfhe->kfhe",
            probability.astype(jnp.bfloat16),
            grad_part,
            preferred_element_type=jnp.float32,
        )
        pair_terms = jnp.stack([key_block, value_block], 2)
        pair_local = lax.psum_scatter(
            pair_terms.astype(jnp.bfloat16), "samp", scatter_dimension=0, tiled=True
        ).astype(jnp.float32)
        query_grads = lax.dynamic_update_slice_in_dim(query_grads, query_block, offset, 1)
        pair_grads = lax.dynamic_update_slice_in_dim(pair_grads, pair_local, offset, 1)
        return (query_grads, pair_grads)

    start_state = (
        jnp.zeros((local_rows, features, HEADS, HEAD_DIM), jnp.float32),
        jnp.zeros((local_rows, features, 2, HEADS, HEAD_DIM), jnp.float32),
    )
    return lax.fori_loop(0, features // block_features, one_block, start_state)


def on_device(
    cells,
    out_grad,
    sample_counts,
    feature_counts,
    sample_block,
    sample_first,
    sample_second,
    feature_block,
    feature_first,
    feature_second,
    mlp_block,
    mlp_first,
    mlp_second,
):
    local_rows, features = (cells.shape[1], cells.shape[2])
    flat_rows = local_rows * features
    seq_all = local_rows * lax.axis_size("samp")
    score_scale = HEAD_DIM ** (-0.5)
    block_features = group_size(features, max(1, 2048 // (HEADS * local_rows)))
    sample_index = lax.axis_index("samp") * local_rows + jnp.arange(local_rows, dtype=jnp.int32)
    sample_live = sample_index < sample_counts[0]
    key_live = jnp.arange(seq_all, dtype=jnp.int32) < sample_counts[0]
    feature_live = jnp.arange(features, dtype=jnp.int32) < feature_counts[0]
    cell_live = sample_live[:, None, None] & feature_live[None, :, None]
    hidden_in = cells[0].astype(jnp.float32)
    gain_one, in_one, out_one = unpack(fetch_forward(sample_block), 3 * D, D)
    normed_one = normalize(hidden_in, gain_one).astype(jnp.bfloat16)
    packed_one = jnp.dot(
        normed_one.reshape(flat_rows, D), in_one, preferred_element_type=jnp.float32
    )
    packed_one = packed_one.astype(jnp.bfloat16).reshape(local_rows, features, 3, HEADS, HEAD_DIM)
    queries_one = packed_one[:, :, 0]
    pairs_local = packed_one[:, :, 1:]
    pairs_all = lax.all_gather(pairs_local, "samp", axis=0, tiled=True)
    attended_one, log_totals = sample_forward(
        queries_one, pairs_all, key_live, block_features, score_scale
    )
    attended_one_rows = attended_one.reshape(flat_rows, D)
    branch_one = jnp.dot(attended_one_rows, out_one, preferred_element_type=jnp.float32)
    hidden_one = hidden_in + branch_one.reshape(local_rows, features, D)
    gain_two, in_two, out_two = unpack(fetch_forward(feature_block), 3 * D, D)
    normed_two = normalize(hidden_one, gain_two).astype(jnp.bfloat16).reshape(flat_rows, D)
    packed_two = jnp.dot(normed_two, in_two, preferred_element_type=jnp.float32)
    packed_two = packed_two.astype(jnp.bfloat16).reshape(local_rows, features, 3, HEADS, HEAD_DIM)
    queries_two, key_two, value_two = (
        packed_two[:, :, 0],
        packed_two[:, :, 1],
        packed_two[:, :, 2],
    )
    scores_two = (
        jnp.einsum("sqhe,skhe->shqk", queries_two, key_two, preferred_element_type=jnp.float32)
        * score_scale
    )
    scores_two = jnp.where(feature_live, scores_two, BIG_NEGATIVE)
    row_top = jnp.max(scores_two, -1, keepdims=True)
    exponent = jnp.exp(scores_two - row_top)
    probability_two = exponent / jnp.sum(exponent, -1, keepdims=True)
    prob_low_two = probability_two.astype(jnp.bfloat16)
    attended_two = jnp.einsum(
        "shqk,skhe->sqhe", prob_low_two, value_two, preferred_element_type=jnp.float32
    )
    attended_two_rows = attended_two.reshape(flat_rows, D).astype(jnp.bfloat16)
    branch_two = jnp.dot(attended_two_rows, out_two, preferred_element_type=jnp.float32)
    hidden_two = hidden_one + branch_two.reshape(local_rows, features, D)
    gain_three, up_weight, down_weight = unpack(fetch_forward(mlp_block), FF, FF)
    normed_three = normalize(hidden_two, gain_three).astype(jnp.bfloat16).reshape(flat_rows, D)
    upward = jnp.dot(normed_three, up_weight, preferred_element_type=jnp.float32)
    activated = gelu_exact(upward).astype(jnp.bfloat16)
    branch_three = jnp.dot(activated, down_weight, preferred_element_type=jnp.float32)
    hidden_three = hidden_two + branch_three.reshape(local_rows, features, D)
    layer_out = jnp.where(cell_live, hidden_three, 0.0).astype(jnp.bfloat16)[None]
    top_grad = jnp.where(cell_live, out_grad[0], jnp.zeros((), jnp.bfloat16))
    top_rows = top_grad.reshape(flat_rows, D)
    gain_three, up_weight, down_weight = unpack(fetch_again(mlp_block), FF, FF)
    down_grad = contract_rows(activated, top_rows)
    act_grad = times_transpose(top_rows, down_weight).astype(jnp.bfloat16)
    _, gelu_pull = jax.vjp(gelu_exact, upward)
    up_grad = gelu_pull(act_grad.astype(jnp.float32))[0].astype(jnp.bfloat16)
    upw_grad = contract_rows(normed_three, up_grad)
    normed_grad = times_transpose(up_grad, up_weight).reshape(local_rows, features, D)
    hidden_grad, gain_three_grad = norm_backward(hidden_two, gain_three, normed_grad)
    grad_two = top_grad.astype(jnp.float32) + hidden_grad
    mlp_shard = reduce_grads(gain_three_grad, upw_grad, down_grad)
    mlp_state = lamb_prepare(mlp_shard, mlp_block, mlp_first, mlp_second, FF)
    gain_two, in_two, out_two = unpack(fetch_again(feature_block), 3 * D, D)
    branch_grad = grad_two.astype(jnp.bfloat16).reshape(flat_rows, D)
    out_two_grad = contract_rows(attended_two_rows, branch_grad)
    attended_grad = (
        times_transpose(branch_grad, out_two)
        .astype(jnp.bfloat16)
        .reshape(local_rows, features, HEADS, HEAD_DIM)
    )
    prob_grad = jnp.einsum(
        "sqhe,skhe->shqk", attended_grad, value_two, preferred_element_type=jnp.float32
    )
    row_inner = jnp.sum(probability_two * prob_grad, -1, keepdims=True)
    score_grad = (probability_two * (prob_grad - row_inner)).astype(jnp.bfloat16)
    query_grad = (
        jnp.einsum("shqk,skhe->sqhe", score_grad, key_two, preferred_element_type=jnp.float32)
        * score_scale
    )
    key_grad = (
        jnp.einsum("shqk,sqhe->skhe", score_grad, queries_two, preferred_element_type=jnp.float32)
        * score_scale
    )
    value_grad = jnp.einsum(
        "shqk,sqhe->skhe", prob_low_two, attended_grad, preferred_element_type=jnp.float32
    )
    packed_grad = (
        jnp.stack([query_grad, key_grad, value_grad], 2)
        .astype(jnp.bfloat16)
        .reshape(flat_rows, 3 * D)
    )
    in_two_grad = contract_rows(normed_two, packed_grad)
    normed_grad = times_transpose(packed_grad, in_two).reshape(local_rows, features, D)
    hidden_grad, gain_two_grad = norm_backward(hidden_one, gain_two, normed_grad)
    grad_one = grad_two + hidden_grad
    feature_shard = reduce_grads(gain_two_grad, in_two_grad, out_two_grad)
    feature_state = lamb_prepare(feature_shard, feature_block, feature_first, feature_second, 3 * D)
    gain_one, in_one, out_one = unpack(fetch_again(sample_block), 3 * D, D)
    pairs_all = lax.all_gather(pairs_local, "samp", axis=0, tiled=True)
    branch_grad = grad_one.astype(jnp.bfloat16).reshape(flat_rows, D)
    out_one_grad = contract_rows(attended_one_rows, branch_grad)
    attended_grad = (
        times_transpose(branch_grad, out_one)
        .astype(jnp.bfloat16)
        .reshape(local_rows, features, HEADS, HEAD_DIM)
    )
    query_grads, pair_grads = sample_backward(
        queries_one, pairs_all, key_live, log_totals, attended_grad, block_features, score_scale
    )
    packed_grad = (
        jnp.concatenate([query_grads[:, :, None], pair_grads], 2)
        .astype(jnp.bfloat16)
        .reshape(flat_rows, 3 * D)
    )
    in_one_grad = contract_rows(normed_one.reshape(flat_rows, D), packed_grad)
    normed_grad = times_transpose(packed_grad, in_one).reshape(local_rows, features, D)
    hidden_grad, gain_one_grad = norm_backward(hidden_in, gain_one, normed_grad)
    cells_grad = (grad_one + hidden_grad)[None]
    sample_shard = reduce_grads(gain_one_grad, in_one_grad, out_one_grad)
    sample_state = lamb_prepare(sample_shard, sample_block, sample_first, sample_second, 3 * D)
    totals = lax.psum(
        jnp.concatenate([sample_state[4], feature_state[4], mlp_state[4]], 0), ("task", "samp")
    )
    norm_pairs = jnp.sqrt(totals)
    trust_ratio = norm_pairs[:, 0] / (norm_pairs[:, 1] + EPS_ADAM)
    sample_master = lamb_finish(sample_block, sample_state, trust_ratio[0:3])
    feature_master = lamb_finish(feature_block, feature_state, trust_ratio[3:6])
    mlp_master = lamb_finish(mlp_block, mlp_state, trust_ratio[6:9])
    return (
        layer_out,
        cells_grad,
        sample_shard,
        sample_state[0],
        sample_state[1],
        sample_master,
        sample_master.astype(jnp.bfloat16),
        feature_shard,
        feature_state[0],
        feature_state[1],
        feature_master,
        feature_master.astype(jnp.bfloat16),
        mlp_shard,
        mlp_state[0],
        mlp_state[1],
        mlp_master,
        mlp_master.astype(jnp.bfloat16),
        norm_pairs,
    )


D = 512
MESH = pl.DeviceIdType.MESH
BF = jnp.bfloat16
F32 = jnp.float32
NEG = -1e30


def mult(value, factor):
    return pl.multiple_of(value, factor)


def nt(left, right):
    return lax.dot_general(left, right, (((1,), (1,)), ((), ())), preferred_element_type=F32)


def nn(left, right):
    return lax.dot_general(left, right, (((1,), (0,)), ((), ())), preferred_element_type=F32)


def here():
    return lax.axis_index("task"), lax.axis_index("samp")


def peers(t, s):
    return (
        (jnp.bitwise_xor(t, 1), s),
        (jnp.bitwise_xor(t, 2), s),
        (jnp.bitwise_xor(t, 4), s),
        (t, (s + 1) % 4),
        (t, (s + 2) % 4),
        (t, (s + 3) % 4),
    )


def enter(t, s):
    barrier = pltpu.get_barrier_semaphore()
    for peer in peers(t, s):
        pl.semaphore_signal(barrier, inc=1, device_id=peer, device_id_type=MESH)
    return barrier


def send(src, dst, ssem, rsem, peer):
    copy = pltpu.make_async_remote_copy(
        src_ref=src, dst_ref=dst, send_sem=ssem, recv_sem=rsem, device_id=peer, device_id_type=MESH
    )
    copy.start()
    return copy


class Gather:
    def __init__(self, buf, half, ssem, rsem, t, s):
        self.buf, self.t, self.s = buf, t, s
        rows = buf.shape[1]
        self.ha, self.hb = pl.ds(0, half), pl.ds(half, rows - half)
        self.all = pl.ds(0, rows)
        self.ssem, self.rsem = ssem, rsem
        self.count = 0
        self.copies = []
        self.tx, self.ty = jnp.bitwise_xor(t, 2), jnp.bitwise_xor(t, 4)
        self.txy, self.tc = jnp.bitwise_xor(t, 6), jnp.bitwise_xor(t, 1)

    def go(self, slots, rows, peer):
        view = self.buf.at[slots, rows]
        i = self.count
        self.count += 1
        copy = send(view, view, self.ssem.at[i], self.rsem.at[i], peer)
        self.copies.append(copy)
        return copy

    def four(self, t):
        return pl.ds(4 * t, 4)

    def z(self):
        t, s = self.t, self.s
        own = pl.ds(4 * t + s, 1)
        self.zc = [self.go(own, self.all, (t, (s + k) % 4)) for k in (1, 2, 3)]

    def one(self):
        for copy in self.zc:
            copy.wait_recv()
        t, s = self.t, self.s
        self.x1 = self.go(self.four(t), self.ha, (self.tx, s))
        self.y1 = self.go(self.four(t), self.hb, (self.ty, s))
        self.c = [self.go(self.four(t), self.all, (self.tc, s))]

    def two(self):
        s = self.s
        t = self.t
        self.x1.wait_recv()
        self.y2 = [
            self.go(self.four(t), self.ha, (self.ty, s)),
            self.go(self.four(self.tx), self.ha, (self.ty, s)),
        ]
        self.y1.wait_recv()
        self.x2 = [
            self.go(self.four(t), self.hb, (self.tx, s)),
            self.go(self.four(self.ty), self.hb, (self.tx, s)),
        ]
        self.c.append(self.go(self.four(self.tx), self.ha, (self.tc, s)))
        self.c.append(self.go(self.four(self.ty), self.hb, (self.tc, s)))

    def three(self):
        s = self.s
        for copy in self.y2 + self.x2:
            copy.wait_recv()
        self.c.append(self.go(self.four(self.ty), self.ha, (self.tc, s)))
        self.c.append(self.go(self.four(self.txy), self.ha, (self.tc, s)))
        self.c.append(self.go(self.four(self.tx), self.hb, (self.tc, s)))
        self.c.append(self.go(self.four(self.txy), self.hb, (self.tc, s)))

    def end(self):
        for copy in self.c:
            copy.wait_recv()

    def drain(self):
        for copy in self.copies:
            copy.wait_send()


def realign(m_ref, sh_ref, d, rows, out_ref, out_at, roll_to):
    whole = 4 * rows
    total = whole + 8
    q, p = d // 8, d % 8
    lane = lax.broadcasted_iota(jnp.int32, (total, 128), 1)
    roll_to[0:8, :] = jnp.zeros((8, 128), F32)
    for i in range(whole // 8):
        sh_ref[8 * i : 8 * i + 8, :] = m_ref[pl.ds(1024 * i, 1024)].reshape(8, 128)
    sh_ref[whole:total, :] = jnp.zeros((8, 128), F32)
    sh_ref[whole : whole + 1, 0:16] = m_ref[pl.ds(128 * whole, 16)].reshape(1, 16)
    rolled = pltpu.roll(sh_ref[0:total, :], 16 * p, 1)
    roll_to[8 : 8 + total, :] = rolled
    sh_ref[0:8, :] = jnp.zeros((8, 128), F32)
    sh_ref[8 : 8 + total, :] = jnp.where(lane < 16 * p, roll_to[7 : 7 + total, :], rolled)
    firsts = []
    for b in range(4):
        out_ref[out_at, 0:rows, 128 * b : 128 * b + 128] = sh_ref[pl.ds(12 - q + b, rows, stride=4), :].astype(BF)
        firsts.append(sh_ref[pl.ds(8 - q + b, 1), :])
    return jnp.concatenate(firsts, 1)


def spread(buf, firsts, kind, rows, lo, hi, put):
    tail = lax.broadcasted_iota(jnp.int32, (8, D), 0) == 7

    def body(i, _):
        nxt = jnp.minimum(i + 1, 31)
        row = firsts[nxt, 64:80, :].astype(F32)[kind : kind + 1, :]
        block = buf[i, 0:rows, :].astype(F32)
        last = block[rows - 8 : rows, :] + jnp.where(tail & (i < 31), row, 0.0)
        put(i - lo, block[0 : rows - 8, :], last)
        return 0

    lax.fori_loop(lo, hi, body, 0)


def put_f32(dst, rows):
    def put(i, head, last):
        for b in range(4):
            cols = slice(128 * b, 128 * b + 128)
            dst[b, pl.ds(mult(i * rows, rows), rows - 8), :] = head[:, cols]
            dst[b, pl.ds(mult(i * rows + rows - 8, 8), 8), :] = last[:, cols]

    return put


def put_bf(dst, rows):
    def put(i, head, last):
        dst[pl.ds(mult(i * rows, rows), rows), :] = jnp.concatenate([head, last], 0).astype(BF)

    return put


def split_columns(wide, ways, dst):
    def body(i, _):
        for j in range(ways):
            for b in range(4):
                piece = wide[b, pl.ds(64 * ways * i + j, 64, stride=ways), :]
                dst[j, pl.ds(mult(64 * i, 64), 64), 128 * b : 128 * b + 128] = piece.astype(BF)
        return 0

    lax.fori_loop(0, 8, body, 0)


def halves():
    lane = lax.broadcasted_iota(jnp.int32, (128, 128), 1)
    return lane < 64


def attend_chunk(qkv, c, live, out):
    left = halves()
    one = jnp.where(left, 0.125, 0.0).astype(BF)
    two = jnp.where(left, 0.0, 0.125).astype(BF)

    def body(h, _):
        cols = pl.ds(mult(h * 128, 128), 128)
        q = qkv[0, pl.ds(mult(c * 128, 128), 128), cols]
        qm = jnp.concatenate([q * one, q * two], 0)
        scores = jnp.where(live, nt(qm, qkv[1, :, cols]), NEG)
        top = jnp.max(scores, 1, keepdims=True)
        e = jnp.exp(scores - top)
        prob = (e * (1.0 / jnp.sum(e, 1, keepdims=True))).astype(BF)
        o = nn(prob, qkv[2, :, cols])
        o = jnp.where(left, o[0:128], o[128:256]).astype(BF)
        for g in range(4):
            out[g, :, cols] = o[32 * g : 32 * g + 32]
        return 0

    lax.fori_loop(0, 4, body, 0)


def kernel_a(
    cnt, cells, m1, m2, m3,
    o1rows, w1, wo1, w2, wo2, wup, wdn, gains, qkv, a1, cf,
    g1, g2, g3, wide, sh, ro, o1c, w1v, wo1v, w2v, wo2v, wupv, wdnv, qkvv,
    gs, gr, as_, ar, os_, or_, lsem,
):
    t, s = here()
    d = 4 * t + s
    barrier = enter(t, s)
    ga = Gather(g1, 32, gs.at[0], gr.at[0], t, s)
    gb = Gather(g2, 32, gs.at[1], gr.at[1], t, s)
    gc = Gather(g3, 64, gs.at[2], gr.at[2], t, s)
    f1 = realign(m1, sh, d, 64, g1, d, ro)
    f2 = realign(m2, sh, d, 64, g2, d, ro)
    f3 = realign(m3, sh, d, 128, g3, d, ro)
    row = lax.broadcasted_iota(jnp.int32, (16, D), 0)
    firsts = jnp.where(row == 0, f1, jnp.where(row == 1, f2, jnp.where(row == 2, f3, 0.0)))
    g1[d, 64:80, :] = firsts.astype(BF)
    pl.semaphore_wait(barrier, 6)
    ga.z()
    cf[s] = cells[:, s, :, :]
    moves = [
        send(cells.at[:, (s + k) % 4], cf.at[s], as_.at[k - 1], ar.at[k - 1], (t, (s + k) % 4)) for k in (1, 2, 3)
    ]
    ga.one()
    ga.two()
    for copy in moves:
        copy.wait_recv()
    gb.z()
    gc.z()
    ga.three()
    ga.end()
    spread(g1, g1, 0, 64, 0, 24, put_f32(wide, 64))
    split_columns(wide, 3, w1v)
    spread(g1, g1, 0, 64, 24, 32, put_bf(wo1v, 64))
    gains[...] = g1[0, 64:80, :].astype(F32)[0:8]
    gain = g1[0, 64:80, :].astype(F32)[0:1]

    def norm(i, _):
        h = cf[i].astype(F32).reshape(128, D)
        mean = jnp.mean(h, 1, keepdims=True)
        x = h - mean
        var = jnp.mean(x * x, 1, keepdims=True)
        a1[pl.ds(mult(i * 128, 128), 128), :] = (x * lax.rsqrt(var + 1e-5) * gain).astype(BF)
        return 0

    lax.fori_loop(0, 4, norm, 0)

    def project(i, _):
        j, r = i // 4, i % 4
        rows = pl.ds(mult(r * 128, 128), 128)
        qkvv[j, rows, :] = nn(a1[rows, :], w1v[j]).astype(BF)
        return 0

    lax.fori_loop(0, 12, project, 0)
    live = lax.broadcasted_iota(jnp.int32, (1, 512), 1) < cnt[0]
    backs = []
    local = []

    def keep(src, dst):
        copy = pltpu.make_async_copy(src, dst, lsem.at[len(local)])
        copy.start()
        local.append(copy)

    keep(w1v, w1)
    keep(wo1v, wo1)
    keep(qkvv, qkv)
    for k in (2, 1, 3, 0):
        c = (s + k) % 4
        if k:
            attend_chunk(qkvv, c, live, o1c.at[k - 1])
            backs.append(send(o1c.at[k - 1], o1rows.at[:, s], os_.at[k - 1], or_.at[k - 1], (t, c)))
        else:
            attend_chunk(qkvv, c, live, o1rows.at[:, s])
        if k == 2:
            gb.one()
            gc.one()
        if k == 1:
            gb.two()
            gc.two()
        if k == 3:
            gb.three()
    gb.end()
    spread(g2, g1, 1, 64, 0, 24, put_f32(wide, 64))
    split_columns(wide, 3, w2v)
    spread(g2, g1, 1, 64, 24, 32, put_bf(wo2v, 64))
    keep(w2v, w2)
    keep(wo2v, wo2)
    gc.three()
    gc.end()
    spread(g3, g1, 2, 128, 0, 16, put_f32(wide, 128))
    split_columns(wide, 4, wupv)
    keep(wupv, wup)
    spread(g3, g1, 2, 128, 16, 32, put_bf(wdnv, 128))
    keep(wdnv, wdn)
    for copy in backs:
        copy.wait_recv()
    for copy in moves + backs:
        copy.wait_send()
    ga.drain()
    gb.drain()
    gc.drain()
    for copy in local:
        copy.wait()


def call_a(cnt, cells_fm, m1, m2, m3):
    sds = jax.ShapeDtypeStruct
    vm = pl.BlockSpec(memory_space=pltpu.VMEM)
    hb = pl.BlockSpec(memory_space=pl.ANY)
    return pl.pallas_call(
        kernel_a,
        name="kernel_a",
        out_shape=(
            sds((4, 4, 32, D), BF), sds((3, D, D), BF), sds((D, D), BF), sds((3, D, D), BF), sds((D, D), BF),
            sds((4, D, D), BF), sds((4 * D, D), BF), sds((8, D), F32), sds((3, D, D), BF), sds((D, D), BF),
            sds((4, 4, 32, D), BF),
        ),
        in_specs=[pl.BlockSpec(memory_space=pltpu.SMEM), vm, vm, vm, vm],
        out_specs=(vm, hb, hb, hb, hb, hb, hb, vm, hb, vm, vm),
        scratch_shapes=[
            pltpu.VMEM((32, 80, D), BF), pltpu.VMEM((32, 64, D), BF), pltpu.VMEM((32, 128, D), BF),
            pltpu.VMEM((4, 4 * D, 128), F32), pltpu.VMEM((536, 128), F32), pltpu.VMEM((536, 128), F32),
            pltpu.VMEM((3, 4, 32, D), BF),
            pltpu.VMEM((3, D, D), BF), pltpu.VMEM((D, D), BF), pltpu.VMEM((3, D, D), BF), pltpu.VMEM((D, D), BF),
            pltpu.VMEM((4, D, D), BF), pltpu.VMEM((4 * D, D), BF), pltpu.VMEM((3, D, D), BF),
            pltpu.SemaphoreType.DMA((3, 16)), pltpu.SemaphoreType.DMA((3, 16)),
            pltpu.SemaphoreType.DMA((3,)), pltpu.SemaphoreType.DMA((3,)),
            pltpu.SemaphoreType.DMA((3,)), pltpu.SemaphoreType.DMA((3,)),
            pltpu.SemaphoreType.DMA((7,)),
        ],
        compiler_params=pltpu.CompilerParams(collective_id=1, has_side_effects=True, vmem_limit_bytes=56 << 20),
    )(cnt, cells_fm, m1, m2, m3)


def edges(d, entries, width):
    begin = d * entries
    return D - begin, D + D * width - begin


def segment(k, ends):
    return (k >= ends[0]).astype(jnp.int32) + (k >= ends[1]).astype(jnp.int32)


def lamb_step(g, m, f, s):
    fn = 0.5 * f + 0.5 * g
    sn = 0.5 * s + 0.5 * g * g
    return fn, sn, fn / (jnp.sqrt(sn) + 1e-6)


def squares(sh, m, f, s, sums, d, width, b):
    entries = m.shape[0]
    whole = entries // 1024
    ends = edges(d, entries, width)
    lane = lax.broadcasted_iota(jnp.int32, (8, 128), 0) * 128 + lax.broadcasted_iota(jnp.int32, (8, 128), 1)
    zero = jnp.zeros((8, 128), F32)

    def body(i, acc):
        at = pl.ds(mult(i * 1024, 1024), 1024)
        old = m[at].reshape(8, 128)
        _, _, r = lamb_step(
            sh[pl.ds(mult(i * 8, 8), 8), :], old, f[at].reshape(8, 128), s[at].reshape(8, 128)
        )
        part = segment(lane + i * 1024, ends)
        out = []
        for n, value in enumerate((old * old, r * r)):
            for k in range(3):
                out.append(acc[3 * n + k] + jnp.where(part == k, value, 0.0))
        return tuple(out)

    acc = lax.fori_loop(0, whole, body, (zero,) * 6)
    at = pl.ds(whole * 1024, 16)
    old = m[at].reshape(1, 16)
    _, _, r = lamb_step(
        sh[8 * whole : 8 * whole + 1, 0:16], old, f[at].reshape(1, 16), s[at].reshape(1, 16)
    )
    part = segment(lax.broadcasted_iota(jnp.int32, (1, 16), 1) + whole * 1024, ends)
    first = lax.broadcasted_iota(jnp.int32, (1, 128), 1) == 0
    for n, value in enumerate((old * old, r * r)):
        for k in range(3):
            row = 16 * n + 3 * b + k
            tail = jnp.sum(jnp.where(part == k, value, 0.0), 1, keepdims=True)
            sums[row : row + 1, :] = jnp.sum(acc[3 * n + k], 0, keepdims=True) + jnp.where(first, tail, 0.0)


def update(sh, m, f, s, grad, fout, sout, mout, wout, ratio, d, width, b):
    entries = m.shape[0]
    whole = entries // 1024
    ends = edges(d, entries, width)
    half = [0.5 * ratio[3 * b + k : 3 * b + k + 1, :] for k in range(3)]

    def put(at, g, part, shape):
        old = m[at].reshape(shape)
        fn, sn, r = lamb_step(g, old, f[at].reshape(shape), s[at].reshape(shape))
        factor = jnp.where(part == 0, half[0], jnp.where(part == 1, half[1], half[2]))
        new = (old - factor * r).reshape(-1)
        grad[at] = g.reshape(-1)
        fout[at] = fn.reshape(-1)
        sout[at] = sn.reshape(-1)
        mout[at] = new
        wout[at] = new.astype(BF)

    lane = lax.broadcasted_iota(jnp.int32, (8, 128), 0) * 128 + lax.broadcasted_iota(jnp.int32, (8, 128), 1)

    def body(i, _):
        at = pl.ds(mult(i * 1024, 1024), 1024)
        put(at, sh[pl.ds(mult(i * 8, 8), 8), :], segment(lane + i * 1024, ends), (8, 128))
        return 0

    lax.fori_loop(0, whole, body, 0)
    part = segment(lax.broadcasted_iota(jnp.int32, (1, 16), 1) + whole * 1024, ends)
    put(pl.ds(whole * 1024, 16), sh[8 * whole : 8 * whole + 1, 0:16], part, (1, 16))


def sum_all(sums, got, zs, ssem, rsem, t, s):
    copies = []
    for i, e in enumerate((1, 2, 4)):
        copy = send(sums.at[i], got.at[i], ssem.at[i], rsem.at[i], (jnp.bitwise_xor(t, e), s))
        copies.append(copy)
        copy.wait_recv()
        if i < 2:
            sums[i + 1] = sums[i] + got[i]
        else:
            zs[s] = sums[i] + got[i]
    last = [
        send(zs.at[s], zs.at[s], ssem.at[2 + k], rsem.at[2 + k], (t, (s + k) % 4)) for k in (1, 2, 3)
    ]
    for copy in last:
        copy.wait_recv()
    return zs[0] + zs[1] + zs[2] + zs[3], copies + last


def kernel_e(
    total, sh1, sh2, sh3, m1, f1, s1, m2, f2, s2, m3, f3, s3,
    g1, fo1, so1, mo1, wo1, g2, fo2, so2, mo2, wo2, g3, fo3, so3, mo3, wo3, pairs,
):
    t, s = here()
    d = 4 * t + s
    norm = jnp.sqrt(jnp.sum(total[...], 1, keepdims=True))
    pairs[...] = jnp.concatenate([norm[0:9], norm[16:25]], 1)
    ratio = norm[0:9] / (norm[16:25] + 1e-6)
    update(sh1, m1, f1, s1, g1, fo1, so1, mo1, wo1, ratio, d, 3 * D, 0)
    update(sh2, m2, f2, s2, g2, fo2, so2, mo2, wo2, ratio, d, 3 * D, 1)
    update(sh3, m3, f3, s3, g3, fo3, so3, mo3, wo3, ratio, d, 4 * D, 2)


def call_e(total, shards, args):
    sds = jax.ShapeDtypeStruct
    vm = pl.BlockSpec(memory_space=pltpu.VMEM)
    shapes = []
    for m in args[0::3]:
        n = m.shape
        shapes += [sds(n, F32)] * 4 + [sds(n, BF)]
    return pl.pallas_call(
        kernel_e,
        name="kernel_e",
        out_shape=(*shapes, sds((9, 2), F32)),
        in_specs=[vm] * 13,
        out_specs=(vm,) * 16,
        compiler_params=pltpu.CompilerParams(vmem_limit_bytes=40 << 20),
    )(total, *shards, *args)


class Scatter:
    def __init__(self, part, r1, acc, ry, rx, ry2, rx2, rz, half, ssem, rsem, t, s):
        self.part, self.r1, self.acc = part, r1, acc
        self.ry, self.rx, self.ry2, self.rx2, self.rz = ry, rx, ry2, rx2, rz
        self.rows = part.shape[1]
        self.ha, self.hb = half, self.rows - half
        self.ssem, self.rsem, self.t, self.s = ssem, rsem, t, s
        self.count = 0
        self.copies = []

    def go(self, src, dst, peer):
        i = self.count
        self.count += 1
        copy = send(src, dst, self.ssem.at[i], self.rsem.at[i], peer)
        self.copies.append(copy)
        return copy

    def xor(self, e):
        return jnp.bitwise_xor(self.t, e)

    def core(self):
        tc = self.xor(1)
        self.c = [
            self.go(self.part.at[pl.ds(4 * jnp.bitwise_xor(tc, 2 * e), 4)], self.r1.at[e], (tc, self.s))
            for e in (2, 3, 1, 0)
        ]

    def core_sum(self):
        for n, e in enumerate((2, 3, 1, 0)):
            self.c[n].wait_recv()
            base = 4 * self.xor(2 * e)

            def body(j, _, e=e, base=base):
                own = self.part[base + j, :, :].astype(F32)
                self.acc[e, j, :, :] = (own + self.r1[e, j, :, :].astype(F32)).astype(BF)
                return 0

            lax.fori_loop(0, 4, body, 0)

    def one(self):
        ha, hb = pl.ds(0, self.ha), pl.ds(self.ha, self.hb)
        ty, tx, s = self.xor(4), self.xor(2), self.s
        self.y = [self.go(self.acc.at[2 + e, :, ha], self.ry.at[e], (ty, s)) for e in (0, 1)]
        self.x = [self.go(self.acc.at[1 + 2 * e, :, hb], self.rx.at[e], (tx, s)) for e in (0, 1)]

    def add(self, e, lo, size, got):
        def body(j, _):
            own = self.acc[e, j, lo : lo + size, :].astype(F32)
            self.acc[e, j, lo : lo + size, :] = (own + got(j).astype(F32)).astype(BF)
            return 0

        lax.fori_loop(0, 4, body, 0)

    def two(self):
        ha, hb = pl.ds(0, self.ha), pl.ds(self.ha, self.hb)
        ty, tx, s = self.xor(4), self.xor(2), self.s
        self.y[1].wait_recv()
        self.add(1, 0, self.ha, lambda j: self.ry[1, j, :, :])
        self.x2 = self.go(self.acc.at[1, :, ha], self.rx2, (tx, s))
        self.x[1].wait_recv()
        self.add(2, self.ha, self.hb, lambda j: self.rx[1, j, :, :])
        self.y2 = self.go(self.acc.at[2, :, hb], self.ry2, (ty, s))
        self.y[0].wait_recv()
        self.add(0, 0, self.ha, lambda j: self.ry[0, j, :, :])
        self.x[0].wait_recv()
        self.add(0, self.ha, self.hb, lambda j: self.rx[0, j, :, :])

    def three(self):
        self.x2.wait_recv()
        self.add(0, 0, self.ha, lambda j: self.rx2[j, :, :])
        self.y2.wait_recv()
        self.add(0, self.ha, self.hb, lambda j: self.ry2[j, :, :])
        t, s = self.t, self.s
        self.z = [self.go(self.acc.at[0, (s + k) % 4], self.rz.at[k - 1], (t, (s + k) % 4)) for k in (1, 2, 3)]

    def result(self):
        for copy in self.z:
            copy.wait_recv()
        total = self.acc[0, self.s, :, :].astype(F32)
        for k in range(3):
            total = total + self.rz[k, :, :].astype(F32)
        return total

    def drain(self):
        for copy in self.copies:
            copy.wait_send()


def to_shard(first, main, fl, d, out_ref):
    q, p = d // 8, d % 8
    rows = main.shape[0]
    total = out_ref.shape[0]
    fl[4 + 4 * rows : total + 8, :] = jnp.zeros((total + 4 - 4 * rows, 128), F32)
    for b in range(4):
        fl[b : b + 1, :] = first[:, 128 * b : 128 * b + 128]
        fl[pl.ds(4 + b, rows, stride=4), :] = main[:, 128 * b : 128 * b + 128]
    turn = (128 - 16 * p) % 128
    lane = lax.broadcasted_iota(jnp.int32, (total, 128), 1)
    low = pltpu.roll(fl[pl.ds(q, total), :], turn, 1)
    high = pltpu.roll(fl[pl.ds(q + 1, total), :], turn, 1)
    out_ref[...] = jnp.where(lane < 128 - 16 * p, low, high)


def last_rows(part, bound, kind, gain_row):
    rows = part.shape[1]
    at = lax.broadcasted_iota(jnp.int32, (16, D), 0) == kind

    def body(i, _):
        prev = jnp.maximum(i - 1, 0)
        row = part[prev, rows - 16 : rows, :].astype(F32)[15:16, :]
        row = jnp.where(i > 0, row, gain_row)
        bound[i, :, :] = jnp.where(at, row, bound[i, :, :].astype(F32)).astype(BF)
        return 0

    lax.fori_loop(0, 32, body, 0)


def backward_heads(h, qkv, do, live, dqkv, kt, dkv):
    left = halves()
    one, two = jnp.where(left, 1.0, 0.0).astype(BF), jnp.where(left, 0.0, 1.0).astype(BF)
    cols = pl.ds(mult(h * 128, 128), 128)
    kt[...] = jnp.transpose(qkv[1, :, cols].astype(F32)).astype(BF)
    top_lane = lax.broadcasted_iota(jnp.int32, (128, 128), 0) < 64

    def chunk(c, _):
        rows = pl.ds(mult(c * 128, 128), 128)
        q = qkv[0, rows, cols] * jnp.asarray(0.125, BF)
        qm = jnp.concatenate([q * one, q * two], 0)
        g = do[c, :, :, cols].reshape(128, 128)
        gm = jnp.concatenate([g * one, g * two], 0)
        scores = jnp.where(live, nt(qkv[1, :, cols], qm), NEG)
        e = jnp.exp(scores - jnp.max(scores, 0, keepdims=True))
        prob = e * (1.0 / jnp.sum(e, 0, keepdims=True))
        pg = nt(qkv[2, :, cols], gm)
        inner = jnp.sum(prob * pg, 0, keepdims=True)
        sg = (prob * (pg - inner)).astype(BF)
        dk = nn(sg, qm)
        dv = nn(prob.astype(BF), gm)
        dqt = nn(kt[...], sg)
        dq = jnp.transpose(jnp.where(top_lane, dqt[:, 0:128], dqt[:, 128:256])) * 0.125
        dqkv[0, rows, cols] = dq.astype(BF)

        @pl.when(c == 0)
        def _():
            dkv[0] = dk
            dkv[1] = dv

        @pl.when(c > 0)
        def _():
            dkv[0] += dk
            dkv[1] += dv

        return 0

    lax.fori_loop(0, 4, chunk, 0)
    dqkv[1, :, cols] = dkv[0].astype(BF)
    dqkv[2, :, cols] = dkv[1].astype(BF)


def kernel_c(
    cnt, do1, qkv, a1, cf, w1, gains, grad1, p1o, p2, p3, dgain,
    m1, f1, s1, m2, f2, s2, m3, f3, s3,
    cgrad, sh1, sh2, sh3, total,
    do, dqkv, kt, dkv, at, wide, p1, pb, dhs, dhr, fl,
    r1a, aa, rya, rxa, rya2, rxa2, rza,
    r1b, ab, ryb, rxb, ryb2, rxb2, rzb,
    r1c, ac, ryc, rxc, ryc2, rxc2, rzc,
    r1d, ad, ryd, rxd, ryd2, rxd2, rzd,
    ssem, rsem, dss, dsr, hss, hsr, sums, got, zs, nss, nsr,
):
    t, s = here()
    d = 4 * t + s
    barrier = enter(t, s)
    do[s] = do1[:, s, :, :]
    pb[...] = jnp.zeros((32, 16, D), BF)
    sa = Scatter(p1, r1a, aa, rya, rxa, rya2, rxa2, rza, 32, ssem.at[0], rsem.at[0], t, s)
    sb = Scatter(p2, r1b, ab, ryb, rxb, ryb2, rxb2, rzb, 32, ssem.at[1], rsem.at[1], t, s)
    sc = Scatter(p3, r1c, ac, ryc, rxc, ryc2, rxc2, rzc, 64, ssem.at[2], rsem.at[2], t, s)
    pl.semaphore_wait(barrier, 6)
    moves = [
        send(do1.at[:, (s + k) % 4], do.at[s], dss.at[k - 1], dsr.at[k - 1], (t, (s + k) % 4)) for k in (1, 2, 3)
    ]
    sc.core()
    sb.core()
    sc.core_sum()
    sc.one()
    at[...] = jnp.transpose(a1[...].astype(F32)).astype(BF)
    sb.core_sum()
    for copy in moves:
        copy.wait_recv()
    live = lax.broadcasted_iota(jnp.int32, (512, 1), 0) < cnt[0]

    def heads(lo, hi):
        def body(h, _):
            backward_heads(h, qkv, do, live, dqkv, kt, dkv)
            return 0

        lax.fori_loop(lo, hi, body, 0)

    heads(0, 2)
    sc.two()
    sb.one()
    heads(2, 3)
    sc.three()
    heads(3, 4)
    sb.two()
    gain = gains[0:1, :]
    dg = jnp.zeros((1, D), F32)

    def norm_back(i, dg):
        rows = pl.ds(mult(i * 128, 128), 128)
        da = nt(dqkv[0, rows, :], w1[0]) + nt(dqkv[1, rows, :], w1[1]) + nt(dqkv[2, rows, :], w1[2])
        h = cf[i].astype(F32).reshape(128, D)
        x = h - jnp.mean(h, 1, keepdims=True)
        rstd = lax.rsqrt(jnp.mean(x * x, 1, keepdims=True) + 1e-5)
        x = x * rstd
        dg = dg + jnp.sum(da * x, 0, keepdims=True)
        dx = da * gain
        dh = rstd * (dx - jnp.mean(dx, 1, keepdims=True) - x * jnp.mean(dx * x, 1, keepdims=True))
        dhs[i] = dh.astype(BF).reshape(4, 32, D)
        return dg

    dg = lax.fori_loop(0, 4, norm_back, dg)

    def weights(i, _):
        j, r = i // 4, i % 4
        part = nn(at[pl.ds(mult(r * 128, 128), 128), :], dqkv[j])
        for b in range(4):
            wide[b, pl.ds(384 * r + j, 128, stride=3), :] = part[:, 128 * b : 128 * b + 128]
        return 0

    lax.fori_loop(0, 12, weights, 0)

    def narrow(i, _):
        rows = pl.ds(mult(i * 64, 64), 64)
        for b in range(4):
            p1[i, :, 128 * b : 128 * b + 128] = wide[b, rows, :].astype(BF)
        return 0

    lax.fori_loop(0, 24, narrow, 0)

    def copy_out(i, _):
        p1[24 + i] = p1o[pl.ds(mult(i * 64, 64), 64), :]
        return 0

    lax.fori_loop(0, 8, copy_out, 0)
    last_rows(p1, pb, 0, dg)
    last_rows(p2, pb, 1, dgain[1:2, :])
    last_rows(p3, pb, 2, dgain[2:3, :])
    sd = Scatter(pb, r1d, ad, ryd, rxd, ryd2, rxd2, rzd, 0, ssem.at[3], rsem.at[3], t, s)
    sd.ha, sd.hb = 16, 16
    sa.core()
    sd.core()
    homes = [
        send(dhs.at[(s + k) % 4], dhr.at[:, s], hss.at[k - 1], hsr.at[k - 1], (t, (s + k) % 4)) for k in (1, 2, 3)
    ]
    sb.three()
    sa.core_sum()
    sa.one()
    sd.core_sum()
    bound_one(sd)
    main3 = sc.result()
    main2 = sb.result()
    sa.two()
    bound_two(sd)
    sa.three()
    bound_three(sd)
    cgrad[:, s, :, :] = grad1[:, s, :, :] + dhs[s].astype(F32)
    for k in (1, 2, 3):
        homes[k - 1].wait_recv()
        f = (s + 4 - k) % 4
        cgrad[:, f, :, :] = grad1[:, f, :, :] + dhr[:, f, :, :].astype(F32)
    main1 = sa.result()
    first = sd.result()
    to_shard(first[0:1, :], main1, fl, d, sh1)
    to_shard(first[1:2, :], main2, fl, d, sh2)
    to_shard(first[2:3, :], main3, fl, d, sh3)
    sums[0] = jnp.zeros((32, 128), F32)
    squares(sh1, m1, f1, s1, sums.at[0], d, 3 * D, 0)
    squares(sh2, m2, f2, s2, sums.at[0], d, 3 * D, 1)
    squares(sh3, m3, f3, s3, sums.at[0], d, 4 * D, 2)
    total[...], adds = sum_all(sums, got, zs, nss, nsr, t, s)
    for one in (sa, sb, sc, sd):
        one.drain()
    for copy in moves + homes + adds:
        copy.wait_send()


def bound_one(sd):
    sd.y = [sd.go(sd.acc.at[2 + e], sd.ry.at[e], (sd.xor(4), sd.s)) for e in (0, 1)]


def bound_two(sd):
    for e in (1, 0):
        sd.y[e].wait_recv()
        sd.add(e, 0, 16, lambda j, e=e: sd.ry[e, j, :, :])
        if e:
            sd.x2 = sd.go(sd.acc.at[1], sd.rx2, (sd.xor(2), sd.s))


def bound_three(sd):
    sd.x2.wait_recv()
    sd.add(0, 0, 16, lambda j: sd.rx2[j, :, :])
    t, s = sd.t, sd.s
    sd.z = [sd.go(sd.acc.at[0, (s + k) % 4], sd.rz.at[k - 1], (t, (s + k) % 4)) for k in (1, 2, 3)]


def scatter_scratch(rows, ha, hb):
    return [
        pltpu.VMEM((4, 4, rows, D), BF), pltpu.VMEM((4, 4, rows, D), BF),
        pltpu.VMEM((2, 4, ha, D), BF), pltpu.VMEM((2, 4, hb, D), BF),
        pltpu.VMEM((4, hb, D), BF), pltpu.VMEM((4, ha, D), BF), pltpu.VMEM((3, rows, D), BF),
    ]


def call_c(cnt, do1, qkv, a1, cf, w1, gains, grad1, p1o, p2, p3, dgain, params):
    sds = jax.ShapeDtypeStruct
    vm = pl.BlockSpec(memory_space=pltpu.VMEM)
    return pl.pallas_call(
        kernel_c,
        name="kernel_c",
        out_shape=(sds((4, 4, 32, D), F32), sds((264, 128), F32), sds((264, 128), F32), sds((520, 128), F32), sds((32, 128), F32)),
        in_specs=[pl.BlockSpec(memory_space=pltpu.SMEM)] + [vm] * 20,
        out_specs=(vm,) * 5,
        scratch_shapes=[
            pltpu.VMEM((4, 4, 32, D), BF), pltpu.VMEM((3, D, D), BF), pltpu.VMEM((128, D), BF),
            pltpu.VMEM((2, D, 128), F32), pltpu.VMEM((D, D), BF), pltpu.VMEM((4, 3 * D, 128), F32),
            pltpu.VMEM((32, 64, D), BF), pltpu.VMEM((32, 16, D), BF),
            pltpu.VMEM((4, 4, 32, D), BF), pltpu.VMEM((4, 4, 32, D), BF), pltpu.VMEM((528, 128), F32),
            *scatter_scratch(64, 32, 32), *scatter_scratch(64, 32, 32), *scatter_scratch(128, 64, 64),
            *scatter_scratch(16, 16, 16),
            pltpu.SemaphoreType.DMA((4, 14)), pltpu.SemaphoreType.DMA((4, 14)),
            pltpu.SemaphoreType.DMA((3,)), pltpu.SemaphoreType.DMA((3,)),
            pltpu.SemaphoreType.DMA((3,)), pltpu.SemaphoreType.DMA((3,)),
            pltpu.VMEM((3, 32, 128), F32), pltpu.VMEM((3, 32, 128), F32), pltpu.VMEM((4, 32, 128), F32),
            pltpu.SemaphoreType.DMA((6,)), pltpu.SemaphoreType.DMA((6,)),
        ],
        compiler_params=pltpu.CompilerParams(collective_id=2, has_side_effects=True, vmem_limit_bytes=60 << 20),
    )(cnt, do1, qkv, a1, cf, w1, gains, grad1, p1o, p2, p3, dgain, *params)


def turn(x):
    return jnp.transpose(x)


def stats(h):
    x = h - jnp.mean(h, 1, keepdims=True)
    rstd = lax.rsqrt(jnp.mean(x * x, 1, keepdims=True) + 1e-5)
    return x * rstd, rstd


def norm_grad(h, da, gain):
    x, rstd = stats(h)
    dgain = jnp.sum(da * x, 0, keepdims=True)
    dx = da * gain
    dh = rstd * (dx - jnp.mean(dx, 1, keepdims=True) - x * jnp.mean(dx * x, 1, keepdims=True))
    return dh, dgain


def block(g):
    return pl.ds(mult(g * 128, 128), 128)


def feature_mask(fcnt, axis):
    shape = (256, 128) if axis else (128, 256)
    query = lax.broadcasted_iota(jnp.int32, shape, 1 - axis)
    key = lax.broadcasted_iota(jnp.int32, shape, axis)
    return (query % 32 == key % 32) & (key // 32 < fcnt)


def feature_forward(qkv, o2, fcnt):
    left = halves()
    one = jnp.where(left, 0.125, 0.0).astype(BF)
    two = jnp.where(left, 0.0, 0.125).astype(BF)
    ok = feature_mask(fcnt, 1)

    def body(n, _):
        rows, cols = block(n // 4), block(n % 4)
        q = qkv[0, rows, cols]
        qm = jnp.concatenate([q * one, q * two], 0)
        scores = jnp.where(ok, nt(qm, qkv[1, rows, cols]), NEG)
        e = jnp.exp(scores - jnp.max(scores, 1, keepdims=True))
        prob = (e * (1.0 / jnp.sum(e, 1, keepdims=True))).astype(BF)
        o = nn(prob, qkv[2, rows, cols])
        o2[rows, cols] = jnp.where(left, o[0:128], o[128:256]).astype(BF)
        return 0

    lax.fori_loop(0, 16, body, 0)


def feature_backward(qkv, do, dqkv, fcnt):
    left = halves()
    one, two = jnp.where(left, 1.0, 0.0).astype(BF), jnp.where(left, 0.0, 1.0).astype(BF)
    ok = feature_mask(fcnt, 0)
    top_lane = lax.broadcasted_iota(jnp.int32, (128, 128), 0) < 64

    def body(n, _):
        rows, cols = block(n // 4), block(n % 4)
        q = qkv[0, rows, cols] * jnp.asarray(0.125, BF)
        qm = jnp.concatenate([q * one, q * two], 0)
        g = do[rows, cols]
        gm = jnp.concatenate([g * one, g * two], 0)
        k = qkv[1, rows, cols]
        scores = jnp.where(ok, nt(k, qm), NEG)
        e = jnp.exp(scores - jnp.max(scores, 0, keepdims=True))
        prob = e * (1.0 / jnp.sum(e, 0, keepdims=True))
        pg = nt(qkv[2, rows, cols], gm)
        sg = (prob * (pg - jnp.sum(prob * pg, 0, keepdims=True))).astype(BF)
        dqt = nn(turn(k), sg)
        dq = turn(jnp.where(top_lane, dqt[:, 0:128], dqt[:, 128:256])) * 0.125
        dqkv[0, rows, cols] = dq.astype(BF)
        dqkv[1, rows, cols] = nn(sg, qm).astype(BF)
        dqkv[2, rows, cols] = nn(prob.astype(BF), gm).astype(BF)
        return 0

    lax.fori_loop(0, 16, body, 0)


def four_blocks(body, init=0):
    return lax.fori_loop(0, 4, body, init)


def flat(x):
    return x.reshape(128, D)


def cube(x):
    return x.reshape(4, 32, D)


def narrow_to(wide, part, slots, rows):
    def body(i, _):
        at = pl.ds(mult(i * rows, rows), rows)
        for b in range(4):
            part[i, :, 128 * b : 128 * b + 128] = wide[b, at, :].astype(BF)
        return 0

    lax.fori_loop(0, slots, body, 0)


def store_wide(wide, j, ways, value):
    for b in range(4):
        wide[b, pl.ds(j, value.shape[0], stride=ways), :] = value[:, 128 * b : 128 * b + 128]


def mlp(a3, a3t, g, h2, wup, wdn, h3, da, zb, dub, u, dz, wide, p3):
    h3[...] = h2[...]
    da[...] = jnp.zeros((512, D), F32)

    def body(j, _):
        u[...] = nn(a3[...], wup[j])
        dz[...] = nt(g[...], wdn[j]).astype(BF)

        def act(r, _):
            rows = pl.ds(mult(r * 64, 64), 64)
            x = u[rows, :]
            cdf = 0.5 * (1.0 + lax.erf(x * 0.7071067811865476))
            zb[rows, :] = (x * cdf).astype(BF)
            slope = cdf + x * (0.3989422804014327 * jnp.exp(-0.5 * x * x))
            dub[rows, :] = (slope * dz[rows, :].astype(F32)).astype(BF)
            return 0

        lax.fori_loop(0, 8, act, 0)
        h3[...] += nn(zb[...], wdn[j])
        da[...] += nt(dub[...], wup[j])
        store_wide(wide, j, 4, nn(a3t[...], dub[...]))
        dw = nn(turn(zb[...]), g[...]).astype(BF)
        for i in range(4):
            p3[16 + 4 * j + i] = dw[128 * i : 128 * i + 128]
        return 0

    lax.fori_loop(0, 4, body, 0)
    narrow_to(wide, p3, 16, 128)


def middle_forward(s, cells, top, o1, wo1, w2, wo2, gains, scnt, fcnt, h1, h2, a2, qkv, o2, a3, g):
    gain2, gain3 = gains[1:2, :], gains[2:3, :]
    h1[...] = nn(o1[...].reshape(512, D), wo1[...])

    def first(r, _):
        rows = block(r)
        h = h1[rows, :] + flat(cells[r].astype(F32))
        h1[rows, :] = h
        x, _ = stats(h)
        a2[rows, :] = (x * gain2).astype(BF)
        n = lax.broadcasted_iota(jnp.int32, (128, 1), 0)
        live = (n // 32 < fcnt) & (128 * s + 32 * r + n % 32 < scnt)
        g[rows, :] = jnp.where(live, flat(top[r].astype(F32)), 0.0).astype(BF)
        return 0

    four_blocks(first)

    def project(j, _):
        qkv[j] = nn(a2[...], w2[j]).astype(BF)
        return 0

    lax.fori_loop(0, 3, project, 0)
    feature_forward(qkv, o2, fcnt)
    h2[...] = h1[...] + nn(o2[...], wo2[...])

    def second(r, _):
        rows = block(r)
        x, _ = stats(h2[rows, :])
        a3[rows, :] = (x * gain3).astype(BF)
        return 0

    four_blocks(second)


def layer_output(s, h3, lout, scnt, fcnt):
    def last(r, _):
        n = lax.broadcasted_iota(jnp.int32, (128, 1), 0)
        live = (n // 32 < fcnt) & (128 * s + 32 * r + n % 32 < scnt)
        lout[r] = cube(jnp.where(live, h3[block(r), :], 0.0).astype(BF))
        return 0

    four_blocks(last)


def feature_grads(o1, wo1, w2, wo2, gains, fcnt, h1, h2, a2, qkv, o2, g, da, b, do, dqkv, wide, p2, dwo1, do1, gr, dgain):
    gain2, gain3 = gains[1:2, :], gains[2:3, :]

    def third(r, dg):
        rows = block(r)
        dh, part = norm_grad(h2[rows, :], da[rows, :], gain3)
        total = g[rows, :].astype(F32) + dh
        gr[r] = cube(total)
        b[rows, :] = total.astype(BF)
        return dg + part

    dg3 = four_blocks(third, jnp.zeros((1, D), F32))
    do[...] = nt(b[...], wo2[...]).astype(BF)
    dw = nn(turn(o2[...]), b[...]).astype(BF)
    for i in range(8):
        p2[24 + i] = dw[64 * i : 64 * i + 64]
    feature_backward(qkv, do, dqkv, fcnt)

    def weights(j, _):
        store_wide(wide, j, 3, nn(turn(a2[...]), dqkv[j]))
        return 0

    lax.fori_loop(0, 3, weights, 0)
    narrow_to(wide, p2, 24, 64)
    da[...] = nt(dqkv[0], w2[0]) + nt(dqkv[1], w2[1]) + nt(dqkv[2], w2[2])

    def fourth(r, dg):
        rows = block(r)
        dh, part = norm_grad(h1[rows, :], da[rows, :], gain2)
        total = flat(gr[r]) + dh
        gr[r] = cube(total)
        b[rows, :] = total.astype(BF)
        return dg + part

    dg2 = four_blocks(fourth, jnp.zeros((1, D), F32))
    do1[...] = nt(b[...], wo1[...]).astype(BF).reshape(4, 4, 32, D)
    dwo1[...] = nn(turn(o1[...].reshape(512, D)), b[...]).astype(BF)
    n = lax.broadcasted_iota(jnp.int32, (8, D), 0)
    dgain[...] = jnp.where(n == 1, dg2, jnp.where(n == 2, dg3, 0.0))


def kernel_b(
    scnt, fcnt, cells, top, o1, wo1, w2, wo2, wup, wdn, gains,
    lout, gr, do1, dwo1, p2, p3, dgain,
    h1, h2, a2, qkv, o2, a3, a3t, g, h3, da, zb, dub, u, dz, wide, b, do, dqkv,
):
    s = lax.axis_index("samp")
    middle_forward(s, cells, top, o1, wo1, w2, wo2, gains, scnt[0], fcnt[0], h1, h2, a2, qkv, o2, a3, g)
    a3t[...] = turn(a3[...])
    mlp(a3, a3t, g, h2, wup, wdn, h3, da, zb, dub, u, dz, wide, p3)
    layer_output(s, h3, lout, scnt[0], fcnt[0])
    feature_grads(
        o1, wo1, w2, wo2, gains, fcnt[0], h1, h2, a2, qkv, o2, g, da, b, do, dqkv, wide, p2, dwo1, do1, gr, dgain
    )


def middle_scratch():
    w = pltpu.VMEM((D, D), F32)
    n = pltpu.VMEM((D, D), BF)
    three = pltpu.VMEM((3, D, D), BF)
    return [w, w, n, three, n, n, n, n, w, w, n, n, w, n, pltpu.VMEM((4, 4 * D, 128), F32), n, n, three]


def call_b(scnt, fcnt, cells, top, o1, wo1, w2, wo2, wup, wdn, gains):
    sds = jax.ShapeDtypeStruct
    vm = pl.BlockSpec(memory_space=pltpu.VMEM)
    sm = pl.BlockSpec(memory_space=pltpu.SMEM)
    return pl.pallas_call(
        kernel_b,
        name="kernel_b",
        out_shape=(
            sds((4, 4, 32, D), BF), sds((4, 4, 32, D), F32), sds((4, 4, 32, D), BF), sds((D, D), BF),
            sds((32, 64, D), BF), sds((32, 128, D), BF), sds((8, D), F32),
        ),
        in_specs=[sm, sm] + [vm] * 9,
        out_specs=(vm,) * 7,
        scratch_shapes=middle_scratch(),
        compiler_params=pltpu.CompilerParams(vmem_limit_bytes=60 << 20),
    )(scnt, fcnt, cells, top, o1, wo1, w2, wo2, wup, wdn.reshape(4, D, D), gains)


class Reduce:
    def __init__(self, part, r1, ry, rx, ry2, rx2, rz, half, ssem, rsem, t, s):
        self.part, self.r1 = part, r1
        self.ry, self.rx, self.ry2, self.rx2, self.rz = ry, rx, ry2, rx2, rz
        self.rows = part.shape[1]
        self.half = half
        self.ssem, self.rsem, self.t, self.s = ssem, rsem, t, s
        self.count = 0
        self.copies = []

    def go(self, src, dst, peer):
        i = self.count
        self.count += 1
        copy = send(src, dst, self.ssem.at[i], self.rsem.at[i], peer)
        self.copies.append(copy)
        return copy

    def xor(self, e):
        return jnp.bitwise_xor(self.t, e)

    def group(self, e, rows=None):
        slots = pl.ds(4 * self.xor(2 * e), 4)
        return self.part.at[slots] if rows is None else self.part.at[slots, rows]

    def core(self):
        tc = self.xor(1)
        self.c = [
            self.go(self.part.at[pl.ds(4 * jnp.bitwise_xor(tc, 2 * e), 4)], self.r1.at[e], (tc, self.s))
            for e in (2, 3, 1, 0)
        ]

    def add(self, e, lo, size, got):
        base = 4 * self.xor(2 * e)

        def body(j, _):
            own = self.part[base + j, lo : lo + size, :].astype(F32)
            self.part[base + j, lo : lo + size, :] = (own + got(j).astype(F32)).astype(BF)
            return 0

        lax.fori_loop(0, 4, body, 0)

    def one(self):
        ha, hb = pl.ds(0, self.half), pl.ds(self.half, self.rows - self.half)
        ty, tx, s = self.xor(4), self.xor(2), self.s
        self.y, self.x = {}, {}
        for n, e in enumerate((2, 3, 1, 0)):
            self.c[n].wait_recv()
            self.add(e, 0, self.rows, lambda j, e=e: self.r1[e, j, :, :])
            if e in (2, 3):
                self.y[e - 2] = self.go(self.group(e, ha), self.ry.at[e - 2], (ty, s))
            if e in (3, 1):
                self.x[e // 2] = self.go(self.group(e, hb), self.rx.at[e // 2], (tx, s))

    def two(self):
        a, b = self.half, self.rows - self.half
        ha, hb = pl.ds(0, a), pl.ds(a, b)
        ty, tx, s = self.xor(4), self.xor(2), self.s
        self.y[1].wait_recv()
        self.add(1, 0, a, lambda j: self.ry[1, j, :, :])
        self.x2 = self.go(self.group(1, ha), self.rx2, (tx, s))
        self.x[1].wait_recv()
        self.add(2, a, b, lambda j: self.rx[1, j, :, :])
        self.y2 = self.go(self.group(2, hb), self.ry2, (ty, s))
        self.y[0].wait_recv()
        self.add(0, 0, a, lambda j: self.ry[0, j, :, :])
        self.x[0].wait_recv()
        self.add(0, a, b, lambda j: self.rx[0, j, :, :])

    def three(self):
        a, b = self.half, self.rows - self.half
        self.x2.wait_recv()
        self.add(0, 0, a, lambda j: self.rx2[j, :, :])
        self.y2.wait_recv()
        self.add(0, a, b, lambda j: self.ry2[j, :, :])
        t, s = self.t, self.s
        self.z = [
            self.go(self.part.at[4 * t + (s + k) % 4], self.rz.at[k - 1], (t, (s + k) % 4)) for k in (1, 2, 3)
        ]

    def result(self):
        for copy in self.z:
            copy.wait_recv()
        total = self.part[4 * self.t + self.s, :, :].astype(F32)
        for k in range(3):
            total = total + self.rz[k, :, :].astype(F32)
        return total

    def drain(self):
        for copy in self.copies:
            copy.wait_send()


def edge_rows(part, bound, kind):
    rows = min(128, part.shape[1])
    end = 64 if rows == 80 else rows
    at = lax.broadcasted_iota(jnp.int32, (16, D), 0) == kind

    def body(i, _):
        row = part[i - 1, end - 16 : end, :].astype(F32)[15:16, :]
        bound[i, 64:80, :] = jnp.where(at, row, bound[i, 64:80, :].astype(F32)).astype(BF)
        return 0

    lax.fori_loop(1, 32, body, 0)


def edge_gains(bound, gain1, dgain):
    n = lax.broadcasted_iota(jnp.int32, (16, D), 0)
    rows = jnp.where(n == 0, gain1, jnp.where(n == 1, dgain[1:2, :], jnp.where(n == 2, dgain[2:3, :], 0.0)))
    bound[0, 64:80, :] = rows.astype(BF)


def to_rows(main, fl):
    rows = main.shape[0]
    for b in range(4):
        fl[pl.ds(4 + b, rows, stride=4), :] = main[:, 128 * b : 128 * b + 128]


def to_shard(first, fl, rows, d, out_ref):
    q, p = d // 8, d % 8
    total = out_ref.shape[0]
    fl[4 + 4 * rows : total + 8, :] = jnp.zeros((total + 4 - 4 * rows, 128), F32)
    for b in range(4):
        fl[b : b + 1, :] = first[:, 128 * b : 128 * b + 128]
    back = (128 - 16 * p) % 128
    lane = lax.broadcasted_iota(jnp.int32, (total, 128), 1)
    low = pltpu.roll(fl[pl.ds(q, total), :], back, 1)
    high = pltpu.roll(fl[pl.ds(q + 1, total), :], back, 1)
    out_ref[...] = jnp.where(lane < 128 - 16 * p, low, high)


class Refs:
    def __init__(self, names, refs):
        for name, ref in zip(names, refs, strict=True):
            setattr(self, name, ref)


def reduce_names(n):
    return [k + n for k in ("r1", "ry", "rx", "ry2", "rx2", "rz")]


def reduce_scratch(rows, a):
    b = rows - a
    return [
        pltpu.VMEM((4, 4, rows, D), BF), pltpu.VMEM((2, 4, a, D), BF), pltpu.VMEM((2, 4, b, D), BF),
        pltpu.VMEM((4, b, D), BF), pltpu.VMEM((4, a, D), BF), pltpu.VMEM((3, rows, D), BF),
    ]


PARAMS = ["m1", "f1", "s1", "m2", "f2", "s2", "m3", "f3", "s3"]
WIDE = pltpu.VMEM((D, D), F32)
NARROW = pltpu.VMEM((D, D), BF)
THREE = pltpu.VMEM((3, D, D), BF)
FOUR = pltpu.VMEM((4, D, D), BF)
TILE = pltpu.VMEM((4, 4, 32, D), BF)
DMA = pltpu.SemaphoreType.DMA
SCRATCH = {
    "g1": pltpu.VMEM((32, 80, D), BF), "g2": pltpu.VMEM((32, 64, D), BF), "g3": pltpu.VMEM((32, 128, D), BF),
    "wide": pltpu.VMEM((4, 4 * D, 128), F32), "sh": pltpu.VMEM((536, 128), F32), "ro": pltpu.VMEM((536, 128), F32),
    "w1": THREE, "wo1": NARROW, "w2": THREE, "wo2": NARROW, "wup": FOUR, "wdn": FOUR,
    "gains": pltpu.VMEM((8, D), F32), "dgain": pltpu.VMEM((8, D), F32),
    "cf": TILE, "a1": NARROW, "qkv1": THREE, "o1c": pltpu.VMEM((3, 4, 32, D), BF), "o1": TILE,
    "h1": WIDE, "h2": WIDE, "a2": NARROW, "qkv2": THREE, "o2": NARROW, "a3": NARROW, "at": NARROW, "g": NARROW,
    "h3": WIDE, "da": WIDE, "zb": NARROW, "dub": NARROW, "u": WIDE, "dz": NARROW, "b": NARROW, "do2": NARROW,
    "dqkv": THREE, "gr": pltpu.VMEM((4, 4, 32, D), F32), "do1": TILE, "do": TILE, "dwo1": NARROW,
    "kt": pltpu.VMEM((128, D), BF), "dkv": pltpu.VMEM((2, D, 128), F32), "dhs": TILE, "dhr": TILE,
    **dict(zip(reduce_names("a"), reduce_scratch(80, 32))),
    **dict(zip(reduce_names("b"), reduce_scratch(64, 32))),
    **dict(zip(reduce_names("c"), reduce_scratch(128, 64))),
    "fl1": pltpu.VMEM((272, 128), F32), "fl2": pltpu.VMEM((272, 128), F32), "fl3": pltpu.VMEM((528, 128), F32),
    "sums": pltpu.VMEM((3, 32, 128), F32), "got": pltpu.VMEM((3, 32, 128), F32), "zs": pltpu.VMEM((4, 32, 128), F32),
    "gs": DMA((3, 16)), "gq": DMA((3, 16)), "rs": DMA((3, 16)), "rq": DMA((3, 16)),
    "as1": DMA((3,)), "aq1": DMA((3,)), "as2": DMA((3,)), "aq2": DMA((3,)),
    "as3": DMA((3,)), "aq3": DMA((3,)), "as4": DMA((3,)), "aq4": DMA((3,)), "ns": DMA((6,)), "nq": DMA((6,)),
}
INPUTS = ["scnt", "fcnt", "cells", "top"] + PARAMS
OUTPUTS = ["lout", "cgrad", "sh1", "sh2", "sh3", "total"]


def kernel_m(*refs):
    r = Refs(INPUTS + OUTPUTS + list(SCRATCH), refs)
    t, s = here()
    d = 4 * t + s
    scnt, fcnt = r.scnt[0], r.fcnt[0]
    barrier = enter(t, s)
    ga = Gather(r.g1, 32, r.gs.at[0], r.gq.at[0], t, s)
    gb = Gather(r.g2, 32, r.gs.at[1], r.gq.at[1], t, s)
    gc = Gather(r.g3, 64, r.gs.at[2], r.gq.at[2], t, s)
    first1 = realign(r.m1, r.sh, d, 64, r.g1, d, r.ro)
    first2 = realign(r.m2, r.sh, d, 64, r.g2, d, r.ro)
    first3 = realign(r.m3, r.sh, d, 128, r.g3, d, r.ro)
    row = lax.broadcasted_iota(jnp.int32, (16, D), 0)
    firsts = jnp.where(row == 0, first1, jnp.where(row == 1, first2, jnp.where(row == 2, first3, 0.0)))
    r.g1[d, 64:80, :] = firsts.astype(BF)
    pl.semaphore_wait(barrier, 6)
    ga.z()
    r.cf[s] = r.cells[:, s, :, :]
    moves = [
        send(r.cells.at[:, (s + k) % 4], r.cf.at[s], r.as1.at[k - 1], r.aq1.at[k - 1], (t, (s + k) % 4))
        for k in (1, 2, 3)
    ]
    ga.one()
    ga.two()
    for copy in moves:
        copy.wait_recv()
    gb.z()
    gc.z()
    ga.three()
    ga.end()
    spread(r.g1, r.g1, 0, 64, 0, 24, put_f32(r.wide, 64))
    split_columns(r.wide, 3, r.w1)
    spread(r.g1, r.g1, 0, 64, 24, 32, put_bf(r.wo1, 64))
    r.gains[...] = r.g1[0, 64:80, :].astype(F32)[0:8]
    gain1 = r.gains[0:1, :]

    def norm(i, _):
        x, _ = stats(r.cf[i].astype(F32).reshape(128, D))
        r.a1[block(i), :] = (x * gain1).astype(BF)
        return 0

    four_blocks(norm)

    def project(j, _):
        r.qkv1[j] = nn(r.a1[...], r.w1[j]).astype(BF)
        return 0

    lax.fori_loop(0, 3, project, 0)
    live = lax.broadcasted_iota(jnp.int32, (1, 512), 1) < scnt
    backs = []
    for k in (2, 1, 3, 0):
        c = (s + k) % 4
        if k:
            attend_chunk(r.qkv1, c, live, r.o1c.at[k - 1])
            backs.append(send(r.o1c.at[k - 1], r.o1.at[:, s], r.as2.at[k - 1], r.aq2.at[k - 1], (t, c)))
        else:
            attend_chunk(r.qkv1, c, live, r.o1.at[:, s])
        if k == 2:
            gb.one()
        if k == 1:
            gc.one()
            gb.two()
        if k == 3:
            gc.two()
            gb.three()
    gb.end()
    spread(r.g2, r.g1, 1, 64, 0, 24, put_f32(r.wide, 64))
    split_columns(r.wide, 3, r.w2)
    spread(r.g2, r.g1, 1, 64, 24, 32, put_bf(r.wo2, 64))
    for copy in backs:
        copy.wait_recv()
    gc.three()
    middle_forward(
        s, r.cells, r.top, r.o1, r.wo1, r.w2, r.wo2, r.gains, scnt, fcnt, r.h1, r.h2, r.a2, r.qkv2, r.o2, r.a3, r.g
    )
    r.at[...] = turn(r.a3[...])
    gc.end()
    spread(r.g3, r.g1, 2, 128, 0, 16, put_f32(r.wide, 128))
    split_columns(r.wide, 4, r.wup)

    def put_down(i, head, last):
        r.wdn[i // 4, pl.ds(mult((i % 4) * 128, 128), 128), :] = jnp.concatenate([head, last], 0).astype(BF)

    spread(r.g3, r.g1, 2, 128, 16, 32, put_down)
    for one in (ga, gb, gc):
        one.drain()
    mlp(r.a3, r.at, r.g, r.h2, r.wup, r.wdn, r.h3, r.da, r.zb, r.dub, r.u, r.dz, r.wide, r.g3)
    edge_rows(r.g3, r.g1, 2)

    def reducer(n, part, half, i):
        bufs = [getattr(r, k) for k in reduce_names(n)]
        return Reduce(part, *bufs, half, r.rs.at[i], r.rq.at[i], t, s)

    sa, sb, sc = reducer("a", r.g1, 32, 0), reducer("b", r.g2, 32, 1), reducer("c", r.g3, 64, 2)
    sc.core()
    layer_output(s, r.h3, r.lout, scnt, fcnt)
    feature_grads(
        r.o1, r.wo1, r.w2, r.wo2, r.gains, fcnt, r.h1, r.h2, r.a2, r.qkv2, r.o2, r.g, r.da, r.b, r.do2, r.dqkv,
        r.wide, r.g2, r.dwo1, r.do1, r.gr, r.dgain,
    )
    edge_rows(r.g2, r.g1, 1)
    moves2 = [
        send(r.do1.at[:, (s + k) % 4], r.do.at[s], r.as3.at[k - 1], r.aq3.at[k - 1], (t, (s + k) % 4))
        for k in (1, 2, 3)
    ]
    r.do[s] = r.do1[:, s, :, :]
    sb.core()
    sc.one()
    r.at[...] = turn(r.a1[...])
    sb.one()
    for copy in moves2:
        copy.wait_recv()
    live = lax.broadcasted_iota(jnp.int32, (512, 1), 0) < scnt

    def heads(lo, hi):
        def body(h, _):
            backward_heads(h, r.qkv1, r.do, live, r.dqkv, r.kt, r.dkv)
            return 0

        lax.fori_loop(lo, hi, body, 0)

    heads(0, 2)
    sc.two()
    heads(2, 3)
    sb.two()
    sc.three()
    heads(3, 4)
    sb.three()

    def norm_back(i, dg):
        rows = block(i)
        da = nt(r.dqkv[0, rows, :], r.w1[0]) + nt(r.dqkv[1, rows, :], r.w1[1]) + nt(r.dqkv[2, rows, :], r.w1[2])
        dh, part = norm_grad(r.cf[i].astype(F32).reshape(128, D), da, gain1)
        r.dhs[i] = dh.astype(BF).reshape(4, 32, D)
        return dg + part

    dg = four_blocks(norm_back, jnp.zeros((1, D), F32))
    homes = [
        send(r.dhs.at[(s + k) % 4], r.dhr.at[:, s], r.as4.at[k - 1], r.aq4.at[k - 1], (t, (s + k) % 4))
        for k in (1, 2, 3)
    ]

    def weights(j, _):
        store_wide(r.wide, j, 3, nn(r.at[...], r.dqkv[j]))
        return 0

    lax.fori_loop(0, 3, weights, 0)

    def narrow(i, _):
        rows = pl.ds(mult(i * 64, 64), 64)
        for b in range(4):
            r.g1[i, 0:64, 128 * b : 128 * b + 128] = r.wide[b, rows, :].astype(BF)
        return 0

    lax.fori_loop(0, 24, narrow, 0)

    def copy_out(i, _):
        r.g1[24 + i, 0:64, :] = r.dwo1[pl.ds(mult(i * 64, 64), 64), :]
        return 0

    lax.fori_loop(0, 8, copy_out, 0)
    edge_rows(r.g1, r.g1, 0)
    edge_gains(r.g1, dg, r.dgain)
    sa.core()
    sa.one()
    main3 = sc.result()
    to_rows(main3, r.fl3)
    main2 = sb.result()
    to_rows(main2, r.fl2)
    sa.two()
    sa.three()
    r.cgrad[:, s, :, :] = r.gr[:, s, :, :] + r.dhs[s].astype(F32)
    for k in (1, 2, 3):
        homes[k - 1].wait_recv()
        f = (s + 4 - k) % 4
        r.cgrad[:, f, :, :] = r.gr[:, f, :, :] + r.dhr[:, f, :, :].astype(F32)
    total = sa.result()
    to_rows(total[0:64, :], r.fl1)
    first = total[64:72, :]
    to_shard(first[0:1, :], r.fl1, 64, d, r.sh1)
    to_shard(first[1:2, :], r.fl2, 64, d, r.sh2)
    to_shard(first[2:3, :], r.fl3, 128, d, r.sh3)
    r.sums[0] = jnp.zeros((32, 128), F32)
    squares(r.sh1, r.m1, r.f1, r.s1, r.sums.at[0], d, 3 * D, 0)
    squares(r.sh2, r.m2, r.f2, r.s2, r.sums.at[0], d, 3 * D, 1)
    squares(r.sh3, r.m3, r.f3, r.s3, r.sums.at[0], d, 4 * D, 2)
    r.total[...], adds = sum_all(r.sums, r.got, r.zs, r.ns, r.nq, t, s)
    for one in (sa, sb, sc):
        one.drain()
    for copy in moves + backs + moves2 + homes + adds:
        copy.wait_send()


def call_m(scnt, fcnt, cells, top, params):
    sds = jax.ShapeDtypeStruct
    vm = pl.BlockSpec(memory_space=pltpu.VMEM)
    sm = pl.BlockSpec(memory_space=pltpu.SMEM)
    return pl.pallas_call(
        kernel_m,
        name="kernel_m",
        out_shape=(
            sds((4, 4, 32, D), BF), sds((4, 4, 32, D), F32), sds((264, 128), F32), sds((264, 128), F32),
            sds((520, 128), F32), sds((32, 128), F32),
        ),
        in_specs=[sm, sm] + [vm] * 11,
        out_specs=(vm,) * 6,
        scratch_shapes=list(SCRATCH.values()),
        compiler_params=pltpu.CompilerParams(collective_id=1, has_side_effects=True, vmem_limit_bytes=63 << 20),
    )(scnt, fcnt, cells, top, *params)


def local(x):
    return jnp.transpose(x.reshape(4, 32, 4, D), (0, 2, 1, 3))


def globe(x):
    return jnp.transpose(x, (0, 2, 1, 3)).reshape(1, 128, 4, D)


def fast_device(cells, out_grad, scnt, fcnt, b1, f1, s1, b2, f2, s2, b3, f3, s3):
    params = (b1, f1, s1, b2, f2, s2, b3, f3, s3)
    out, cgrad, sh1, sh2, sh3, total = call_m(scnt, fcnt, local(cells), local(out_grad), params)
    outs = call_e(total, (sh1, sh2, sh3), params)
    return (globe(out), globe(cgrad), *outs)


def step(*args):
    cells = args[0]
    fits = lax.axis_size("task") == 8 and lax.axis_size("samp") == 4 and cells.shape == (1, 128, 4, D)
    return fast_device(*args) if fits else on_device(*args)


def solution(mesh):
    placed = (
        P("task", "samp", None, None),
        P("task", "samp", None, None),
        P("task"),
        P("task"),
        P(("task", "samp")),
        P(("task", "samp")),
        P(("task", "samp")),
        P(("task", "samp")),
        P(("task", "samp")),
        P(("task", "samp")),
        P(("task", "samp")),
        P(("task", "samp")),
        P(("task", "samp")),
    )
    return jax.shard_map(
        step,
        mesh=mesh,
        in_specs=placed,
        out_specs=(
            P("task", "samp", None, None),
            P("task", "samp", None, None),
            P(("task", "samp")),
            P(("task", "samp")),
            P(("task", "samp")),
            P(("task", "samp")),
            P(("task", "samp")),
            P(("task", "samp")),
            P(("task", "samp")),
            P(("task", "samp")),
            P(("task", "samp")),
            P(("task", "samp")),
            P(("task", "samp")),
            P(("task", "samp")),
            P(("task", "samp")),
            P(("task", "samp")),
            P(("task", "samp")),
            P(),
        ),
        check_vma=False,
    )
```

```python
import jax
import jax.numpy as jnp
from jax import lax
from jax.experimental import pallas as pl
from jax.experimental.pallas import tpu as pltpu
from jax.sharding import PartitionSpec as P

D = 512
HEADS = 8
HEAD_DIM = 64
FF = 2048


EPS_NORM = 1e-05
EPS_ADAM = 1e-06
STEP_RATE = 0.5
BIG_NEGATIVE = -1e30


def normalize(hidden, gain_row):
    centre = jnp.mean(hidden, -1, keepdims=True)
    shifted = hidden - centre
    spread = jnp.mean(shifted * shifted, -1, keepdims=True)
    return shifted * lax.rsqrt(spread + EPS_NORM) * gain_row


def norm_backward(hidden, gain_row, normed_grad):
    _, pullback = jax.vjp(normalize, hidden, gain_row)
    return pullback(normed_grad)


def gelu_exact(upward):
    return jax.nn.gelu(upward, approximate=False)


def contract_rows(left, right):
    return lax.dot_general(
        left, right, (((0,), (0,)), ((), ())), preferred_element_type=jnp.float32
    )


def times_transpose(left, right):
    return lax.dot_general(
        left, right, (((1,), (1,)), ((), ())), preferred_element_type=jnp.float32
    )


def unpack(flat_params, width_in, width_mid):
    gain_row = flat_params[:D].astype(jnp.float32)
    w_in = flat_params[D : D + D * width_in].reshape(D, width_in)
    w_out = flat_params[D + D * width_in :].reshape(width_mid, D)
    return (gain_row, w_in, w_out)


def fetch_forward(master):
    return lax.all_gather(master.astype(jnp.bfloat16), ("task", "samp"), axis=0, tiled=True)


def fetch_again(master):
    return lax.all_gather(master.astype(jnp.bfloat16), ("task", "samp"), axis=0, tiled=True)


def reduce_grads(gain_grad, in_grad, out_grad_matrix):
    flat_grads = jnp.concatenate([gain_grad, in_grad.reshape(-1), out_grad_matrix.reshape(-1)])
    return lax.psum_scatter(flat_grads, ("task", "samp"), scatter_dimension=0, tiled=True)


def group_size(feature_total, most):
    chosen = 1
    for candidate in range(1, most + 1):
        if feature_total % candidate == 0:
            chosen = candidate
    return chosen


def lamb_prepare(grad_shard, master, first, second, width_in):
    first_new = 0.5 * first + 0.5 * grad_shard
    second_new = 0.5 * second + 0.5 * grad_shard * grad_shard
    direction = first_new / (jnp.sqrt(second_new) + EPS_ADAM)
    entries = master.shape[0]
    position = lax.axis_index(("task", "samp")) * entries + jnp.arange(entries, dtype=jnp.int32)
    segment = (position >= D).astype(jnp.int32) + (position >= D + D * width_in).astype(jnp.int32)
    member = segment[None, :] == jnp.arange(3, dtype=jnp.int32)[:, None]
    weight_sums = jnp.sum(jnp.where(member, (master * master)[None, :], 0.0), 1)
    update_sums = jnp.sum(jnp.where(member, (direction * direction)[None, :], 0.0), 1)
    return (first_new, second_new, direction, member, jnp.stack([weight_sums, update_sums], 1))


def lamb_finish(master, block_state, trust_ratio):
    factor = jnp.sum(jnp.where(block_state[3], trust_ratio[:, None], 0.0), 0)
    return master - STEP_RATE * factor * block_state[2]


def sample_scores(query_part, key_part, key_live, score_scale):
    scores = (
        jnp.einsum("qfhe,kfhe->fhqk", query_part, key_part, preferred_element_type=jnp.float32)
        * score_scale
    )
    return jnp.where(key_live, scores, BIG_NEGATIVE)


def sample_forward(queries, pairs_all, key_live, block_features, score_scale):
    local_rows, features = (queries.shape[0], queries.shape[1])

    def one_block(block_index, results):
        attended, log_totals = results
        offset = block_index * block_features
        query_part = lax.dynamic_slice_in_dim(queries, offset, block_features, 1)
        pair_part = lax.dynamic_slice_in_dim(pairs_all, offset, block_features, 1)
        scores = sample_scores(query_part, pair_part[:, :, 0], key_live, score_scale)
        row_top = jnp.max(scores, -1, keepdims=True)
        exponent = jnp.exp(scores - row_top)
        row_total = jnp.sum(exponent, -1, keepdims=True)
        probability = (exponent / row_total).astype(jnp.bfloat16)
        block_out = jnp.einsum(
            "fhqk,kfhe->qfhe", probability, pair_part[:, :, 1], preferred_element_type=jnp.float32
        )
        attended = lax.dynamic_update_slice_in_dim(
            attended, block_out.astype(jnp.bfloat16), offset, 1
        )
        log_totals = lax.dynamic_update_slice_in_dim(
            log_totals, (row_top + jnp.log(row_total))[..., 0], offset, 0
        )
        return (attended, log_totals)

    start_state = (
        jnp.zeros(queries.shape, jnp.bfloat16),
        jnp.zeros((features, HEADS, local_rows), jnp.float32),
    )
    return lax.fori_loop(0, features // block_features, one_block, start_state)


def query_side(query_part, pair_part, grad_part, log_part, key_live, score_scale):
    key_part = pair_part[:, :, 0]
    value_part = pair_part[:, :, 1]
    scores = sample_scores(query_part, key_part, key_live, score_scale)
    probability = jnp.exp(scores - log_part[..., None])
    prob_grad = jnp.einsum(
        "qfhe,kfhe->fhqk", grad_part, value_part, preferred_element_type=jnp.float32
    )
    row_inner = jnp.sum(probability * prob_grad, -1, keepdims=True)
    score_grad = (probability * (prob_grad - row_inner)).astype(jnp.bfloat16)
    query_block = (
        jnp.einsum("fhqk,kfhe->qfhe", score_grad, key_part, preferred_element_type=jnp.float32)
        * score_scale
    )
    return (probability, score_grad, row_inner, query_block)


def sample_backward(
    queries, pairs_all, key_live, log_totals, attended_grad, block_features, score_scale
):
    local_rows, features = (queries.shape[0], queries.shape[1])

    def one_block(block_index, results):
        query_grads, pair_grads = results
        offset = block_index * block_features
        query_part = lax.dynamic_slice_in_dim(queries, offset, block_features, 1)
        pair_part = lax.dynamic_slice_in_dim(pairs_all, offset, block_features, 1)
        grad_part = lax.dynamic_slice_in_dim(attended_grad, offset, block_features, 1)
        log_part = lax.dynamic_slice_in_dim(log_totals, offset, block_features, 0)
        probability, score_grad, row_inner, query_block = query_side(
            query_part, pair_part, grad_part, log_part, key_live, score_scale
        )
        key_block = (
            jnp.einsum(
                "fhqk,qfhe->kfhe", score_grad, query_part, preferred_element_type=jnp.float32
            )
            * score_scale
        )
        value_block = jnp.einsum(
            "fhqk,qfhe->kfhe",
            probability.astype(jnp.bfloat16),
            grad_part,
            preferred_element_type=jnp.float32,
        )
        pair_terms = jnp.stack([key_block, value_block], 2)
        pair_local = lax.psum_scatter(
            pair_terms.astype(jnp.bfloat16), "samp", scatter_dimension=0, tiled=True
        ).astype(jnp.float32)
        query_grads = lax.dynamic_update_slice_in_dim(query_grads, query_block, offset, 1)
        pair_grads = lax.dynamic_update_slice_in_dim(pair_grads, pair_local, offset, 1)
        return (query_grads, pair_grads)

    start_state = (
        jnp.zeros((local_rows, features, HEADS, HEAD_DIM), jnp.float32),
        jnp.zeros((local_rows, features, 2, HEADS, HEAD_DIM), jnp.float32),
    )
    return lax.fori_loop(0, features // block_features, one_block, start_state)


def on_device(
    cells,
    out_grad,
    sample_counts,
    feature_counts,
    sample_block,
    sample_first,
    sample_second,
    feature_block,
    feature_first,
    feature_second,
    mlp_block,
    mlp_first,
    mlp_second,
):
    local_rows, features = (cells.shape[1], cells.shape[2])
    flat_rows = local_rows * features
    seq_all = local_rows * lax.axis_size("samp")
    score_scale = HEAD_DIM ** (-0.5)
    block_features = group_size(features, max(1, 2048 // (HEADS * local_rows)))
    sample_index = lax.axis_index("samp") * local_rows + jnp.arange(local_rows, dtype=jnp.int32)
    sample_live = sample_index < sample_counts[0]
    key_live = jnp.arange(seq_all, dtype=jnp.int32) < sample_counts[0]
    feature_live = jnp.arange(features, dtype=jnp.int32) < feature_counts[0]
    cell_live = sample_live[:, None, None] & feature_live[None, :, None]
    hidden_in = cells[0].astype(jnp.float32)
    gain_one, in_one, out_one = unpack(fetch_forward(sample_block), 3 * D, D)
    normed_one = normalize(hidden_in, gain_one).astype(jnp.bfloat16)
    packed_one = jnp.dot(
        normed_one.reshape(flat_rows, D), in_one, preferred_element_type=jnp.float32
    )
    packed_one = packed_one.astype(jnp.bfloat16).reshape(local_rows, features, 3, HEADS, HEAD_DIM)
    queries_one = packed_one[:, :, 0]
    pairs_local = packed_one[:, :, 1:]
    pairs_all = lax.all_gather(pairs_local, "samp", axis=0, tiled=True)
    attended_one, log_totals = sample_forward(
        queries_one, pairs_all, key_live, block_features, score_scale
    )
    attended_one_rows = attended_one.reshape(flat_rows, D)
    branch_one = jnp.dot(attended_one_rows, out_one, preferred_element_type=jnp.float32)
    hidden_one = hidden_in + branch_one.reshape(local_rows, features, D)
    gain_two, in_two, out_two = unpack(fetch_forward(feature_block), 3 * D, D)
    normed_two = normalize(hidden_one, gain_two).astype(jnp.bfloat16).reshape(flat_rows, D)
    packed_two = jnp.dot(normed_two, in_two, preferred_element_type=jnp.float32)
    packed_two = packed_two.astype(jnp.bfloat16).reshape(local_rows, features, 3, HEADS, HEAD_DIM)
    queries_two, key_two, value_two = (
        packed_two[:, :, 0],
        packed_two[:, :, 1],
        packed_two[:, :, 2],
    )
    scores_two = (
        jnp.einsum("sqhe,skhe->shqk", queries_two, key_two, preferred_element_type=jnp.float32)
        * score_scale
    )
    scores_two = jnp.where(feature_live, scores_two, BIG_NEGATIVE)
    row_top = jnp.max(scores_two, -1, keepdims=True)
    exponent = jnp.exp(scores_two - row_top)
    probability_two = exponent / jnp.sum(exponent, -1, keepdims=True)
    prob_low_two = probability_two.astype(jnp.bfloat16)
    attended_two = jnp.einsum(
        "shqk,skhe->sqhe", prob_low_two, value_two, preferred_element_type=jnp.float32
    )
    attended_two_rows = attended_two.reshape(flat_rows, D).astype(jnp.bfloat16)
    branch_two = jnp.dot(attended_two_rows, out_two, preferred_element_type=jnp.float32)
    hidden_two = hidden_one + branch_two.reshape(local_rows, features, D)
    gain_three, up_weight, down_weight = unpack(fetch_forward(mlp_block), FF, FF)
    normed_three = normalize(hidden_two, gain_three).astype(jnp.bfloat16).reshape(flat_rows, D)
    upward = jnp.dot(normed_three, up_weight, preferred_element_type=jnp.float32)
    activated = gelu_exact(upward).astype(jnp.bfloat16)
    branch_three = jnp.dot(activated, down_weight, preferred_element_type=jnp.float32)
    hidden_three = hidden_two + branch_three.reshape(local_rows, features, D)
    layer_out = jnp.where(cell_live, hidden_three, 0.0).astype(jnp.bfloat16)[None]
    top_grad = jnp.where(cell_live, out_grad[0], jnp.zeros((), jnp.bfloat16))
    top_rows = top_grad.reshape(flat_rows, D)
    gain_three, up_weight, down_weight = unpack(fetch_again(mlp_block), FF, FF)
    down_grad = contract_rows(activated, top_rows)
    act_grad = times_transpose(top_rows, down_weight).astype(jnp.bfloat16)
    _, gelu_pull = jax.vjp(gelu_exact, upward)
    up_grad = gelu_pull(act_grad.astype(jnp.float32))[0].astype(jnp.bfloat16)
    upw_grad = contract_rows(normed_three, up_grad)
    normed_grad = times_transpose(up_grad, up_weight).reshape(local_rows, features, D)
    hidden_grad, gain_three_grad = norm_backward(hidden_two, gain_three, normed_grad)
    grad_two = top_grad.astype(jnp.float32) + hidden_grad
    mlp_shard = reduce_grads(gain_three_grad, upw_grad, down_grad)
    mlp_state = lamb_prepare(mlp_shard, mlp_block, mlp_first, mlp_second, FF)
    gain_two, in_two, out_two = unpack(fetch_again(feature_block), 3 * D, D)
    branch_grad = grad_two.astype(jnp.bfloat16).reshape(flat_rows, D)
    out_two_grad = contract_rows(attended_two_rows, branch_grad)
    attended_grad = (
        times_transpose(branch_grad, out_two)
        .astype(jnp.bfloat16)
        .reshape(local_rows, features, HEADS, HEAD_DIM)
    )
    prob_grad = jnp.einsum(
        "sqhe,skhe->shqk", attended_grad, value_two, preferred_element_type=jnp.float32
    )
    row_inner = jnp.sum(probability_two * prob_grad, -1, keepdims=True)
    score_grad = (probability_two * (prob_grad - row_inner)).astype(jnp.bfloat16)
    query_grad = (
        jnp.einsum("shqk,skhe->sqhe", score_grad, key_two, preferred_element_type=jnp.float32)
        * score_scale
    )
    key_grad = (
        jnp.einsum("shqk,sqhe->skhe", score_grad, queries_two, preferred_element_type=jnp.float32)
        * score_scale
    )
    value_grad = jnp.einsum(
        "shqk,sqhe->skhe", prob_low_two, attended_grad, preferred_element_type=jnp.float32
    )
    packed_grad = (
        jnp.stack([query_grad, key_grad, value_grad], 2)
        .astype(jnp.bfloat16)
        .reshape(flat_rows, 3 * D)
    )
    in_two_grad = contract_rows(normed_two, packed_grad)
    normed_grad = times_transpose(packed_grad, in_two).reshape(local_rows, features, D)
    hidden_grad, gain_two_grad = norm_backward(hidden_one, gain_two, normed_grad)
    grad_one = grad_two + hidden_grad
    feature_shard = reduce_grads(gain_two_grad, in_two_grad, out_two_grad)
    feature_state = lamb_prepare(feature_shard, feature_block, feature_first, feature_second, 3 * D)
    gain_one, in_one, out_one = unpack(fetch_again(sample_block), 3 * D, D)
    pairs_all = lax.all_gather(pairs_local, "samp", axis=0, tiled=True)
    branch_grad = grad_one.astype(jnp.bfloat16).reshape(flat_rows, D)
    out_one_grad = contract_rows(attended_one_rows, branch_grad)
    attended_grad = (
        times_transpose(branch_grad, out_one)
        .astype(jnp.bfloat16)
        .reshape(local_rows, features, HEADS, HEAD_DIM)
    )
    query_grads, pair_grads = sample_backward(
        queries_one, pairs_all, key_live, log_totals, attended_grad, block_features, score_scale
    )
    packed_grad = (
        jnp.concatenate([query_grads[:, :, None], pair_grads], 2)
        .astype(jnp.bfloat16)
        .reshape(flat_rows, 3 * D)
    )
    in_one_grad = contract_rows(normed_one.reshape(flat_rows, D), packed_grad)
    normed_grad = times_transpose(packed_grad, in_one).reshape(local_rows, features, D)
    hidden_grad, gain_one_grad = norm_backward(hidden_in, gain_one, normed_grad)
    cells_grad = (grad_one + hidden_grad)[None]
    sample_shard = reduce_grads(gain_one_grad, in_one_grad, out_one_grad)
    sample_state = lamb_prepare(sample_shard, sample_block, sample_first, sample_second, 3 * D)
    totals = lax.psum(
        jnp.concatenate([sample_state[4], feature_state[4], mlp_state[4]], 0), ("task", "samp")
    )
    norm_pairs = jnp.sqrt(totals)
    trust_ratio = norm_pairs[:, 0] / (norm_pairs[:, 1] + EPS_ADAM)
    sample_master = lamb_finish(sample_block, sample_state, trust_ratio[0:3])
    feature_master = lamb_finish(feature_block, feature_state, trust_ratio[3:6])
    mlp_master = lamb_finish(mlp_block, mlp_state, trust_ratio[6:9])
    return (
        layer_out,
        cells_grad,
        sample_shard,
        sample_state[0],
        sample_state[1],
        sample_master,
        sample_master.astype(jnp.bfloat16),
        feature_shard,
        feature_state[0],
        feature_state[1],
        feature_master,
        feature_master.astype(jnp.bfloat16),
        mlp_shard,
        mlp_state[0],
        mlp_state[1],
        mlp_master,
        mlp_master.astype(jnp.bfloat16),
        norm_pairs,
    )


D = 512
MESH = pl.DeviceIdType.MESH
BF = jnp.bfloat16
F32 = jnp.float32
NEG = -1e30


def mult(value, factor):
    return value if isinstance(value, int) else pl.multiple_of(value, factor)


def nt(left, right):
    return lax.dot_general(left, right, (((1,), (1,)), ((), ())), preferred_element_type=F32)


def nn(left, right):
    return lax.dot_general(left, right, (((1,), (0,)), ((), ())), preferred_element_type=F32)


def here():
    return lax.axis_index("task"), lax.axis_index("samp")


def peers(t, s):
    return [(jnp.bitwise_xor(t, e), s) for e in range(1, 8)] + [(t, jnp.bitwise_xor(s, e)) for e in (1, 2, 3)]


def enter(t, s):
    barrier = pltpu.get_barrier_semaphore()
    for peer in peers(t, s):
        pl.semaphore_signal(barrier, inc=1, device_id=peer, device_id_type=MESH)
    return barrier


def send(src, dst, ssem, rsem, peer):
    copy = pltpu.make_async_remote_copy(
        src_ref=src, dst_ref=dst, send_sem=ssem, recv_sem=rsem, device_id=peer, device_id_type=MESH
    )
    copy.start()
    return copy


class Gather:
    def __init__(self, buf, ssem, rsem, t, s):
        self.buf, self.t, self.s = buf, t, s
        half = buf.shape[2] // 2
        self.ha, self.hb, self.all = pl.ds(0, half), pl.ds(half, half), pl.ds(0, 2 * half)
        self.rows = pl.ds(0, buf.shape[1])
        self.ssem, self.rsem = ssem, rsem
        self.moves = []
        self.tx, self.ty = jnp.bitwise_xor(t, 2), jnp.bitwise_xor(t, 4)
        self.txy, self.tc = jnp.bitwise_xor(t, 6), jnp.bitwise_xor(t, 1)
        self.hops, self.sent = {}, {k: {} for k in ("x", "y", "c", "xy", "yx", "cx", "cy")}

    def z(self, key):
        return jnp.bitwise_xor(self.s, key)

    def go(self, slots, cols, peer):
        view = self.buf.at[slots, self.rows, cols]
        i = len(self.moves)
        copy = send(view, view, self.ssem.at[i], self.rsem.at[i], peer)
        self.moves.append(copy)
        return copy

    def pass_on(self, kind, key, t, cols, to):
        self.sent[kind][key] = self.go(pl.ds(4 * t + self.z(key), 1), cols, (to, self.s))

    def spread(self, key):
        self.pass_on("x", key, self.t, self.all, self.tx)
        self.pass_on("y", key, self.t, self.all, self.ty)
        self.pass_on("c", key, self.t, self.all, self.tc)

    def hop(self, key, slot, to):
        self.hops[key] = self.go(pl.ds(4 * self.t + self.z(slot), 1), self.all, (self.t, self.z(to)))

    def start_z(self):
        self.hop(2, 0, 2)
        self.hop(1, 0, 1)

    def zin(self, *keys):
        for key in keys:
            self.hops[key].wait_recv()
            if key == 2:
                self.hop(3, 2, 1)
            self.spread(key)

    def near(self, *keys):
        for key in keys:
            self.sent["x"][key].wait_recv()
            self.pass_on("xy", key, self.tx, self.ha, self.ty)
            self.pass_on("cx", key, self.tx, self.all, self.tc)
            self.sent["y"][key].wait_recv()
            self.pass_on("yx", key, self.ty, self.hb, self.tx)
            self.pass_on("cy", key, self.ty, self.all, self.tc)

    def far(self):
        for kind in ("xy", "yx"):
            for copy in self.sent[kind].values():
                copy.wait_recv()
        self.last = self.go(pl.ds(4 * self.txy, 4), self.all, (self.tc, self.s))

    def end(self):
        for kind in ("c", "cx", "cy"):
            for copy in self.sent[kind].values():
                copy.wait_recv()
        self.last.wait_recv()

    def drain(self):
        for copy in self.moves:
            copy.wait_send()


def realign(m_ref, sh_ref, d, rows, out_ref, out_at, roll_to):
    whole = 4 * rows
    total = whole + 8
    q, p = d // 8, d % 8
    lane = lax.broadcasted_iota(jnp.int32, (total, 128), 1)
    roll_to[0:8, :] = jnp.zeros((8, 128), F32)
    for i in range(whole // 8):
        sh_ref[8 * i : 8 * i + 8, :] = m_ref[pl.ds(1024 * i, 1024)].reshape(8, 128)
    sh_ref[whole:total, :] = jnp.zeros((8, 128), F32)
    sh_ref[whole : whole + 1, 0:16] = m_ref[pl.ds(128 * whole, 16)].reshape(1, 16)
    rolled = pltpu.roll(sh_ref[0:total, :], 16 * p, 1)
    roll_to[8 : 8 + total, :] = rolled
    sh_ref[0:8, :] = jnp.zeros((8, 128), F32)
    sh_ref[8 : 8 + total, :] = jnp.where(lane < 16 * p, roll_to[7 : 7 + total, :], rolled)
    firsts = []
    for b in range(4):
        out_ref[out_at, 0:rows, 128 * b : 128 * b + 128] = sh_ref[pl.ds(12 - q + b, rows, stride=4), :].astype(BF)
        firsts.append(sh_ref[pl.ds(8 - q + b, 1), :])
    return jnp.concatenate(firsts, 1)


def spread(buf, firsts, kind, rows, lo, hi, put):
    tail = lax.broadcasted_iota(jnp.int32, (8, D), 0) == 7

    def body(i, _):
        nxt = jnp.minimum(i + 1, 31)
        row = firsts[nxt, :, D * kind : D * kind + D]
        block = buf[i, 0:rows, :].astype(F32)
        last = block[rows - 8 : rows, :] + jnp.where(tail & (i < 31), row, 0.0)
        put(i - lo, block[0 : rows - 8, :], last)
        return 0

    lax.fori_loop(lo, hi, body, 0)


def put_f32(dst, rows):
    def put(i, head, last):
        for b in range(4):
            cols = slice(128 * b, 128 * b + 128)
            dst[b, pl.ds(mult(i * rows, rows), rows - 8), :] = head[:, cols]
            dst[b, pl.ds(mult(i * rows + rows - 8, 8), 8), :] = last[:, cols]

    return put


def put_bf(dst, rows):
    def put(i, head, last):
        dst[pl.ds(mult(i * rows, rows), rows), :] = jnp.concatenate([head, last], 0).astype(BF)

    return put


def split_columns(wide, ways, dst):
    def body(i, _):
        for j in range(ways):
            for b in range(4):
                piece = wide[b, pl.ds(64 * ways * i + j, 64, stride=ways), :]
                dst[j, pl.ds(mult(64 * i, 64), 64), 128 * b : 128 * b + 128] = piece.astype(BF)
        return 0

    lax.fori_loop(0, 8, body, 0)


def halves():
    lane = lax.broadcasted_iota(jnp.int32, (128, 128), 1)
    return lane < 64


def two_heads(x, one, two):
    return jnp.concatenate([x * one, x * two], 0)


def soft(scores, axis):
    e = [jnp.exp(x - jnp.max(x, axis, keepdims=True)) for x in scores]
    return [x * (1.0 / jnp.sum(x, axis, keepdims=True)) for x in e]


def attend_chunk(qkv, c, live, out):
    left = halves()
    one = jnp.where(left, 0.125, 0.0).astype(BF)
    two = jnp.where(left, 0.0, 0.125).astype(BF)
    rows = pl.ds(mult(c * 128, 128), 128)

    def body(h, _):
        cols = [pl.ds(128 * i, 128) for i in range(4)]
        scores = [jnp.where(live, nt(two_heads(qkv[0, rows, w], one, two), qkv[1, :, w]), NEG) for w in cols]
        prob = [p.astype(BF) for p in soft(scores, 1)]
        outs = [nn(p, qkv[2, :, w]) for p, w in zip(prob, cols)]
        for o, w in zip(outs, cols):
            o = jnp.where(left, o[0:128], o[128:256]).astype(BF)
            for g in range(4):
                out[g, :, w] = o[32 * g : 32 * g + 32]
        return 0

    body(0, 0)


def edges(d, entries, width):
    begin = d * entries
    return D - begin, D + D * width - begin


def segment(k, ends):
    return (k >= ends[0]).astype(jnp.int32) + (k >= ends[1]).astype(jnp.int32)


def lamb_step(g, m, f, s):
    fn = 0.5 * f + 0.5 * g
    sn = 0.5 * s + 0.5 * g * g
    return fn, sn, fn / (jnp.sqrt(sn) + 1e-6)


def flat_index():
    rows = lax.broadcasted_iota(jnp.int32, (32, 128), 0)
    return rows * 128 + lax.broadcasted_iota(jnp.int32, (32, 128), 1)


def fold(x):
    return x.reshape(-1, 8, 128).sum(0)


def squares(sh, m, f, s, sums, d, width, b, lo, hi):
    entries = m.shape[0]
    ends = edges(d, entries, width)
    index = flat_index()

    def body(i, acc):
        at = pl.ds(mult(i * 4096, 4096), 4096)
        old = m[at].reshape(32, 128)
        _, _, r = lamb_step(sh[pl.ds(mult(i * 32, 32), 32), :], old, f[at].reshape(32, 128), s[at].reshape(32, 128))
        part = segment(index + i * 4096, ends)
        out = []
        for n, value in enumerate((old * old, r * r)):
            for k in range(3):
                out.append(acc[3 * n + k] + fold(jnp.where(part == k, value, 0.0)))
        return tuple(out)

    acc = lax.fori_loop(lo, hi, body, (jnp.zeros((8, 128), F32),) * 6)
    for n in range(2):
        for k in range(3):
            row = 16 * n + 3 * b + k
            sums[row : row + 1, :] += jnp.sum(acc[3 * n + k], 0, keepdims=True)


def squares_tail(sh, m, f, s, sums, d, width, b):
    entries = m.shape[0]
    base = entries - 16
    ends = edges(d, entries, width)
    at = pl.ds(base, 16)
    old = m[at].reshape(1, 16)
    row = base // 128
    _, _, r = lamb_step(sh[row : row + 1, 0:16], old, f[at].reshape(1, 16), s[at].reshape(1, 16))
    part = segment(lax.broadcasted_iota(jnp.int32, (1, 16), 1) + base, ends)
    for n, value in enumerate((old * old, r * r)):
        for k in range(3):
            row = 16 * n + 3 * b + k
            sums[row : row + 1, 0:16] += jnp.where(part == k, value, 0.0)


def update(sh, m, f, s, grad, fout, sout, mout, wout, ratio, d, width, b):
    entries = m.shape[0]
    whole = entries // 4096
    ends = edges(d, entries, width)
    half = [0.5 * ratio[3 * b + k : 3 * b + k + 1, :] for k in range(3)]

    def put(at, g, part, shape):
        old = m[at].reshape(shape)
        fn, sn, r = lamb_step(g, old, f[at].reshape(shape), s[at].reshape(shape))
        factor = jnp.where(part == 0, half[0], jnp.where(part == 1, half[1], half[2]))
        new = (old - factor * r).reshape(-1)
        grad[at] = g.reshape(-1)
        fout[at] = fn.reshape(-1)
        sout[at] = sn.reshape(-1)
        mout[at] = new
        wout[at] = new.astype(BF)

    index = flat_index()

    def body(i, _):
        at = pl.ds(mult(i * 4096, 4096), 4096)
        put(at, sh[pl.ds(mult(i * 32, 32), 32), :], segment(index + i * 4096, ends), (32, 128))
        return 0

    lax.fori_loop(0, whole, body, 0)
    part = segment(lax.broadcasted_iota(jnp.int32, (1, 16), 1) + whole * 4096, ends)
    put(pl.ds(whole * 4096, 16), sh[32 * whole : 32 * whole + 1, 0:16], part, (1, 16))


def diagonal(rows):
    lane = lax.broadcasted_iota(jnp.int32, (32, 128), 1)
    return lane == lax.broadcasted_iota(jnp.int32, (32, 128), 0)


def sum_all(sums, ts, zs, ssem, rsem, t, s):
    column = jnp.sum(sums[...], 1, keepdims=True)
    ts[t] = jnp.broadcast_to(jnp.sum(jnp.where(diagonal(32), column, 0.0), 0, keepdims=True), (8, 128))
    plane = [
        send(ts.at[t], ts.at[t], ssem.at[e - 1], rsem.at[e - 1], (jnp.bitwise_xor(t, e), s)) for e in range(1, 8)
    ]
    for copy in plane:
        copy.wait_recv()
    zs[s] = ((ts[0] + ts[1]) + (ts[2] + ts[3])) + ((ts[4] + ts[5]) + (ts[6] + ts[7]))
    last = [
        send(zs.at[s], zs.at[s], ssem.at[6 + e], rsem.at[6 + e], (t, jnp.bitwise_xor(s, e))) for e in (1, 2, 3)
    ]
    for copy in last:
        copy.wait_recv()
    return (zs[0] + zs[1]) + (zs[2] + zs[3]), plane + last


def kernel_e(
    total, sh1, sh2, sh3, m1, f1, s1, m2, f2, s2, m3, f3, s3,
    g1, fo1, so1, mo1, wo1, g2, fo2, so2, mo2, wo2, g3, fo3, so3, mo3, wo3, pairs,
):
    t, s = here()
    d = 4 * t + s
    norm = jnp.sqrt(jnp.sum(jnp.where(diagonal(32), total[0:1, :], 0.0), 1, keepdims=True))
    pairs[...] = jnp.concatenate([norm[0:9], norm[16:25]], 1)
    ratio = norm[0:9] / (norm[16:25] + 1e-6)
    update(sh1, m1, f1, s1, g1, fo1, so1, mo1, wo1, ratio, d, 3 * D, 0)
    update(sh2, m2, f2, s2, g2, fo2, so2, mo2, wo2, ratio, d, 3 * D, 1)
    update(sh3, m3, f3, s3, g3, fo3, so3, mo3, wo3, ratio, d, 4 * D, 2)


def call_e(total, shards, args):
    sds = jax.ShapeDtypeStruct
    vm = pl.BlockSpec(memory_space=pltpu.VMEM)
    shapes = []
    for m in args[0::3]:
        n = m.shape
        shapes += [sds(n, F32)] * 4 + [sds(n, BF)]
    return pl.pallas_call(
        kernel_e,
        name="kernel_e",
        out_shape=(*shapes, sds((9, 2), F32)),
        in_specs=[vm] * 13,
        out_specs=(vm,) * 16,
        compiler_params=pltpu.CompilerParams(vmem_limit_bytes=40 << 20),
    )(total, *shards, *args)


def backward_heads(h, qkv, do, live, dqkv, kt, dkv):
    left = halves()
    one, two = jnp.where(left, 1.0, 0.0).astype(BF), jnp.where(left, 0.0, 1.0).astype(BF)
    cols = pl.ds(mult(h * 128, 128), 128)
    kt[...] = jnp.transpose(qkv[1, :, cols])
    top_lane = lax.broadcasted_iota(jnp.int32, (128, 128), 0) < 64

    def chunk(n, _):
        each = [0, 1, 2, 3]
        rows = [pl.ds(c * 128, 128) for c in each]
        qm = [two_heads(qkv[0, r, cols] * jnp.asarray(0.125, BF), one, two) for r in rows]
        gm = [two_heads(do[c, :, :, cols].reshape(128, 128), one, two) for c in each]
        prob = soft([jnp.where(live, nt(qkv[1, :, cols], q), NEG) for q in qm], 0)
        pg = [nt(qkv[2, :, cols], g) for g in gm]
        sg = [(p * (x - jnp.sum(p * x, 0, keepdims=True))).astype(BF) for p, x in zip(prob, pg)]
        dqkv[1, :, cols] = (nn(sg[0], qm[0]) + nn(sg[1], qm[1]) + nn(sg[2], qm[2]) + nn(sg[3], qm[3])).astype(BF)
        pb = [p.astype(BF) for p in prob]
        dqkv[2, :, cols] = (nn(pb[0], gm[0]) + nn(pb[1], gm[1]) + nn(pb[2], gm[2]) + nn(pb[3], gm[3])).astype(BF)
        for r, x in zip(rows, sg):
            dqt = nn(kt[...], x)
            dq = jnp.transpose(jnp.where(top_lane, dqt[:, 0:128], dqt[:, 128:256])) * 0.125
            dqkv[0, r, cols] = dq.astype(BF)
        return 0

    chunk(0, 0)


def turn(x):
    return jnp.transpose(x)


def stats(h):
    x = h - jnp.mean(h, 1, keepdims=True)
    rstd = lax.rsqrt(jnp.mean(x * x, 1, keepdims=True) + 1e-5)
    return x * rstd, rstd


def norm_grad(h, da, gain):
    x, rstd = stats(h)
    dgain = jnp.sum(da * x, 0, keepdims=True)
    dx = da * gain
    dh = rstd * (dx - jnp.mean(dx, 1, keepdims=True) - x * jnp.mean(dx * x, 1, keepdims=True))
    return dh, dgain


def block(g):
    return pl.ds(mult(g * 128, 128), 128)


def feature_mask(fcnt, axis):
    shape = (256, 128) if axis else (128, 256)
    query = lax.broadcasted_iota(jnp.int32, shape, 1 - axis)
    key = lax.broadcasted_iota(jnp.int32, shape, axis)
    return (query % 32 == key % 32) & (key // 32 < fcnt)


def feature_forward(qkv, o2, fcnt):
    left = halves()
    one = jnp.where(left, 0.125, 0.0).astype(BF)
    two = jnp.where(left, 0.0, 0.125).astype(BF)
    ok = feature_mask(fcnt, 1)
    cols = [slice(128 * h, 128 * h + 128) for h in range(4)]

    def body(n, _):
        rows = block(n)
        scores = [
            jnp.where(ok, nt(two_heads(qkv[0, rows, c], one, two), qkv[1, rows, c]), NEG) for c in cols
        ]
        prob = [p.astype(BF) for p in soft(scores, 1)]
        out = [nn(p, qkv[2, rows, c]) for p, c in zip(prob, cols)]
        for o, c in zip(out, cols):
            o2[rows, c] = jnp.where(left, o[0:128], o[128:256]).astype(BF)
        return 0

    lax.fori_loop(0, 4, body, 0)


def feature_backward(qkv, do, dqkv, fcnt):
    left = halves()
    one, two = jnp.where(left, 1.0, 0.0).astype(BF), jnp.where(left, 0.0, 1.0).astype(BF)
    ok = feature_mask(fcnt, 0)
    top_lane = lax.broadcasted_iota(jnp.int32, (128, 128), 0) < 64
    cols = [slice(128 * h, 128 * h + 128) for h in range(4)]

    def body(n, _):
        rows = block(n)
        qm = [two_heads(qkv[0, rows, c] * jnp.asarray(0.125, BF), one, two) for c in cols]
        gm = [two_heads(do[rows, c], one, two) for c in cols]
        prob = soft([jnp.where(ok, nt(qkv[1, rows, c], q), NEG) for c, q in zip(cols, qm)], 0)
        pg = [nt(qkv[2, rows, c], g) for c, g in zip(cols, gm)]
        sg = [(p * (x - jnp.sum(p * x, 0, keepdims=True))).astype(BF) for p, x in zip(prob, pg)]
        dqt = [nn(turn(qkv[1, rows, c]), x) for c, x in zip(cols, sg)]
        dk = [nn(x, q).astype(BF) for x, q in zip(sg, qm)]
        dv = [nn(p.astype(BF), g).astype(BF) for p, g in zip(prob, gm)]
        dq = [turn(jnp.where(top_lane, x[:, 0:128], x[:, 128:256])) * 0.125 for x in dqt]
        for i, c in enumerate(cols):
            dqkv[0, rows, c] = dq[i].astype(BF)
            dqkv[1, rows, c] = dk[i]
            dqkv[2, rows, c] = dv[i]
        return 0

    lax.fori_loop(0, 4, body, 0)


def four_blocks(body, init=0):
    for r in range(4):
        init = body(r, init)
    return init


def flat(x):
    return x.reshape(128, D)


def cube(x):
    return x.reshape(4, 32, D)


def narrow_to(wide, part, slots, rows):
    def body(i, _):
        at = pl.ds(mult(i * rows, rows), rows)
        for b in range(4):
            part[i, :, 128 * b : 128 * b + 128] = wide[b, at, :].astype(BF)
        return 0

    lax.fori_loop(0, slots, body, 0)


def store_wide(wide, j, ways, value):
    for b in range(4):
        wide[b, pl.ds(j, value.shape[0], stride=ways), :] = value[:, 128 * b : 128 * b + 128]


def mlp(a3, a3t, g, h2, wup, wdn, h3, da, zb, dub, u, dz, wide, p3):
    h3[...] = h2[...]
    da[...] = jnp.zeros((512, D), F32)

    def body(j, _):
        u[...] = nn(a3[...], wup[j])
        dz[...] = nt(g[...], wdn[j]).astype(BF)

        def act(r, _):
            rows = pl.ds(mult(r * 64, 64), 64)
            x = u[rows, :]
            cdf = 0.5 * (1.0 + lax.erf(x * 0.7071067811865476))
            zb[rows, :] = (x * cdf).astype(BF)
            slope = cdf + x * (0.3989422804014327 * jnp.exp(-0.5 * x * x))
            dub[rows, :] = (slope * dz[rows, :].astype(F32)).astype(BF)
            return 0

        lax.fori_loop(0, 8, act, 0)
        h3[...] += nn(zb[...], wdn[j])
        da[...] += nt(dub[...], wup[j])
        store_wide(wide, j, 4, nn(a3t[...], dub[...]))
        dw = nn(turn(zb[...]), g[...]).astype(BF)
        for i in range(4):
            p3[16 + 4 * j + i] = dw[128 * i : 128 * i + 128]
        return 0

    lax.fori_loop(0, 4, body, 0)
    narrow_to(wide, p3, 16, 128)


def middle_forward(s, cells, top, o1, wo1, w2, wo2, gains, scnt, fcnt, h1, h2, a2, qkv, o2, a3, g):
    gain2, gain3 = gains[1:2, :], gains[2:3, :]
    h1[...] = nn(o1[...].reshape(512, D), wo1[...])

    def first(r, _):
        rows = block(r)
        h = h1[rows, :] + flat(cells[r].astype(F32))
        h1[rows, :] = h
        x, _ = stats(h)
        a2[rows, :] = (x * gain2).astype(BF)
        n = lax.broadcasted_iota(jnp.int32, (128, 1), 0)
        live = (n // 32 < fcnt) & (128 * s + 32 * r + n % 32 < scnt)
        g[rows, :] = jnp.where(live, flat(top[r].astype(F32)), 0.0).astype(BF)
        return 0

    four_blocks(first)

    def project(j, _):
        qkv[j] = nn(a2[...], w2[j]).astype(BF)
        return 0

    lax.fori_loop(0, 3, project, 0)
    feature_forward(qkv, o2, fcnt)
    h2[...] = h1[...] + nn(o2[...], wo2[...])

    def second(r, _):
        rows = block(r)
        x, _ = stats(h2[rows, :])
        a3[rows, :] = (x * gain3).astype(BF)
        return 0

    four_blocks(second)


def layer_output(s, h3, lout, scnt, fcnt):
    def last(r, _):
        n = lax.broadcasted_iota(jnp.int32, (128, 1), 0)
        live = (n // 32 < fcnt) & (128 * s + 32 * r + n % 32 < scnt)
        lout[r] = cube(jnp.where(live, h3[block(r), :], 0.0).astype(BF))
        return 0

    four_blocks(last)


def feature_grads(wo1, w2, wo2, gains, fcnt, h1, h2, qkv, g, da, b2, b1, do, dqkv, do1, gr, dgain, hook):
    gain2, gain3 = gains[1:2, :], gains[2:3, :]

    def third(r, dg):
        rows = block(r)
        dh, part = norm_grad(h2[rows, :], da[rows, :], gain3)
        total = g[rows, :].astype(F32) + dh
        gr[r] = cube(total)
        b2[rows, :] = total.astype(BF)
        return dg + part

    dg3 = four_blocks(third, jnp.zeros((1, D), F32))
    do[...] = nt(b2[...], wo2[...]).astype(BF)
    feature_backward(qkv, do, dqkv, fcnt)
    hook()
    da[...] = nt(dqkv[0], w2[0]) + nt(dqkv[1], w2[1]) + nt(dqkv[2], w2[2])

    def fourth(r, dg):
        rows = block(r)
        dh, part = norm_grad(h1[rows, :], da[rows, :], gain2)
        total = flat(gr[r]) + dh
        gr[r] = cube(total)
        b1[rows, :] = total.astype(BF)
        return dg + part

    dg2 = four_blocks(fourth, jnp.zeros((1, D), F32))
    do1[...] = nt(b1[...], wo1[...]).astype(BF).reshape(4, 4, 32, D)
    n = lax.broadcasted_iota(jnp.int32, (8, D), 0)
    dgain[...] = jnp.where(n == 1, dg2, jnp.where(n == 2, dg3, 0.0))


def feature_weights(o1, a2, o2, b2, b1, dqkv, wide, p2, dwo1):
    def weights(j, _):
        store_wide(wide, j, 3, nn(turn(a2[...]), dqkv[j]))
        return 0

    lax.fori_loop(0, 3, weights, 0)
    narrow_to(wide, p2, 24, 64)
    dw = nn(turn(o2[...]), b2[...]).astype(BF)
    for i in range(8):
        p2[24 + i] = dw[64 * i : 64 * i + 64]
    dwo1[...] = nn(turn(o1[...].reshape(512, D)), b1[...]).astype(BF)


class Reduce:
    def __init__(self, part, r1, ry, rx, ry2, rx2, rz, ssem, rsem, t, s):
        self.part, self.r1 = part, r1
        self.ry, self.rx, self.ry2, self.rx2, self.rz = ry, rx, ry2, rx2, rz
        half = part.shape[2] // 2
        self.ha, self.hb, self.all = pl.ds(0, half), pl.ds(half, half), pl.ds(0, 2 * half)
        self.ssem, self.rsem, self.t, self.s = ssem, rsem, t, s
        self.copies = []

    def go(self, src, dst, peer):
        i = len(self.copies)
        copy = send(src, dst, self.ssem.at[i], self.rsem.at[i], peer)
        self.copies.append(copy)
        return copy

    def xor(self, e):
        return jnp.bitwise_xor(self.t, e)

    def group(self, e, cols):
        return self.part.at[pl.ds(4 * self.xor(2 * e), 4), :, cols]

    def core(self):
        tc = self.xor(1)
        self.c = [
            self.go(self.part.at[pl.ds(4 * jnp.bitwise_xor(tc, 2 * e), 4)], self.r1.at[e], (tc, self.s))
            for e in (2, 3, 1, 0)
        ]

    def add(self, e, cols, got):
        base = 4 * self.xor(2 * e)
        for j in range(4):
            own = self.part[base + j, :, cols].astype(F32)
            self.part[base + j, :, cols] = (own + got[j].astype(F32)).astype(self.part.dtype)

    def one(self):
        ty, tx, s = self.xor(4), self.xor(2), self.s
        self.y, self.x = {}, {}
        for n, e in enumerate((2, 3, 1, 0)):
            self.c[n].wait_recv()
            self.add(e, self.all, self.r1.at[e])
            if e in (2, 3):
                self.y[e - 2] = self.go(self.group(e, self.ha), self.ry.at[e - 2], (ty, s))
            if e in (3, 1):
                self.x[e // 2] = self.go(self.group(e, self.hb), self.rx.at[e // 2], (tx, s))

    def two(self):
        ty, tx, s = self.xor(4), self.xor(2), self.s
        self.y[1].wait_recv()
        self.add(1, self.ha, self.ry.at[1])
        self.x2 = self.go(self.group(1, self.ha), self.rx2, (tx, s))
        self.x[1].wait_recv()
        self.add(2, self.hb, self.rx.at[1])
        self.y2 = self.go(self.group(2, self.hb), self.ry2, (ty, s))
        self.y[0].wait_recv()
        self.add(0, self.ha, self.ry.at[0])
        self.x[0].wait_recv()
        self.add(0, self.hb, self.rx.at[0])

    def three(self):
        self.x2.wait_recv()
        self.add(0, self.ha, self.rx2)
        self.y2.wait_recv()
        self.add(0, self.hb, self.ry2)
        self.z = [self.z_send(1, 0), self.z_send(3, 1)]

    def z_send(self, slot, into):
        t, s = self.t, self.s
        to = jnp.bitwise_xor(s, 2 if into == 2 else 1)
        return self.go(self.part.at[4 * t + jnp.bitwise_xor(s, slot)], self.rz.at[into], (t, to))

    def four(self):
        self.z[1].wait_recv()
        mine = 4 * self.t + jnp.bitwise_xor(self.s, 2)
        own = self.part[mine, :, :].astype(F32)
        self.part[mine, :, :] = (own + self.rz[1, :, :].astype(F32)).astype(self.part.dtype)
        self.z.append(self.z_send(2, 2))

    def result(self):
        self.z[0].wait_recv()
        self.z[2].wait_recv()
        own = self.part[4 * self.t + self.s, :, :].astype(F32)
        return own + self.rz[0, :, :].astype(F32) + self.rz[2, :, :].astype(F32)

    def drain(self):
        for copy in self.copies:
            copy.wait_send()


def edge_rows(part, edges, kind):
    rows = part.shape[1]

    def body(i, _):
        row = part[i - 1, rows - 16 : rows, :].astype(F32)[15:16, :]
        edges[i, :, D * kind : D * kind + D] = row
        return 0

    lax.fori_loop(1, 32, body, 0)


def to_rows(main, fl):
    rows = main.shape[0]
    for b in range(4):
        fl[pl.ds(4 + b, rows, stride=4), :] = main[:, 128 * b : 128 * b + 128]


def first_row(row, fl):
    for b in range(4):
        fl[b : b + 1, :] = row[:, 128 * b : 128 * b + 128]


def shifted(fl, d, total):
    q, p = d // 8, d % 8
    back = (128 - 16 * p) % 128
    lane = lax.broadcasted_iota(jnp.int32, (total, 128), 1)
    low = pltpu.roll(fl[pl.ds(q, total), :], back, 1)
    high = pltpu.roll(fl[pl.ds(q + 1, total), :], back, 1)
    return jnp.where(lane < 128 - 16 * p, low, high)


def to_shard(fl, rows, d, out_ref):
    total = out_ref.shape[0]
    fl[4 + 4 * rows : total + 8, :] = jnp.zeros((total + 4 - 4 * rows, 128), F32)
    out_ref[...] = shifted(fl, d, total)


def top_shard(fl, d, out_ref):
    out_ref[0:8, :] = shifted(fl, d, 8)


class Refs:
    def __init__(self, names, refs):
        for name, ref in zip(names, refs, strict=True):
            setattr(self, name, ref)


def reduce_names(n):
    return [k + n for k in ("r1", "ry", "rx", "ry2", "rx2", "rz")]


def reduce_scratch(rows, width=D, kind=BF):
    half = width // 2
    return [
        pltpu.VMEM((4, 4, rows, width), kind), pltpu.VMEM((2, 4, rows, half), kind),
        pltpu.VMEM((2, 4, rows, half), kind), pltpu.VMEM((4, rows, half), kind), pltpu.VMEM((4, rows, half), kind),
        pltpu.VMEM((3, rows, width), kind),
    ]


PARAMS = ["m1", "f1", "s1", "m2", "f2", "s2", "m3", "f3", "s3"]
WIDE = pltpu.VMEM((D, D), F32)
NARROW = pltpu.VMEM((D, D), BF)
THREE = pltpu.VMEM((3, D, D), BF)
FOUR = pltpu.VMEM((4, D, D), BF)
TILE = pltpu.VMEM((4, 4, 32, D), BF)
DMA = pltpu.SemaphoreType.DMA
SCRATCH = {
    "g1": pltpu.VMEM((32, 64, D), BF), "ge": pltpu.VMEM((32, 1, 3 * D), F32), "g2": pltpu.VMEM((32, 64, D), BF), "g3": pltpu.VMEM((32, 128, D), BF),
    "wide": pltpu.VMEM((4, 4 * D, 128), F32), "sh": pltpu.VMEM((536, 128), F32), "ro": pltpu.VMEM((536, 128), F32),
    "w1": THREE, "wo1": NARROW, "w2": THREE, "wo2": NARROW, "wup": FOUR, "wdn": FOUR,
    "gains": pltpu.VMEM((8, D), F32), "dgain": pltpu.VMEM((8, D), F32),
    "cf": TILE, "a1": NARROW, "qkv1": THREE, "o1c": pltpu.VMEM((3, 4, 32, D), BF), "o1": TILE,
    "h1": WIDE, "h2": WIDE, "a2": NARROW, "qkv2": THREE, "o2": NARROW, "a3": NARROW, "at": NARROW, "g": NARROW,
    "h3": WIDE, "da": WIDE, "zb": NARROW, "dub": NARROW, "u": WIDE, "dz": NARROW, "b": NARROW, "b1": NARROW, "do2": NARROW,
    "dqkv": THREE, "gr": pltpu.VMEM((4, 4, 32, D), F32), "do1": TILE, "do": TILE, "dwo1": NARROW,
    "kt": pltpu.VMEM((128, D), BF), "dkv": pltpu.VMEM((2, D, 128), F32), "dhs": TILE, "dhr": TILE,
    **dict(zip(reduce_names("a"), reduce_scratch(64))),
    **dict(zip(reduce_names("b"), reduce_scratch(64))),
    **dict(zip(reduce_names("c"), reduce_scratch(128))),
    **dict(zip(reduce_names("d"), reduce_scratch(1, 3 * D, F32))),
    "fl1": pltpu.VMEM((272, 128), F32), "fl2": pltpu.VMEM((272, 128), F32), "fl3": pltpu.VMEM((528, 128), F32),
    "sums": pltpu.VMEM((32, 128), F32), "ts": pltpu.VMEM((8, 8, 128), F32), "zs": pltpu.VMEM((4, 8, 128), F32),
    "gs": DMA((4, 32)), "gq": DMA((4, 32)), "rs": DMA((4, 16)), "rq": DMA((4, 16)),
    "as1": DMA((3,)), "aq1": DMA((3,)), "as2": DMA((3,)), "aq2": DMA((3,)),
    "as3": DMA((3,)), "aq3": DMA((3,)), "as4": DMA((3,)), "aq4": DMA((3,)), "ns": DMA((10,)), "nq": DMA((10,)),
}
INPUTS = ["scnt", "fcnt", "cells", "top"] + PARAMS
OUTPUTS = ["lout", "cgrad", "sh1", "sh2", "sh3", "total"]


def kernel_m(*refs):
    r = Refs(INPUTS + OUTPUTS + list(SCRATCH), refs)
    t, s = here()
    d = 4 * t + s
    scnt, fcnt = r.scnt[0], r.fcnt[0]
    barrier = enter(t, s)
    ga, gb, gc, ge = [
        Gather(buf, r.gs.at[i], r.gq.at[i], t, s) for i, buf in enumerate((r.g1, r.g2, r.g3, r.ge))
    ]
    first1 = realign(r.m1, r.sh, d, 64, r.g1, d, r.ro)
    first2 = realign(r.m2, r.sh, d, 64, r.g2, d, r.ro)
    first3 = realign(r.m3, r.sh, d, 128, r.g3, d, r.ro)
    r.ge[d] = jnp.concatenate([first1, first2, first3], 1).astype(BF).astype(F32)
    pl.semaphore_wait(barrier, 10)
    for one in (ge, ga, gb, gc):
        one.start_z()
        one.spread(0)
    r.cf[s] = r.cells[:, s, :, :]
    for one in (ge, ga):
        one.near(0)
        one.zin(2, 1)
    for one in (ge, ga):
        one.near(2, 1)
        one.zin(3)
    moves = [
        send(r.cells.at[:, (s + k) % 4], r.cf.at[s], r.as1.at[k - 1], r.aq1.at[k - 1], (t, (s + k) % 4))
        for k in (1, 2, 3)
    ]
    for one in (ge, ga):
        one.near(3)
    for one in (ge, ga):
        one.far()
    for one in (gb, gc):
        one.near(0)
        one.zin(2)
    gb.zin(1)
    gc.zin(1)
    for copy in moves:
        copy.wait_recv()
    ge.end()
    ga.end()
    for one in (gb, gc):
        one.near(2)
        one.zin(3)
    gb.near(1)
    gc.near(1)
    spread(r.g1, r.ge, 0, 64, 0, 24, put_f32(r.wide, 64))
    split_columns(r.wide, 3, r.w1)
    spread(r.g1, r.ge, 0, 64, 24, 32, put_bf(r.wo1, 64))
    for k in range(3):
        r.gains[k : k + 1, :] = r.ge[0, :, D * k : D * k + D]
    gain1 = r.gains[0:1, :]

    def norm(i, _):
        x, _ = stats(r.cf[i].astype(F32).reshape(128, D))
        r.a1[block(i), :] = (x * gain1).astype(BF)
        return 0

    four_blocks(norm)

    def project(j, _):
        r.qkv1[j] = nn(r.a1[...], r.w1[j]).astype(BF)
        return 0

    lax.fori_loop(0, 3, project, 0)
    live = lax.broadcasted_iota(jnp.int32, (1, 512), 1) < scnt
    backs = []
    for k in (2, 1, 3, 0):
        c = (s + k) % 4
        if k:
            attend_chunk(r.qkv1, c, live, r.o1c.at[k - 1])
            backs.append(send(r.o1c.at[k - 1], r.o1.at[:, s], r.as2.at[k - 1], r.aq2.at[k - 1], (t, c)))
        else:
            attend_chunk(r.qkv1, c, live, r.o1.at[:, s])
        if k == 2:
            gb.near(3)
            gc.near(3)
    gb.far()
    gb.end()
    spread(r.g2, r.ge, 1, 64, 0, 24, put_f32(r.wide, 64))
    split_columns(r.wide, 3, r.w2)
    spread(r.g2, r.ge, 1, 64, 24, 32, put_bf(r.wo2, 64))
    for copy in backs:
        copy.wait_recv()
    middle_forward(
        s, r.cells, r.top, r.o1, r.wo1, r.w2, r.wo2, r.gains, scnt, fcnt, r.h1, r.h2, r.a2, r.qkv2, r.o2, r.a3, r.g
    )
    r.at[...] = turn(r.a3[...])
    gc.far()
    gc.end()
    spread(r.g3, r.ge, 2, 128, 0, 16, put_f32(r.wide, 128))
    split_columns(r.wide, 4, r.wup)

    def put_down(i, head, last):
        r.wdn[i // 4, pl.ds(mult((i % 4) * 128, 128), 128), :] = jnp.concatenate([head, last], 0).astype(BF)

    spread(r.g3, r.ge, 2, 128, 16, 32, put_down)
    for one in (ga, gb, gc, ge):
        one.drain()
    mlp(r.a3, r.at, r.g, r.h2, r.wup, r.wdn, r.h3, r.da, r.zb, r.dub, r.u, r.dz, r.wide, r.g3)
    edge_rows(r.g3, r.ge, 2)

    def reducer(n, part, i):
        bufs = [getattr(r, k + n) for k in ("r1", "ry", "rx", "ry2", "rx2", "rz")]
        return Reduce(part, *bufs, r.rs.at[i], r.rq.at[i], t, s)

    parts = zip("abcd", (r.g1, r.g2, r.g3, r.ge))
    sa, sb, sc, sd = [reducer(n, part, i) for i, (n, part) in enumerate(parts)]
    sc.core()
    layer_output(s, r.h3, r.lout, scnt, fcnt)
    feature_grads(
        r.wo1, r.w2, r.wo2, r.gains, fcnt, r.h1, r.h2, r.qkv2, r.g, r.da, r.b, r.b1, r.do2, r.dqkv, r.do1, r.gr,
        r.dgain, sc.one,
    )
    moves2 = [
        send(r.do1.at[:, (s + k) % 4], r.do.at[s], r.as3.at[k - 1], r.aq3.at[k - 1], (t, (s + k) % 4))
        for k in (1, 2, 3)
    ]
    feature_weights(r.o1, r.a2, r.o2, r.b, r.b1, r.dqkv, r.wide, r.g2, r.dwo1)
    edge_rows(r.g2, r.ge, 1)
    r.do[s] = r.do1[:, s, :, :]
    sb.core()
    r.at[...] = turn(r.a1[...])
    sb.one()
    sc.two()
    for copy in moves2:
        copy.wait_recv()
    live = lax.broadcasted_iota(jnp.int32, (512, 1), 0) < scnt

    def heads(lo, hi):
        def body(h, _):
            backward_heads(h, r.qkv1, r.do, live, r.dqkv, r.kt, r.dkv)
            return 0

        lax.fori_loop(lo, hi, body, 0)

    heads(0, 2)
    sc.three()
    sb.two()
    heads(2, 3)
    sb.three()
    sc.four()
    heads(3, 4)
    def weights(j, _):
        store_wide(r.wide, j, 3, nn(r.at[...], r.dqkv[j]))
        return 0

    lax.fori_loop(0, 3, weights, 0)

    def narrow(i, _):
        rows = pl.ds(mult(i * 64, 64), 64)
        for b in range(4):
            r.g1[i, :, 128 * b : 128 * b + 128] = r.wide[b, rows, :].astype(BF)
        return 0

    lax.fori_loop(0, 24, narrow, 0)

    def copy_out(i, _):
        r.g1[24 + i] = r.dwo1[pl.ds(mult(i * 64, 64), 64), :]
        return 0

    lax.fori_loop(0, 8, copy_out, 0)
    edge_rows(r.g1, r.ge, 0)
    sa.core()
    r.da[...] = nt(r.dqkv[0], r.w1[0]) + nt(r.dqkv[1], r.w1[1]) + nt(r.dqkv[2], r.w1[2])
    sb.four()
    sa.one()

    def norm_back(i, dg):
        dh, part = norm_grad(r.cf[i].astype(F32).reshape(128, D), r.da[block(i), :], gain1)
        r.dhs[i] = dh.astype(BF).reshape(4, 32, D)
        return dg + part

    dg = four_blocks(norm_back, jnp.zeros((1, D), F32))
    homes = [
        send(r.dhs.at[(s + k) % 4], r.dhr.at[:, s], r.as4.at[k - 1], r.aq4.at[k - 1], (t, (s + k) % 4))
        for k in (1, 2, 3)
    ]
    r.ge[0] = jnp.concatenate([dg, r.dgain[1:2, :], r.dgain[2:3, :]], 1)
    sd.core()
    r.sums[...] = jnp.zeros((32, 128), F32)
    for fl in (r.fl2, r.fl3):
        fl[0:4, :] = jnp.zeros((4, 128), F32)
    to_rows(sc.result(), r.fl3)
    to_shard(r.fl3, 128, d, r.sh3)
    squares(r.sh3, r.m3, r.f3, r.s3, r.sums, d, 4 * D, 2, 1, 16)
    squares_tail(r.sh3, r.m3, r.f3, r.s3, r.sums, d, 4 * D, 2)
    sd.one()
    sa.two()
    to_rows(sb.result(), r.fl2)
    to_shard(r.fl2, 64, d, r.sh2)
    squares(r.sh2, r.m2, r.f2, r.s2, r.sums, d, 3 * D, 1, 1, 8)
    squares_tail(r.sh2, r.m2, r.f2, r.s2, r.sums, d, 3 * D, 1)
    sd.two()
    sa.three()
    r.cgrad[:, s, :, :] = r.gr[:, s, :, :] + r.dhs[s].astype(F32)
    for k in (1, 2, 3):
        homes[k - 1].wait_recv()
        f = (s + 4 - k) % 4
        r.cgrad[:, f, :, :] = r.gr[:, f, :, :] + r.dhr[:, f, :, :].astype(F32)
    sd.three()
    sa.four()
    sd.four()
    to_rows(sa.result(), r.fl1)
    first = sd.result()
    for k, fl in enumerate((r.fl1, r.fl2, r.fl3)):
        first_row(first[:, D * k : D * k + D], fl)
    to_shard(r.fl1, 64, d, r.sh1)
    top_shard(r.fl2, d, r.sh2)
    top_shard(r.fl3, d, r.sh3)
    squares(r.sh1, r.m1, r.f1, r.s1, r.sums, d, 3 * D, 0, 0, 8)
    squares_tail(r.sh1, r.m1, r.f1, r.s1, r.sums, d, 3 * D, 0)
    squares(r.sh2, r.m2, r.f2, r.s2, r.sums, d, 3 * D, 1, 0, 1)
    squares(r.sh3, r.m3, r.f3, r.s3, r.sums, d, 4 * D, 2, 0, 1)
    r.total[...], adds = sum_all(r.sums, r.ts, r.zs, r.ns, r.nq, t, s)
    for one in (sa, sb, sc, sd):
        one.drain()
    for copy in moves + backs + moves2 + homes + adds:
        copy.wait_send()


def call_m(scnt, fcnt, cells, top, params, name="kernel_m"):
    sds = jax.ShapeDtypeStruct
    vm = pl.BlockSpec(memory_space=pltpu.VMEM)
    sm = pl.BlockSpec(memory_space=pltpu.SMEM)
    return pl.pallas_call(
        kernel_m,
        name=name,
        out_shape=(
            sds((4, 4, 32, D), BF), sds((4, 4, 32, D), F32), sds((264, 128), F32), sds((264, 128), F32),
            sds((520, 128), F32), sds((8, 128), F32),
        ),
        in_specs=[sm, sm] + [vm] * 11,
        out_specs=(vm,) * 6,
        scratch_shapes=list(SCRATCH.values()),
        compiler_params=pltpu.CompilerParams(collective_id=1, has_side_effects=True, vmem_limit_bytes=63 << 20),
    )(scnt, fcnt, cells, top, *params)


def local(x):
    return jnp.transpose(x.reshape(4, 32, 4, D), (0, 2, 1, 3))


def globe(x):
    return jnp.transpose(x, (0, 2, 1, 3)).reshape(1, 128, 4, D)


def fast_device(cells, out_grad, scnt, fcnt, b1, f1, s1, b2, f2, s2, b3, f3, s3):
    params = (b1, f1, s1, b2, f2, s2, b3, f3, s3)
    out, cgrad, sh1, sh2, sh3, total = call_m(scnt, fcnt, local(cells), local(out_grad), params)
    outs = call_e(total, (sh1, sh2, sh3), params)
    return (globe(out), globe(cgrad), *outs)


def step(*args):
    cells = args[0]
    fits = lax.axis_size("task") == 8 and lax.axis_size("samp") == 4 and cells.shape == (1, 128, 4, D)
    return fast_device(*args) if fits else on_device(*args)


def solution(mesh):
    placed = (
        P("task", "samp", None, None),
        P("task", "samp", None, None),
        P("task"),
        P("task"),
        P(("task", "samp")),
        P(("task", "samp")),
        P(("task", "samp")),
        P(("task", "samp")),
        P(("task", "samp")),
        P(("task", "samp")),
        P(("task", "samp")),
        P(("task", "samp")),
        P(("task", "samp")),
    )
    return jax.shard_map(
        step,
        mesh=mesh,
        in_specs=placed,
        out_specs=(
            P("task", "samp", None, None),
            P("task", "samp", None, None),
            P(("task", "samp")),
            P(("task", "samp")),
            P(("task", "samp")),
            P(("task", "samp")),
            P(("task", "samp")),
            P(("task", "samp")),
            P(("task", "samp")),
            P(("task", "samp")),
            P(("task", "samp")),
            P(("task", "samp")),
            P(("task", "samp")),
            P(("task", "samp")),
            P(("task", "samp")),
            P(("task", "samp")),
            P(("task", "samp")),
            P(),
        ),
        check_vma=False,
    )
```

```python
import jax
import jax.numpy as jnp
from jax import lax
from jax.experimental import pallas as pl
from jax.experimental.pallas import tpu as pltpu
from jax.sharding import PartitionSpec as P

D = 512
HEADS = 8
HEAD_DIM = 64
FF = 2048


EPS_NORM = 1e-05
EPS_ADAM = 1e-06
STEP_RATE = 0.5
BIG_NEGATIVE = -1e30


def normalize(hidden, gain_row):
    centre = jnp.mean(hidden, -1, keepdims=True)
    shifted = hidden - centre
    spread = jnp.mean(shifted * shifted, -1, keepdims=True)
    return shifted * lax.rsqrt(spread + EPS_NORM) * gain_row


def norm_backward(hidden, gain_row, normed_grad):
    _, pullback = jax.vjp(normalize, hidden, gain_row)
    return pullback(normed_grad)


def gelu_exact(upward):
    return jax.nn.gelu(upward, approximate=False)


def contract_rows(left, right):
    return lax.dot_general(
        left, right, (((0,), (0,)), ((), ())), preferred_element_type=jnp.float32
    )


def times_transpose(left, right):
    return lax.dot_general(
        left, right, (((1,), (1,)), ((), ())), preferred_element_type=jnp.float32
    )


def unpack(flat_params, width_in, width_mid):
    gain_row = flat_params[:D].astype(jnp.float32)
    w_in = flat_params[D : D + D * width_in].reshape(D, width_in)
    w_out = flat_params[D + D * width_in :].reshape(width_mid, D)
    return (gain_row, w_in, w_out)


def fetch_forward(master):
    return lax.all_gather(master.astype(jnp.bfloat16), ("task", "samp"), axis=0, tiled=True)


def fetch_again(master):
    return lax.all_gather(master.astype(jnp.bfloat16), ("task", "samp"), axis=0, tiled=True)


def reduce_grads(gain_grad, in_grad, out_grad_matrix):
    flat_grads = jnp.concatenate([gain_grad, in_grad.reshape(-1), out_grad_matrix.reshape(-1)])
    return lax.psum_scatter(flat_grads, ("task", "samp"), scatter_dimension=0, tiled=True)


def group_size(feature_total, most):
    chosen = 1
    for candidate in range(1, most + 1):
        if feature_total % candidate == 0:
            chosen = candidate
    return chosen


def lamb_prepare(grad_shard, master, first, second, width_in):
    first_new = 0.5 * first + 0.5 * grad_shard
    second_new = 0.5 * second + 0.5 * grad_shard * grad_shard
    direction = first_new / (jnp.sqrt(second_new) + EPS_ADAM)
    entries = master.shape[0]
    position = lax.axis_index(("task", "samp")) * entries + jnp.arange(entries, dtype=jnp.int32)
    segment = (position >= D).astype(jnp.int32) + (position >= D + D * width_in).astype(jnp.int32)
    member = segment[None, :] == jnp.arange(3, dtype=jnp.int32)[:, None]
    weight_sums = jnp.sum(jnp.where(member, (master * master)[None, :], 0.0), 1)
    update_sums = jnp.sum(jnp.where(member, (direction * direction)[None, :], 0.0), 1)
    return (first_new, second_new, direction, member, jnp.stack([weight_sums, update_sums], 1))


def lamb_finish(master, block_state, trust_ratio):
    factor = jnp.sum(jnp.where(block_state[3], trust_ratio[:, None], 0.0), 0)
    return master - STEP_RATE * factor * block_state[2]


def sample_scores(query_part, key_part, key_live, score_scale):
    scores = (
        jnp.einsum("qfhe,kfhe->fhqk", query_part, key_part, preferred_element_type=jnp.float32)
        * score_scale
    )
    return jnp.where(key_live, scores, BIG_NEGATIVE)


def sample_forward(queries, pairs_all, key_live, block_features, score_scale):
    local_rows, features = (queries.shape[0], queries.shape[1])

    def one_block(block_index, results):
        attended, log_totals = results
        offset = block_index * block_features
        query_part = lax.dynamic_slice_in_dim(queries, offset, block_features, 1)
        pair_part = lax.dynamic_slice_in_dim(pairs_all, offset, block_features, 1)
        scores = sample_scores(query_part, pair_part[:, :, 0], key_live, score_scale)
        row_top = jnp.max(scores, -1, keepdims=True)
        exponent = jnp.exp(scores - row_top)
        row_total = jnp.sum(exponent, -1, keepdims=True)
        probability = (exponent / row_total).astype(jnp.bfloat16)
        block_out = jnp.einsum(
            "fhqk,kfhe->qfhe", probability, pair_part[:, :, 1], preferred_element_type=jnp.float32
        )
        attended = lax.dynamic_update_slice_in_dim(
            attended, block_out.astype(jnp.bfloat16), offset, 1
        )
        log_totals = lax.dynamic_update_slice_in_dim(
            log_totals, (row_top + jnp.log(row_total))[..., 0], offset, 0
        )
        return (attended, log_totals)

    start_state = (
        jnp.zeros(queries.shape, jnp.bfloat16),
        jnp.zeros((features, HEADS, local_rows), jnp.float32),
    )
    return lax.fori_loop(0, features // block_features, one_block, start_state)


def query_side(query_part, pair_part, grad_part, log_part, key_live, score_scale):
    key_part = pair_part[:, :, 0]
    value_part = pair_part[:, :, 1]
    scores = sample_scores(query_part, key_part, key_live, score_scale)
    probability = jnp.exp(scores - log_part[..., None])
    prob_grad = jnp.einsum(
        "qfhe,kfhe->fhqk", grad_part, value_part, preferred_element_type=jnp.float32
    )
    row_inner = jnp.sum(probability * prob_grad, -1, keepdims=True)
    score_grad = (probability * (prob_grad - row_inner)).astype(jnp.bfloat16)
    query_block = (
        jnp.einsum("fhqk,kfhe->qfhe", score_grad, key_part, preferred_element_type=jnp.float32)
        * score_scale
    )
    return (probability, score_grad, row_inner, query_block)


def sample_backward(
    queries, pairs_all, key_live, log_totals, attended_grad, block_features, score_scale
):
    local_rows, features = (queries.shape[0], queries.shape[1])

    def one_block(block_index, results):
        query_grads, pair_grads = results
        offset = block_index * block_features
        query_part = lax.dynamic_slice_in_dim(queries, offset, block_features, 1)
        pair_part = lax.dynamic_slice_in_dim(pairs_all, offset, block_features, 1)
        grad_part = lax.dynamic_slice_in_dim(attended_grad, offset, block_features, 1)
        log_part = lax.dynamic_slice_in_dim(log_totals, offset, block_features, 0)
        probability, score_grad, row_inner, query_block = query_side(
            query_part, pair_part, grad_part, log_part, key_live, score_scale
        )
        key_block = (
            jnp.einsum(
                "fhqk,qfhe->kfhe", score_grad, query_part, preferred_element_type=jnp.float32
            )
            * score_scale
        )
        value_block = jnp.einsum(
            "fhqk,qfhe->kfhe",
            probability.astype(jnp.bfloat16),
            grad_part,
            preferred_element_type=jnp.float32,
        )
        pair_terms = jnp.stack([key_block, value_block], 2)
        pair_local = lax.psum_scatter(
            pair_terms.astype(jnp.bfloat16), "samp", scatter_dimension=0, tiled=True
        ).astype(jnp.float32)
        query_grads = lax.dynamic_update_slice_in_dim(query_grads, query_block, offset, 1)
        pair_grads = lax.dynamic_update_slice_in_dim(pair_grads, pair_local, offset, 1)
        return (query_grads, pair_grads)

    start_state = (
        jnp.zeros((local_rows, features, HEADS, HEAD_DIM), jnp.float32),
        jnp.zeros((local_rows, features, 2, HEADS, HEAD_DIM), jnp.float32),
    )
    return lax.fori_loop(0, features // block_features, one_block, start_state)


def on_device(
    cells,
    out_grad,
    sample_counts,
    feature_counts,
    sample_block,
    sample_first,
    sample_second,
    feature_block,
    feature_first,
    feature_second,
    mlp_block,
    mlp_first,
    mlp_second,
):
    local_rows, features = (cells.shape[1], cells.shape[2])
    flat_rows = local_rows * features
    seq_all = local_rows * lax.axis_size("samp")
    score_scale = HEAD_DIM ** (-0.5)
    block_features = group_size(features, max(1, 2048 // (HEADS * local_rows)))
    sample_index = lax.axis_index("samp") * local_rows + jnp.arange(local_rows, dtype=jnp.int32)
    sample_live = sample_index < sample_counts[0]
    key_live = jnp.arange(seq_all, dtype=jnp.int32) < sample_counts[0]
    feature_live = jnp.arange(features, dtype=jnp.int32) < feature_counts[0]
    cell_live = sample_live[:, None, None] & feature_live[None, :, None]
    hidden_in = cells[0].astype(jnp.float32)
    gain_one, in_one, out_one = unpack(fetch_forward(sample_block), 3 * D, D)
    normed_one = normalize(hidden_in, gain_one).astype(jnp.bfloat16)
    packed_one = jnp.dot(
        normed_one.reshape(flat_rows, D), in_one, preferred_element_type=jnp.float32
    )
    packed_one = packed_one.astype(jnp.bfloat16).reshape(local_rows, features, 3, HEADS, HEAD_DIM)
    queries_one = packed_one[:, :, 0]
    pairs_local = packed_one[:, :, 1:]
    pairs_all = lax.all_gather(pairs_local, "samp", axis=0, tiled=True)
    attended_one, log_totals = sample_forward(
        queries_one, pairs_all, key_live, block_features, score_scale
    )
    attended_one_rows = attended_one.reshape(flat_rows, D)
    branch_one = jnp.dot(attended_one_rows, out_one, preferred_element_type=jnp.float32)
    hidden_one = hidden_in + branch_one.reshape(local_rows, features, D)
    gain_two, in_two, out_two = unpack(fetch_forward(feature_block), 3 * D, D)
    normed_two = normalize(hidden_one, gain_two).astype(jnp.bfloat16).reshape(flat_rows, D)
    packed_two = jnp.dot(normed_two, in_two, preferred_element_type=jnp.float32)
    packed_two = packed_two.astype(jnp.bfloat16).reshape(local_rows, features, 3, HEADS, HEAD_DIM)
    queries_two, key_two, value_two = (
        packed_two[:, :, 0],
        packed_two[:, :, 1],
        packed_two[:, :, 2],
    )
    scores_two = (
        jnp.einsum("sqhe,skhe->shqk", queries_two, key_two, preferred_element_type=jnp.float32)
        * score_scale
    )
    scores_two = jnp.where(feature_live, scores_two, BIG_NEGATIVE)
    row_top = jnp.max(scores_two, -1, keepdims=True)
    exponent = jnp.exp(scores_two - row_top)
    probability_two = exponent / jnp.sum(exponent, -1, keepdims=True)
    prob_low_two = probability_two.astype(jnp.bfloat16)
    attended_two = jnp.einsum(
        "shqk,skhe->sqhe", prob_low_two, value_two, preferred_element_type=jnp.float32
    )
    attended_two_rows = attended_two.reshape(flat_rows, D).astype(jnp.bfloat16)
    branch_two = jnp.dot(attended_two_rows, out_two, preferred_element_type=jnp.float32)
    hidden_two = hidden_one + branch_two.reshape(local_rows, features, D)
    gain_three, up_weight, down_weight = unpack(fetch_forward(mlp_block), FF, FF)
    normed_three = normalize(hidden_two, gain_three).astype(jnp.bfloat16).reshape(flat_rows, D)
    upward = jnp.dot(normed_three, up_weight, preferred_element_type=jnp.float32)
    activated = gelu_exact(upward).astype(jnp.bfloat16)
    branch_three = jnp.dot(activated, down_weight, preferred_element_type=jnp.float32)
    hidden_three = hidden_two + branch_three.reshape(local_rows, features, D)
    layer_out = jnp.where(cell_live, hidden_three, 0.0).astype(jnp.bfloat16)[None]
    top_grad = jnp.where(cell_live, out_grad[0], jnp.zeros((), jnp.bfloat16))
    top_rows = top_grad.reshape(flat_rows, D)
    gain_three, up_weight, down_weight = unpack(fetch_again(mlp_block), FF, FF)
    down_grad = contract_rows(activated, top_rows)
    act_grad = times_transpose(top_rows, down_weight).astype(jnp.bfloat16)
    _, gelu_pull = jax.vjp(gelu_exact, upward)
    up_grad = gelu_pull(act_grad.astype(jnp.float32))[0].astype(jnp.bfloat16)
    upw_grad = contract_rows(normed_three, up_grad)
    normed_grad = times_transpose(up_grad, up_weight).reshape(local_rows, features, D)
    hidden_grad, gain_three_grad = norm_backward(hidden_two, gain_three, normed_grad)
    grad_two = top_grad.astype(jnp.float32) + hidden_grad
    mlp_shard = reduce_grads(gain_three_grad, upw_grad, down_grad)
    mlp_state = lamb_prepare(mlp_shard, mlp_block, mlp_first, mlp_second, FF)
    gain_two, in_two, out_two = unpack(fetch_again(feature_block), 3 * D, D)
    branch_grad = grad_two.astype(jnp.bfloat16).reshape(flat_rows, D)
    out_two_grad = contract_rows(attended_two_rows, branch_grad)
    attended_grad = (
        times_transpose(branch_grad, out_two)
        .astype(jnp.bfloat16)
        .reshape(local_rows, features, HEADS, HEAD_DIM)
    )
    prob_grad = jnp.einsum(
        "sqhe,skhe->shqk", attended_grad, value_two, preferred_element_type=jnp.float32
    )
    row_inner = jnp.sum(probability_two * prob_grad, -1, keepdims=True)
    score_grad = (probability_two * (prob_grad - row_inner)).astype(jnp.bfloat16)
    query_grad = (
        jnp.einsum("shqk,skhe->sqhe", score_grad, key_two, preferred_element_type=jnp.float32)
        * score_scale
    )
    key_grad = (
        jnp.einsum("shqk,sqhe->skhe", score_grad, queries_two, preferred_element_type=jnp.float32)
        * score_scale
    )
    value_grad = jnp.einsum(
        "shqk,sqhe->skhe", prob_low_two, attended_grad, preferred_element_type=jnp.float32
    )
    packed_grad = (
        jnp.stack([query_grad, key_grad, value_grad], 2)
        .astype(jnp.bfloat16)
        .reshape(flat_rows, 3 * D)
    )
    in_two_grad = contract_rows(normed_two, packed_grad)
    normed_grad = times_transpose(packed_grad, in_two).reshape(local_rows, features, D)
    hidden_grad, gain_two_grad = norm_backward(hidden_one, gain_two, normed_grad)
    grad_one = grad_two + hidden_grad
    feature_shard = reduce_grads(gain_two_grad, in_two_grad, out_two_grad)
    feature_state = lamb_prepare(feature_shard, feature_block, feature_first, feature_second, 3 * D)
    gain_one, in_one, out_one = unpack(fetch_again(sample_block), 3 * D, D)
    pairs_all = lax.all_gather(pairs_local, "samp", axis=0, tiled=True)
    branch_grad = grad_one.astype(jnp.bfloat16).reshape(flat_rows, D)
    out_one_grad = contract_rows(attended_one_rows, branch_grad)
    attended_grad = (
        times_transpose(branch_grad, out_one)
        .astype(jnp.bfloat16)
        .reshape(local_rows, features, HEADS, HEAD_DIM)
    )
    query_grads, pair_grads = sample_backward(
        queries_one, pairs_all, key_live, log_totals, attended_grad, block_features, score_scale
    )
    packed_grad = (
        jnp.concatenate([query_grads[:, :, None], pair_grads], 2)
        .astype(jnp.bfloat16)
        .reshape(flat_rows, 3 * D)
    )
    in_one_grad = contract_rows(normed_one.reshape(flat_rows, D), packed_grad)
    normed_grad = times_transpose(packed_grad, in_one).reshape(local_rows, features, D)
    hidden_grad, gain_one_grad = norm_backward(hidden_in, gain_one, normed_grad)
    cells_grad = (grad_one + hidden_grad)[None]
    sample_shard = reduce_grads(gain_one_grad, in_one_grad, out_one_grad)
    sample_state = lamb_prepare(sample_shard, sample_block, sample_first, sample_second, 3 * D)
    totals = lax.psum(
        jnp.concatenate([sample_state[4], feature_state[4], mlp_state[4]], 0), ("task", "samp")
    )
    norm_pairs = jnp.sqrt(totals)
    trust_ratio = norm_pairs[:, 0] / (norm_pairs[:, 1] + EPS_ADAM)
    sample_master = lamb_finish(sample_block, sample_state, trust_ratio[0:3])
    feature_master = lamb_finish(feature_block, feature_state, trust_ratio[3:6])
    mlp_master = lamb_finish(mlp_block, mlp_state, trust_ratio[6:9])
    return (
        layer_out,
        cells_grad,
        sample_shard,
        sample_state[0],
        sample_state[1],
        sample_master,
        sample_master.astype(jnp.bfloat16),
        feature_shard,
        feature_state[0],
        feature_state[1],
        feature_master,
        feature_master.astype(jnp.bfloat16),
        mlp_shard,
        mlp_state[0],
        mlp_state[1],
        mlp_master,
        mlp_master.astype(jnp.bfloat16),
        norm_pairs,
    )


D = 512
MESH = pl.DeviceIdType.MESH
BF = jnp.bfloat16
F32 = jnp.float32
NEG = -1e30


def mult(value, factor):
    return value if isinstance(value, int) else pl.multiple_of(value, factor)


def nt(left, right):
    return lax.dot_general(left, right, (((1,), (1,)), ((), ())), preferred_element_type=F32)


def nn(left, right):
    return lax.dot_general(left, right, (((1,), (0,)), ((), ())), preferred_element_type=F32)


def here():
    return lax.axis_index("task"), lax.axis_index("samp")


def peers(t, s):
    return [(jnp.bitwise_xor(t, e), s) for e in range(1, 8)] + [(t, jnp.bitwise_xor(s, e)) for e in (1, 2, 3)]


def enter(t, s):
    barrier = pltpu.get_barrier_semaphore()
    for peer in peers(t, s):
        pl.semaphore_signal(barrier, inc=1, device_id=peer, device_id_type=MESH)
    return barrier


def send(src, dst, ssem, rsem, peer):
    copy = pltpu.make_async_remote_copy(
        src_ref=src, dst_ref=dst, send_sem=ssem, recv_sem=rsem, device_id=peer, device_id_type=MESH
    )
    copy.start()
    return copy


class Gather:
    def __init__(self, buf, ssem, rsem, t, s):
        self.buf, self.t, self.s = buf, t, s
        half = buf.shape[2] // 2
        self.ha, self.hb, self.all = pl.ds(0, half), pl.ds(half, half), pl.ds(0, 2 * half)
        self.rows = pl.ds(0, buf.shape[1])
        self.ssem, self.rsem = ssem, rsem
        self.moves = []
        self.tx, self.ty = jnp.bitwise_xor(t, 2), jnp.bitwise_xor(t, 4)
        self.txy, self.tc = jnp.bitwise_xor(t, 6), jnp.bitwise_xor(t, 1)
        self.hops, self.sent = {}, {k: {} for k in ("x", "y", "c", "xy", "yx", "cx", "cy")}

    def z(self, key):
        return jnp.bitwise_xor(self.s, key)

    def go(self, slots, cols, peer):
        view = self.buf.at[slots, self.rows, cols]
        i = len(self.moves)
        copy = send(view, view, self.ssem.at[i], self.rsem.at[i], peer)
        self.moves.append(copy)
        return copy

    def pass_on(self, kind, key, t, cols, to):
        self.sent[kind][key] = self.go(pl.ds(4 * t + self.z(key), 1), cols, (to, self.s))

    def spread(self, key):
        self.pass_on("x", key, self.t, self.all, self.tx)
        self.pass_on("y", key, self.t, self.all, self.ty)
        self.pass_on("c", key, self.t, self.all, self.tc)

    def hop(self, key, slot, to):
        self.hops[key] = self.go(pl.ds(4 * self.t + self.z(slot), 1), self.all, (self.t, self.z(to)))

    def start_z(self):
        self.hop(2, 0, 2)
        self.hop(1, 0, 1)

    def zin(self, *keys):
        for key in keys:
            self.hops[key].wait_recv()
            if key == 2:
                self.hop(3, 2, 1)
            self.spread(key)

    def near(self, *keys):
        for key in keys:
            self.sent["x"][key].wait_recv()
            self.pass_on("xy", key, self.tx, self.ha, self.ty)
            self.pass_on("cx", key, self.tx, self.all, self.tc)
            self.sent["y"][key].wait_recv()
            self.pass_on("yx", key, self.ty, self.hb, self.tx)
            self.pass_on("cy", key, self.ty, self.all, self.tc)

    def far(self):
        for kind in ("xy", "yx"):
            for copy in self.sent[kind].values():
                copy.wait_recv()
        self.last = self.go(pl.ds(4 * self.txy, 4), self.all, (self.tc, self.s))

    def end(self):
        for kind in ("c", "cx", "cy"):
            for copy in self.sent[kind].values():
                copy.wait_recv()
        self.last.wait_recv()

    def drain(self):
        for copy in self.moves:
            copy.wait_send()


def realign(m_ref, sh_ref, d, rows, out_ref, out_at, roll_to, split=False):
    whole = 4 * rows
    total = whole + 8
    q, p = d // 8, d % 8
    lane = lax.broadcasted_iota(jnp.int32, (total, 128), 1)
    roll_to[0:8, :] = jnp.zeros((8, 128), F32)
    for i in range(whole // 8):
        sh_ref[8 * i : 8 * i + 8, :] = m_ref[pl.ds(1024 * i, 1024)].reshape(8, 128)
    sh_ref[whole:total, :] = jnp.zeros((8, 128), F32)
    sh_ref[whole : whole + 1, 0:16] = m_ref[pl.ds(128 * whole, 16)].reshape(1, 16)
    rolled = pltpu.roll(sh_ref[0:total, :], 16 * p, 1)
    roll_to[8 : 8 + total, :] = rolled
    sh_ref[0:8, :] = jnp.zeros((8, 128), F32)
    sh_ref[8 : 8 + total, :] = jnp.where(lane < 16 * p, roll_to[7 : 7 + total, :], rolled)
    firsts = []

    def straight():
        for b in range(4):
            cols = slice(128 * b, 128 * b + 128)
            out_ref[out_at, 0:rows, cols] = sh_ref[pl.ds(12 - q + b, rows, stride=4), :].astype(BF)

    def by_piece():
        for b in range(4):
            cols = slice(128 * b, 128 * b + 128)
            for j in range(4):
                piece = sh_ref[pl.ds(12 - q + b + 4 * j, rows // 4, stride=16), :]
                out_ref[out_at, rows // 4 * j : rows // 4 * (j + 1), cols] = piece.astype(BF)

    if split:
        pl.when(d < 16)(by_piece)
        pl.when(d >= 16)(straight)
    else:
        straight()
    for b in range(4):
        firsts.append(sh_ref[pl.ds(8 - q + b, 1), :])
    return jnp.concatenate(firsts, 1)


def spread(buf, firsts, kind, rows, lo, hi, put):
    tail = lax.broadcasted_iota(jnp.int32, (8, D), 0) == 7

    def body(i, _):
        nxt = jnp.minimum(i + 1, 31)
        row = firsts[nxt, :, D * kind : D * kind + D]
        block = buf[i, 0:rows, :].astype(F32)
        last = block[rows - 8 : rows, :] + jnp.where(tail & (i < 31), row, 0.0)
        put(i - lo, block[0 : rows - 8, :], last)
        return 0

    lax.fori_loop(lo, hi, body, 0)


def put_f32(dst, rows):
    def put(i, head, last):
        for b in range(4):
            cols = slice(128 * b, 128 * b + 128)
            dst[b, pl.ds(mult(i * rows, rows), rows - 8), :] = head[:, cols]
            dst[b, pl.ds(mult(i * rows + rows - 8, 8), 8), :] = last[:, cols]

    return put


def put_bf(dst, rows):
    def put(i, head, last):
        dst[pl.ds(mult(i * rows, rows), rows), :] = jnp.concatenate([head, last], 0).astype(BF)

    return put


def split_columns(wide, ways, dst):
    def body(i, _):
        for j in range(ways):
            for b in range(4):
                piece = wide[b, pl.ds(64 * ways * i + j, 64, stride=ways), :]
                dst[j, pl.ds(mult(64 * i, 64), 64), 128 * b : 128 * b + 128] = piece.astype(BF)
        return 0

    lax.fori_loop(0, 8, body, 0)


def halves():
    lane = lax.broadcasted_iota(jnp.int32, (128, 128), 1)
    return lane < 64


def two_heads(x, one, two):
    return jnp.concatenate([x * one, x * two], 0)


def soft(scores, axis):
    e = [jnp.exp(x - jnp.max(x, axis, keepdims=True)) for x in scores]
    return [x * (1.0 / jnp.sum(x, axis, keepdims=True)) for x in e]


def attend_chunk(qkv, c, live, out):
    left = halves()
    one = jnp.where(left, 0.125, 0.0).astype(BF)
    two = jnp.where(left, 0.0, 0.125).astype(BF)
    rows = pl.ds(mult(c * 128, 128), 128)

    def body(h, _):
        cols = [pl.ds(128 * i, 128) for i in range(4)]
        scores = [jnp.where(live, nt(two_heads(qkv[0, rows, w], one, two), qkv[1, :, w]), NEG) for w in cols]
        prob = [p.astype(BF) for p in soft(scores, 1)]
        outs = [nn(p, qkv[2, :, w]) for p, w in zip(prob, cols)]
        for o, w in zip(outs, cols):
            o = jnp.where(left, o[0:128], o[128:256]).astype(BF)
            for g in range(4):
                out[g, :, w] = o[32 * g : 32 * g + 32]
        return 0

    body(0, 0)


def edges(d, entries, width):
    begin = d * entries
    return D - begin, D + D * width - begin


def segment(k, ends):
    return (k >= ends[0]).astype(jnp.int32) + (k >= ends[1]).astype(jnp.int32)


def lamb_step(g, m, f, s):
    fn = 0.5 * f + 0.5 * g
    sn = 0.5 * s + 0.5 * g * g
    return fn, sn, fn / (jnp.sqrt(sn) + 1e-6)


def flat_index():
    rows = lax.broadcasted_iota(jnp.int32, (32, 128), 0)
    return rows * 128 + lax.broadcasted_iota(jnp.int32, (32, 128), 1)


def fold(x):
    return x.reshape(-1, 8, 128).sum(0)


def squares(sh, m, f, s, sums, d, width, b, lo, hi):
    entries = m.shape[0]
    ends = edges(d, entries, width)
    index = flat_index()

    def body(i, acc):
        at = pl.ds(mult(i * 4096, 4096), 4096)
        old = m[at].reshape(32, 128)
        _, _, r = lamb_step(sh[pl.ds(mult(i * 32, 32), 32), :], old, f[at].reshape(32, 128), s[at].reshape(32, 128))
        part = segment(index + i * 4096, ends)
        out = []
        for n, value in enumerate((old * old, r * r)):
            for k in range(3):
                out.append(acc[3 * n + k] + fold(jnp.where(part == k, value, 0.0)))
        return tuple(out)

    acc = lax.fori_loop(lo, hi, body, (jnp.zeros((8, 128), F32),) * 6)
    for n in range(2):
        for k in range(3):
            row = 16 * n + 3 * b + k
            sums[row : row + 1, :] += jnp.sum(acc[3 * n + k], 0, keepdims=True)


def squares_tail(sh, m, f, s, sums, d, width, b):
    entries = m.shape[0]
    base = entries - 16
    ends = edges(d, entries, width)
    at = pl.ds(base, 16)
    old = m[at].reshape(1, 16)
    row = base // 128
    _, _, r = lamb_step(sh[row : row + 1, 0:16], old, f[at].reshape(1, 16), s[at].reshape(1, 16))
    part = segment(lax.broadcasted_iota(jnp.int32, (1, 16), 1) + base, ends)
    for n, value in enumerate((old * old, r * r)):
        for k in range(3):
            row = 16 * n + 3 * b + k
            sums[row : row + 1, 0:16] += jnp.where(part == k, value, 0.0)


def update(sh, m, f, s, grad, fout, sout, mout, wout, ratio, d, width, b):
    entries = m.shape[0]
    whole = entries // 4096
    ends = edges(d, entries, width)
    half = [0.5 * ratio[3 * b + k : 3 * b + k + 1, :] for k in range(3)]

    def put(at, g, part, shape):
        old = m[at].reshape(shape)
        fn, sn, r = lamb_step(g, old, f[at].reshape(shape), s[at].reshape(shape))
        factor = jnp.where(part == 0, half[0], jnp.where(part == 1, half[1], half[2]))
        new = (old - factor * r).reshape(-1)
        grad[at] = g.reshape(-1)
        fout[at] = fn.reshape(-1)
        sout[at] = sn.reshape(-1)
        mout[at] = new
        wout[at] = new.astype(BF)

    index = flat_index()

    def body(i, _):
        at = pl.ds(mult(i * 4096, 4096), 4096)
        put(at, sh[pl.ds(mult(i * 32, 32), 32), :], segment(index + i * 4096, ends), (32, 128))
        return 0

    lax.fori_loop(0, whole, body, 0)
    part = segment(lax.broadcasted_iota(jnp.int32, (1, 16), 1) + whole * 4096, ends)
    put(pl.ds(whole * 4096, 16), sh[32 * whole : 32 * whole + 1, 0:16], part, (1, 16))


def diagonal(rows):
    lane = lax.broadcasted_iota(jnp.int32, (32, 128), 1)
    return lane == lax.broadcasted_iota(jnp.int32, (32, 128), 0)


def sum_all(sums, ts, zs, ssem, rsem, t, s):
    column = jnp.sum(sums[...], 1, keepdims=True)
    ts[t] = jnp.broadcast_to(jnp.sum(jnp.where(diagonal(32), column, 0.0), 0, keepdims=True), (8, 128))
    plane = [
        send(ts.at[t], ts.at[t], ssem.at[e - 1], rsem.at[e - 1], (jnp.bitwise_xor(t, e), s)) for e in range(1, 8)
    ]
    for copy in plane:
        copy.wait_recv()
    zs[s] = ((ts[0] + ts[1]) + (ts[2] + ts[3])) + ((ts[4] + ts[5]) + (ts[6] + ts[7]))
    last = [
        send(zs.at[s], zs.at[s], ssem.at[6 + e], rsem.at[6 + e], (t, jnp.bitwise_xor(s, e))) for e in (1, 2, 3)
    ]
    for copy in last:
        copy.wait_recv()
    return (zs[0] + zs[1]) + (zs[2] + zs[3]), plane + last


def by_sample(x, out):
    for g in range(4):
        out[32 * g : 32 * g + 32, :, :] = jnp.transpose(x[g].astype(F32), (1, 0, 2)).astype(out.dtype)


def kernel_e(
    total, sh1, sh2, sh3, m1, f1, s1, m2, f2, s2, m3, f3, s3, lout, cgrad,
    g1, fo1, so1, mo1, wo1, g2, fo2, so2, mo2, wo2, g3, fo3, so3, mo3, wo3, pairs, layer, grad,
):
    t, s = here()
    d = 4 * t + s
    norms = jnp.sqrt(total[0:1, :])
    pairs[0:1, :] = norms[:, 0:9]
    pairs[1:2, :] = pltpu.roll(norms, 112, 1)[:, 0:9]
    norm = jnp.sum(jnp.where(diagonal(32), norms, 0.0), 1, keepdims=True)
    ratio = norm[0:9] / (norm[16:25] + 1e-6)
    by_sample(lout, layer)
    by_sample(cgrad, grad)
    update(sh1, m1, f1, s1, g1, fo1, so1, mo1, wo1, ratio, d, 3 * D, 0)
    update(sh2, m2, f2, s2, g2, fo2, so2, mo2, wo2, ratio, d, 3 * D, 1)
    update(sh3, m3, f3, s3, g3, fo3, so3, mo3, wo3, ratio, d, 4 * D, 2)


def call_e(total, shards, args, lout, cgrad):
    sds = jax.ShapeDtypeStruct
    vm = pl.BlockSpec(memory_space=pltpu.VMEM)
    shapes = []
    for m in args[0::3]:
        n = m.shape
        shapes += [sds(n, F32)] * 4 + [sds(n, BF)]
    return pl.pallas_call(
        kernel_e,
        name="kernel_e",
        out_shape=(*shapes, sds((2, 9), F32), sds((128, 4, D), BF), sds((128, 4, D), F32)),
        in_specs=[vm] * 15,
        out_specs=(vm,) * 18,
        compiler_params=pltpu.CompilerParams(vmem_limit_bytes=63 << 20),
    )(total, *shards, *args, lout, cgrad)


def backward_heads(h, qkv, do, live, dqkv, kt, dkv):
    left = halves()
    one, two = jnp.where(left, 1.0, 0.0).astype(BF), jnp.where(left, 0.0, 1.0).astype(BF)
    cols = pl.ds(mult(h * 128, 128), 128)
    kt[...] = jnp.transpose(qkv[1, :, cols])
    top_lane = lax.broadcasted_iota(jnp.int32, (128, 128), 0) < 64

    def chunk(n, _):
        each = [0, 1, 2, 3]
        rows = [pl.ds(c * 128, 128) for c in each]
        qm = [two_heads(qkv[0, r, cols] * jnp.asarray(0.125, BF), one, two) for r in rows]
        gm = [two_heads(do[c, :, :, cols].reshape(128, 128), one, two) for c in each]
        prob = soft([jnp.where(live, nt(qkv[1, :, cols], q), NEG) for q in qm], 0)
        pg = [nt(qkv[2, :, cols], g) for g in gm]
        sg = [(p * (x - jnp.sum(p * x, 0, keepdims=True))).astype(BF) for p, x in zip(prob, pg)]
        dqkv[1, :, cols] = (nn(sg[0], qm[0]) + nn(sg[1], qm[1]) + nn(sg[2], qm[2]) + nn(sg[3], qm[3])).astype(BF)
        pb = [p.astype(BF) for p in prob]
        dqkv[2, :, cols] = (nn(pb[0], gm[0]) + nn(pb[1], gm[1]) + nn(pb[2], gm[2]) + nn(pb[3], gm[3])).astype(BF)
        for r, x in zip(rows, sg):
            dqt = nn(kt[...], x)
            dq = jnp.transpose(jnp.where(top_lane, dqt[:, 0:128], dqt[:, 128:256])) * 0.125
            dqkv[0, r, cols] = dq.astype(BF)
        return 0

    chunk(0, 0)


def turn(x):
    return jnp.transpose(x)


def stats(h):
    x = h - jnp.mean(h, 1, keepdims=True)
    rstd = lax.rsqrt(jnp.mean(x * x, 1, keepdims=True) + 1e-5)
    return x * rstd, rstd


def norm_grad(h, da, gain):
    x, rstd = stats(h)
    dgain = jnp.sum(da * x, 0, keepdims=True)
    dx = da * gain
    dh = rstd * (dx - jnp.mean(dx, 1, keepdims=True) - x * jnp.mean(dx * x, 1, keepdims=True))
    return dh, dgain


def block(g):
    return pl.ds(mult(g * 128, 128), 128)


def feature_mask(fcnt, axis):
    shape = (256, 128) if axis else (128, 256)
    query = lax.broadcasted_iota(jnp.int32, shape, 1 - axis)
    key = lax.broadcasted_iota(jnp.int32, shape, axis)
    return (query % 32 == key % 32) & (key // 32 < fcnt)


def feature_forward(qkv, o2, fcnt):
    left = halves()
    one = jnp.where(left, 0.125, 0.0).astype(BF)
    two = jnp.where(left, 0.0, 0.125).astype(BF)
    ok = feature_mask(fcnt, 1)
    cols = [slice(128 * h, 128 * h + 128) for h in range(4)]

    def body(n, _):
        rows = block(n)
        scores = [
            jnp.where(ok, nt(two_heads(qkv[0, rows, c], one, two), qkv[1, rows, c]), NEG) for c in cols
        ]
        prob = [p.astype(BF) for p in soft(scores, 1)]
        out = [nn(p, qkv[2, rows, c]) for p, c in zip(prob, cols)]
        for o, c in zip(out, cols):
            o2[rows, c] = jnp.where(left, o[0:128], o[128:256]).astype(BF)
        return 0

    lax.fori_loop(0, 4, body, 0)


def feature_backward(qkv, do, dqkv, fcnt):
    left = halves()
    one, two = jnp.where(left, 1.0, 0.0).astype(BF), jnp.where(left, 0.0, 1.0).astype(BF)
    ok = feature_mask(fcnt, 0)
    top_lane = lax.broadcasted_iota(jnp.int32, (128, 128), 0) < 64
    cols = [slice(128 * h, 128 * h + 128) for h in range(4)]

    def body(n, _):
        rows = block(n)
        qm = [two_heads(qkv[0, rows, c] * jnp.asarray(0.125, BF), one, two) for c in cols]
        gm = [two_heads(do[rows, c], one, two) for c in cols]
        prob = soft([jnp.where(ok, nt(qkv[1, rows, c], q), NEG) for c, q in zip(cols, qm)], 0)
        pg = [nt(qkv[2, rows, c], g) for c, g in zip(cols, gm)]
        sg = [(p * (x - jnp.sum(p * x, 0, keepdims=True))).astype(BF) for p, x in zip(prob, pg)]
        dqt = [nn(turn(qkv[1, rows, c]), x) for c, x in zip(cols, sg)]
        dk = [nn(x, q).astype(BF) for x, q in zip(sg, qm)]
        dv = [nn(p.astype(BF), g).astype(BF) for p, g in zip(prob, gm)]
        dq = [turn(jnp.where(top_lane, x[:, 0:128], x[:, 128:256])) * 0.125 for x in dqt]
        for i, c in enumerate(cols):
            dqkv[0, rows, c] = dq[i].astype(BF)
            dqkv[1, rows, c] = dk[i]
            dqkv[2, rows, c] = dv[i]
        return 0

    lax.fori_loop(0, 4, body, 0)


def four_blocks(body, init=0):
    for r in range(4):
        init = body(r, init)
    return init


def flat(x):
    return x.reshape(128, D)


def cube(x):
    return x.reshape(4, 32, D)


def narrow_to(wide, part, slots, rows):
    def body(i, _):
        at = pl.ds(mult(i * rows, rows), rows)
        for b in range(4):
            part[i, :, 128 * b : 128 * b + 128] = wide[b, at, :].astype(BF)
        return 0

    lax.fori_loop(0, slots, body, 0)


def store_wide(wide, j, ways, value):
    for b in range(4):
        wide[b, pl.ds(j, value.shape[0], stride=ways), :] = value[:, 128 * b : 128 * b + 128]


def mlp(a3, a3t, g, h2, wup, wdn, h3, da, zb, dub, u, dz, p3):
    h3[...] = h2[...]
    da[...] = jnp.zeros((512, D), F32)

    def body(j, _):
        u[...] = nn(a3[...], wup[j])
        dz[...] = nt(g[...], wdn[j]).astype(BF)

        def act(r, _):
            rows = pl.ds(mult(r * 64, 64), 64)
            x = u[rows, :]
            cdf = 0.5 * (1.0 + lax.erf(x * 0.7071067811865476))
            zb[rows, :] = (x * cdf).astype(BF)
            slope = cdf + x * (0.3989422804014327 * jnp.exp(-0.5 * x * x))
            dub[rows, :] = (slope * dz[rows, :].astype(F32)).astype(BF)
            return 0

        lax.fori_loop(0, 8, act, 0)
        h3[...] += nn(zb[...], wdn[j])
        da[...] += nt(dub[...], wup[j])
        up = nn(a3t[...], dub[...]).astype(BF)
        for i in range(16):
            p3[i, pl.ds(mult(32 * j, 32), 32), :] = up[32 * i : 32 * i + 32]
        dw = nn(turn(zb[...]), g[...]).astype(BF)
        for i in range(4):
            p3[16 + 4 * j + i] = dw[128 * i : 128 * i + 128]
        return 0

    lax.fori_loop(0, 4, body, 0)


def middle_forward(s, cells, top, o1, wo1, w2, wo2, gains, scnt, fcnt, h1, h2, a2, qkv, o2, a3, g, hook):
    gain2, gain3 = gains[1:2, :], gains[2:3, :]
    h1[...] = nn(o1[...].reshape(512, D), wo1[...])

    def first(r, _):
        rows = block(r)
        h = h1[rows, :] + flat(cells[r].astype(F32))
        h1[rows, :] = h
        x, _ = stats(h)
        a2[rows, :] = (x * gain2).astype(BF)
        n = lax.broadcasted_iota(jnp.int32, (128, 1), 0)
        live = (n // 32 < fcnt) & (128 * s + 32 * r + n % 32 < scnt)
        g[rows, :] = jnp.where(live, flat(top[r].astype(F32)), 0.0).astype(BF)
        return 0

    four_blocks(first)

    def project(j, _):
        qkv[j] = nn(a2[...], w2[j]).astype(BF)
        return 0

    lax.fori_loop(0, 3, project, 0)
    hook()
    feature_forward(qkv, o2, fcnt)
    h2[...] = h1[...] + nn(o2[...], wo2[...])

    def second(r, _):
        rows = block(r)
        x, _ = stats(h2[rows, :])
        a3[rows, :] = (x * gain3).astype(BF)
        return 0

    four_blocks(second)


def layer_output(s, h3, lout, scnt, fcnt):
    def last(r, _):
        n = lax.broadcasted_iota(jnp.int32, (128, 1), 0)
        live = (n // 32 < fcnt) & (128 * s + 32 * r + n % 32 < scnt)
        lout[r] = cube(jnp.where(live, h3[block(r), :], 0.0).astype(BF))
        return 0

    four_blocks(last)


def feature_grads(wo1, w2, wo2, gains, fcnt, h1, h2, qkv, g, da, b2, b1, do, dqkv, do1, gr, dgain):
    gain2, gain3 = gains[1:2, :], gains[2:3, :]

    def third(r, dg):
        rows = block(r)
        dh, part = norm_grad(h2[rows, :], da[rows, :], gain3)
        total = g[rows, :].astype(F32) + dh
        gr[r] = cube(total)
        b2[rows, :] = total.astype(BF)
        return dg + part

    dg3 = four_blocks(third, jnp.zeros((1, D), F32))
    do[...] = nt(b2[...], wo2[...]).astype(BF)
    feature_backward(qkv, do, dqkv, fcnt)
    da[...] = nt(dqkv[0], w2[0]) + nt(dqkv[1], w2[1]) + nt(dqkv[2], w2[2])

    def fourth(r, dg):
        rows = block(r)
        dh, part = norm_grad(h1[rows, :], da[rows, :], gain2)
        total = flat(gr[r]) + dh
        gr[r] = cube(total)
        b1[rows, :] = total.astype(BF)
        return dg + part

    dg2 = four_blocks(fourth, jnp.zeros((1, D), F32))
    do1[...] = nt(b1[...], wo1[...]).astype(BF).reshape(4, 4, 32, D)
    n = lax.broadcasted_iota(jnp.int32, (8, D), 0)
    dgain[...] = jnp.where(n == 1, dg2, jnp.where(n == 2, dg3, 0.0))


def feature_weights(o1, a2, o2, b2, b1, dqkv, wide, p2, dwo1):
    def weights(j, _):
        store_wide(wide, j, 3, nn(turn(a2[...]), dqkv[j]))
        return 0

    lax.fori_loop(0, 3, weights, 0)
    narrow_to(wide, p2, 24, 64)
    dw = nn(turn(o2[...]), b2[...]).astype(BF)
    for i in range(8):
        p2[24 + i] = dw[64 * i : 64 * i + 64]
    dwo1[...] = nn(turn(o1[...].reshape(512, D)), b1[...]).astype(BF)


class Reduce:
    def __init__(self, part, r1, ry, rx, ry2, rx2, rz, ssem, rsem, t, s, chunk=None):
        self.part, self.r1 = part, r1
        self.ry, self.rx, self.ry2, self.rx2, self.rz = ry, rx, ry2, rx2, rz
        rows, half = part.shape[1], part.shape[2] // 2
        if chunk is None:
            every = pl.ds(0, rows)
            self.ha, self.hb, self.all = [(every, pl.ds(o, n)) for o, n in ((0, half), (half, half), (0, 2 * half))]
        else:
            cols, half = pl.ds(128 * chunk, 128), rows // 2
            self.ha, self.hb, self.all = [(pl.ds(o, n), cols) for o, n in ((0, half), (half, half), (0, rows))]
        self.ssem, self.rsem, self.t, self.s = ssem, rsem, t, s
        self.copies = []

    def go(self, src, dst, peer):
        i = len(self.copies)
        copy = send(src, dst, self.ssem.at[i], self.rsem.at[i], peer)
        self.copies.append(copy)
        return copy

    def xor(self, e):
        return jnp.bitwise_xor(self.t, e)

    def group(self, e, box, t=None):
        t = self.t if t is None else t
        return self.part.at[pl.ds(4 * jnp.bitwise_xor(t, 2 * e), 4), *box]

    def core(self):
        tc = self.xor(1)
        self.c = [
            self.go(self.group(e, self.all, tc), self.r1.at[e], (tc, self.s))
            for e in (2, 3, 1, 0)
        ]

    def add(self, e, box, got):
        base = 4 * self.xor(2 * e)
        for j in range(4):
            own = self.part[base + j, *box].astype(F32)
            self.part[base + j, *box] = (own + got[j].astype(F32)).astype(self.part.dtype)

    def one(self):
        ty, tx, s = self.xor(4), self.xor(2), self.s
        self.y, self.x = {}, {}
        for n, e in enumerate((2, 3, 1, 0)):
            self.c[n].wait_recv()
            self.add(e, self.all, self.r1.at[e])
            if e in (2, 3):
                self.y[e - 2] = self.go(self.group(e, self.ha), self.ry.at[e - 2], (ty, s))
            if e in (3, 1):
                self.x[e // 2] = self.go(self.group(e, self.hb), self.rx.at[e // 2], (tx, s))

    def two(self):
        ty, tx, s = self.xor(4), self.xor(2), self.s
        self.y[1].wait_recv()
        self.add(1, self.ha, self.ry.at[1])
        self.x2 = self.go(self.group(1, self.ha), self.rx2, (tx, s))
        self.x[1].wait_recv()
        self.add(2, self.hb, self.rx.at[1])
        self.y2 = self.go(self.group(2, self.hb), self.ry2, (ty, s))
        self.y[0].wait_recv()
        self.add(0, self.ha, self.ry.at[0])
        self.x[0].wait_recv()
        self.add(0, self.hb, self.rx.at[0])

    def three(self):
        self.x2.wait_recv()
        self.add(0, self.ha, self.rx2)
        self.y2.wait_recv()
        self.add(0, self.hb, self.ry2)
        self.z = [self.z_send(1, 0), self.z_send(3, 1)]

    def z_send(self, slot, into):
        t, s = self.t, self.s
        to = jnp.bitwise_xor(s, 2 if into == 2 else 1)
        return self.go(self.part.at[4 * t + jnp.bitwise_xor(s, slot), *self.all], self.rz.at[into], (t, to))

    def four(self):
        self.z[1].wait_recv()
        mine = 4 * self.t + jnp.bitwise_xor(self.s, 2)
        own = self.part[mine, *self.all].astype(F32)
        self.part[mine, *self.all] = (own + self.rz[1, :, :].astype(F32)).astype(self.part.dtype)
        self.z.append(self.z_send(2, 2))

    def result(self):
        self.z[0].wait_recv()
        self.z[2].wait_recv()
        own = self.part[4 * self.t + self.s, *self.all].astype(F32)
        return own + self.rz[0, :, :].astype(F32) + self.rz[2, :, :].astype(F32)

    def drain(self):
        for copy in self.copies:
            copy.wait_send()


def edge_rows(part, edges, kind, lo=0, size=D):
    rows = part.shape[1]

    def body(i, _):
        row = part[i - 1, rows - 16 : rows, lo : lo + size].astype(F32)[15:16, :]
        edges[i, :, D * kind + lo : D * kind + lo + size] = row
        return 0

    lax.fori_loop(1, 32, body, 0)


def by_feature(x, out):
    for g in range(4):
        out[g] = jnp.transpose(x[32 * g : 32 * g + 32, :, :].astype(F32), (1, 0, 2)).astype(BF)


def to_rows(main, fl):
    rows = main.shape[0]
    for b in range(4):
        fl[pl.ds(4 + b, rows, stride=4), :] = main[:, 128 * b : 128 * b + 128]


def first_row(row, fl):
    for b in range(4):
        fl[b : b + 1, :] = row[:, 128 * b : 128 * b + 128]


def shifted(fl, d, total):
    q, p = d // 8, d % 8
    back = (128 - 16 * p) % 128
    lane = lax.broadcasted_iota(jnp.int32, (total, 128), 1)
    low = pltpu.roll(fl[pl.ds(q, total), :], back, 1)
    high = pltpu.roll(fl[pl.ds(q + 1, total), :], back, 1)
    return jnp.where(lane < 128 - 16 * p, low, high)


def to_shard(fl, rows, d, out_ref):
    total = out_ref.shape[0]
    fl[4 + 4 * rows : total + 8, :] = jnp.zeros((total + 4 - 4 * rows, 128), F32)
    out_ref[...] = shifted(fl, d, total)


def top_shard(fl, d, out_ref):
    out_ref[0:8, :] = shifted(fl, d, 8)


class Refs:
    def __init__(self, names, refs):
        for name, ref in zip(names, refs, strict=True):
            setattr(self, name, ref)


def reduce_names(n):
    return [k + n for k in ("r1", "ry", "rx", "ry2", "rx2", "rz")]


def reduce_scratch(rows, width=D, kind=BF):
    half = width // 2
    return [
        pltpu.VMEM((4, 4, rows, width), kind), pltpu.VMEM((2, 4, rows, half), kind),
        pltpu.VMEM((2, 4, rows, half), kind), pltpu.VMEM((4, rows, half), kind), pltpu.VMEM((4, rows, half), kind),
        pltpu.VMEM((3, rows, width), kind),
    ]


def chunk_scratch(rows):
    half = rows // 2
    shapes = [(4, 4, rows), (2, 4, half), (2, 4, half), (4, half), (4, half), (3, rows)]
    return [pltpu.VMEM((*shape, 128), BF) for shape in shapes]


PARAMS = ["m1", "f1", "s1", "m2", "f2", "s2", "m3", "f3", "s3"]
WIDE = pltpu.VMEM((D, D), F32)
NARROW = pltpu.VMEM((D, D), BF)
THREE = pltpu.VMEM((3, D, D), BF)
FOUR = pltpu.VMEM((4, D, D), BF)
TILE = pltpu.VMEM((4, 4, 32, D), BF)
DMA = pltpu.SemaphoreType.DMA
SCRATCH = {
    "g1": pltpu.VMEM((32, 64, D), BF), "ge": pltpu.VMEM((32, 1, 3 * D), F32), "g2": pltpu.VMEM((32, 64, D), BF), "g3": pltpu.VMEM((32, 128, D), BF),
    "wide": pltpu.VMEM((4, 4 * D, 128), F32), "sh": pltpu.VMEM((536, 128), F32), "ro": pltpu.VMEM((536, 128), F32),
    "w1": THREE, "wo1": NARROW, "w2": THREE, "wo2": NARROW, "wup": FOUR, "wdn": FOUR,
    "gains": pltpu.VMEM((8, D), F32), "dgain": pltpu.VMEM((8, D), F32),
    "cells": TILE, "top": TILE, "cf": TILE, "a1": NARROW, "qkv1": THREE, "o1c": pltpu.VMEM((3, 4, 32, D), BF), "o1": TILE,
    "h1": WIDE, "h2": WIDE, "a2": NARROW, "qkv2": THREE, "o2": NARROW, "a3": NARROW, "at": NARROW, "g": NARROW,
    "h3": WIDE, "da": WIDE, "zb": NARROW, "dub": NARROW, "u": WIDE, "dz": NARROW, "b": NARROW, "b1": NARROW, "do2": NARROW,
    "dqkv": THREE, "gr": pltpu.VMEM((4, 4, 32, D), F32), "do1": TILE, "do": TILE, "dwo1": NARROW,
    "kt": pltpu.VMEM((128, D), BF), "dkv": pltpu.VMEM((2, D, 128), F32), "dhs": TILE, "dhr": TILE,
    **{k: v for h in range(4) for k, v in zip(reduce_names(f"a{h}"), chunk_scratch(64))},
    **dict(zip(reduce_names("b"), reduce_scratch(64))),
    **dict(zip(reduce_names("c"), reduce_scratch(128))),
    **dict(zip(reduce_names("d"), reduce_scratch(1, 3 * D, F32))),
    "fl1": pltpu.VMEM((272, 128), F32), "fl2": pltpu.VMEM((272, 128), F32), "fl3": pltpu.VMEM((528, 128), F32),
    "sums": pltpu.VMEM((32, 128), F32), "ts": pltpu.VMEM((8, 8, 128), F32), "zs": pltpu.VMEM((4, 8, 128), F32),
    "gs": DMA((4, 32)), "gq": DMA((4, 32)), "rs": DMA((7, 16)), "rq": DMA((7, 16)),
    "as1": DMA((3,)), "aq1": DMA((3,)), "as2": DMA((3,)), "aq2": DMA((3,)),
    "as3": DMA((3,)), "aq3": DMA((3,)), "as4": DMA((3,)), "aq4": DMA((3,)), "ns": DMA((10,)), "nq": DMA((10,)),
}
INPUTS = ["scnt", "fcnt", "cells_in", "top_in"] + PARAMS
OUTPUTS = ["lout", "cgrad", "sh1", "sh2", "sh3", "total"]


def kernel_m(*refs):
    r = Refs(INPUTS + OUTPUTS + list(SCRATCH), refs)
    t, s = here()
    d = 4 * t + s
    scnt, fcnt = r.scnt[0], r.fcnt[0]
    barrier = enter(t, s)
    ga, gb, gc, ge = [
        Gather(buf, r.gs.at[i], r.gq.at[i], t, s) for i, buf in enumerate((r.g1, r.g2, r.g3, r.ge))
    ]
    first1 = realign(r.m1, r.sh, d, 64, r.g1, d, r.ro)
    first2 = realign(r.m2, r.sh, d, 64, r.g2, d, r.ro)
    first3 = realign(r.m3, r.sh, d, 128, r.g3, d, r.ro, True)
    r.ge[d] = jnp.concatenate([first1, first2, first3], 1).astype(BF).astype(F32)
    pl.semaphore_wait(barrier, 10)
    for one in (ge, ga, gb, gc):
        one.start_z()
        one.spread(0)
    by_feature(r.cells_in, r.cells)
    r.cf[s] = r.cells[:, s, :, :]
    for one in (ge, ga):
        one.near(0)
        one.zin(2, 1)
    for one in (ge, ga):
        one.near(2, 1)
        one.zin(3)
    moves = [
        send(r.cells.at[:, (s + k) % 4], r.cf.at[s], r.as1.at[k - 1], r.aq1.at[k - 1], (t, (s + k) % 4))
        for k in (1, 2, 3)
    ]
    for one in (ge, ga):
        one.near(3)
    by_feature(r.top_in, r.top)
    for one in (ge, ga):
        one.far()
    for one in (gb, gc):
        one.near(0)
        one.zin(2)
    gb.zin(1)
    for copy in moves:
        copy.wait_recv()
    ge.end()
    ga.end()
    gb.near(2)
    gb.zin(3)
    gc.zin(1)
    gb.near(1)
    spread(r.g1, r.ge, 0, 64, 0, 24, put_f32(r.wide, 64))
    split_columns(r.wide, 3, r.w1)
    spread(r.g1, r.ge, 0, 64, 24, 32, put_bf(r.wo1, 64))
    for k in range(3):
        r.gains[k : k + 1, :] = r.ge[0, :, D * k : D * k + D]
    gain1 = r.gains[0:1, :]

    def norm(i, _):
        x, _ = stats(r.cf[i].astype(F32).reshape(128, D))
        r.a1[block(i), :] = (x * gain1).astype(BF)
        return 0

    four_blocks(norm)

    def project(j, _):
        r.qkv1[j] = nn(r.a1[...], r.w1[j]).astype(BF)
        return 0

    lax.fori_loop(0, 3, project, 0)
    live = lax.broadcasted_iota(jnp.int32, (1, 512), 1) < scnt
    backs = []
    gb.near(3)
    gc.near(2)
    gc.zin(3)
    for k in (2, 1, 3, 0):
        c = (s + k) % 4
        if k:
            attend_chunk(r.qkv1, c, live, r.o1c.at[k - 1])
            backs.append(send(r.o1c.at[k - 1], r.o1.at[:, s], r.as2.at[k - 1], r.aq2.at[k - 1], (t, c)))
        else:
            attend_chunk(r.qkv1, c, live, r.o1.at[:, s])
        if k == 1:
            gb.far()
            gc.near(1)
    gb.end()
    spread(r.g2, r.ge, 1, 64, 0, 24, put_f32(r.wide, 64))
    split_columns(r.wide, 3, r.w2)
    spread(r.g2, r.ge, 1, 64, 24, 32, put_bf(r.wo2, 64))
    gc.near(3)
    for copy in backs:
        copy.wait_recv()
    middle_forward(
        s, r.cells, r.top, r.o1, r.wo1, r.w2, r.wo2, r.gains, scnt, fcnt, r.h1, r.h2, r.a2, r.qkv2, r.o2, r.a3, r.g,
        gc.far,
    )
    r.at[...] = turn(r.a3[...])
    gc.end()

    def put_up(i, head, last):
        block = jnp.concatenate([head, last], 0).astype(BF)
        for j in range(4):
            r.wup[j, pl.ds(mult(i * 32, 32), 32), :] = block[32 * j : 32 * j + 32]

    spread(r.g3, r.ge, 2, 128, 0, 16, put_up)

    def put_down(i, head, last):
        r.wdn[i // 4, pl.ds(mult((i % 4) * 128, 128), 128), :] = jnp.concatenate([head, last], 0).astype(BF)

    spread(r.g3, r.ge, 2, 128, 16, 32, put_down)
    for one in (ga, gb, gc, ge):
        one.drain()
    mlp(r.a3, r.at, r.g, r.h2, r.wup, r.wdn, r.h3, r.da, r.zb, r.dub, r.u, r.dz, r.g3)
    edge_rows(r.g3, r.ge, 2)

    def reducer(n, part, i, chunk=None):
        bufs = [getattr(r, k) for k in reduce_names(n)]
        return Reduce(part, *bufs, r.rs.at[i], r.rq.at[i], t, s, chunk)

    sb, sc, sd = reducer("b", r.g2, 0), reducer("c", r.g3, 1), reducer("d", r.ge, 2)
    sa = [reducer(f"a{h}", r.g1, 3 + h, h) for h in range(4)]
    sc.core()
    layer_output(s, r.h3, r.lout, scnt, fcnt)
    feature_grads(
        r.wo1, r.w2, r.wo2, r.gains, fcnt, r.h1, r.h2, r.qkv2, r.g, r.da, r.b, r.b1, r.do2, r.dqkv, r.do1, r.gr,
        r.dgain,
    )
    moves2 = [
        send(r.do1.at[:, (s + k) % 4], r.do.at[s], r.as3.at[k - 1], r.aq3.at[k - 1], (t, (s + k) % 4))
        for k in (1, 2, 3)
    ]
    sc.one()
    feature_weights(r.o1, r.a2, r.o2, r.b, r.b1, r.dqkv, r.wide, r.g2, r.dwo1)
    edge_rows(r.g2, r.ge, 1)
    r.do[s] = r.do1[:, s, :, :]
    sb.core()
    r.at[...] = turn(r.a1[...])
    for copy in moves2:
        copy.wait_recv()
    live = lax.broadcasted_iota(jnp.int32, (512, 1), 0) < scnt

    def copy_out(i, _):
        r.g1[24 + i] = r.dwo1[pl.ds(mult(i * 64, 64), 64), :]
        return 0

    lax.fori_loop(0, 8, copy_out, 0)

    def heads(h):
        backward_heads(h, r.qkv1, r.do, live, r.dqkv, r.kt, r.dkv)
        cols = slice(128 * h, 128 * h + 128)
        for j in range(3):
            r.wide[h, pl.ds(j, D, stride=3), :] = nn(r.at[...], r.dqkv[j, :, cols])

        def narrow(i, _):
            r.g1[i, :, cols] = r.wide[h, pl.ds(mult(i * 64, 64), 64), :].astype(BF)
            return 0

        lax.fori_loop(0, 24, narrow, 0)
        edge_rows(r.g1, r.ge, 0, 128 * h, 128)
        sa[h].core()

    heads(0)
    sc.two()
    sb.one()
    heads(1)
    sa[0].one()
    heads(2)
    sc.three()
    sa[1].one()
    sa[0].two()
    heads(3)
    r.da[...] = nt(r.dqkv[0], r.w1[0]) + nt(r.dqkv[1], r.w1[1]) + nt(r.dqkv[2], r.w1[2])
    sb.two()
    sa[2].one()
    sa[1].two()

    def norm_back(i, dg):
        dh, part = norm_grad(r.cf[i].astype(F32).reshape(128, D), r.da[block(i), :], gain1)
        r.dhs[i] = dh.astype(BF).reshape(4, 32, D)
        return dg + part

    dg = four_blocks(norm_back, jnp.zeros((1, D), F32))
    r.ge[0] = jnp.concatenate([dg, r.dgain[1:2, :], r.dgain[2:3, :]], 1)
    sd.core()
    sa[3].one()
    sc.four()
    sb.three()
    sa[0].three()
    sa[2].two()
    sa[1].three()
    sd.one()
    sa[0].four()
    sa[3].two()
    sa[2].three()
    sa[1].four()
    sd.two()
    sb.four()
    sa[3].three()
    sa[2].four()
    sd.three()
    homes = [
        send(r.dhs.at[(s + k) % 4], r.dhr.at[:, s], r.as4.at[k - 1], r.aq4.at[k - 1], (t, (s + k) % 4))
        for k in (1, 2, 3)
    ]
    r.sums[...] = jnp.zeros((32, 128), F32)
    for fl in (r.fl2, r.fl3):
        fl[0:4, :] = jnp.zeros((4, 128), F32)
    main = sc.result()

    @pl.when(d < 16)
    def _():
        for j in range(4):
            for b in range(4):
                piece = main[32 * j : 32 * j + 32, 128 * b : 128 * b + 128]
                r.fl3[pl.ds(4 + b + 4 * j, 32, stride=16), :] = piece

    @pl.when(d >= 16)
    def _():
        to_rows(main, r.fl3)

    to_shard(r.fl3, 128, d, r.sh3)
    squares(r.sh3, r.m3, r.f3, r.s3, r.sums, d, 4 * D, 2, 1, 16)
    squares_tail(r.sh3, r.m3, r.f3, r.s3, r.sums, d, 4 * D, 2)
    sa[3].four()
    sd.four()
    to_rows(sb.result(), r.fl2)
    to_shard(r.fl2, 64, d, r.sh2)
    squares(r.sh2, r.m2, r.f2, r.s2, r.sums, d, 3 * D, 1, 1, 8)
    squares_tail(r.sh2, r.m2, r.f2, r.s2, r.sums, d, 3 * D, 1)
    for h in range(4):
        r.fl1[pl.ds(4 + h, 64, stride=4), :] = sa[h].result()
    first = sd.result()
    for k, fl in enumerate((r.fl1, r.fl2, r.fl3)):
        first_row(first[:, D * k : D * k + D], fl)
    to_shard(r.fl1, 64, d, r.sh1)
    top_shard(r.fl2, d, r.sh2)
    top_shard(r.fl3, d, r.sh3)
    squares(r.sh1, r.m1, r.f1, r.s1, r.sums, d, 3 * D, 0, 0, 8)
    squares_tail(r.sh1, r.m1, r.f1, r.s1, r.sums, d, 3 * D, 0)
    squares(r.sh2, r.m2, r.f2, r.s2, r.sums, d, 3 * D, 1, 0, 1)
    squares(r.sh3, r.m3, r.f3, r.s3, r.sums, d, 4 * D, 2, 0, 1)

    def finish_input():
        r.cgrad[:, s, :, :] = r.gr[:, s, :, :] + r.dhs[s].astype(F32)
        for k in (1, 2, 3):
            homes[k - 1].wait_recv()
            f = (s + 4 - k) % 4
            r.cgrad[:, f, :, :] = r.gr[:, f, :, :] + r.dhr[:, f, :, :].astype(F32)

    r.total[...], adds = sum_all(r.sums, r.ts, r.zs, r.ns, r.nq, t, s)
    finish_input()
    for one in (*sa, sb, sc, sd):
        one.drain()
    for copy in moves + backs + moves2 + homes + adds:
        copy.wait_send()


def call_m(scnt, fcnt, cells, top, params, name="kernel_m"):
    sds = jax.ShapeDtypeStruct
    vm = pl.BlockSpec(memory_space=pltpu.VMEM)
    sm = pl.BlockSpec(memory_space=pltpu.SMEM)
    return pl.pallas_call(
        kernel_m,
        name=name,
        out_shape=(
            sds((4, 4, 32, D), BF), sds((4, 4, 32, D), F32), sds((264, 128), F32), sds((264, 128), F32),
            sds((520, 128), F32), sds((8, 128), F32),
        ),
        in_specs=[sm, sm] + [vm] * 11,
        out_specs=(vm,) * 6,
        scratch_shapes=list(SCRATCH.values()),
        compiler_params=pltpu.CompilerParams(collective_id=1, has_side_effects=True, vmem_limit_bytes=63 << 20),
    )(scnt, fcnt, cells, top, *params)


def fast_device(cells, out_grad, scnt, fcnt, b1, f1, s1, b2, f2, s2, b3, f3, s3):
    params = (b1, f1, s1, b2, f2, s2, b3, f3, s3)
    out, cgrad, sh1, sh2, sh3, total = call_m(scnt, fcnt, cells[0], out_grad[0], params)
    *outs, pairs, out, cgrad = call_e(total, (sh1, sh2, sh3), params, out, cgrad)
    return (out[None], cgrad[None], *outs, pairs.T)


def step(*args):
    cells = args[0]
    fits = lax.axis_size("task") == 8 and lax.axis_size("samp") == 4 and cells.shape == (1, 128, 4, D)
    return fast_device(*args) if fits else on_device(*args)


def solution(mesh):
    placed = (
        P("task", "samp", None, None),
        P("task", "samp", None, None),
        P("task"),
        P("task"),
        P(("task", "samp")),
        P(("task", "samp")),
        P(("task", "samp")),
        P(("task", "samp")),
        P(("task", "samp")),
        P(("task", "samp")),
        P(("task", "samp")),
        P(("task", "samp")),
        P(("task", "samp")),
    )
    return jax.shard_map(
        step,
        mesh=mesh,
        in_specs=placed,
        out_specs=(
            P("task", "samp", None, None),
            P("task", "samp", None, None),
            P(("task", "samp")),
            P(("task", "samp")),
            P(("task", "samp")),
            P(("task", "samp")),
            P(("task", "samp")),
            P(("task", "samp")),
            P(("task", "samp")),
            P(("task", "samp")),
            P(("task", "samp")),
            P(("task", "samp")),
            P(("task", "samp")),
            P(("task", "samp")),
            P(("task", "samp")),
            P(("task", "samp")),
            P(("task", "samp")),
            P(),
        ),
        check_vma=False,
    )
```

```python
import jax
import jax.numpy as jnp
from jax import lax
from jax.experimental import pallas as pl
from jax.experimental.pallas import tpu as pltpu
from jax.sharding import PartitionSpec as P

D = 512
HEADS = 8
HEAD_DIM = 64
FF = 2048


EPS_NORM = 1e-05
EPS_ADAM = 1e-06
STEP_RATE = 0.5
BIG_NEGATIVE = -1e30


def normalize(hidden, gain_row):
    centre = jnp.mean(hidden, -1, keepdims=True)
    shifted = hidden - centre
    spread = jnp.mean(shifted * shifted, -1, keepdims=True)
    return shifted * lax.rsqrt(spread + EPS_NORM) * gain_row


def norm_backward(hidden, gain_row, normed_grad):
    _, pullback = jax.vjp(normalize, hidden, gain_row)
    return pullback(normed_grad)


def gelu_exact(upward):
    return jax.nn.gelu(upward, approximate=False)


def contract_rows(left, right):
    return lax.dot_general(
        left, right, (((0,), (0,)), ((), ())), preferred_element_type=jnp.float32
    )


def times_transpose(left, right):
    return lax.dot_general(
        left, right, (((1,), (1,)), ((), ())), preferred_element_type=jnp.float32
    )


def unpack(flat_params, width_in, width_mid):
    gain_row = flat_params[:D].astype(jnp.float32)
    w_in = flat_params[D : D + D * width_in].reshape(D, width_in)
    w_out = flat_params[D + D * width_in :].reshape(width_mid, D)
    return (gain_row, w_in, w_out)


def fetch_forward(master):
    return lax.all_gather(master.astype(jnp.bfloat16), ("task", "samp"), axis=0, tiled=True)


def fetch_again(master):
    return lax.all_gather(master.astype(jnp.bfloat16), ("task", "samp"), axis=0, tiled=True)


def reduce_grads(gain_grad, in_grad, out_grad_matrix):
    flat_grads = jnp.concatenate([gain_grad, in_grad.reshape(-1), out_grad_matrix.reshape(-1)])
    return lax.psum_scatter(flat_grads, ("task", "samp"), scatter_dimension=0, tiled=True)


def group_size(feature_total, most):
    chosen = 1
    for candidate in range(1, most + 1):
        if feature_total % candidate == 0:
            chosen = candidate
    return chosen


def lamb_prepare(grad_shard, master, first, second, width_in):
    first_new = 0.5 * first + 0.5 * grad_shard
    second_new = 0.5 * second + 0.5 * grad_shard * grad_shard
    direction = first_new / (jnp.sqrt(second_new) + EPS_ADAM)
    entries = master.shape[0]
    position = lax.axis_index(("task", "samp")) * entries + jnp.arange(entries, dtype=jnp.int32)
    segment = (position >= D).astype(jnp.int32) + (position >= D + D * width_in).astype(jnp.int32)
    member = segment[None, :] == jnp.arange(3, dtype=jnp.int32)[:, None]
    weight_sums = jnp.sum(jnp.where(member, (master * master)[None, :], 0.0), 1)
    update_sums = jnp.sum(jnp.where(member, (direction * direction)[None, :], 0.0), 1)
    return (first_new, second_new, direction, member, jnp.stack([weight_sums, update_sums], 1))


def lamb_finish(master, block_state, trust_ratio):
    factor = jnp.sum(jnp.where(block_state[3], trust_ratio[:, None], 0.0), 0)
    return master - STEP_RATE * factor * block_state[2]


def sample_scores(query_part, key_part, key_live, score_scale):
    scores = (
        jnp.einsum("qfhe,kfhe->fhqk", query_part, key_part, preferred_element_type=jnp.float32)
        * score_scale
    )
    return jnp.where(key_live, scores, BIG_NEGATIVE)


def sample_forward(queries, pairs_all, key_live, block_features, score_scale):
    local_rows, features = (queries.shape[0], queries.shape[1])

    def one_block(block_index, results):
        attended, log_totals = results
        offset = block_index * block_features
        query_part = lax.dynamic_slice_in_dim(queries, offset, block_features, 1)
        pair_part = lax.dynamic_slice_in_dim(pairs_all, offset, block_features, 1)
        scores = sample_scores(query_part, pair_part[:, :, 0], key_live, score_scale)
        row_top = jnp.max(scores, -1, keepdims=True)
        exponent = jnp.exp(scores - row_top)
        row_total = jnp.sum(exponent, -1, keepdims=True)
        probability = (exponent / row_total).astype(jnp.bfloat16)
        block_out = jnp.einsum(
            "fhqk,kfhe->qfhe", probability, pair_part[:, :, 1], preferred_element_type=jnp.float32
        )
        attended = lax.dynamic_update_slice_in_dim(
            attended, block_out.astype(jnp.bfloat16), offset, 1
        )
        log_totals = lax.dynamic_update_slice_in_dim(
            log_totals, (row_top + jnp.log(row_total))[..., 0], offset, 0
        )
        return (attended, log_totals)

    start_state = (
        jnp.zeros(queries.shape, jnp.bfloat16),
        jnp.zeros((features, HEADS, local_rows), jnp.float32),
    )
    return lax.fori_loop(0, features // block_features, one_block, start_state)


def query_side(query_part, pair_part, grad_part, log_part, key_live, score_scale):
    key_part = pair_part[:, :, 0]
    value_part = pair_part[:, :, 1]
    scores = sample_scores(query_part, key_part, key_live, score_scale)
    probability = jnp.exp(scores - log_part[..., None])
    prob_grad = jnp.einsum(
        "qfhe,kfhe->fhqk", grad_part, value_part, preferred_element_type=jnp.float32
    )
    row_inner = jnp.sum(probability * prob_grad, -1, keepdims=True)
    score_grad = (probability * (prob_grad - row_inner)).astype(jnp.bfloat16)
    query_block = (
        jnp.einsum("fhqk,kfhe->qfhe", score_grad, key_part, preferred_element_type=jnp.float32)
        * score_scale
    )
    return (probability, score_grad, row_inner, query_block)


def sample_backward(
    queries, pairs_all, key_live, log_totals, attended_grad, block_features, score_scale
):
    local_rows, features = (queries.shape[0], queries.shape[1])

    def one_block(block_index, results):
        query_grads, pair_grads = results
        offset = block_index * block_features
        query_part = lax.dynamic_slice_in_dim(queries, offset, block_features, 1)
        pair_part = lax.dynamic_slice_in_dim(pairs_all, offset, block_features, 1)
        grad_part = lax.dynamic_slice_in_dim(attended_grad, offset, block_features, 1)
        log_part = lax.dynamic_slice_in_dim(log_totals, offset, block_features, 0)
        probability, score_grad, row_inner, query_block = query_side(
            query_part, pair_part, grad_part, log_part, key_live, score_scale
        )
        key_block = (
            jnp.einsum(
                "fhqk,qfhe->kfhe", score_grad, query_part, preferred_element_type=jnp.float32
            )
            * score_scale
        )
        value_block = jnp.einsum(
            "fhqk,qfhe->kfhe",
            probability.astype(jnp.bfloat16),
            grad_part,
            preferred_element_type=jnp.float32,
        )
        pair_terms = jnp.stack([key_block, value_block], 2)
        pair_local = lax.psum_scatter(
            pair_terms.astype(jnp.bfloat16), "samp", scatter_dimension=0, tiled=True
        ).astype(jnp.float32)
        query_grads = lax.dynamic_update_slice_in_dim(query_grads, query_block, offset, 1)
        pair_grads = lax.dynamic_update_slice_in_dim(pair_grads, pair_local, offset, 1)
        return (query_grads, pair_grads)

    start_state = (
        jnp.zeros((local_rows, features, HEADS, HEAD_DIM), jnp.float32),
        jnp.zeros((local_rows, features, 2, HEADS, HEAD_DIM), jnp.float32),
    )
    return lax.fori_loop(0, features // block_features, one_block, start_state)


def on_device(
    cells,
    out_grad,
    sample_counts,
    feature_counts,
    sample_block,
    sample_first,
    sample_second,
    feature_block,
    feature_first,
    feature_second,
    mlp_block,
    mlp_first,
    mlp_second,
):
    local_rows, features = (cells.shape[1], cells.shape[2])
    flat_rows = local_rows * features
    seq_all = local_rows * lax.axis_size("samp")
    score_scale = HEAD_DIM ** (-0.5)
    block_features = group_size(features, max(1, 2048 // (HEADS * local_rows)))
    sample_index = lax.axis_index("samp") * local_rows + jnp.arange(local_rows, dtype=jnp.int32)
    sample_live = sample_index < sample_counts[0]
    key_live = jnp.arange(seq_all, dtype=jnp.int32) < sample_counts[0]
    feature_live = jnp.arange(features, dtype=jnp.int32) < feature_counts[0]
    cell_live = sample_live[:, None, None] & feature_live[None, :, None]
    hidden_in = cells[0].astype(jnp.float32)
    gain_one, in_one, out_one = unpack(fetch_forward(sample_block), 3 * D, D)
    normed_one = normalize(hidden_in, gain_one).astype(jnp.bfloat16)
    packed_one = jnp.dot(
        normed_one.reshape(flat_rows, D), in_one, preferred_element_type=jnp.float32
    )
    packed_one = packed_one.astype(jnp.bfloat16).reshape(local_rows, features, 3, HEADS, HEAD_DIM)
    queries_one = packed_one[:, :, 0]
    pairs_local = packed_one[:, :, 1:]
    pairs_all = lax.all_gather(pairs_local, "samp", axis=0, tiled=True)
    attended_one, log_totals = sample_forward(
        queries_one, pairs_all, key_live, block_features, score_scale
    )
    attended_one_rows = attended_one.reshape(flat_rows, D)
    branch_one = jnp.dot(attended_one_rows, out_one, preferred_element_type=jnp.float32)
    hidden_one = hidden_in + branch_one.reshape(local_rows, features, D)
    gain_two, in_two, out_two = unpack(fetch_forward(feature_block), 3 * D, D)
    normed_two = normalize(hidden_one, gain_two).astype(jnp.bfloat16).reshape(flat_rows, D)
    packed_two = jnp.dot(normed_two, in_two, preferred_element_type=jnp.float32)
    packed_two = packed_two.astype(jnp.bfloat16).reshape(local_rows, features, 3, HEADS, HEAD_DIM)
    queries_two, key_two, value_two = (
        packed_two[:, :, 0],
        packed_two[:, :, 1],
        packed_two[:, :, 2],
    )
    scores_two = (
        jnp.einsum("sqhe,skhe->shqk", queries_two, key_two, preferred_element_type=jnp.float32)
        * score_scale
    )
    scores_two = jnp.where(feature_live, scores_two, BIG_NEGATIVE)
    row_top = jnp.max(scores_two, -1, keepdims=True)
    exponent = jnp.exp(scores_two - row_top)
    probability_two = exponent / jnp.sum(exponent, -1, keepdims=True)
    prob_low_two = probability_two.astype(jnp.bfloat16)
    attended_two = jnp.einsum(
        "shqk,skhe->sqhe", prob_low_two, value_two, preferred_element_type=jnp.float32
    )
    attended_two_rows = attended_two.reshape(flat_rows, D).astype(jnp.bfloat16)
    branch_two = jnp.dot(attended_two_rows, out_two, preferred_element_type=jnp.float32)
    hidden_two = hidden_one + branch_two.reshape(local_rows, features, D)
    gain_three, up_weight, down_weight = unpack(fetch_forward(mlp_block), FF, FF)
    normed_three = normalize(hidden_two, gain_three).astype(jnp.bfloat16).reshape(flat_rows, D)
    upward = jnp.dot(normed_three, up_weight, preferred_element_type=jnp.float32)
    activated = gelu_exact(upward).astype(jnp.bfloat16)
    branch_three = jnp.dot(activated, down_weight, preferred_element_type=jnp.float32)
    hidden_three = hidden_two + branch_three.reshape(local_rows, features, D)
    layer_out = jnp.where(cell_live, hidden_three, 0.0).astype(jnp.bfloat16)[None]
    top_grad = jnp.where(cell_live, out_grad[0], jnp.zeros((), jnp.bfloat16))
    top_rows = top_grad.reshape(flat_rows, D)
    gain_three, up_weight, down_weight = unpack(fetch_again(mlp_block), FF, FF)
    down_grad = contract_rows(activated, top_rows)
    act_grad = times_transpose(top_rows, down_weight).astype(jnp.bfloat16)
    _, gelu_pull = jax.vjp(gelu_exact, upward)
    up_grad = gelu_pull(act_grad.astype(jnp.float32))[0].astype(jnp.bfloat16)
    upw_grad = contract_rows(normed_three, up_grad)
    normed_grad = times_transpose(up_grad, up_weight).reshape(local_rows, features, D)
    hidden_grad, gain_three_grad = norm_backward(hidden_two, gain_three, normed_grad)
    grad_two = top_grad.astype(jnp.float32) + hidden_grad
    mlp_shard = reduce_grads(gain_three_grad, upw_grad, down_grad)
    mlp_state = lamb_prepare(mlp_shard, mlp_block, mlp_first, mlp_second, FF)
    gain_two, in_two, out_two = unpack(fetch_again(feature_block), 3 * D, D)
    branch_grad = grad_two.astype(jnp.bfloat16).reshape(flat_rows, D)
    out_two_grad = contract_rows(attended_two_rows, branch_grad)
    attended_grad = (
        times_transpose(branch_grad, out_two)
        .astype(jnp.bfloat16)
        .reshape(local_rows, features, HEADS, HEAD_DIM)
    )
    prob_grad = jnp.einsum(
        "sqhe,skhe->shqk", attended_grad, value_two, preferred_element_type=jnp.float32
    )
    row_inner = jnp.sum(probability_two * prob_grad, -1, keepdims=True)
    score_grad = (probability_two * (prob_grad - row_inner)).astype(jnp.bfloat16)
    query_grad = (
        jnp.einsum("shqk,skhe->sqhe", score_grad, key_two, preferred_element_type=jnp.float32)
        * score_scale
    )
    key_grad = (
        jnp.einsum("shqk,sqhe->skhe", score_grad, queries_two, preferred_element_type=jnp.float32)
        * score_scale
    )
    value_grad = jnp.einsum(
        "shqk,sqhe->skhe", prob_low_two, attended_grad, preferred_element_type=jnp.float32
    )
    packed_grad = (
        jnp.stack([query_grad, key_grad, value_grad], 2)
        .astype(jnp.bfloat16)
        .reshape(flat_rows, 3 * D)
    )
    in_two_grad = contract_rows(normed_two, packed_grad)
    normed_grad = times_transpose(packed_grad, in_two).reshape(local_rows, features, D)
    hidden_grad, gain_two_grad = norm_backward(hidden_one, gain_two, normed_grad)
    grad_one = grad_two + hidden_grad
    feature_shard = reduce_grads(gain_two_grad, in_two_grad, out_two_grad)
    feature_state = lamb_prepare(feature_shard, feature_block, feature_first, feature_second, 3 * D)
    gain_one, in_one, out_one = unpack(fetch_again(sample_block), 3 * D, D)
    pairs_all = lax.all_gather(pairs_local, "samp", axis=0, tiled=True)
    branch_grad = grad_one.astype(jnp.bfloat16).reshape(flat_rows, D)
    out_one_grad = contract_rows(attended_one_rows, branch_grad)
    attended_grad = (
        times_transpose(branch_grad, out_one)
        .astype(jnp.bfloat16)
        .reshape(local_rows, features, HEADS, HEAD_DIM)
    )
    query_grads, pair_grads = sample_backward(
        queries_one, pairs_all, key_live, log_totals, attended_grad, block_features, score_scale
    )
    packed_grad = (
        jnp.concatenate([query_grads[:, :, None], pair_grads], 2)
        .astype(jnp.bfloat16)
        .reshape(flat_rows, 3 * D)
    )
    in_one_grad = contract_rows(normed_one.reshape(flat_rows, D), packed_grad)
    normed_grad = times_transpose(packed_grad, in_one).reshape(local_rows, features, D)
    hidden_grad, gain_one_grad = norm_backward(hidden_in, gain_one, normed_grad)
    cells_grad = (grad_one + hidden_grad)[None]
    sample_shard = reduce_grads(gain_one_grad, in_one_grad, out_one_grad)
    sample_state = lamb_prepare(sample_shard, sample_block, sample_first, sample_second, 3 * D)
    totals = lax.psum(
        jnp.concatenate([sample_state[4], feature_state[4], mlp_state[4]], 0), ("task", "samp")
    )
    norm_pairs = jnp.sqrt(totals)
    trust_ratio = norm_pairs[:, 0] / (norm_pairs[:, 1] + EPS_ADAM)
    sample_master = lamb_finish(sample_block, sample_state, trust_ratio[0:3])
    feature_master = lamb_finish(feature_block, feature_state, trust_ratio[3:6])
    mlp_master = lamb_finish(mlp_block, mlp_state, trust_ratio[6:9])
    return (
        layer_out,
        cells_grad,
        sample_shard,
        sample_state[0],
        sample_state[1],
        sample_master,
        sample_master.astype(jnp.bfloat16),
        feature_shard,
        feature_state[0],
        feature_state[1],
        feature_master,
        feature_master.astype(jnp.bfloat16),
        mlp_shard,
        mlp_state[0],
        mlp_state[1],
        mlp_master,
        mlp_master.astype(jnp.bfloat16),
        norm_pairs,
    )


D = 512
MESH = pl.DeviceIdType.MESH
BF = jnp.bfloat16
F32 = jnp.float32
NEG = -1e30


def mult(value, factor):
    return value if isinstance(value, int) else pl.multiple_of(value, factor)


def nt(left, right):
    return lax.dot_general(left, right, (((1,), (1,)), ((), ())), preferred_element_type=F32)


def nn(left, right):
    return lax.dot_general(left, right, (((1,), (0,)), ((), ())), preferred_element_type=F32)


def here():
    return lax.axis_index("task"), lax.axis_index("samp")


def peers(t, s):
    return [(jnp.bitwise_xor(t, e), s) for e in range(1, 8)] + [(t, jnp.bitwise_xor(s, e)) for e in (1, 2, 3)]


def enter(t, s):
    barrier = pltpu.get_barrier_semaphore()
    for peer in peers(t, s):
        pl.semaphore_signal(barrier, inc=1, device_id=peer, device_id_type=MESH)
    return barrier


def send(src, dst, ssem, rsem, peer):
    copy = pltpu.make_async_remote_copy(
        src_ref=src, dst_ref=dst, send_sem=ssem, recv_sem=rsem, device_id=peer, device_id_type=MESH
    )
    copy.start()
    return copy


class Gather:
    def __init__(self, buf, ssem, rsem, t, s):
        self.buf, self.t, self.s = buf, t, s
        half = buf.shape[2] // 2
        self.ha, self.hb, self.all = pl.ds(0, half), pl.ds(half, half), pl.ds(0, 2 * half)
        self.rows = pl.ds(0, buf.shape[1])
        self.ssem, self.rsem = ssem, rsem
        self.moves = []
        self.tx, self.ty = jnp.bitwise_xor(t, 2), jnp.bitwise_xor(t, 4)
        self.txy, self.tc = jnp.bitwise_xor(t, 6), jnp.bitwise_xor(t, 1)
        self.hops, self.sent = {}, {k: {} for k in ("x", "y", "c", "xy", "yx", "cx", "cy")}

    def z(self, key):
        return jnp.bitwise_xor(self.s, key)

    def go(self, slots, cols, peer):
        view = self.buf.at[slots, self.rows, cols]
        i = len(self.moves)
        copy = send(view, view, self.ssem.at[i], self.rsem.at[i], peer)
        self.moves.append(copy)
        return copy

    def pass_on(self, kind, key, t, cols, to):
        self.sent[kind][key] = self.go(pl.ds(4 * t + self.z(key), 1), cols, (to, self.s))

    def spread(self, key):
        self.pass_on("x", key, self.t, self.all, self.tx)
        self.pass_on("y", key, self.t, self.all, self.ty)
        self.pass_on("c", key, self.t, self.all, self.tc)

    def hop(self, key, slot, to):
        self.hops[key] = self.go(pl.ds(4 * self.t + self.z(slot), 1), self.all, (self.t, self.z(to)))

    def start_z(self):
        self.hop(2, 0, 2)
        self.hop(1, 0, 1)

    def zin(self, *keys):
        for key in keys:
            self.hops[key].wait_recv()
            if key == 2:
                self.hop(3, 2, 1)
            self.spread(key)

    def near(self, *keys):
        for key in keys:
            self.sent["x"][key].wait_recv()
            self.pass_on("xy", key, self.tx, self.ha, self.ty)
            self.pass_on("cx", key, self.tx, self.all, self.tc)
            self.sent["y"][key].wait_recv()
            self.pass_on("yx", key, self.ty, self.hb, self.tx)
            self.pass_on("cy", key, self.ty, self.all, self.tc)

    def far(self):
        for kind in ("xy", "yx"):
            for copy in self.sent[kind].values():
                copy.wait_recv()
        self.last = self.go(pl.ds(4 * self.txy, 4), self.all, (self.tc, self.s))

    def end(self):
        for kind in ("c", "cx", "cy"):
            for copy in self.sent[kind].values():
                copy.wait_recv()
        self.last.wait_recv()

    def drain(self):
        for copy in self.moves:
            copy.wait_send()


def realign(m_ref, sh_ref, d, rows, out_ref, out_at, roll_to, split=False):
    whole = 4 * rows
    total = whole + 8
    q, p = d // 8, d % 8
    lane = lax.broadcasted_iota(jnp.int32, (total, 128), 1)
    roll_to[0:8, :] = jnp.zeros((8, 128), F32)
    for i in range(whole // 8):
        sh_ref[8 * i : 8 * i + 8, :] = m_ref[pl.ds(1024 * i, 1024)].reshape(8, 128)
    sh_ref[whole:total, :] = jnp.zeros((8, 128), F32)
    sh_ref[whole : whole + 1, 0:16] = m_ref[pl.ds(128 * whole, 16)].reshape(1, 16)
    rolled = pltpu.roll(sh_ref[0:total, :], 16 * p, 1)
    roll_to[8 : 8 + total, :] = rolled
    sh_ref[0:8, :] = jnp.zeros((8, 128), F32)
    sh_ref[8 : 8 + total, :] = jnp.where(lane < 16 * p, roll_to[7 : 7 + total, :], rolled)
    firsts = []

    def straight():
        for b in range(4):
            cols = slice(128 * b, 128 * b + 128)
            out_ref[out_at, 0:rows, cols] = sh_ref[pl.ds(12 - q + b, rows, stride=4), :].astype(BF)

    def by_piece():
        for b in range(4):
            cols = slice(128 * b, 128 * b + 128)
            for j in range(4):
                piece = sh_ref[pl.ds(12 - q + b + 4 * j, rows // 4, stride=16), :]
                out_ref[out_at, rows // 4 * j : rows // 4 * (j + 1), cols] = piece.astype(BF)

    if split:
        pl.when(d < 16)(by_piece)
        pl.when(d >= 16)(straight)
    else:
        straight()
    for b in range(4):
        firsts.append(sh_ref[pl.ds(8 - q + b, 1), :])
    return jnp.concatenate(firsts, 1)


def spread(buf, firsts, kind, rows, lo, hi, put):
    tail = lax.broadcasted_iota(jnp.int32, (8, D), 0) == 7

    def body(i, _):
        nxt = jnp.minimum(i + 1, 31)
        row = firsts[nxt, :, D * kind : D * kind + D]
        block = buf[i, 0:rows, :].astype(F32)
        last = block[rows - 8 : rows, :] + jnp.where(tail & (i < 31), row, 0.0)
        put(i - lo, block[0 : rows - 8, :], last)
        return 0

    lax.fori_loop(lo, hi, body, 0)


def put_f32(dst, rows):
    def put(i, head, last):
        for b in range(4):
            cols = slice(128 * b, 128 * b + 128)
            dst[b, pl.ds(mult(i * rows, rows), rows - 8), :] = head[:, cols]
            dst[b, pl.ds(mult(i * rows + rows - 8, 8), 8), :] = last[:, cols]

    return put


def put_bf(dst, rows):
    def put(i, head, last):
        dst[pl.ds(mult(i * rows, rows), rows), :] = jnp.concatenate([head, last], 0).astype(BF)

    return put


def split_columns(wide, ways, dst):
    def body(i, _):
        for j in range(ways):
            for b in range(4):
                piece = wide[b, pl.ds(64 * ways * i + j, 64, stride=ways), :]
                dst[j, pl.ds(mult(64 * i, 64), 64), 128 * b : 128 * b + 128] = piece.astype(BF)
        return 0

    lax.fori_loop(0, 8, body, 0)


def halves():
    lane = lax.broadcasted_iota(jnp.int32, (128, 128), 1)
    return lane < 64


def two_heads(x, one, two):
    return jnp.concatenate([x * one, x * two], 0)


def soft(scores, axis):
    e = [jnp.exp(x - jnp.max(x, axis, keepdims=True)) for x in scores]
    return [x * (1.0 / jnp.sum(x, axis, keepdims=True)) for x in e]


def attend_chunk(qkv, c, live, out):
    left = halves()
    one = jnp.where(left, 0.125, 0.0).astype(BF)
    two = jnp.where(left, 0.0, 0.125).astype(BF)
    rows = pl.ds(mult(c * 128, 128), 128)

    def body(h, _):
        cols = [pl.ds(128 * i, 128) for i in range(4)]
        scores = [jnp.where(live, nt(two_heads(qkv[0, rows, w], one, two), qkv[1, :, w]), NEG) for w in cols]
        prob = [p.astype(BF) for p in soft(scores, 1)]
        outs = [nn(p, qkv[2, :, w]) for p, w in zip(prob, cols)]
        for o, w in zip(outs, cols):
            o = jnp.where(left, o[0:128], o[128:256]).astype(BF)
            for g in range(4):
                out[g, :, w] = o[32 * g : 32 * g + 32]
        return 0

    body(0, 0)


def edges(d, entries, width):
    begin = d * entries
    return D - begin, D + D * width - begin


def segment(k, ends):
    return (k >= ends[0]).astype(jnp.int32) + (k >= ends[1]).astype(jnp.int32)


def lamb_step(g, m, f, s):
    fn = 0.5 * f + 0.5 * g
    sn = 0.5 * s + 0.5 * g * g
    return fn, sn, fn / (jnp.sqrt(sn) + 1e-6)


def flat_index():
    rows = lax.broadcasted_iota(jnp.int32, (32, 128), 0)
    return rows * 128 + lax.broadcasted_iota(jnp.int32, (32, 128), 1)


def fold(x):
    return x.reshape(-1, 8, 128).sum(0)


def squares(sh, m, f, s, sums, d, width, b, lo, hi):
    entries = m.shape[0]
    ends = edges(d, entries, width)
    index = flat_index()

    def body(i, acc):
        at = pl.ds(mult(i * 4096, 4096), 4096)
        old = m[at].reshape(32, 128)
        _, _, r = lamb_step(sh[pl.ds(mult(i * 32, 32), 32), :], old, f[at].reshape(32, 128), s[at].reshape(32, 128))
        part = segment(index + i * 4096, ends)
        out = []
        for n, value in enumerate((old * old, r * r)):
            for k in range(3):
                out.append(acc[3 * n + k] + fold(jnp.where(part == k, value, 0.0)))
        return tuple(out)

    acc = lax.fori_loop(lo, hi, body, (jnp.zeros((8, 128), F32),) * 6)
    for n in range(2):
        for k in range(3):
            row = 16 * n + 3 * b + k
            sums[row : row + 1, :] += jnp.sum(acc[3 * n + k], 0, keepdims=True)


def squares_tail(sh, m, f, s, sums, d, width, b):
    entries = m.shape[0]
    base = entries - 16
    ends = edges(d, entries, width)
    at = pl.ds(base, 16)
    old = m[at].reshape(1, 16)
    row = base // 128
    _, _, r = lamb_step(sh[row : row + 1, 0:16], old, f[at].reshape(1, 16), s[at].reshape(1, 16))
    part = segment(lax.broadcasted_iota(jnp.int32, (1, 16), 1) + base, ends)
    for n, value in enumerate((old * old, r * r)):
        for k in range(3):
            row = 16 * n + 3 * b + k
            sums[row : row + 1, 0:16] += jnp.where(part == k, value, 0.0)


def update(sh, m, f, s, grad, fout, sout, mout, wout, ratio, d, width, b):
    entries = m.shape[0]
    whole = entries // 4096
    ends = edges(d, entries, width)
    half = [0.5 * ratio[3 * b + k : 3 * b + k + 1, :] for k in range(3)]

    def put(at, g, part, shape):
        old = m[at].reshape(shape)
        fn, sn, r = lamb_step(g, old, f[at].reshape(shape), s[at].reshape(shape))
        factor = jnp.where(part == 0, half[0], jnp.where(part == 1, half[1], half[2]))
        new = (old - factor * r).reshape(-1)
        grad[at] = g.reshape(-1)
        fout[at] = fn.reshape(-1)
        sout[at] = sn.reshape(-1)
        mout[at] = new
        wout[at] = new.astype(BF)

    index = flat_index()

    def body(i, _):
        at = pl.ds(mult(i * 4096, 4096), 4096)
        put(at, sh[pl.ds(mult(i * 32, 32), 32), :], segment(index + i * 4096, ends), (32, 128))
        return 0

    lax.fori_loop(0, whole, body, 0)
    part = segment(lax.broadcasted_iota(jnp.int32, (1, 16), 1) + whole * 4096, ends)
    put(pl.ds(whole * 4096, 16), sh[32 * whole : 32 * whole + 1, 0:16], part, (1, 16))


def diagonal(rows):
    lane = lax.broadcasted_iota(jnp.int32, (32, 128), 1)
    return lane == lax.broadcasted_iota(jnp.int32, (32, 128), 0)


def sum_all(sums, ts, zs, ssem, rsem, t, s, meanwhile):
    column = jnp.sum(sums[...], 1, keepdims=True)
    ts[t] = jnp.broadcast_to(jnp.sum(jnp.where(diagonal(32), column, 0.0), 0, keepdims=True), (8, 128))
    plane = [
        send(ts.at[t], ts.at[t], ssem.at[e - 1], rsem.at[e - 1], (jnp.bitwise_xor(t, e), s)) for e in range(1, 8)
    ]
    meanwhile()
    for copy in plane:
        copy.wait_recv()
    zs[s] = ((ts[0] + ts[1]) + (ts[2] + ts[3])) + ((ts[4] + ts[5]) + (ts[6] + ts[7]))
    last = [
        send(zs.at[s], zs.at[s], ssem.at[6 + e], rsem.at[6 + e], (t, jnp.bitwise_xor(s, e))) for e in (1, 2, 3)
    ]
    for copy in last:
        copy.wait_recv()
    return (zs[0] + zs[1]) + (zs[2] + zs[3]), plane + last


def by_sample(x, out):
    for g in range(4):
        out[32 * g : 32 * g + 32, :, :] = jnp.transpose(x[g].astype(F32), (1, 0, 2)).astype(out.dtype)


def kernel_e(
    total, sh1, sh2, sh3, m1, f1, s1, m2, f2, s2, m3, f3, s3, lout, cgrad,
    g1, fo1, so1, mo1, wo1, g2, fo2, so2, mo2, wo2, g3, fo3, so3, mo3, wo3, pairs, layer, grad,
):
    t, s = here()
    d = 4 * t + s
    norms = jnp.sqrt(total[0:1, :])
    pairs[0:1, :] = norms[:, 0:9]
    pairs[1:2, :] = pltpu.roll(norms, 112, 1)[:, 0:9]
    norm = jnp.sum(jnp.where(diagonal(32), norms, 0.0), 1, keepdims=True)
    ratio = norm[0:9] / (norm[16:25] + 1e-6)
    by_sample(lout, layer)
    by_sample(cgrad, grad)
    update(sh1, m1, f1, s1, g1, fo1, so1, mo1, wo1, ratio, d, 3 * D, 0)
    update(sh2, m2, f2, s2, g2, fo2, so2, mo2, wo2, ratio, d, 3 * D, 1)
    update(sh3, m3, f3, s3, g3, fo3, so3, mo3, wo3, ratio, d, 4 * D, 2)


def call_e(total, shards, args, lout, cgrad):
    sds = jax.ShapeDtypeStruct
    vm = pl.BlockSpec(memory_space=pltpu.VMEM)
    shapes = []
    for m in args[0::3]:
        n = m.shape
        shapes += [sds(n, F32)] * 4 + [sds(n, BF)]
    return pl.pallas_call(
        kernel_e,
        name="kernel_e",
        out_shape=(*shapes, sds((2, 9), F32), sds((128, 4, D), BF), sds((128, 4, D), F32)),
        in_specs=[vm] * 15,
        out_specs=(vm,) * 18,
        compiler_params=pltpu.CompilerParams(vmem_limit_bytes=63 << 20),
    )(total, *shards, *args, lout, cgrad)


def backward_heads(h, qkv, do, live, dqkv, kt, dkv):
    left = halves()
    one, two = jnp.where(left, 1.0, 0.0).astype(BF), jnp.where(left, 0.0, 1.0).astype(BF)
    cols = pl.ds(mult(h * 128, 128), 128)
    kt[...] = jnp.transpose(qkv[1, :, cols])
    top_lane = lax.broadcasted_iota(jnp.int32, (128, 128), 0) < 64

    def chunk(n, _):
        each = [0, 1, 2, 3]
        rows = [pl.ds(c * 128, 128) for c in each]
        qm = [two_heads(qkv[0, r, cols] * jnp.asarray(0.125, BF), one, two) for r in rows]
        gm = [two_heads(do[c, :, :, cols].reshape(128, 128), one, two) for c in each]
        prob = soft([jnp.where(live, nt(qkv[1, :, cols], q), NEG) for q in qm], 0)
        pg = [nt(qkv[2, :, cols], g) for g in gm]
        sg = [(p * (x - jnp.sum(p * x, 0, keepdims=True))).astype(BF) for p, x in zip(prob, pg)]
        dqkv[1, :, cols] = (nn(sg[0], qm[0]) + nn(sg[1], qm[1]) + nn(sg[2], qm[2]) + nn(sg[3], qm[3])).astype(BF)
        pb = [p.astype(BF) for p in prob]
        dqkv[2, :, cols] = (nn(pb[0], gm[0]) + nn(pb[1], gm[1]) + nn(pb[2], gm[2]) + nn(pb[3], gm[3])).astype(BF)
        for r, x in zip(rows, sg):
            dqt = nn(kt[...], x)
            dq = jnp.transpose(jnp.where(top_lane, dqt[:, 0:128], dqt[:, 128:256])) * 0.125
            dqkv[0, r, cols] = dq.astype(BF)
        return 0

    chunk(0, 0)


def turn(x):
    return jnp.transpose(x)


def stats(h):
    x = h - jnp.mean(h, 1, keepdims=True)
    rstd = lax.rsqrt(jnp.mean(x * x, 1, keepdims=True) + 1e-5)
    return x * rstd, rstd


def norm_grad(h, da, gain):
    x, rstd = stats(h)
    dgain = jnp.sum(da * x, 0, keepdims=True)
    dx = da * gain
    dh = rstd * (dx - jnp.mean(dx, 1, keepdims=True) - x * jnp.mean(dx * x, 1, keepdims=True))
    return dh, dgain


def block(g):
    return pl.ds(mult(g * 128, 128), 128)


def feature_mask(fcnt, axis):
    shape = (256, 128) if axis else (128, 256)
    query = lax.broadcasted_iota(jnp.int32, shape, 1 - axis)
    key = lax.broadcasted_iota(jnp.int32, shape, axis)
    return (query % 32 == key % 32) & (key // 32 < fcnt)


def feature_forward(qkv, o2, fcnt, half):
    left = halves()
    one = jnp.where(left, 0.125, 0.0).astype(BF)
    two = jnp.where(left, 0.0, 0.125).astype(BF)
    ok = feature_mask(fcnt, 1)
    cols = [slice(128 * h, 128 * h + 128) for h in range(4)]

    def body(n, _):
        rows = block(n)
        scores = [
            jnp.where(ok, nt(two_heads(qkv[0, rows, c], one, two), qkv[1, rows, c]), NEG) for c in cols
        ]
        prob = [p.astype(BF) for p in soft(scores, 1)]
        out = [nn(p, qkv[2, rows, c]) for p, c in zip(prob, cols)]
        for o, c in zip(out, cols):
            o2[rows, c] = jnp.where(left, o[0:128], o[128:256]).astype(BF)
        return 0

    lax.fori_loop(2 * half, 2 * half + 2, body, 0)


def feature_backward(qkv, do, dqkv, fcnt, half):
    left = halves()
    one, two = jnp.where(left, 1.0, 0.0).astype(BF), jnp.where(left, 0.0, 1.0).astype(BF)
    ok = feature_mask(fcnt, 0)
    top_lane = lax.broadcasted_iota(jnp.int32, (128, 128), 0) < 64
    cols = [slice(128 * h, 128 * h + 128) for h in range(4)]

    def body(n, _):
        rows = block(n)
        qm = [two_heads(qkv[0, rows, c] * jnp.asarray(0.125, BF), one, two) for c in cols]
        gm = [two_heads(do[rows, c], one, two) for c in cols]
        prob = soft([jnp.where(ok, nt(qkv[1, rows, c], q), NEG) for c, q in zip(cols, qm)], 0)
        pg = [nt(qkv[2, rows, c], g) for c, g in zip(cols, gm)]
        sg = [(p * (x - jnp.sum(p * x, 0, keepdims=True))).astype(BF) for p, x in zip(prob, pg)]
        dqt = [nn(turn(qkv[1, rows, c]), x) for c, x in zip(cols, sg)]
        dk = [nn(x, q).astype(BF) for x, q in zip(sg, qm)]
        dv = [nn(p.astype(BF), g).astype(BF) for p, g in zip(prob, gm)]
        dq = [turn(jnp.where(top_lane, x[:, 0:128], x[:, 128:256])) * 0.125 for x in dqt]
        for i, c in enumerate(cols):
            dqkv[0, rows, c] = dq[i].astype(BF)
            dqkv[1, rows, c] = dk[i]
            dqkv[2, rows, c] = dv[i]
        return 0

    lax.fori_loop(2 * half, 2 * half + 2, body, 0)


def four_blocks(body, init=0):
    for r in range(4):
        init = body(r, init)
    return init


def two_blocks(half, body, init=0):
    for r in (2 * half, 2 * half + 1):
        init = body(r, init)
    return init


def flat(x):
    return x.reshape(128, D)


def cube(x):
    return x.reshape(4, 32, D)


def narrow_to(wide, part, slots, rows):
    def body(i, _):
        at = pl.ds(mult(i * rows, rows), rows)
        for b in range(4):
            part[i, :, 128 * b : 128 * b + 128] = wide[b, at, :].astype(BF)
        return 0

    lax.fori_loop(0, slots, body, 0)


def store_wide(wide, j, ways, value):
    for b in range(4):
        wide[b, pl.ds(j, value.shape[0], stride=ways), :] = value[:, 128 * b : 128 * b + 128]


def mlp(a3, a3t, g, h2, wup, wdn, h3, da, zb, dub, u, dz, p3, after):
    h3[...] = h2[...]
    da[...] = jnp.zeros((512, D), F32)

    def body(j, _):
        u[...] = nn(a3[...], wup[j])
        dz[...] = nt(g[...], wdn[j]).astype(BF)

        def act(r, _):
            rows = pl.ds(mult(r * 64, 64), 64)
            x = u[rows, :]
            cdf = 0.5 * (1.0 + lax.erf(x * 0.7071067811865476))
            zb[rows, :] = (x * cdf).astype(BF)
            slope = cdf + x * (0.3989422804014327 * jnp.exp(-0.5 * x * x))
            dub[rows, :] = (slope * dz[rows, :].astype(F32)).astype(BF)
            return 0

        lax.fori_loop(0, 8, act, 0)
        h3[...] += nn(zb[...], wdn[j])
        da[...] += nt(dub[...], wup[j])
        up = nn(a3t[...], dub[...]).astype(BF)
        for i in range(16):
            p3[i, pl.ds(mult(32 * j, 32), 32), :] = up[32 * i : 32 * i + 32]
        dw = nn(turn(zb[...]), g[...]).astype(BF)
        for i in range(4):
            p3[16 + 4 * j + i] = dw[128 * i : 128 * i + 128]
        after(j)
        return 0

    lax.fori_loop(0, 4, body, 0)


def middle_forward(half, s, cells, top, o1, wo1, w2, wo2, gains, scnt, fcnt, h1, h2, a2, qkv, o2, a3, g):
    gain2, gain3 = gains[1:2, :], gains[2:3, :]
    every = pl.ds(256 * half, 256)
    h1[every, :] = nn(o1[2 * half : 2 * half + 2].reshape(256, D), wo1[...])

    def first(r, _):
        rows = block(r)
        h = h1[rows, :] + flat(cells[r].astype(F32))
        h1[rows, :] = h
        x, _ = stats(h)
        a2[rows, :] = (x * gain2).astype(BF)
        n = lax.broadcasted_iota(jnp.int32, (128, 1), 0)
        live = (n // 32 < fcnt) & (128 * s + 32 * r + n % 32 < scnt)
        g[rows, :] = jnp.where(live, flat(top[r].astype(F32)), 0.0).astype(BF)
        return 0

    two_blocks(half, first)
    for j in range(3):
        qkv[j, every, :] = nn(a2[every, :], w2[j]).astype(BF)
    feature_forward(qkv, o2, fcnt, half)
    h2[every, :] = h1[every, :] + nn(o2[every, :], wo2[...])

    def second(r, _):
        rows = block(r)
        x, _ = stats(h2[rows, :])
        a3[rows, :] = (x * gain3).astype(BF)
        return 0

    two_blocks(half, second)


def layer_output(s, h3, lout, scnt, fcnt):
    def last(r, _):
        n = lax.broadcasted_iota(jnp.int32, (128, 1), 0)
        live = (n // 32 < fcnt) & (128 * s + 32 * r + n % 32 < scnt)
        lout[r] = cube(jnp.where(live, h3[block(r), :], 0.0).astype(BF))
        return 0

    four_blocks(last)


def feature_grads(half, wo1, w2, wo2, gains, fcnt, h1, h2, qkv, g, da, b2, b1, do, dqkv, do1, gr, dg2, dg3):
    gain2, gain3 = gains[1:2, :], gains[2:3, :]
    every = pl.ds(256 * half, 256)

    def third(r, dg):
        rows = block(r)
        dh, part = norm_grad(h2[rows, :], da[rows, :], gain3)
        total = g[rows, :].astype(F32) + dh
        gr[r] = cube(total)
        b2[rows, :] = total.astype(BF)
        return dg + part

    dg3 = two_blocks(half, third, dg3)
    do[every, :] = nt(b2[every, :], wo2[...]).astype(BF)
    feature_backward(qkv, do, dqkv, fcnt, half)
    da[every, :] = nt(dqkv[0, every, :], w2[0]) + nt(dqkv[1, every, :], w2[1]) + nt(dqkv[2, every, :], w2[2])

    def fourth(r, dg):
        rows = block(r)
        dh, part = norm_grad(h1[rows, :], da[rows, :], gain2)
        total = flat(gr[r]) + dh
        gr[r] = cube(total)
        b1[rows, :] = total.astype(BF)
        return dg + part

    dg2 = two_blocks(half, fourth, dg2)
    do1[2 * half : 2 * half + 2] = nt(b1[every, :], wo1[...]).astype(BF).reshape(2, 4, 32, D)
    return dg2, dg3


def feature_weights(o1, a2, o2, b2, b1, dqkv, wide, p2, dwo1):
    def weights(j, _):
        store_wide(wide, j, 3, nn(turn(a2[...]), dqkv[j]))
        return 0

    lax.fori_loop(0, 3, weights, 0)
    narrow_to(wide, p2, 24, 64)
    dw = nn(turn(o2[...]), b2[...]).astype(BF)
    for i in range(8):
        p2[24 + i] = dw[64 * i : 64 * i + 64]
    dwo1[...] = nn(turn(o1[...].reshape(512, D)), b1[...]).astype(BF)


class Reduce:
    def __init__(self, part, r1, ry, rx, ry2, rx2, rz, ssem, rsem, t, s, chunk=None):
        self.part, self.r1 = part, r1
        self.ry, self.rx, self.ry2, self.rx2, self.rz = ry, rx, ry2, rx2, rz
        rows, half = part.shape[1], part.shape[2] // 2
        if chunk is None:
            every = pl.ds(0, rows)
            self.ha, self.hb, self.all = [(every, pl.ds(o, n)) for o, n in ((0, half), (half, half), (0, 2 * half))]
        else:
            cols, half = pl.ds(128 * chunk, 128), rows // 2
            self.ha, self.hb, self.all = [(pl.ds(o, n), cols) for o, n in ((0, half), (half, half), (0, rows))]
        self.ssem, self.rsem, self.t, self.s = ssem, rsem, t, s
        self.copies = []

    def go(self, src, dst, peer):
        i = len(self.copies)
        copy = send(src, dst, self.ssem.at[i], self.rsem.at[i], peer)
        self.copies.append(copy)
        return copy

    def xor(self, e):
        return jnp.bitwise_xor(self.t, e)

    def group(self, e, box, t=None):
        t = self.t if t is None else t
        return self.part.at[pl.ds(4 * jnp.bitwise_xor(t, 2 * e), 4), *box]

    def core_copy(self, e):
        tc = self.xor(1)
        return pltpu.make_async_remote_copy(
            src_ref=self.group(e, self.all, tc), dst_ref=self.r1.at[e], send_sem=self.ssem.at[e],
            recv_sem=self.rsem.at[e], device_id=(tc, self.s), device_id_type=MESH,
        )

    def core(self, start=True):
        self.c = {e: self.core_copy(e) for e in (2, 3, 1, 0)}
        for copy in self.c.values():
            if start:
                copy.start()
            self.copies.append(copy)

    def add(self, e, box, got):
        base = 4 * self.xor(2 * e)
        for j in range(4):
            own = self.part[base + j, *box].astype(F32)
            self.part[base + j, *box] = (own + got[j].astype(F32)).astype(self.part.dtype)

    def one(self):
        ty, tx, s = self.xor(4), self.xor(2), self.s
        self.y, self.x = {}, {}
        for e in (2, 3, 1, 0):
            self.c[e].wait_recv()
            self.add(e, self.all, self.r1.at[e])
            if e in (2, 3):
                self.y[e - 2] = self.go(self.group(e, self.ha), self.ry.at[e - 2], (ty, s))
            if e in (3, 1):
                self.x[e // 2] = self.go(self.group(e, self.hb), self.rx.at[e // 2], (tx, s))

    def two(self):
        ty, tx, s = self.xor(4), self.xor(2), self.s
        self.y[1].wait_recv()
        self.add(1, self.ha, self.ry.at[1])
        self.x2 = self.go(self.group(1, self.ha), self.rx2, (tx, s))
        self.x[1].wait_recv()
        self.add(2, self.hb, self.rx.at[1])
        self.y2 = self.go(self.group(2, self.hb), self.ry2, (ty, s))
        self.y[0].wait_recv()
        self.add(0, self.ha, self.ry.at[0])
        self.x[0].wait_recv()
        self.add(0, self.hb, self.rx.at[0])

    def three(self):
        self.x2.wait_recv()
        self.add(0, self.ha, self.rx2)
        self.y2.wait_recv()
        self.add(0, self.hb, self.ry2)
        self.z = [self.z_send(1, 0), self.z_send(3, 1)]

    def z_send(self, slot, into):
        t, s = self.t, self.s
        to = jnp.bitwise_xor(s, 2 if into == 2 else 1)
        return self.go(self.part.at[4 * t + jnp.bitwise_xor(s, slot), *self.all], self.rz.at[into], (t, to))

    def four(self):
        self.z[1].wait_recv()
        mine = 4 * self.t + jnp.bitwise_xor(self.s, 2)
        own = self.part[mine, *self.all].astype(F32)
        self.part[mine, *self.all] = (own + self.rz[1, :, :].astype(F32)).astype(self.part.dtype)
        self.z.append(self.z_send(2, 2))

    def result(self):
        self.z[0].wait_recv()
        self.z[2].wait_recv()
        own = self.part[4 * self.t + self.s, *self.all].astype(F32)
        return own + self.rz[0, :, :].astype(F32) + self.rz[2, :, :].astype(F32)

    def drain(self):
        for copy in self.copies:
            copy.wait_send()


def edge_rows(part, edges, kind, lo=0, size=D):
    rows = part.shape[1]

    def body(i, _):
        row = part[i - 1, rows - 16 : rows, lo : lo + size].astype(F32)[15:16, :]
        edges[i, :, D * kind + lo : D * kind + lo + size] = row
        return 0

    lax.fori_loop(1, 32, body, 0)


def by_feature(x, out):
    for g in range(4):
        out[g] = jnp.transpose(x[32 * g : 32 * g + 32, :, :].astype(F32), (1, 0, 2)).astype(BF)


def to_rows(main, fl):
    rows = main.shape[0]
    for b in range(4):
        fl[pl.ds(4 + b, rows, stride=4), :] = main[:, 128 * b : 128 * b + 128]


def first_row(row, fl):
    for b in range(4):
        fl[b : b + 1, :] = row[:, 128 * b : 128 * b + 128]


def shifted(fl, d, total):
    q, p = d // 8, d % 8
    back = (128 - 16 * p) % 128
    lane = lax.broadcasted_iota(jnp.int32, (total, 128), 1)
    low = pltpu.roll(fl[pl.ds(q, total), :], back, 1)
    high = pltpu.roll(fl[pl.ds(q + 1, total), :], back, 1)
    return jnp.where(lane < 128 - 16 * p, low, high)


def to_shard(fl, rows, d, out_ref):
    total = out_ref.shape[0]
    fl[4 + 4 * rows : total + 8, :] = jnp.zeros((total + 4 - 4 * rows, 128), F32)
    out_ref[...] = shifted(fl, d, total)


def top_shard(fl, d, out_ref):
    out_ref[0:8, :] = shifted(fl, d, 8)


def early_core(red, j):
    tc = red.xor(1)

    def piece(group, rows):
        e = jnp.bitwise_xor(tc, group) // 2
        pltpu.make_async_remote_copy(
            src_ref=red.part.at[pl.ds(4 * group, 4), rows], dst_ref=red.r1.at[e, :, rows], send_sem=red.ssem.at[e],
            recv_sem=red.rsem.at[e], device_id=(tc, red.s), device_id_type=MESH,
        ).start()

    for k in (0, 2):
        piece(jnp.bitwise_xor(tc % 4, k), pl.ds(mult(32 * j, 32), 32))

    @pl.when(j % 2 == tc % 2)
    def _():
        piece(4 + j, pl.ds(0, 128))


class Refs:
    def __init__(self, names, refs):
        for name, ref in zip(names, refs, strict=True):
            setattr(self, name, ref)


def reduce_names(n):
    return [k + n for k in ("r1", "ry", "rx", "ry2", "rx2", "rz")]


def reduce_scratch(rows, width=D, kind=BF):
    half = width // 2
    return [
        pltpu.VMEM((4, 4, rows, width), kind), pltpu.VMEM((2, 4, rows, half), kind),
        pltpu.VMEM((2, 4, rows, half), kind), pltpu.VMEM((4, rows, half), kind), pltpu.VMEM((4, rows, half), kind),
        pltpu.VMEM((3, rows, width), kind),
    ]


def chunk_scratch(rows):
    half = rows // 2
    shapes = [(4, 4, rows), (2, 4, half), (2, 4, half), (4, half), (4, half), (3, rows)]
    return [pltpu.VMEM((*shape, 128), BF) for shape in shapes]


PARAMS = ["m1", "f1", "s1", "m2", "f2", "s2", "m3", "f3", "s3"]
WIDE = pltpu.VMEM((D, D), F32)
NARROW = pltpu.VMEM((D, D), BF)
THREE = pltpu.VMEM((3, D, D), BF)
FOUR = pltpu.VMEM((4, D, D), BF)
TILE = pltpu.VMEM((4, 4, 32, D), BF)
DMA = pltpu.SemaphoreType.DMA
SCRATCH = {
    "g1": pltpu.VMEM((32, 64, D), BF), "ge": pltpu.VMEM((32, 1, 3 * D), F32), "g2": pltpu.VMEM((32, 64, D), BF), "g3": pltpu.VMEM((32, 128, D), BF),
    "wide": pltpu.VMEM((4, 4 * D, 128), F32), "sh": pltpu.VMEM((536, 128), F32), "ro": pltpu.VMEM((536, 128), F32),
    "w1": THREE, "wo1": NARROW, "w2": THREE, "wo2": NARROW, "wup": FOUR, "wdn": FOUR,
    "gains": pltpu.VMEM((8, D), F32), "dgain": pltpu.VMEM((8, D), F32),
    "cells": TILE, "top": TILE, "cf": TILE, "a1": NARROW, "qkv1": THREE, "o1c": pltpu.VMEM((3, 4, 32, D), BF), "o1": TILE,
    "h1": WIDE, "h2": WIDE, "a2": NARROW, "qkv2": THREE, "o2": NARROW, "a3": NARROW, "at": NARROW, "g": NARROW,
    "h3": WIDE, "da": WIDE, "zb": NARROW, "dub": NARROW, "u": WIDE, "dz": NARROW, "b": NARROW, "b1": NARROW, "do2": NARROW,
    "dqkv": THREE, "gr": pltpu.VMEM((4, 4, 32, D), F32), "do1": TILE, "do": TILE, "dwo1": NARROW,
    "kt": pltpu.VMEM((128, D), BF), "dkv": pltpu.VMEM((2, D, 128), F32), "dhs": TILE, "dhr": TILE,
    **{k: v for h in range(4) for k, v in zip(reduce_names(f"a{h}"), chunk_scratch(64))},
    **dict(zip(reduce_names("b"), reduce_scratch(64))),
    **dict(zip(reduce_names("c"), reduce_scratch(128))),
    **dict(zip(reduce_names("d"), reduce_scratch(1, 3 * D, F32))),
    "fl1": pltpu.VMEM((272, 128), F32), "fl2": pltpu.VMEM((272, 128), F32), "fl3": pltpu.VMEM((528, 128), F32),
    "sums": pltpu.VMEM((32, 128), F32), "ts": pltpu.VMEM((8, 8, 128), F32), "zs": pltpu.VMEM((4, 8, 128), F32),
    "gs": DMA((4, 32)), "gq": DMA((4, 32)), "rs": DMA((7, 16)), "rq": DMA((7, 16)),
    "as1": DMA((3,)), "aq1": DMA((3,)), "as2": DMA((6,)), "aq2": DMA((6,)),
    "as3": DMA((6,)), "aq3": DMA((6,)), "as4": DMA((3,)), "aq4": DMA((3,)), "ns": DMA((10,)), "nq": DMA((10,)),
}
INPUTS = ["scnt", "fcnt", "cells_in", "top_in"] + PARAMS
OUTPUTS = ["lout", "cgrad", "sh1", "sh2", "sh3", "total"]


def kernel_m(*refs):
    r = Refs(INPUTS + OUTPUTS + list(SCRATCH), refs)
    t, s = here()
    d = 4 * t + s
    scnt, fcnt = r.scnt[0], r.fcnt[0]
    barrier = enter(t, s)
    ga, gb, gc, ge = [
        Gather(buf, r.gs.at[i], r.gq.at[i], t, s) for i, buf in enumerate((r.g1, r.g2, r.g3, r.ge))
    ]
    first1 = realign(r.m1, r.sh, d, 64, r.g1, d, r.ro)
    pl.semaphore_wait(barrier, 10)
    ga.start_z()
    ga.spread(0)
    first2 = realign(r.m2, r.sh, d, 64, r.g2, d, r.ro)
    first3 = realign(r.m3, r.sh, d, 128, r.g3, d, r.ro, True)
    r.ge[d] = jnp.concatenate([first1, first2, first3], 1).astype(BF).astype(F32)
    ge.start_z()
    ge.spread(0)
    gb.start_z()
    gb.spread(0)
    by_feature(r.cells_in, r.cells)
    r.cf[s] = r.cells[:, s, :, :]
    for one in (ge, ga):
        one.near(0)
        one.zin(2, 1)
    for one in (ge, ga):
        one.near(2, 1)
        one.zin(3)
    gc.start_z()
    gc.spread(0)
    moves = [
        send(r.cells.at[:, (s + k) % 4], r.cf.at[s], r.as1.at[k - 1], r.aq1.at[k - 1], (t, (s + k) % 4))
        for k in (1, 2, 3)
    ]
    for one in (ge, ga):
        one.near(3)
    by_feature(r.top_in, r.top)
    for one in (ge, ga):
        one.far()
    for one in (gb, gc):
        one.near(0)
        one.zin(2)
    gb.zin(1)
    ge.end()
    ga.end()
    gb.near(2)
    gb.zin(3)
    gc.zin(1)
    gb.near(1)
    spread(r.g1, r.ge, 0, 64, 0, 24, put_f32(r.wide, 64))
    split_columns(r.wide, 3, r.w1)
    spread(r.g1, r.ge, 0, 64, 24, 32, put_bf(r.wo1, 64))
    for copy in moves:
        copy.wait_recv()
    for k in range(3):
        r.gains[k : k + 1, :] = r.ge[0, :, D * k : D * k + D]
    gain1 = r.gains[0:1, :]

    def norm(i, _):
        x, _ = stats(r.cf[i].astype(F32).reshape(128, D))
        r.a1[block(i), :] = (x * gain1).astype(BF)
        return 0

    four_blocks(norm)

    def project(j, _):
        r.qkv1[j] = nn(r.a1[...], r.w1[j]).astype(BF)
        return 0

    lax.fori_loop(0, 3, project, 0)
    live = lax.broadcasted_iota(jnp.int32, (1, 512), 1) < scnt
    gb.near(3)
    gc.near(2)
    gc.zin(3)
    backs = ([], [])

    def give_back(k, half):
        two = pl.ds(2 * half, 2)
        at = 3 * half + k - 1
        peer = (t, (s + k) % 4)
        backs[half].append(send(r.o1c.at[k - 1, two], r.o1.at[two, s], r.as2.at[at], r.aq2.at[at], peer))

    for k in (2, 1, 3, 0):
        if k:
            attend_chunk(r.qkv1, (s + k) % 4, live, r.o1c.at[k - 1])
            give_back(k, 0)
        else:
            for j in (2, 1, 3):
                give_back(j, 1)
            attend_chunk(r.qkv1, s, live, r.o1.at[:, s])
        if k == 1:
            gb.far()
            gc.near(1)
    gb.end()
    spread(r.g2, r.ge, 1, 64, 0, 24, put_f32(r.wide, 64))
    split_columns(r.wide, 3, r.w2)
    spread(r.g2, r.ge, 1, 64, 24, 32, put_bf(r.wo2, 64))
    gc.near(3)
    for half in range(2):
        for copy in backs[half]:
            copy.wait_recv()
        middle_forward(
            half, s, r.cells, r.top, r.o1, r.wo1, r.w2, r.wo2, r.gains, scnt, fcnt, r.h1, r.h2, r.a2, r.qkv2, r.o2,
            r.a3, r.g,
        )
        if half == 0:
            gc.far()
    r.at[...] = turn(r.a3[...])
    gc.end()

    def put_up(i, head, last):
        block = jnp.concatenate([head, last], 0).astype(BF)
        for j in range(4):
            r.wup[j, pl.ds(mult(i * 32, 32), 32), :] = block[32 * j : 32 * j + 32]

    spread(r.g3, r.ge, 2, 128, 0, 16, put_up)

    def put_down(i, head, last):
        r.wdn[i // 4, pl.ds(mult((i % 4) * 128, 128), 128), :] = jnp.concatenate([head, last], 0).astype(BF)

    spread(r.g3, r.ge, 2, 128, 16, 32, put_down)
    for one in (ga, gb, gc, ge):
        one.drain()
    def reducer(n, part, i, chunk=None):
        bufs = [getattr(r, k) for k in reduce_names(n)]
        return Reduce(part, *bufs, r.rs.at[i], r.rq.at[i], t, s, chunk)

    sb, sc, sd = reducer("b", r.g2, 0), reducer("c", r.g3, 1), reducer("d", r.ge, 2)
    sa = [reducer(f"a{h}", r.g1, 3 + h, h) for h in range(4)]
    mlp(r.a3, r.at, r.g, r.h2, r.wup, r.wdn, r.h3, r.da, r.zb, r.dub, r.u, r.dz, r.g3, lambda j: early_core(sc, j))
    edge_rows(r.g3, r.ge, 2)

    sc.core(False)
    layer_output(s, r.h3, r.lout, scnt, fcnt)
    dg2 = dg3 = jnp.zeros((1, D), F32)
    moves2 = []
    for half in range(2):
        if half:
            sc.one()
        dg2, dg3 = feature_grads(
            half, r.wo1, r.w2, r.wo2, r.gains, fcnt, r.h1, r.h2, r.qkv2, r.g, r.da, r.b, r.b1, r.do2, r.dqkv, r.do1,
            r.gr, dg2, dg3,
        )
        two = pl.ds(2 * half, 2)
        for k in (1, 2, 3):
            at, f = 3 * half + k - 1, (s + k) % 4
            moves2.append(send(r.do1.at[two, f], r.do.at[s, two], r.as3.at[at], r.aq3.at[at], (t, f)))
    n = lax.broadcasted_iota(jnp.int32, (8, D), 0)
    r.dgain[...] = jnp.where(n == 1, dg2, jnp.where(n == 2, dg3, 0.0))
    feature_weights(r.o1, r.a2, r.o2, r.b, r.b1, r.dqkv, r.wide, r.g2, r.dwo1)
    edge_rows(r.g2, r.ge, 1)
    r.do[s] = r.do1[:, s, :, :]
    sb.core()
    r.at[...] = turn(r.a1[...])
    sb.one()
    for copy in moves2:
        copy.wait_recv()
    live = lax.broadcasted_iota(jnp.int32, (512, 1), 0) < scnt

    def copy_out(i, _):
        r.g1[24 + i] = r.dwo1[pl.ds(mult(i * 64, 64), 64), :]
        return 0

    lax.fori_loop(0, 8, copy_out, 0)

    def heads(h):
        backward_heads(h, r.qkv1, r.do, live, r.dqkv, r.kt, r.dkv)
        cols = slice(128 * h, 128 * h + 128)
        for j in range(3):
            r.wide[h, pl.ds(j, D, stride=3), :] = nn(r.at[...], r.dqkv[j, :, cols])

        def narrow(i, _):
            r.g1[i, :, cols] = r.wide[h, pl.ds(mult(i * 64, 64), 64), :].astype(BF)
            return 0

        lax.fori_loop(0, 24, narrow, 0)
        edge_rows(r.g1, r.ge, 0, 128 * h, 128)
        sa[h].core()

    heads(0)
    sc.two()
    heads(1)
    sa[0].one()
    sb.two()
    heads(2)
    sa[1].one()
    sa[0].two()
    heads(3)
    sc.three()
    r.da[...] = nt(r.dqkv[0], r.w1[0]) + nt(r.dqkv[1], r.w1[1]) + nt(r.dqkv[2], r.w1[2])
    sa[2].one()
    sa[1].two()
    sb.three()

    def norm_back(i, dg):
        dh, part = norm_grad(r.cf[i].astype(F32).reshape(128, D), r.da[block(i), :], gain1)
        r.dhs[i] = dh.astype(BF).reshape(4, 32, D)
        return dg + part

    dg = four_blocks(norm_back, jnp.zeros((1, D), F32))
    r.ge[0] = jnp.concatenate([dg, r.dgain[1:2, :], r.dgain[2:3, :]], 1)
    sd.core()
    sa[3].one()
    sa[0].three()
    sc.four()
    sa[2].two()
    sa[1].three()
    sd.one()
    sa[0].four()
    sa[3].two()
    sa[2].three()
    sa[1].four()
    sd.two()
    sb.four()
    sa[3].three()
    sa[2].four()
    sd.three()
    homes = [
        send(r.dhs.at[(s + k) % 4], r.dhr.at[:, s], r.as4.at[k - 1], r.aq4.at[k - 1], (t, (s + k) % 4))
        for k in (1, 2, 3)
    ]
    r.sums[...] = jnp.zeros((32, 128), F32)
    for fl in (r.fl2, r.fl3):
        fl[0:4, :] = jnp.zeros((4, 128), F32)
    main = sc.result()

    @pl.when(d < 16)
    def _():
        for j in range(4):
            for b in range(4):
                piece = main[32 * j : 32 * j + 32, 128 * b : 128 * b + 128]
                r.fl3[pl.ds(4 + b + 4 * j, 32, stride=16), :] = piece

    @pl.when(d >= 16)
    def _():
        to_rows(main, r.fl3)

    to_shard(r.fl3, 128, d, r.sh3)
    squares(r.sh3, r.m3, r.f3, r.s3, r.sums, d, 4 * D, 2, 1, 16)
    squares_tail(r.sh3, r.m3, r.f3, r.s3, r.sums, d, 4 * D, 2)
    sa[3].four()
    sd.four()
    to_rows(sb.result(), r.fl2)
    to_shard(r.fl2, 64, d, r.sh2)
    squares(r.sh2, r.m2, r.f2, r.s2, r.sums, d, 3 * D, 1, 1, 8)
    squares_tail(r.sh2, r.m2, r.f2, r.s2, r.sums, d, 3 * D, 1)
    for h in range(4):
        r.fl1[pl.ds(4 + h, 64, stride=4), :] = sa[h].result()
    first = sd.result()
    for k, fl in enumerate((r.fl1, r.fl2, r.fl3)):
        first_row(first[:, D * k : D * k + D], fl)
    to_shard(r.fl1, 64, d, r.sh1)
    top_shard(r.fl2, d, r.sh2)
    top_shard(r.fl3, d, r.sh3)
    squares(r.sh1, r.m1, r.f1, r.s1, r.sums, d, 3 * D, 0, 0, 8)
    squares_tail(r.sh1, r.m1, r.f1, r.s1, r.sums, d, 3 * D, 0)
    squares(r.sh2, r.m2, r.f2, r.s2, r.sums, d, 3 * D, 1, 0, 1)
    squares(r.sh3, r.m3, r.f3, r.s3, r.sums, d, 4 * D, 2, 0, 1)

    def finish_input():
        r.cgrad[:, s, :, :] = r.gr[:, s, :, :] + r.dhs[s].astype(F32)
        for k in (1, 2, 3):
            homes[k - 1].wait_recv()
            f = (s + 4 - k) % 4
            r.cgrad[:, f, :, :] = r.gr[:, f, :, :] + r.dhr[:, f, :, :].astype(F32)

    r.total[...], adds = sum_all(r.sums, r.ts, r.zs, r.ns, r.nq, t, s, finish_input)
    for one in (*sa, sb, sc, sd):
        one.drain()
    for copy in moves + backs[0] + backs[1] + moves2 + homes + adds:
        copy.wait_send()


def call_m(scnt, fcnt, cells, top, params, name="kernel_m"):
    sds = jax.ShapeDtypeStruct
    vm = pl.BlockSpec(memory_space=pltpu.VMEM)
    sm = pl.BlockSpec(memory_space=pltpu.SMEM)
    return pl.pallas_call(
        kernel_m,
        name=name,
        out_shape=(
            sds((4, 4, 32, D), BF), sds((4, 4, 32, D), F32), sds((264, 128), F32), sds((264, 128), F32),
            sds((520, 128), F32), sds((8, 128), F32),
        ),
        in_specs=[sm, sm] + [vm] * 11,
        out_specs=(vm,) * 6,
        scratch_shapes=list(SCRATCH.values()),
        compiler_params=pltpu.CompilerParams(collective_id=1, has_side_effects=True, vmem_limit_bytes=63 << 20),
    )(scnt, fcnt, cells, top, *params)


def fast_device(cells, out_grad, scnt, fcnt, b1, f1, s1, b2, f2, s2, b3, f3, s3):
    params = (b1, f1, s1, b2, f2, s2, b3, f3, s3)
    out, cgrad, sh1, sh2, sh3, total = call_m(scnt, fcnt, cells[0], out_grad[0], params)
    *outs, pairs, out, cgrad = call_e(total, (sh1, sh2, sh3), params, out, cgrad)
    return (out[None], cgrad[None], *outs, pairs.T)


def step(*args):
    cells = args[0]
    fits = lax.axis_size("task") == 8 and lax.axis_size("samp") == 4 and cells.shape == (1, 128, 4, D)
    return fast_device(*args) if fits else on_device(*args)


def solution(mesh):
    placed = (
        P("task", "samp", None, None),
        P("task", "samp", None, None),
        P("task"),
        P("task"),
        P(("task", "samp")),
        P(("task", "samp")),
        P(("task", "samp")),
        P(("task", "samp")),
        P(("task", "samp")),
        P(("task", "samp")),
        P(("task", "samp")),
        P(("task", "samp")),
        P(("task", "samp")),
    )
    return jax.shard_map(
        step,
        mesh=mesh,
        in_specs=placed,
        out_specs=(
            P("task", "samp", None, None),
            P("task", "samp", None, None),
            P(("task", "samp")),
            P(("task", "samp")),
            P(("task", "samp")),
            P(("task", "samp")),
            P(("task", "samp")),
            P(("task", "samp")),
            P(("task", "samp")),
            P(("task", "samp")),
            P(("task", "samp")),
            P(("task", "samp")),
            P(("task", "samp")),
            P(("task", "samp")),
            P(("task", "samp")),
            P(("task", "samp")),
            P(("task", "samp")),
            P(),
        ),
        check_vma=False,
    )
```

```python
import jax
import jax.numpy as jnp
from jax import lax
from jax.experimental import pallas as pl
from jax.experimental.pallas import tpu as pltpu
from jax.sharding import PartitionSpec as P

D = 512
HEADS = 8
HEAD_DIM = 64
FF = 2048


EPS_NORM = 1e-05
EPS_ADAM = 1e-06
STEP_RATE = 0.5
BIG_NEGATIVE = -1e30


def normalize(hidden, gain_row):
    centre = jnp.mean(hidden, -1, keepdims=True)
    shifted = hidden - centre
    spread = jnp.mean(shifted * shifted, -1, keepdims=True)
    return shifted * lax.rsqrt(spread + EPS_NORM) * gain_row


def norm_backward(hidden, gain_row, normed_grad):
    _, pullback = jax.vjp(normalize, hidden, gain_row)
    return pullback(normed_grad)


def gelu_exact(upward):
    return jax.nn.gelu(upward, approximate=False)


def contract_rows(left, right):
    return lax.dot_general(
        left, right, (((0,), (0,)), ((), ())), preferred_element_type=jnp.float32
    )


def times_transpose(left, right):
    return lax.dot_general(
        left, right, (((1,), (1,)), ((), ())), preferred_element_type=jnp.float32
    )


def unpack(flat_params, width_in, width_mid):
    gain_row = flat_params[:D].astype(jnp.float32)
    w_in = flat_params[D : D + D * width_in].reshape(D, width_in)
    w_out = flat_params[D + D * width_in :].reshape(width_mid, D)
    return (gain_row, w_in, w_out)


def fetch_forward(master):
    return lax.all_gather(master.astype(jnp.bfloat16), ("task", "samp"), axis=0, tiled=True)


def fetch_again(master):
    return lax.all_gather(master.astype(jnp.bfloat16), ("task", "samp"), axis=0, tiled=True)


def reduce_grads(gain_grad, in_grad, out_grad_matrix):
    flat_grads = jnp.concatenate([gain_grad, in_grad.reshape(-1), out_grad_matrix.reshape(-1)])
    return lax.psum_scatter(flat_grads, ("task", "samp"), scatter_dimension=0, tiled=True)


def group_size(feature_total, most):
    chosen = 1
    for candidate in range(1, most + 1):
        if feature_total % candidate == 0:
            chosen = candidate
    return chosen


def lamb_prepare(grad_shard, master, first, second, width_in):
    first_new = 0.5 * first + 0.5 * grad_shard
    second_new = 0.5 * second + 0.5 * grad_shard * grad_shard
    direction = first_new / (jnp.sqrt(second_new) + EPS_ADAM)
    entries = master.shape[0]
    position = lax.axis_index(("task", "samp")) * entries + jnp.arange(entries, dtype=jnp.int32)
    segment = (position >= D).astype(jnp.int32) + (position >= D + D * width_in).astype(jnp.int32)
    member = segment[None, :] == jnp.arange(3, dtype=jnp.int32)[:, None]
    weight_sums = jnp.sum(jnp.where(member, (master * master)[None, :], 0.0), 1)
    update_sums = jnp.sum(jnp.where(member, (direction * direction)[None, :], 0.0), 1)
    return (first_new, second_new, direction, member, jnp.stack([weight_sums, update_sums], 1))


def lamb_finish(master, block_state, trust_ratio):
    factor = jnp.sum(jnp.where(block_state[3], trust_ratio[:, None], 0.0), 0)
    return master - STEP_RATE * factor * block_state[2]


def sample_scores(query_part, key_part, key_live, score_scale):
    scores = (
        jnp.einsum("qfhe,kfhe->fhqk", query_part, key_part, preferred_element_type=jnp.float32)
        * score_scale
    )
    return jnp.where(key_live, scores, BIG_NEGATIVE)


def sample_forward(queries, pairs_all, key_live, block_features, score_scale):
    local_rows, features = (queries.shape[0], queries.shape[1])

    def one_block(block_index, results):
        attended, log_totals = results
        offset = block_index * block_features
        query_part = lax.dynamic_slice_in_dim(queries, offset, block_features, 1)
        pair_part = lax.dynamic_slice_in_dim(pairs_all, offset, block_features, 1)
        scores = sample_scores(query_part, pair_part[:, :, 0], key_live, score_scale)
        row_top = jnp.max(scores, -1, keepdims=True)
        exponent = jnp.exp(scores - row_top)
        row_total = jnp.sum(exponent, -1, keepdims=True)
        probability = (exponent / row_total).astype(jnp.bfloat16)
        block_out = jnp.einsum(
            "fhqk,kfhe->qfhe", probability, pair_part[:, :, 1], preferred_element_type=jnp.float32
        )
        attended = lax.dynamic_update_slice_in_dim(
            attended, block_out.astype(jnp.bfloat16), offset, 1
        )
        log_totals = lax.dynamic_update_slice_in_dim(
            log_totals, (row_top + jnp.log(row_total))[..., 0], offset, 0
        )
        return (attended, log_totals)

    start_state = (
        jnp.zeros(queries.shape, jnp.bfloat16),
        jnp.zeros((features, HEADS, local_rows), jnp.float32),
    )
    return lax.fori_loop(0, features // block_features, one_block, start_state)


def query_side(query_part, pair_part, grad_part, log_part, key_live, score_scale):
    key_part = pair_part[:, :, 0]
    value_part = pair_part[:, :, 1]
    scores = sample_scores(query_part, key_part, key_live, score_scale)
    probability = jnp.exp(scores - log_part[..., None])
    prob_grad = jnp.einsum(
        "qfhe,kfhe->fhqk", grad_part, value_part, preferred_element_type=jnp.float32
    )
    row_inner = jnp.sum(probability * prob_grad, -1, keepdims=True)
    score_grad = (probability * (prob_grad - row_inner)).astype(jnp.bfloat16)
    query_block = (
        jnp.einsum("fhqk,kfhe->qfhe", score_grad, key_part, preferred_element_type=jnp.float32)
        * score_scale
    )
    return (probability, score_grad, row_inner, query_block)


def sample_backward(
    queries, pairs_all, key_live, log_totals, attended_grad, block_features, score_scale
):
    local_rows, features = (queries.shape[0], queries.shape[1])

    def one_block(block_index, results):
        query_grads, pair_grads = results
        offset = block_index * block_features
        query_part = lax.dynamic_slice_in_dim(queries, offset, block_features, 1)
        pair_part = lax.dynamic_slice_in_dim(pairs_all, offset, block_features, 1)
        grad_part = lax.dynamic_slice_in_dim(attended_grad, offset, block_features, 1)
        log_part = lax.dynamic_slice_in_dim(log_totals, offset, block_features, 0)
        probability, score_grad, row_inner, query_block = query_side(
            query_part, pair_part, grad_part, log_part, key_live, score_scale
        )
        key_block = (
            jnp.einsum(
                "fhqk,qfhe->kfhe", score_grad, query_part, preferred_element_type=jnp.float32
            )
            * score_scale
        )
        value_block = jnp.einsum(
            "fhqk,qfhe->kfhe",
            probability.astype(jnp.bfloat16),
            grad_part,
            preferred_element_type=jnp.float32,
        )
        pair_terms = jnp.stack([key_block, value_block], 2)
        pair_local = lax.psum_scatter(
            pair_terms.astype(jnp.bfloat16), "samp", scatter_dimension=0, tiled=True
        ).astype(jnp.float32)
        query_grads = lax.dynamic_update_slice_in_dim(query_grads, query_block, offset, 1)
        pair_grads = lax.dynamic_update_slice_in_dim(pair_grads, pair_local, offset, 1)
        return (query_grads, pair_grads)

    start_state = (
        jnp.zeros((local_rows, features, HEADS, HEAD_DIM), jnp.float32),
        jnp.zeros((local_rows, features, 2, HEADS, HEAD_DIM), jnp.float32),
    )
    return lax.fori_loop(0, features // block_features, one_block, start_state)


def on_device(
    cells,
    out_grad,
    sample_counts,
    feature_counts,
    sample_block,
    sample_first,
    sample_second,
    feature_block,
    feature_first,
    feature_second,
    mlp_block,
    mlp_first,
    mlp_second,
):
    local_rows, features = (cells.shape[1], cells.shape[2])
    flat_rows = local_rows * features
    seq_all = local_rows * lax.axis_size("samp")
    score_scale = HEAD_DIM ** (-0.5)
    block_features = group_size(features, max(1, 2048 // (HEADS * local_rows)))
    sample_index = lax.axis_index("samp") * local_rows + jnp.arange(local_rows, dtype=jnp.int32)
    sample_live = sample_index < sample_counts[0]
    key_live = jnp.arange(seq_all, dtype=jnp.int32) < sample_counts[0]
    feature_live = jnp.arange(features, dtype=jnp.int32) < feature_counts[0]
    cell_live = sample_live[:, None, None] & feature_live[None, :, None]
    hidden_in = cells[0].astype(jnp.float32)
    gain_one, in_one, out_one = unpack(fetch_forward(sample_block), 3 * D, D)
    normed_one = normalize(hidden_in, gain_one).astype(jnp.bfloat16)
    packed_one = jnp.dot(
        normed_one.reshape(flat_rows, D), in_one, preferred_element_type=jnp.float32
    )
    packed_one = packed_one.astype(jnp.bfloat16).reshape(local_rows, features, 3, HEADS, HEAD_DIM)
    queries_one = packed_one[:, :, 0]
    pairs_local = packed_one[:, :, 1:]
    pairs_all = lax.all_gather(pairs_local, "samp", axis=0, tiled=True)
    attended_one, log_totals = sample_forward(
        queries_one, pairs_all, key_live, block_features, score_scale
    )
    attended_one_rows = attended_one.reshape(flat_rows, D)
    branch_one = jnp.dot(attended_one_rows, out_one, preferred_element_type=jnp.float32)
    hidden_one = hidden_in + branch_one.reshape(local_rows, features, D)
    gain_two, in_two, out_two = unpack(fetch_forward(feature_block), 3 * D, D)
    normed_two = normalize(hidden_one, gain_two).astype(jnp.bfloat16).reshape(flat_rows, D)
    packed_two = jnp.dot(normed_two, in_two, preferred_element_type=jnp.float32)
    packed_two = packed_two.astype(jnp.bfloat16).reshape(local_rows, features, 3, HEADS, HEAD_DIM)
    queries_two, key_two, value_two = (
        packed_two[:, :, 0],
        packed_two[:, :, 1],
        packed_two[:, :, 2],
    )
    scores_two = (
        jnp.einsum("sqhe,skhe->shqk", queries_two, key_two, preferred_element_type=jnp.float32)
        * score_scale
    )
    scores_two = jnp.where(feature_live, scores_two, BIG_NEGATIVE)
    row_top = jnp.max(scores_two, -1, keepdims=True)
    exponent = jnp.exp(scores_two - row_top)
    probability_two = exponent / jnp.sum(exponent, -1, keepdims=True)
    prob_low_two = probability_two.astype(jnp.bfloat16)
    attended_two = jnp.einsum(
        "shqk,skhe->sqhe", prob_low_two, value_two, preferred_element_type=jnp.float32
    )
    attended_two_rows = attended_two.reshape(flat_rows, D).astype(jnp.bfloat16)
    branch_two = jnp.dot(attended_two_rows, out_two, preferred_element_type=jnp.float32)
    hidden_two = hidden_one + branch_two.reshape(local_rows, features, D)
    gain_three, up_weight, down_weight = unpack(fetch_forward(mlp_block), FF, FF)
    normed_three = normalize(hidden_two, gain_three).astype(jnp.bfloat16).reshape(flat_rows, D)
    upward = jnp.dot(normed_three, up_weight, preferred_element_type=jnp.float32)
    activated = gelu_exact(upward).astype(jnp.bfloat16)
    branch_three = jnp.dot(activated, down_weight, preferred_element_type=jnp.float32)
    hidden_three = hidden_two + branch_three.reshape(local_rows, features, D)
    layer_out = jnp.where(cell_live, hidden_three, 0.0).astype(jnp.bfloat16)[None]
    top_grad = jnp.where(cell_live, out_grad[0], jnp.zeros((), jnp.bfloat16))
    top_rows = top_grad.reshape(flat_rows, D)
    gain_three, up_weight, down_weight = unpack(fetch_again(mlp_block), FF, FF)
    down_grad = contract_rows(activated, top_rows)
    act_grad = times_transpose(top_rows, down_weight).astype(jnp.bfloat16)
    _, gelu_pull = jax.vjp(gelu_exact, upward)
    up_grad = gelu_pull(act_grad.astype(jnp.float32))[0].astype(jnp.bfloat16)
    upw_grad = contract_rows(normed_three, up_grad)
    normed_grad = times_transpose(up_grad, up_weight).reshape(local_rows, features, D)
    hidden_grad, gain_three_grad = norm_backward(hidden_two, gain_three, normed_grad)
    grad_two = top_grad.astype(jnp.float32) + hidden_grad
    mlp_shard = reduce_grads(gain_three_grad, upw_grad, down_grad)
    mlp_state = lamb_prepare(mlp_shard, mlp_block, mlp_first, mlp_second, FF)
    gain_two, in_two, out_two = unpack(fetch_again(feature_block), 3 * D, D)
    branch_grad = grad_two.astype(jnp.bfloat16).reshape(flat_rows, D)
    out_two_grad = contract_rows(attended_two_rows, branch_grad)
    attended_grad = (
        times_transpose(branch_grad, out_two)
        .astype(jnp.bfloat16)
        .reshape(local_rows, features, HEADS, HEAD_DIM)
    )
    prob_grad = jnp.einsum(
        "sqhe,skhe->shqk", attended_grad, value_two, preferred_element_type=jnp.float32
    )
    row_inner = jnp.sum(probability_two * prob_grad, -1, keepdims=True)
    score_grad = (probability_two * (prob_grad - row_inner)).astype(jnp.bfloat16)
    query_grad = (
        jnp.einsum("shqk,skhe->sqhe", score_grad, key_two, preferred_element_type=jnp.float32)
        * score_scale
    )
    key_grad = (
        jnp.einsum("shqk,sqhe->skhe", score_grad, queries_two, preferred_element_type=jnp.float32)
        * score_scale
    )
    value_grad = jnp.einsum(
        "shqk,sqhe->skhe", prob_low_two, attended_grad, preferred_element_type=jnp.float32
    )
    packed_grad = (
        jnp.stack([query_grad, key_grad, value_grad], 2)
        .astype(jnp.bfloat16)
        .reshape(flat_rows, 3 * D)
    )
    in_two_grad = contract_rows(normed_two, packed_grad)
    normed_grad = times_transpose(packed_grad, in_two).reshape(local_rows, features, D)
    hidden_grad, gain_two_grad = norm_backward(hidden_one, gain_two, normed_grad)
    grad_one = grad_two + hidden_grad
    feature_shard = reduce_grads(gain_two_grad, in_two_grad, out_two_grad)
    feature_state = lamb_prepare(feature_shard, feature_block, feature_first, feature_second, 3 * D)
    gain_one, in_one, out_one = unpack(fetch_again(sample_block), 3 * D, D)
    pairs_all = lax.all_gather(pairs_local, "samp", axis=0, tiled=True)
    branch_grad = grad_one.astype(jnp.bfloat16).reshape(flat_rows, D)
    out_one_grad = contract_rows(attended_one_rows, branch_grad)
    attended_grad = (
        times_transpose(branch_grad, out_one)
        .astype(jnp.bfloat16)
        .reshape(local_rows, features, HEADS, HEAD_DIM)
    )
    query_grads, pair_grads = sample_backward(
        queries_one, pairs_all, key_live, log_totals, attended_grad, block_features, score_scale
    )
    packed_grad = (
        jnp.concatenate([query_grads[:, :, None], pair_grads], 2)
        .astype(jnp.bfloat16)
        .reshape(flat_rows, 3 * D)
    )
    in_one_grad = contract_rows(normed_one.reshape(flat_rows, D), packed_grad)
    normed_grad = times_transpose(packed_grad, in_one).reshape(local_rows, features, D)
    hidden_grad, gain_one_grad = norm_backward(hidden_in, gain_one, normed_grad)
    cells_grad = (grad_one + hidden_grad)[None]
    sample_shard = reduce_grads(gain_one_grad, in_one_grad, out_one_grad)
    sample_state = lamb_prepare(sample_shard, sample_block, sample_first, sample_second, 3 * D)
    totals = lax.psum(
        jnp.concatenate([sample_state[4], feature_state[4], mlp_state[4]], 0), ("task", "samp")
    )
    norm_pairs = jnp.sqrt(totals)
    trust_ratio = norm_pairs[:, 0] / (norm_pairs[:, 1] + EPS_ADAM)
    sample_master = lamb_finish(sample_block, sample_state, trust_ratio[0:3])
    feature_master = lamb_finish(feature_block, feature_state, trust_ratio[3:6])
    mlp_master = lamb_finish(mlp_block, mlp_state, trust_ratio[6:9])
    return (
        layer_out,
        cells_grad,
        sample_shard,
        sample_state[0],
        sample_state[1],
        sample_master,
        sample_master.astype(jnp.bfloat16),
        feature_shard,
        feature_state[0],
        feature_state[1],
        feature_master,
        feature_master.astype(jnp.bfloat16),
        mlp_shard,
        mlp_state[0],
        mlp_state[1],
        mlp_master,
        mlp_master.astype(jnp.bfloat16),
        norm_pairs,
    )


D = 512
MESH = pl.DeviceIdType.MESH
BF = jnp.bfloat16
F32 = jnp.float32
NEG = -1e30


def mult(value, factor):
    return value if isinstance(value, int) else pl.multiple_of(value, factor)


def repeat(lo, hi, body, ways):
    def step(i, _):
        for k in range(ways):
            body(lo + i * ways + k)
        return 0

    lax.fori_loop(0, (hi - lo) // ways, step, 0)


def nt(left, right):
    return lax.dot_general(left, right, (((1,), (1,)), ((), ())), preferred_element_type=F32)


def nn(left, right):
    return lax.dot_general(left, right, (((1,), (0,)), ((), ())), preferred_element_type=F32)


def here():
    return lax.axis_index("task"), lax.axis_index("samp")


def peers(t, s):
    return [(jnp.bitwise_xor(t, e), s) for e in range(1, 8)] + [(t, jnp.bitwise_xor(s, e)) for e in (1, 2, 3)]


def enter(t, s):
    barrier = pltpu.get_barrier_semaphore()
    for peer in peers(t, s):
        pl.semaphore_signal(barrier, inc=1, device_id=peer, device_id_type=MESH)
    return barrier


def send(src, dst, ssem, rsem, peer):
    copy = pltpu.make_async_remote_copy(
        src_ref=src, dst_ref=dst, send_sem=ssem, recv_sem=rsem, device_id=peer, device_id_type=MESH
    )
    copy.start()
    return copy


class Gather:
    def __init__(self, buf, ssem, rsem, t, s):
        self.buf, self.t, self.s = buf, t, s
        half = buf.shape[2] // 2
        self.ha, self.hb, self.all = pl.ds(0, half), pl.ds(half, half), pl.ds(0, 2 * half)
        self.rows = pl.ds(0, buf.shape[1])
        self.ssem, self.rsem = ssem, rsem
        self.moves = []
        self.tx, self.ty = jnp.bitwise_xor(t, 2), jnp.bitwise_xor(t, 4)
        self.txy, self.tc = jnp.bitwise_xor(t, 6), jnp.bitwise_xor(t, 1)
        self.hops, self.sent = {}, {k: {} for k in ("x", "y", "c", "xy", "yx", "cx", "cy")}

    def z(self, key):
        return jnp.bitwise_xor(self.s, key)

    def go(self, slots, cols, peer):
        view = self.buf.at[slots, self.rows, cols]
        i = len(self.moves)
        copy = send(view, view, self.ssem.at[i], self.rsem.at[i], peer)
        self.moves.append(copy)
        return copy

    def pass_on(self, kind, key, t, cols, to):
        self.sent[kind][key] = self.go(pl.ds(4 * t + self.z(key), 1), cols, (to, self.s))

    def spread(self, key):
        self.pass_on("x", key, self.t, self.all, self.tx)
        self.pass_on("y", key, self.t, self.all, self.ty)
        self.pass_on("c", key, self.t, self.all, self.tc)

    def hop(self, key, slot, to):
        self.hops[key] = self.go(pl.ds(4 * self.t + self.z(slot), 1), self.all, (self.t, self.z(to)))

    def start_z(self):
        self.hop(2, 0, 2)
        self.hop(1, 0, 1)

    def zin(self, *keys):
        for key in keys:
            self.hops[key].wait_recv()
            if key == 2:
                self.hop(3, 2, 1)
            self.spread(key)

    def near(self, *keys):
        for key in keys:
            self.sent["x"][key].wait_recv()
            self.pass_on("xy", key, self.tx, self.ha, self.ty)
            self.pass_on("cx", key, self.tx, self.all, self.tc)
            self.sent["y"][key].wait_recv()
            self.pass_on("yx", key, self.ty, self.hb, self.tx)
            self.pass_on("cy", key, self.ty, self.all, self.tc)

    def far(self):
        for kind in ("xy", "yx"):
            for copy in self.sent[kind].values():
                copy.wait_recv()
        self.last = self.go(pl.ds(4 * self.txy, 4), self.all, (self.tc, self.s))

    def end(self):
        for kind in ("c", "cx", "cy"):
            for copy in self.sent[kind].values():
                copy.wait_recv()
        self.last.wait_recv()

    def drain(self):
        for copy in self.moves:
            copy.wait_send()


def realign(m_ref, sh_ref, d, rows, out_ref, out_at, roll_to, split=False):
    whole = 4 * rows
    total = whole + 8
    q, p = d // 8, d % 8
    lane = lax.broadcasted_iota(jnp.int32, (total, 128), 1)
    roll_to[0:8, :] = jnp.zeros((8, 128), F32)
    for i in range(whole // 8):
        sh_ref[8 * i : 8 * i + 8, :] = m_ref[pl.ds(1024 * i, 1024)].reshape(8, 128)
    sh_ref[whole:total, :] = jnp.zeros((8, 128), F32)
    sh_ref[whole : whole + 1, 0:16] = m_ref[pl.ds(128 * whole, 16)].reshape(1, 16)
    rolled = pltpu.roll(sh_ref[0:total, :], 16 * p, 1)
    roll_to[8 : 8 + total, :] = rolled
    sh_ref[0:8, :] = jnp.zeros((8, 128), F32)
    sh_ref[8 : 8 + total, :] = jnp.where(lane < 16 * p, roll_to[7 : 7 + total, :], rolled)
    firsts = []

    def straight():
        for b in range(4):
            cols = slice(128 * b, 128 * b + 128)
            out_ref[out_at, 0:rows, cols] = sh_ref[pl.ds(12 - q + b, rows, stride=4), :].astype(BF)

    def by_piece():
        for b in range(4):
            cols = slice(128 * b, 128 * b + 128)
            for j in range(4):
                piece = sh_ref[pl.ds(12 - q + b + 4 * j, rows // 4, stride=16), :]
                out_ref[out_at, rows // 4 * j : rows // 4 * (j + 1), cols] = piece.astype(BF)

    if split:
        pl.when(d < 16)(by_piece)
        pl.when(d >= 16)(straight)
    else:
        straight()
    for b in range(4):
        firsts.append(sh_ref[pl.ds(8 - q + b, 1), :])
    return jnp.concatenate(firsts, 1)


def spread(buf, firsts, kind, rows, lo, hi, put):
    tail = lax.broadcasted_iota(jnp.int32, (8, D), 0) == 7

    def body(i):
        nxt = jnp.minimum(i + 1, 31)
        row = firsts[nxt, :, D * kind : D * kind + D]
        block = buf[i, 0:rows, :].astype(F32)
        last = block[rows - 8 : rows, :] + jnp.where(tail & (i < 31), row, 0.0)
        put(i - lo, block[0 : rows - 8, :], last)

    repeat(lo, hi, body, 4 if rows == 64 else 2)


def put_f32(dst, rows):
    def put(i, head, last):
        for b in range(4):
            cols = slice(128 * b, 128 * b + 128)
            dst[b, pl.ds(mult(i * rows, rows), rows - 8), :] = head[:, cols]
            dst[b, pl.ds(mult(i * rows + rows - 8, 8), 8), :] = last[:, cols]

    return put


def put_bf(dst, rows):
    def put(i, head, last):
        dst[pl.ds(mult(i * rows, rows), rows), :] = jnp.concatenate([head, last], 0).astype(BF)

    return put


def split_columns(wide, ways, dst):
    def body(i):
        for j in range(ways):
            for b in range(4):
                piece = wide[b, pl.ds(64 * ways * i + j, 64, stride=ways), :]
                dst[j, pl.ds(mult(64 * i, 64), 64), 128 * b : 128 * b + 128] = piece.astype(BF)

    repeat(0, 8, body, 2)


def halves():
    lane = lax.broadcasted_iota(jnp.int32, (128, 128), 1)
    return lane < 64


def two_heads(x, one, two):
    return jnp.concatenate([x * one, x * two], 0)


def soft(scores, axis):
    e = [jnp.exp(x - jnp.max(x, axis, keepdims=True)) for x in scores]
    return [x * (1.0 / jnp.sum(x, axis, keepdims=True)) for x in e]


def attend_chunk(qkv, c, live, out):
    left = halves()
    one = jnp.where(left, 0.125, 0.0).astype(BF)
    two = jnp.where(left, 0.0, 0.125).astype(BF)
    rows = pl.ds(mult(c * 128, 128), 128)

    def body(h, _):
        cols = [pl.ds(128 * i, 128) for i in range(4)]
        scores = [jnp.where(live, nt(two_heads(qkv[0, rows, w], one, two), qkv[1, :, w]), NEG) for w in cols]
        prob = [p.astype(BF) for p in soft(scores, 1)]
        outs = [nn(p, qkv[2, :, w]) for p, w in zip(prob, cols)]
        for o, w in zip(outs, cols):
            o = jnp.where(left, o[0:128], o[128:256]).astype(BF)
            for g in range(4):
                out[g, :, w] = o[32 * g : 32 * g + 32]
        return 0

    body(0, 0)


def edges(d, entries, width):
    begin = d * entries
    return D - begin, D + D * width - begin


def segment(k, ends):
    return (k >= ends[0]).astype(jnp.int32) + (k >= ends[1]).astype(jnp.int32)


def lamb_step(g, m, f, s):
    fn = 0.5 * f + 0.5 * g
    sn = 0.5 * s + 0.5 * g * g
    return fn, sn, fn / (jnp.sqrt(sn) + 1e-6)


def flat_index():
    rows = lax.broadcasted_iota(jnp.int32, (32, 128), 0)
    return rows * 128 + lax.broadcasted_iota(jnp.int32, (32, 128), 1)


def fold(x):
    return x.reshape(-1, 8, 128).sum(0)


def squares(sh, m, f, s, sums, d, width, b, lo, hi):
    entries = m.shape[0]
    ends = edges(d, entries, width)
    index = flat_index()

    def body(i, acc):
        at = pl.ds(mult(i * 4096, 4096), 4096)
        old = m[at].reshape(32, 128)
        _, _, r = lamb_step(sh[pl.ds(mult(i * 32, 32), 32), :], old, f[at].reshape(32, 128), s[at].reshape(32, 128))
        part = segment(index + i * 4096, ends)
        out = []
        for n, value in enumerate((old * old, r * r)):
            for k in range(3):
                out.append(acc[3 * n + k] + fold(jnp.where(part == k, value, 0.0)))
        return tuple(out)

    acc = lax.fori_loop(lo, hi, body, (jnp.zeros((8, 128), F32),) * 6)
    for n in range(2):
        for k in range(3):
            row = 16 * n + 3 * b + k
            sums[row : row + 1, :] += jnp.sum(acc[3 * n + k], 0, keepdims=True)


def squares_tail(sh, m, f, s, sums, d, width, b):
    entries = m.shape[0]
    base = entries - 16
    ends = edges(d, entries, width)
    at = pl.ds(base, 16)
    old = m[at].reshape(1, 16)
    row = base // 128
    _, _, r = lamb_step(sh[row : row + 1, 0:16], old, f[at].reshape(1, 16), s[at].reshape(1, 16))
    part = segment(lax.broadcasted_iota(jnp.int32, (1, 16), 1) + base, ends)
    for n, value in enumerate((old * old, r * r)):
        for k in range(3):
            row = 16 * n + 3 * b + k
            sums[row : row + 1, 0:16] += jnp.where(part == k, value, 0.0)


def update(sh, m, f, s, grad, fout, sout, mout, wout, ratio, d, width, b):
    entries = m.shape[0]
    whole = entries // 4096
    ends = edges(d, entries, width)
    half = [0.5 * ratio[3 * b + k : 3 * b + k + 1, :] for k in range(3)]

    def put(at, g, part, shape):
        old = m[at].reshape(shape)
        fn, sn, r = lamb_step(g, old, f[at].reshape(shape), s[at].reshape(shape))
        factor = jnp.where(part == 0, half[0], jnp.where(part == 1, half[1], half[2]))
        new = (old - factor * r).reshape(-1)
        grad[at] = g.reshape(-1)
        fout[at] = fn.reshape(-1)
        sout[at] = sn.reshape(-1)
        mout[at] = new
        wout[at] = new.astype(BF)

    index = flat_index()

    def body(i, _):
        at = pl.ds(mult(i * 4096, 4096), 4096)
        put(at, sh[pl.ds(mult(i * 32, 32), 32), :], segment(index + i * 4096, ends), (32, 128))
        return 0

    lax.fori_loop(0, whole, body, 0)
    part = segment(lax.broadcasted_iota(jnp.int32, (1, 16), 1) + whole * 4096, ends)
    put(pl.ds(whole * 4096, 16), sh[32 * whole : 32 * whole + 1, 0:16], part, (1, 16))


def diagonal(rows):
    lane = lax.broadcasted_iota(jnp.int32, (32, 128), 1)
    return lane == lax.broadcasted_iota(jnp.int32, (32, 128), 0)


def sum_all(sums, ts, zs, ssem, rsem, t, s, meanwhile):
    column = jnp.sum(sums[...], 1, keepdims=True)
    ts[t] = jnp.broadcast_to(jnp.sum(jnp.where(diagonal(32), column, 0.0), 0, keepdims=True), (8, 128))
    plane = [
        send(ts.at[t], ts.at[t], ssem.at[e - 1], rsem.at[e - 1], (jnp.bitwise_xor(t, e), s)) for e in range(1, 8)
    ]
    meanwhile()
    for copy in plane:
        copy.wait_recv()
    zs[s] = ((ts[0] + ts[1]) + (ts[2] + ts[3])) + ((ts[4] + ts[5]) + (ts[6] + ts[7]))
    last = [
        send(zs.at[s], zs.at[s], ssem.at[6 + e], rsem.at[6 + e], (t, jnp.bitwise_xor(s, e))) for e in (1, 2, 3)
    ]
    for copy in last:
        copy.wait_recv()
    return (zs[0] + zs[1]) + (zs[2] + zs[3]), plane + last


def by_sample(x, out):
    for g in range(4):
        out[32 * g : 32 * g + 32, :, :] = jnp.transpose(x[g].astype(F32), (1, 0, 2)).astype(out.dtype)


def kernel_e(*refs):
    ins, outs, vin, vout, sin, sout = refs[:15], refs[15:33], refs[33:48], refs[48:66], refs[66], refs[67]
    t, s = here()
    d = 4 * t + s
    loads = [pltpu.make_async_copy(a, b, sin.at[i]) for i, (a, b) in enumerate(zip(ins, vin))]
    stores = [pltpu.make_async_copy(a, b, sout.at[i]) for i, (a, b) in enumerate(zip(vout, outs))]
    order = [0, 1, 4, 5, 6, 2, 7, 8, 9, 3, 10, 11, 12, 13, 14]
    for i in order:
        loads[i].start()
    loads[0].wait()
    norms = jnp.sqrt(vin[0][0:1, :])
    vout[15][0:1, :] = norms[:, 0:9]
    vout[15][1:2, :] = pltpu.roll(norms, 112, 1)[:, 0:9]
    stores[15].start()
    norm = jnp.sum(jnp.where(diagonal(32), norms, 0.0), 1, keepdims=True)
    ratio = norm[0:9] / (norm[16:25] + 1e-6)
    for b in range(3):
        used = [1 + b, 4 + 3 * b, 5 + 3 * b, 6 + 3 * b]
        for i in used:
            loads[i].wait()
        width = 4 * D if b == 2 else 3 * D
        update(*[vin[i] for i in used], *vout[5 * b : 5 * b + 5], ratio, d, width, b)
        for i in range(5 * b, 5 * b + 5):
            stores[i].start()
    for i in (13, 14):
        loads[i].wait()
        by_sample(vin[i], vout[i + 3])
        stores[i + 3].start()
    for copy in stores:
        copy.wait()


def call_e(total, shards, args, lout, cgrad):
    sds = jax.ShapeDtypeStruct
    hb = pl.BlockSpec(memory_space=pl.ANY)
    shapes = []
    for m in args[0::3]:
        n = m.shape
        shapes += [sds(n, F32)] * 4 + [sds(n, BF)]
    shapes += [sds((2, 9), F32), sds((128, 4, D), BF), sds((128, 4, D), F32)]
    given = (total, *shards, *args, lout, cgrad)
    return pl.pallas_call(
        kernel_e,
        name="kernel_e",
        out_shape=tuple(shapes),
        in_specs=[hb] * 15,
        out_specs=(hb,) * 18,
        scratch_shapes=[pltpu.VMEM(x.shape, x.dtype) for x in (*given, *shapes)]
        + [pltpu.SemaphoreType.DMA((15,)), pltpu.SemaphoreType.DMA((18,))],
        compiler_params=pltpu.CompilerParams(vmem_limit_bytes=63 << 20),
    )(*given)


def backward_heads(h, qkv, do, live, dqkv, kt, dkv):
    left = halves()
    one, two = jnp.where(left, 1.0, 0.0).astype(BF), jnp.where(left, 0.0, 1.0).astype(BF)
    cols = pl.ds(mult(h * 128, 128), 128)
    kt[...] = jnp.transpose(qkv[1, :, cols])
    top_lane = lax.broadcasted_iota(jnp.int32, (128, 128), 0) < 64

    def chunk(n, _):
        each = [0, 1, 2, 3]
        rows = [pl.ds(c * 128, 128) for c in each]
        qm = [two_heads(qkv[0, r, cols] * jnp.asarray(0.125, BF), one, two) for r in rows]
        gm = [two_heads(do[c, :, :, cols].reshape(128, 128), one, two) for c in each]
        prob = soft([jnp.where(live, nt(qkv[1, :, cols], q), NEG) for q in qm], 0)
        pg = [nt(qkv[2, :, cols], g) for g in gm]
        sg = [(p * (x - jnp.sum(p * x, 0, keepdims=True))).astype(BF) for p, x in zip(prob, pg)]
        dqkv[1, :, cols] = (nn(sg[0], qm[0]) + nn(sg[1], qm[1]) + nn(sg[2], qm[2]) + nn(sg[3], qm[3])).astype(BF)
        pb = [p.astype(BF) for p in prob]
        dqkv[2, :, cols] = (nn(pb[0], gm[0]) + nn(pb[1], gm[1]) + nn(pb[2], gm[2]) + nn(pb[3], gm[3])).astype(BF)
        for r, x in zip(rows, sg):
            dqt = nn(kt[...], x)
            dq = jnp.transpose(jnp.where(top_lane, dqt[:, 0:128], dqt[:, 128:256])) * 0.125
            dqkv[0, r, cols] = dq.astype(BF)
        return 0

    chunk(0, 0)


def turn(x):
    return jnp.transpose(x)


def stats(h):
    x = h - jnp.mean(h, 1, keepdims=True)
    rstd = lax.rsqrt(jnp.mean(x * x, 1, keepdims=True) + 1e-5)
    return x * rstd, rstd


def norm_grad(h, da, gain):
    x, rstd = stats(h)
    dgain = jnp.sum(da * x, 0, keepdims=True)
    dx = da * gain
    dh = rstd * (dx - jnp.mean(dx, 1, keepdims=True) - x * jnp.mean(dx * x, 1, keepdims=True))
    return dh, dgain


def block(g):
    return pl.ds(mult(g * 128, 128), 128)


def feature_mask(fcnt, axis):
    shape = (256, 128) if axis else (128, 256)
    query = lax.broadcasted_iota(jnp.int32, shape, 1 - axis)
    key = lax.broadcasted_iota(jnp.int32, shape, axis)
    return (query % 32 == key % 32) & (key // 32 < fcnt)


def feature_forward(qkv, o2, fcnt, half):
    left = halves()
    one = jnp.where(left, 0.125, 0.0).astype(BF)
    two = jnp.where(left, 0.0, 0.125).astype(BF)
    ok = feature_mask(fcnt, 1)
    cols = [slice(128 * h, 128 * h + 128) for h in range(4)]

    def body(n, _):
        rows = block(n)
        scores = [
            jnp.where(ok, nt(two_heads(qkv[0, rows, c], one, two), qkv[1, rows, c]), NEG) for c in cols
        ]
        prob = [p.astype(BF) for p in soft(scores, 1)]
        out = [nn(p, qkv[2, rows, c]) for p, c in zip(prob, cols)]
        for o, c in zip(out, cols):
            o2[rows, c] = jnp.where(left, o[0:128], o[128:256]).astype(BF)
        return 0

    lax.fori_loop(2 * half, 2 * half + 2, body, 0)


def feature_backward(qkv, do, dqkv, fcnt, half):
    left = halves()
    one, two = jnp.where(left, 1.0, 0.0).astype(BF), jnp.where(left, 0.0, 1.0).astype(BF)
    ok = feature_mask(fcnt, 0)
    top_lane = lax.broadcasted_iota(jnp.int32, (128, 128), 0) < 64
    cols = [slice(128 * h, 128 * h + 128) for h in range(4)]

    def body(n, _):
        rows = block(n)
        qm = [two_heads(qkv[0, rows, c] * jnp.asarray(0.125, BF), one, two) for c in cols]
        gm = [two_heads(do[rows, c], one, two) for c in cols]
        prob = soft([jnp.where(ok, nt(qkv[1, rows, c], q), NEG) for c, q in zip(cols, qm)], 0)
        pg = [nt(qkv[2, rows, c], g) for c, g in zip(cols, gm)]
        sg = [(p * (x - jnp.sum(p * x, 0, keepdims=True))).astype(BF) for p, x in zip(prob, pg)]
        dqt = [nn(turn(qkv[1, rows, c]), x) for c, x in zip(cols, sg)]
        dk = [nn(x, q).astype(BF) for x, q in zip(sg, qm)]
        dv = [nn(p.astype(BF), g).astype(BF) for p, g in zip(prob, gm)]
        dq = [turn(jnp.where(top_lane, x[:, 0:128], x[:, 128:256])) * 0.125 for x in dqt]
        for i, c in enumerate(cols):
            dqkv[0, rows, c] = dq[i].astype(BF)
            dqkv[1, rows, c] = dk[i]
            dqkv[2, rows, c] = dv[i]
        return 0

    lax.fori_loop(2 * half, 2 * half + 2, body, 0)


def four_blocks(body, init=0):
    for r in range(4):
        init = body(r, init)
    return init


def two_blocks(half, body, init=0):
    for r in (2 * half, 2 * half + 1):
        init = body(r, init)
    return init


def flat(x):
    return x.reshape(128, D)


def cube(x):
    return x.reshape(4, 32, D)


def narrow_to(wide, part, slots, rows):
    def body(i):
        at = pl.ds(mult(i * rows, rows), rows)
        for b in range(4):
            part[i, :, 128 * b : 128 * b + 128] = wide[b, at, :].astype(BF)

    repeat(0, slots, body, 2)


def store_wide(wide, j, ways, value):
    for b in range(4):
        wide[b, pl.ds(j, value.shape[0], stride=ways), :] = value[:, 128 * b : 128 * b + 128]


def mlp(a3, a3t, g, h2, wup, wdn, h3, da, zb, dub, u, dz, p3, after):
    def act(rows):
        x = u[rows, :]
        cdf = 0.5 * (1.0 + lax.erf(x * 0.7071067811865476))
        zb[rows, :] = (x * cdf).astype(BF)
        slope = cdf + x * (0.3989422804014327 * jnp.exp(-0.5 * x * x))
        dub[rows, :] = (slope * dz[rows, :].astype(F32)).astype(BF)

    h3[...] = h2[...]
    da[...] = jnp.zeros((512, D), F32)

    def body(j, _):
        u[...] = nn(a3[...], wup[j])
        dz[...] = nt(g[...], wdn[j]).astype(BF)
        for n in range(2):
            rows = slice(256 * n, 256 * n + 256)
            act(rows)
            h3[rows, :] += nn(zb[rows, :], wdn[j])
            da[rows, :] += nt(dub[rows, :], wup[j])
        up = nn(a3t[...], dub[...]).astype(BF)
        for i in range(16):
            p3[i, pl.ds(mult(32 * j, 32), 32), :] = up[32 * i : 32 * i + 32]
        dw = nn(turn(zb[...]), g[...]).astype(BF)
        for i in range(4):
            p3[16 + 4 * j + i] = dw[128 * i : 128 * i + 128]
        after(j)
        return 0

    lax.fori_loop(0, 4, body, 0)


def middle_forward(half, s, cells, top, o1, wo1, w2, wo2, gains, scnt, fcnt, h1, h2, a2, qkv, o2, a3, g):
    gain2, gain3 = gains[1:2, :], gains[2:3, :]
    every = pl.ds(256 * half, 256)
    h1[every, :] = nn(o1[2 * half : 2 * half + 2].reshape(256, D), wo1[...])

    def first(r, _):
        rows = block(r)
        h = h1[rows, :] + flat(cells[r].astype(F32))
        h1[rows, :] = h
        x, _ = stats(h)
        a2[rows, :] = (x * gain2).astype(BF)
        n = lax.broadcasted_iota(jnp.int32, (128, 1), 0)
        live = (n // 32 < fcnt) & (128 * s + 32 * r + n % 32 < scnt)
        g[rows, :] = jnp.where(live, flat(top[r].astype(F32)), 0.0).astype(BF)
        return 0

    two_blocks(half, first)
    for j in range(3):
        qkv[j, every, :] = nn(a2[every, :], w2[j]).astype(BF)
    feature_forward(qkv, o2, fcnt, half)
    h2[every, :] = h1[every, :] + nn(o2[every, :], wo2[...])

    def second(r, _):
        rows = block(r)
        x, _ = stats(h2[rows, :])
        a3[rows, :] = (x * gain3).astype(BF)
        return 0

    two_blocks(half, second)


def layer_output(s, h3, lout, scnt, fcnt):
    def last(r, _):
        n = lax.broadcasted_iota(jnp.int32, (128, 1), 0)
        live = (n // 32 < fcnt) & (128 * s + 32 * r + n % 32 < scnt)
        lout[r] = cube(jnp.where(live, h3[block(r), :], 0.0).astype(BF))
        return 0

    four_blocks(last)


def feature_grads(half, wo1, w2, wo2, gains, fcnt, h1, h2, qkv, g, da, b2, b1, do, dqkv, do1, gr, dg2, dg3):
    gain2, gain3 = gains[1:2, :], gains[2:3, :]
    every = pl.ds(256 * half, 256)

    def third(r, dg):
        rows = block(r)
        dh, part = norm_grad(h2[rows, :], da[rows, :], gain3)
        total = g[rows, :].astype(F32) + dh
        gr[r] = cube(total)
        b2[rows, :] = total.astype(BF)
        return dg + part

    dg3 = two_blocks(half, third, dg3)
    do[every, :] = nt(b2[every, :], wo2[...]).astype(BF)
    feature_backward(qkv, do, dqkv, fcnt, half)
    da[every, :] = nt(dqkv[0, every, :], w2[0]) + nt(dqkv[1, every, :], w2[1]) + nt(dqkv[2, every, :], w2[2])

    def fourth(r, dg):
        rows = block(r)
        dh, part = norm_grad(h1[rows, :], da[rows, :], gain2)
        total = flat(gr[r]) + dh
        gr[r] = cube(total)
        b1[rows, :] = total.astype(BF)
        return dg + part

    dg2 = two_blocks(half, fourth, dg2)
    do1[2 * half : 2 * half + 2] = nt(b1[every, :], wo1[...]).astype(BF).reshape(2, 4, 32, D)
    return dg2, dg3


def feature_weights(o1, a2, o2, b2, b1, dqkv, wide, p2, dwo1):
    def weights(j, _):
        store_wide(wide, j, 3, nn(turn(a2[...]), dqkv[j]))
        return 0

    lax.fori_loop(0, 3, weights, 0)
    narrow_to(wide, p2, 24, 64)
    dw = nn(turn(o2[...]), b2[...]).astype(BF)
    for i in range(8):
        p2[24 + i] = dw[64 * i : 64 * i + 64]
    dwo1[...] = nn(turn(o1[...].reshape(512, D)), b1[...]).astype(BF)


class Reduce:
    def __init__(self, part, r1, ry, rx, ry2, rx2, rz, ssem, rsem, t, s, chunk=None):
        self.part, self.r1 = part, r1
        self.ry, self.rx, self.ry2, self.rx2, self.rz = ry, rx, ry2, rx2, rz
        rows, half = part.shape[1], part.shape[2] // 2
        if chunk is None:
            every = pl.ds(0, rows)
            self.ha, self.hb, self.all = [(every, pl.ds(o, n)) for o, n in ((0, half), (half, half), (0, 2 * half))]
        else:
            cols, half = pl.ds(128 * chunk, 128), rows // 2
            self.ha, self.hb, self.all = [(pl.ds(o, n), cols) for o, n in ((0, half), (half, half), (0, rows))]
        self.ssem, self.rsem, self.t, self.s = ssem, rsem, t, s
        self.copies = []

    def go(self, src, dst, peer):
        i = len(self.copies)
        copy = send(src, dst, self.ssem.at[i], self.rsem.at[i], peer)
        self.copies.append(copy)
        return copy

    def xor(self, e):
        return jnp.bitwise_xor(self.t, e)

    def group(self, e, box, t=None):
        t = self.t if t is None else t
        return self.part.at[pl.ds(4 * jnp.bitwise_xor(t, 2 * e), 4), *box]

    def core_copy(self, e):
        tc = self.xor(1)
        return pltpu.make_async_remote_copy(
            src_ref=self.group(e, self.all, tc), dst_ref=self.r1.at[e], send_sem=self.ssem.at[e],
            recv_sem=self.rsem.at[e], device_id=(tc, self.s), device_id_type=MESH,
        )

    def core(self, start=True):
        self.c = {e: self.core_copy(e) for e in (2, 3, 1, 0)}
        for copy in self.c.values():
            if start:
                copy.start()
            self.copies.append(copy)

    def add(self, e, box, got):
        base = 4 * self.xor(2 * e)
        for j in range(4):
            own = self.part[base + j, *box].astype(F32)
            self.part[base + j, *box] = (own + got[j].astype(F32)).astype(self.part.dtype)

    def one(self):
        ty, tx, s = self.xor(4), self.xor(2), self.s
        self.y, self.x = {}, {}
        for e in (2, 3, 1, 0):
            self.c[e].wait_recv()
            self.add(e, self.all, self.r1.at[e])
            if e in (2, 3):
                self.y[e - 2] = self.go(self.group(e, self.ha), self.ry.at[e - 2], (ty, s))
            if e in (3, 1):
                self.x[e // 2] = self.go(self.group(e, self.hb), self.rx.at[e // 2], (tx, s))

    def two(self):
        ty, tx, s = self.xor(4), self.xor(2), self.s
        self.y[1].wait_recv()
        self.add(1, self.ha, self.ry.at[1])
        self.x2 = self.go(self.group(1, self.ha), self.rx2, (tx, s))
        self.x[1].wait_recv()
        self.add(2, self.hb, self.rx.at[1])
        self.y2 = self.go(self.group(2, self.hb), self.ry2, (ty, s))
        self.y[0].wait_recv()
        self.add(0, self.ha, self.ry.at[0])
        self.x[0].wait_recv()
        self.add(0, self.hb, self.rx.at[0])

    def three(self):
        self.x2.wait_recv()
        self.add(0, self.ha, self.rx2)
        self.y2.wait_recv()
        self.add(0, self.hb, self.ry2)
        self.z = [self.z_send(1, 0), self.z_send(3, 1)]

    def z_send(self, slot, into):
        t, s = self.t, self.s
        to = jnp.bitwise_xor(s, 2 if into == 2 else 1)
        return self.go(self.part.at[4 * t + jnp.bitwise_xor(s, slot), *self.all], self.rz.at[into], (t, to))

    def four(self):
        self.z[1].wait_recv()
        mine = 4 * self.t + jnp.bitwise_xor(self.s, 2)
        own = self.part[mine, *self.all].astype(F32)
        self.part[mine, *self.all] = (own + self.rz[1, :, :].astype(F32)).astype(self.part.dtype)
        self.z.append(self.z_send(2, 2))

    def result(self):
        self.z[0].wait_recv()
        self.z[2].wait_recv()
        own = self.part[4 * self.t + self.s, *self.all].astype(F32)
        return own + self.rz[0, :, :].astype(F32) + self.rz[2, :, :].astype(F32)

    def drain(self):
        for copy in self.copies:
            copy.wait_send()


def edge_rows(part, edges, kind, lo=0, size=D):
    rows = part.shape[1]

    for i in range(1, 32):
        row = part[i - 1, rows - 16 : rows, lo : lo + size].astype(F32)[15:16, :]
        edges[i, :, D * kind + lo : D * kind + lo + size] = row


def by_feature(x, out):
    for g in range(4):
        out[g] = jnp.transpose(x[32 * g : 32 * g + 32, :, :].astype(F32), (1, 0, 2)).astype(BF)


def to_rows(main, fl):
    rows = main.shape[0]
    for b in range(4):
        fl[pl.ds(4 + b, rows, stride=4), :] = main[:, 128 * b : 128 * b + 128]


def first_row(row, fl):
    for b in range(4):
        fl[b : b + 1, :] = row[:, 128 * b : 128 * b + 128]


def shifted(fl, d, total):
    q, p = d // 8, d % 8
    back = (128 - 16 * p) % 128
    lane = lax.broadcasted_iota(jnp.int32, (total, 128), 1)
    low = pltpu.roll(fl[pl.ds(q, total), :], back, 1)
    high = pltpu.roll(fl[pl.ds(q + 1, total), :], back, 1)
    return jnp.where(lane < 128 - 16 * p, low, high)


def to_shard(fl, rows, d, out_ref):
    total = out_ref.shape[0]
    fl[4 + 4 * rows : total + 8, :] = jnp.zeros((total + 4 - 4 * rows, 128), F32)
    out_ref[...] = shifted(fl, d, total)


def top_shard(fl, d, out_ref):
    out_ref[0:8, :] = shifted(fl, d, 8)


def early_core(red, j):
    tc = red.xor(1)

    def piece(group, rows):
        e = jnp.bitwise_xor(tc, group) // 2
        pltpu.make_async_remote_copy(
            src_ref=red.part.at[pl.ds(4 * group, 4), rows], dst_ref=red.r1.at[e, :, rows], send_sem=red.ssem.at[e],
            recv_sem=red.rsem.at[e], device_id=(tc, red.s), device_id_type=MESH,
        ).start()

    for k in (0, 2):
        piece(jnp.bitwise_xor(tc % 4, k), pl.ds(mult(32 * j, 32), 32))

    @pl.when(j % 2 == tc % 2)
    def _():
        piece(4 + j, pl.ds(0, 128))


class Refs:
    def __init__(self, names, refs):
        for name, ref in zip(names, refs, strict=True):
            setattr(self, name, ref)


def reduce_names(n):
    return [k + n for k in ("r1", "ry", "rx", "ry2", "rx2", "rz")]


def reduce_scratch(rows, width=D, kind=BF):
    half = width // 2
    return [
        pltpu.VMEM((4, 4, rows, width), kind), pltpu.VMEM((2, 4, rows, half), kind),
        pltpu.VMEM((2, 4, rows, half), kind), pltpu.VMEM((4, rows, half), kind), pltpu.VMEM((4, rows, half), kind),
        pltpu.VMEM((3, rows, width), kind),
    ]


def chunk_scratch(rows):
    half = rows // 2
    shapes = [(4, 4, rows), (2, 4, half), (2, 4, half), (4, half), (4, half), (3, rows)]
    return [pltpu.VMEM((*shape, 128), BF) for shape in shapes]


PARAMS = ["m1", "f1", "s1", "m2", "f2", "s2", "m3", "f3", "s3"]
WIDE = pltpu.VMEM((D, D), F32)
NARROW = pltpu.VMEM((D, D), BF)
THREE = pltpu.VMEM((3, D, D), BF)
FOUR = pltpu.VMEM((4, D, D), BF)
TILE = pltpu.VMEM((4, 4, 32, D), BF)
DMA = pltpu.SemaphoreType.DMA
SCRATCH = {
    "cells_in": pltpu.VMEM((128, 4, D), BF), "top_in": pltpu.VMEM((128, 4, D), BF),
    **{k + n: pltpu.VMEM((size,), F32) for n, size in (("1", 32784), ("2", 32784), ("3", 65552)) for k in "mfs"},
    "lout": TILE, "cgrad": pltpu.VMEM((4, 4, 32, D), F32), "sh1": pltpu.VMEM((264, 128), F32),
    "sh2": pltpu.VMEM((264, 128), F32), "sh3": pltpu.VMEM((520, 128), F32), "total": pltpu.VMEM((8, 128), F32),
    "ls": DMA((11,)), "os": DMA((6,)),
    "g1": pltpu.VMEM((32, 64, D), BF), "ge": pltpu.VMEM((32, 1, 3 * D), F32), "g2": pltpu.VMEM((32, 64, D), BF), "g3": pltpu.VMEM((32, 128, D), BF),
    "wide": pltpu.VMEM((4, 4 * D, 128), F32), "sh": pltpu.VMEM((536, 128), F32), "ro": pltpu.VMEM((536, 128), F32),
    "w1": THREE, "wo1": NARROW, "w2": THREE, "wo2": NARROW, "wup": FOUR, "wdn": FOUR,
    "gains": pltpu.VMEM((8, D), F32), "dgain": pltpu.VMEM((8, D), F32),
    "cells": TILE, "top": TILE, "cf": TILE, "a1": NARROW, "qkv1": THREE, "o1c": pltpu.VMEM((3, 4, 32, D), BF), "o1": TILE,
    "h1": WIDE, "h2": WIDE, "a2": NARROW, "qkv2": THREE, "o2": NARROW, "a3": NARROW, "at": NARROW, "g": NARROW,
    "h3": WIDE, "da": WIDE, "zb": NARROW, "dub": NARROW, "u": WIDE, "dz": NARROW, "b": NARROW, "b1": NARROW, "do2": NARROW,
    "dqkv": THREE, "gr": pltpu.VMEM((4, 4, 32, D), F32), "do1": TILE, "do": TILE, "dwo1": NARROW,
    "kt": pltpu.VMEM((128, D), BF), "dkv": pltpu.VMEM((2, D, 128), F32), "dhs": TILE, "dhr": TILE,
    **{k: v for h in range(4) for k, v in zip(reduce_names(f"a{h}"), chunk_scratch(64))},
    **dict(zip(reduce_names("b"), reduce_scratch(64))),
    **dict(zip(reduce_names("c"), reduce_scratch(128))),
    **dict(zip(reduce_names("d"), reduce_scratch(1, 3 * D, F32))),
    "fl1": pltpu.VMEM((272, 128), F32), "fl2": pltpu.VMEM((272, 128), F32), "fl3": pltpu.VMEM((528, 128), F32),
    "sums": pltpu.VMEM((32, 128), F32), "ts": pltpu.VMEM((8, 8, 128), F32), "zs": pltpu.VMEM((4, 8, 128), F32),
    "gs": DMA((4, 32)), "gq": DMA((4, 32)), "rs": DMA((7, 16)), "rq": DMA((7, 16)),
    "as1": DMA((3,)), "aq1": DMA((3,)), "as2": DMA((6,)), "aq2": DMA((6,)),
    "as3": DMA((6,)), "aq3": DMA((6,)), "as4": DMA((3,)), "aq4": DMA((3,)), "ns": DMA((10,)), "nq": DMA((10,)),
}
LOADED = ["m1", "cells_in", "m2", "m3", "top_in", "f3", "s3", "f2", "s2", "f1", "s1"]
INPUTS = ["scnt", "fcnt", "cells_any", "top_any"] + [k + "_any" for k in PARAMS]
STORED = ["lout", "cgrad", "sh1", "sh2", "sh3", "total"]
OUTPUTS = [k + "_any" for k in STORED]


def kernel_m(*refs):
    r = Refs(INPUTS + OUTPUTS + list(SCRATCH), refs)
    t, s = here()
    d = 4 * t + s
    scnt, fcnt = r.scnt[0], r.fcnt[0]
    barrier = enter(t, s)
    loads, stores = {}, []
    for i, name in enumerate(LOADED):
        source = name.replace("_in", "") + "_any"
        loads[name] = pltpu.make_async_copy(getattr(r, source), getattr(r, name), r.ls.at[i])
        loads[name].start()

    def store(name):
        i = STORED.index(name)
        copy = pltpu.make_async_copy(getattr(r, name), getattr(r, name + "_any"), r.os.at[i])
        copy.start()
        stores.append(copy)

    def params(n):
        loads["f" + n].wait()
        loads["s" + n].wait()

    loads["m1"].wait()
    ga, gb, gc, ge = [
        Gather(buf, r.gs.at[i], r.gq.at[i], t, s) for i, buf in enumerate((r.g1, r.g2, r.g3, r.ge))
    ]
    first1 = realign(r.m1, r.sh, d, 64, r.g1, d, r.ro)
    pl.semaphore_wait(barrier, 10)
    ga.start_z()
    ga.spread(0)
    loads["m2"].wait()
    loads["m3"].wait()
    first2 = realign(r.m2, r.sh, d, 64, r.g2, d, r.ro)
    first3 = realign(r.m3, r.sh, d, 128, r.g3, d, r.ro, True)
    r.ge[d] = jnp.concatenate([first1, first2, first3], 1).astype(BF).astype(F32)
    ge.start_z()
    ge.spread(0)
    gb.start_z()
    gb.spread(0)
    loads["cells_in"].wait()
    by_feature(r.cells_in, r.cells)
    r.cf[s] = r.cells[:, s, :, :]
    for one in (ge, ga):
        one.near(0)
        one.zin(2, 1)
    for one in (ge, ga):
        one.near(2, 1)
        one.zin(3)
    gc.start_z()
    gc.spread(0)
    moves = [
        send(r.cells.at[:, (s + k) % 4], r.cf.at[s], r.as1.at[k - 1], r.aq1.at[k - 1], (t, (s + k) % 4))
        for k in (1, 2, 3)
    ]
    for one in (ge, ga):
        one.near(3)
    loads["top_in"].wait()
    by_feature(r.top_in, r.top)
    for one in (ge, ga):
        one.far()
    for one in (gb, gc):
        one.near(0)
        one.zin(2)
    gb.zin(1)
    ge.end()
    ga.end()
    gb.near(2)
    gb.zin(3)
    gc.zin(1)
    gb.near(1)
    spread(r.g1, r.ge, 0, 64, 0, 24, put_f32(r.wide, 64))
    split_columns(r.wide, 3, r.w1)
    spread(r.g1, r.ge, 0, 64, 24, 32, put_bf(r.wo1, 64))
    for copy in moves:
        copy.wait_recv()
    for k in range(3):
        r.gains[k : k + 1, :] = r.ge[0, :, D * k : D * k + D]
    gain1 = r.gains[0:1, :]

    def norm(i, _):
        x, _ = stats(r.cf[i].astype(F32).reshape(128, D))
        r.a1[block(i), :] = (x * gain1).astype(BF)
        return 0

    four_blocks(norm)

    def project(j, _):
        r.qkv1[j] = nn(r.a1[...], r.w1[j]).astype(BF)
        return 0

    lax.fori_loop(0, 3, project, 0)
    live = lax.broadcasted_iota(jnp.int32, (1, 512), 1) < scnt
    gb.near(3)
    gc.near(2)
    gc.zin(3)
    backs = ([], [])

    def give_back(k, half):
        two = pl.ds(2 * half, 2)
        at = 3 * half + k - 1
        peer = (t, (s + k) % 4)
        backs[half].append(send(r.o1c.at[k - 1, two], r.o1.at[two, s], r.as2.at[at], r.aq2.at[at], peer))

    for k in (2, 1, 3, 0):
        if k:
            attend_chunk(r.qkv1, (s + k) % 4, live, r.o1c.at[k - 1])
            give_back(k, 0)
        else:
            for j in (2, 1, 3):
                give_back(j, 1)
            attend_chunk(r.qkv1, s, live, r.o1.at[:, s])
        if k == 1:
            gb.far()
            gc.near(1)
    gb.end()
    spread(r.g2, r.ge, 1, 64, 0, 24, put_f32(r.wide, 64))
    split_columns(r.wide, 3, r.w2)
    spread(r.g2, r.ge, 1, 64, 24, 32, put_bf(r.wo2, 64))
    gc.near(3)
    for half in range(2):
        for copy in backs[half]:
            copy.wait_recv()
        middle_forward(
            half, s, r.cells, r.top, r.o1, r.wo1, r.w2, r.wo2, r.gains, scnt, fcnt, r.h1, r.h2, r.a2, r.qkv2, r.o2,
            r.a3, r.g,
        )
        if half == 0:
            gc.far()
    r.at[...] = turn(r.a3[...])
    gc.end()

    def put_up(i, head, last):
        block = jnp.concatenate([head, last], 0).astype(BF)
        for j in range(4):
            r.wup[j, pl.ds(mult(i * 32, 32), 32), :] = block[32 * j : 32 * j + 32]

    spread(r.g3, r.ge, 2, 128, 0, 16, put_up)

    def put_down(i, head, last):
        r.wdn[i // 4, pl.ds(mult((i % 4) * 128, 128), 128), :] = jnp.concatenate([head, last], 0).astype(BF)

    spread(r.g3, r.ge, 2, 128, 16, 32, put_down)
    for one in (ga, gb, gc, ge):
        one.drain()
    def reducer(n, part, i, chunk=None):
        bufs = [getattr(r, k) for k in reduce_names(n)]
        return Reduce(part, *bufs, r.rs.at[i], r.rq.at[i], t, s, chunk)

    sb, sc, sd = reducer("b", r.g2, 0), reducer("c", r.g3, 1), reducer("d", r.ge, 2)
    sa = [reducer(f"a{h}", r.g1, 3 + h, h) for h in range(4)]
    mlp(r.a3, r.at, r.g, r.h2, r.wup, r.wdn, r.h3, r.da, r.zb, r.dub, r.u, r.dz, r.g3, lambda j: early_core(sc, j))
    edge_rows(r.g3, r.ge, 2)

    sc.core(False)
    layer_output(s, r.h3, r.lout, scnt, fcnt)
    store("lout")
    dg2 = dg3 = jnp.zeros((1, D), F32)
    moves2 = []
    for half in range(2):
        if half:
            sc.one()
        dg2, dg3 = feature_grads(
            half, r.wo1, r.w2, r.wo2, r.gains, fcnt, r.h1, r.h2, r.qkv2, r.g, r.da, r.b, r.b1, r.do2, r.dqkv, r.do1,
            r.gr, dg2, dg3,
        )
        two = pl.ds(2 * half, 2)
        for k in (1, 2, 3):
            at, f = 3 * half + k - 1, (s + k) % 4
            moves2.append(send(r.do1.at[two, f], r.do.at[s, two], r.as3.at[at], r.aq3.at[at], (t, f)))
    n = lax.broadcasted_iota(jnp.int32, (8, D), 0)
    r.dgain[...] = jnp.where(n == 1, dg2, jnp.where(n == 2, dg3, 0.0))
    feature_weights(r.o1, r.a2, r.o2, r.b, r.b1, r.dqkv, r.wide, r.g2, r.dwo1)
    edge_rows(r.g2, r.ge, 1)
    r.do[s] = r.do1[:, s, :, :]
    sb.core()
    r.at[...] = turn(r.a1[...])
    sb.one()
    for copy in moves2:
        copy.wait_recv()
    live = lax.broadcasted_iota(jnp.int32, (512, 1), 0) < scnt

    for i in range(8):
        r.g1[24 + i] = r.dwo1[64 * i : 64 * i + 64, :]

    def heads(h):
        backward_heads(h, r.qkv1, r.do, live, r.dqkv, r.kt, r.dkv)
        cols = slice(128 * h, 128 * h + 128)
        for j in range(3):
            r.wide[h, pl.ds(j, D, stride=3), :] = nn(r.at[...], r.dqkv[j, :, cols])

        def narrow(i):
            r.g1[i, :, cols] = r.wide[h, pl.ds(mult(i * 64, 64), 64), :].astype(BF)

        repeat(0, 24, narrow, 4)
        edge_rows(r.g1, r.ge, 0, 128 * h, 128)
        sa[h].core()

    heads(0)
    sc.two()
    heads(1)
    sa[0].one()
    sb.two()
    heads(2)
    sa[1].one()
    sa[0].two()
    heads(3)
    sc.three()
    r.da[...] = nt(r.dqkv[0], r.w1[0]) + nt(r.dqkv[1], r.w1[1]) + nt(r.dqkv[2], r.w1[2])
    sa[2].one()
    sa[1].two()
    sb.three()

    def norm_back(i, dg):
        dh, part = norm_grad(r.cf[i].astype(F32).reshape(128, D), r.da[block(i), :], gain1)
        r.dhs[i] = dh.astype(BF).reshape(4, 32, D)
        return dg + part

    dg = four_blocks(norm_back, jnp.zeros((1, D), F32))
    r.ge[0] = jnp.concatenate([dg, r.dgain[1:2, :], r.dgain[2:3, :]], 1)
    sd.core()
    sa[3].one()
    sa[0].three()
    sc.four()
    sa[2].two()
    sa[1].three()
    sd.one()
    sa[0].four()
    sa[3].two()
    sa[2].three()
    sa[1].four()
    sd.two()
    sb.four()
    sa[3].three()
    sa[2].four()
    sd.three()
    homes = [
        send(r.dhs.at[(s + k) % 4], r.dhr.at[:, s], r.as4.at[k - 1], r.aq4.at[k - 1], (t, (s + k) % 4))
        for k in (1, 2, 3)
    ]
    r.sums[...] = jnp.zeros((32, 128), F32)
    for fl in (r.fl2, r.fl3):
        fl[0:4, :] = jnp.zeros((4, 128), F32)
    main = sc.result()

    @pl.when(d < 16)
    def _():
        for j in range(4):
            for b in range(4):
                piece = main[32 * j : 32 * j + 32, 128 * b : 128 * b + 128]
                r.fl3[pl.ds(4 + b + 4 * j, 32, stride=16), :] = piece

    @pl.when(d >= 16)
    def _():
        to_rows(main, r.fl3)

    to_shard(r.fl3, 128, d, r.sh3)
    params("3")
    squares(r.sh3, r.m3, r.f3, r.s3, r.sums, d, 4 * D, 2, 1, 16)
    squares_tail(r.sh3, r.m3, r.f3, r.s3, r.sums, d, 4 * D, 2)
    sa[3].four()
    sd.four()
    to_rows(sb.result(), r.fl2)
    to_shard(r.fl2, 64, d, r.sh2)
    params("2")
    squares(r.sh2, r.m2, r.f2, r.s2, r.sums, d, 3 * D, 1, 1, 8)
    squares_tail(r.sh2, r.m2, r.f2, r.s2, r.sums, d, 3 * D, 1)
    for h in range(4):
        r.fl1[pl.ds(4 + h, 64, stride=4), :] = sa[h].result()
    first = sd.result()
    for k, fl in enumerate((r.fl1, r.fl2, r.fl3)):
        first_row(first[:, D * k : D * k + D], fl)
    to_shard(r.fl1, 64, d, r.sh1)
    top_shard(r.fl2, d, r.sh2)
    top_shard(r.fl3, d, r.sh3)
    for name in ("sh1", "sh2", "sh3"):
        store(name)
    params("1")
    squares(r.sh1, r.m1, r.f1, r.s1, r.sums, d, 3 * D, 0, 0, 8)
    squares_tail(r.sh1, r.m1, r.f1, r.s1, r.sums, d, 3 * D, 0)
    squares(r.sh2, r.m2, r.f2, r.s2, r.sums, d, 3 * D, 1, 0, 1)
    squares(r.sh3, r.m3, r.f3, r.s3, r.sums, d, 4 * D, 2, 0, 1)

    def finish_input():
        r.cgrad[:, s, :, :] = r.gr[:, s, :, :] + r.dhs[s].astype(F32)
        for k in (1, 2, 3):
            homes[k - 1].wait_recv()
            f = (s + 4 - k) % 4
            r.cgrad[:, f, :, :] = r.gr[:, f, :, :] + r.dhr[:, f, :, :].astype(F32)
        store("cgrad")

    r.total[...], adds = sum_all(r.sums, r.ts, r.zs, r.ns, r.nq, t, s, finish_input)
    store("total")
    for one in (*sa, sb, sc, sd):
        one.drain()
    for copy in moves + backs[0] + backs[1] + moves2 + homes + adds:
        copy.wait_send()
    for copy in stores:
        copy.wait()


def call_m(scnt, fcnt, cells, top, params, name="kernel_m"):
    sds = jax.ShapeDtypeStruct
    hb = pl.BlockSpec(memory_space=pl.ANY)
    sm = pl.BlockSpec(memory_space=pltpu.SMEM)
    return pl.pallas_call(
        kernel_m,
        name=name,
        out_shape=(
            sds((4, 4, 32, D), BF), sds((4, 4, 32, D), F32), sds((264, 128), F32), sds((264, 128), F32),
            sds((520, 128), F32), sds((8, 128), F32),
        ),
        in_specs=[sm, sm] + [hb] * 11,
        out_specs=(hb,) * 6,
        scratch_shapes=list(SCRATCH.values()),
        compiler_params=pltpu.CompilerParams(collective_id=1, has_side_effects=True, vmem_limit_bytes=63 << 20),
    )(scnt, fcnt, cells, top, *params)


def fast_device(cells, out_grad, scnt, fcnt, b1, f1, s1, b2, f2, s2, b3, f3, s3):
    params = (b1, f1, s1, b2, f2, s2, b3, f3, s3)
    out, cgrad, sh1, sh2, sh3, total = call_m(scnt, fcnt, cells[0], out_grad[0], params)
    *outs, pairs, out, cgrad = call_e(total, (sh1, sh2, sh3), params, out, cgrad)
    return (out[None], cgrad[None], *outs, pairs.T)


def step(*args):
    cells = args[0]
    fits = lax.axis_size("task") == 8 and lax.axis_size("samp") == 4 and cells.shape == (1, 128, 4, D)
    return fast_device(*args) if fits else on_device(*args)


def solution(mesh):
    placed = (
        P("task", "samp", None, None),
        P("task", "samp", None, None),
        P("task"),
        P("task"),
        P(("task", "samp")),
        P(("task", "samp")),
        P(("task", "samp")),
        P(("task", "samp")),
        P(("task", "samp")),
        P(("task", "samp")),
        P(("task", "samp")),
        P(("task", "samp")),
        P(("task", "samp")),
    )
    return jax.shard_map(
        step,
        mesh=mesh,
        in_specs=placed,
        out_specs=(
            P("task", "samp", None, None),
            P("task", "samp", None, None),
            P(("task", "samp")),
            P(("task", "samp")),
            P(("task", "samp")),
            P(("task", "samp")),
            P(("task", "samp")),
            P(("task", "samp")),
            P(("task", "samp")),
            P(("task", "samp")),
            P(("task", "samp")),
            P(("task", "samp")),
            P(("task", "samp")),
            P(("task", "samp")),
            P(("task", "samp")),
            P(("task", "samp")),
            P(("task", "samp")),
            P(),
        ),
        check_vma=False,
    )
```

```python
import jax
import jax.numpy as jnp
from jax import lax
from jax.experimental import pallas as pl
from jax.experimental.pallas import tpu as pltpu
from jax.sharding import PartitionSpec as P

D = 512
HEADS = 8
HEAD_DIM = 64
FF = 2048


EPS_NORM = 1e-05
EPS_ADAM = 1e-06
STEP_RATE = 0.5
BIG_NEGATIVE = -1e30


def normalize(hidden, gain_row):
    centre = jnp.mean(hidden, -1, keepdims=True)
    shifted = hidden - centre
    spread = jnp.mean(shifted * shifted, -1, keepdims=True)
    return shifted * lax.rsqrt(spread + EPS_NORM) * gain_row


def norm_backward(hidden, gain_row, normed_grad):
    _, pullback = jax.vjp(normalize, hidden, gain_row)
    return pullback(normed_grad)


def gelu_exact(upward):
    return jax.nn.gelu(upward, approximate=False)


def contract_rows(left, right):
    return lax.dot_general(
        left, right, (((0,), (0,)), ((), ())), preferred_element_type=jnp.float32
    )


def times_transpose(left, right):
    return lax.dot_general(
        left, right, (((1,), (1,)), ((), ())), preferred_element_type=jnp.float32
    )


def unpack(flat_params, width_in, width_mid):
    gain_row = flat_params[:D].astype(jnp.float32)
    w_in = flat_params[D : D + D * width_in].reshape(D, width_in)
    w_out = flat_params[D + D * width_in :].reshape(width_mid, D)
    return (gain_row, w_in, w_out)


def fetch_forward(master):
    return lax.all_gather(master.astype(jnp.bfloat16), ("task", "samp"), axis=0, tiled=True)


def fetch_again(master):
    return lax.all_gather(master.astype(jnp.bfloat16), ("task", "samp"), axis=0, tiled=True)


def reduce_grads(gain_grad, in_grad, out_grad_matrix):
    flat_grads = jnp.concatenate([gain_grad, in_grad.reshape(-1), out_grad_matrix.reshape(-1)])
    return lax.psum_scatter(flat_grads, ("task", "samp"), scatter_dimension=0, tiled=True)


def group_size(feature_total, most):
    chosen = 1
    for candidate in range(1, most + 1):
        if feature_total % candidate == 0:
            chosen = candidate
    return chosen


def lamb_prepare(grad_shard, master, first, second, width_in):
    first_new = 0.5 * first + 0.5 * grad_shard
    second_new = 0.5 * second + 0.5 * grad_shard * grad_shard
    direction = first_new / (jnp.sqrt(second_new) + EPS_ADAM)
    entries = master.shape[0]
    position = lax.axis_index(("task", "samp")) * entries + jnp.arange(entries, dtype=jnp.int32)
    segment = (position >= D).astype(jnp.int32) + (position >= D + D * width_in).astype(jnp.int32)
    member = segment[None, :] == jnp.arange(3, dtype=jnp.int32)[:, None]
    weight_sums = jnp.sum(jnp.where(member, (master * master)[None, :], 0.0), 1)
    update_sums = jnp.sum(jnp.where(member, (direction * direction)[None, :], 0.0), 1)
    return (first_new, second_new, direction, member, jnp.stack([weight_sums, update_sums], 1))


def lamb_finish(master, block_state, trust_ratio):
    factor = jnp.sum(jnp.where(block_state[3], trust_ratio[:, None], 0.0), 0)
    return master - STEP_RATE * factor * block_state[2]


def sample_scores(query_part, key_part, key_live, score_scale):
    scores = (
        jnp.einsum("qfhe,kfhe->fhqk", query_part, key_part, preferred_element_type=jnp.float32)
        * score_scale
    )
    return jnp.where(key_live, scores, BIG_NEGATIVE)


def sample_forward(queries, pairs_all, key_live, block_features, score_scale):
    local_rows, features = (queries.shape[0], queries.shape[1])

    def one_block(block_index, results):
        attended, log_totals = results
        offset = block_index * block_features
        query_part = lax.dynamic_slice_in_dim(queries, offset, block_features, 1)
        pair_part = lax.dynamic_slice_in_dim(pairs_all, offset, block_features, 1)
        scores = sample_scores(query_part, pair_part[:, :, 0], key_live, score_scale)
        row_top = jnp.max(scores, -1, keepdims=True)
        exponent = jnp.exp(scores - row_top)
        row_total = jnp.sum(exponent, -1, keepdims=True)
        probability = (exponent / row_total).astype(jnp.bfloat16)
        block_out = jnp.einsum(
            "fhqk,kfhe->qfhe", probability, pair_part[:, :, 1], preferred_element_type=jnp.float32
        )
        attended = lax.dynamic_update_slice_in_dim(
            attended, block_out.astype(jnp.bfloat16), offset, 1
        )
        log_totals = lax.dynamic_update_slice_in_dim(
            log_totals, (row_top + jnp.log(row_total))[..., 0], offset, 0
        )
        return (attended, log_totals)

    start_state = (
        jnp.zeros(queries.shape, jnp.bfloat16),
        jnp.zeros((features, HEADS, local_rows), jnp.float32),
    )
    return lax.fori_loop(0, features // block_features, one_block, start_state)


def query_side(query_part, pair_part, grad_part, log_part, key_live, score_scale):
    key_part = pair_part[:, :, 0]
    value_part = pair_part[:, :, 1]
    scores = sample_scores(query_part, key_part, key_live, score_scale)
    probability = jnp.exp(scores - log_part[..., None])
    prob_grad = jnp.einsum(
        "qfhe,kfhe->fhqk", grad_part, value_part, preferred_element_type=jnp.float32
    )
    row_inner = jnp.sum(probability * prob_grad, -1, keepdims=True)
    score_grad = (probability * (prob_grad - row_inner)).astype(jnp.bfloat16)
    query_block = (
        jnp.einsum("fhqk,kfhe->qfhe", score_grad, key_part, preferred_element_type=jnp.float32)
        * score_scale
    )
    return (probability, score_grad, row_inner, query_block)


def sample_backward(
    queries, pairs_all, key_live, log_totals, attended_grad, block_features, score_scale
):
    local_rows, features = (queries.shape[0], queries.shape[1])

    def one_block(block_index, results):
        query_grads, pair_grads = results
        offset = block_index * block_features
        query_part = lax.dynamic_slice_in_dim(queries, offset, block_features, 1)
        pair_part = lax.dynamic_slice_in_dim(pairs_all, offset, block_features, 1)
        grad_part = lax.dynamic_slice_in_dim(attended_grad, offset, block_features, 1)
        log_part = lax.dynamic_slice_in_dim(log_totals, offset, block_features, 0)
        probability, score_grad, row_inner, query_block = query_side(
            query_part, pair_part, grad_part, log_part, key_live, score_scale
        )
        key_block = (
            jnp.einsum(
                "fhqk,qfhe->kfhe", score_grad, query_part, preferred_element_type=jnp.float32
            )
            * score_scale
        )
        value_block = jnp.einsum(
            "fhqk,qfhe->kfhe",
            probability.astype(jnp.bfloat16),
            grad_part,
            preferred_element_type=jnp.float32,
        )
        pair_terms = jnp.stack([key_block, value_block], 2)
        pair_local = lax.psum_scatter(
            pair_terms.astype(jnp.bfloat16), "samp", scatter_dimension=0, tiled=True
        ).astype(jnp.float32)
        query_grads = lax.dynamic_update_slice_in_dim(query_grads, query_block, offset, 1)
        pair_grads = lax.dynamic_update_slice_in_dim(pair_grads, pair_local, offset, 1)
        return (query_grads, pair_grads)

    start_state = (
        jnp.zeros((local_rows, features, HEADS, HEAD_DIM), jnp.float32),
        jnp.zeros((local_rows, features, 2, HEADS, HEAD_DIM), jnp.float32),
    )
    return lax.fori_loop(0, features // block_features, one_block, start_state)


def on_device(
    cells,
    out_grad,
    sample_counts,
    feature_counts,
    sample_block,
    sample_first,
    sample_second,
    feature_block,
    feature_first,
    feature_second,
    mlp_block,
    mlp_first,
    mlp_second,
):
    local_rows, features = (cells.shape[1], cells.shape[2])
    flat_rows = local_rows * features
    seq_all = local_rows * lax.axis_size("samp")
    score_scale = HEAD_DIM ** (-0.5)
    block_features = group_size(features, max(1, 2048 // (HEADS * local_rows)))
    sample_index = lax.axis_index("samp") * local_rows + jnp.arange(local_rows, dtype=jnp.int32)
    sample_live = sample_index < sample_counts[0]
    key_live = jnp.arange(seq_all, dtype=jnp.int32) < sample_counts[0]
    feature_live = jnp.arange(features, dtype=jnp.int32) < feature_counts[0]
    cell_live = sample_live[:, None, None] & feature_live[None, :, None]
    hidden_in = cells[0].astype(jnp.float32)
    gain_one, in_one, out_one = unpack(fetch_forward(sample_block), 3 * D, D)
    normed_one = normalize(hidden_in, gain_one).astype(jnp.bfloat16)
    packed_one = jnp.dot(
        normed_one.reshape(flat_rows, D), in_one, preferred_element_type=jnp.float32
    )
    packed_one = packed_one.astype(jnp.bfloat16).reshape(local_rows, features, 3, HEADS, HEAD_DIM)
    queries_one = packed_one[:, :, 0]
    pairs_local = packed_one[:, :, 1:]
    pairs_all = lax.all_gather(pairs_local, "samp", axis=0, tiled=True)
    attended_one, log_totals = sample_forward(
        queries_one, pairs_all, key_live, block_features, score_scale
    )
    attended_one_rows = attended_one.reshape(flat_rows, D)
    branch_one = jnp.dot(attended_one_rows, out_one, preferred_element_type=jnp.float32)
    hidden_one = hidden_in + branch_one.reshape(local_rows, features, D)
    gain_two, in_two, out_two = unpack(fetch_forward(feature_block), 3 * D, D)
    normed_two = normalize(hidden_one, gain_two).astype(jnp.bfloat16).reshape(flat_rows, D)
    packed_two = jnp.dot(normed_two, in_two, preferred_element_type=jnp.float32)
    packed_two = packed_two.astype(jnp.bfloat16).reshape(local_rows, features, 3, HEADS, HEAD_DIM)
    queries_two, key_two, value_two = (
        packed_two[:, :, 0],
        packed_two[:, :, 1],
        packed_two[:, :, 2],
    )
    scores_two = (
        jnp.einsum("sqhe,skhe->shqk", queries_two, key_two, preferred_element_type=jnp.float32)
        * score_scale
    )
    scores_two = jnp.where(feature_live, scores_two, BIG_NEGATIVE)
    row_top = jnp.max(scores_two, -1, keepdims=True)
    exponent = jnp.exp(scores_two - row_top)
    probability_two = exponent / jnp.sum(exponent, -1, keepdims=True)
    prob_low_two = probability_two.astype(jnp.bfloat16)
    attended_two = jnp.einsum(
        "shqk,skhe->sqhe", prob_low_two, value_two, preferred_element_type=jnp.float32
    )
    attended_two_rows = attended_two.reshape(flat_rows, D).astype(jnp.bfloat16)
    branch_two = jnp.dot(attended_two_rows, out_two, preferred_element_type=jnp.float32)
    hidden_two = hidden_one + branch_two.reshape(local_rows, features, D)
    gain_three, up_weight, down_weight = unpack(fetch_forward(mlp_block), FF, FF)
    normed_three = normalize(hidden_two, gain_three).astype(jnp.bfloat16).reshape(flat_rows, D)
    upward = jnp.dot(normed_three, up_weight, preferred_element_type=jnp.float32)
    activated = gelu_exact(upward).astype(jnp.bfloat16)
    branch_three = jnp.dot(activated, down_weight, preferred_element_type=jnp.float32)
    hidden_three = hidden_two + branch_three.reshape(local_rows, features, D)
    layer_out = jnp.where(cell_live, hidden_three, 0.0).astype(jnp.bfloat16)[None]
    top_grad = jnp.where(cell_live, out_grad[0], jnp.zeros((), jnp.bfloat16))
    top_rows = top_grad.reshape(flat_rows, D)
    gain_three, up_weight, down_weight = unpack(fetch_again(mlp_block), FF, FF)
    down_grad = contract_rows(activated, top_rows)
    act_grad = times_transpose(top_rows, down_weight).astype(jnp.bfloat16)
    _, gelu_pull = jax.vjp(gelu_exact, upward)
    up_grad = gelu_pull(act_grad.astype(jnp.float32))[0].astype(jnp.bfloat16)
    upw_grad = contract_rows(normed_three, up_grad)
    normed_grad = times_transpose(up_grad, up_weight).reshape(local_rows, features, D)
    hidden_grad, gain_three_grad = norm_backward(hidden_two, gain_three, normed_grad)
    grad_two = top_grad.astype(jnp.float32) + hidden_grad
    mlp_shard = reduce_grads(gain_three_grad, upw_grad, down_grad)
    mlp_state = lamb_prepare(mlp_shard, mlp_block, mlp_first, mlp_second, FF)
    gain_two, in_two, out_two = unpack(fetch_again(feature_block), 3 * D, D)
    branch_grad = grad_two.astype(jnp.bfloat16).reshape(flat_rows, D)
    out_two_grad = contract_rows(attended_two_rows, branch_grad)
    attended_grad = (
        times_transpose(branch_grad, out_two)
        .astype(jnp.bfloat16)
        .reshape(local_rows, features, HEADS, HEAD_DIM)
    )
    prob_grad = jnp.einsum(
        "sqhe,skhe->shqk", attended_grad, value_two, preferred_element_type=jnp.float32
    )
    row_inner = jnp.sum(probability_two * prob_grad, -1, keepdims=True)
    score_grad = (probability_two * (prob_grad - row_inner)).astype(jnp.bfloat16)
    query_grad = (
        jnp.einsum("shqk,skhe->sqhe", score_grad, key_two, preferred_element_type=jnp.float32)
        * score_scale
    )
    key_grad = (
        jnp.einsum("shqk,sqhe->skhe", score_grad, queries_two, preferred_element_type=jnp.float32)
        * score_scale
    )
    value_grad = jnp.einsum(
        "shqk,sqhe->skhe", prob_low_two, attended_grad, preferred_element_type=jnp.float32
    )
    packed_grad = (
        jnp.stack([query_grad, key_grad, value_grad], 2)
        .astype(jnp.bfloat16)
        .reshape(flat_rows, 3 * D)
    )
    in_two_grad = contract_rows(normed_two, packed_grad)
    normed_grad = times_transpose(packed_grad, in_two).reshape(local_rows, features, D)
    hidden_grad, gain_two_grad = norm_backward(hidden_one, gain_two, normed_grad)
    grad_one = grad_two + hidden_grad
    feature_shard = reduce_grads(gain_two_grad, in_two_grad, out_two_grad)
    feature_state = lamb_prepare(feature_shard, feature_block, feature_first, feature_second, 3 * D)
    gain_one, in_one, out_one = unpack(fetch_again(sample_block), 3 * D, D)
    pairs_all = lax.all_gather(pairs_local, "samp", axis=0, tiled=True)
    branch_grad = grad_one.astype(jnp.bfloat16).reshape(flat_rows, D)
    out_one_grad = contract_rows(attended_one_rows, branch_grad)
    attended_grad = (
        times_transpose(branch_grad, out_one)
        .astype(jnp.bfloat16)
        .reshape(local_rows, features, HEADS, HEAD_DIM)
    )
    query_grads, pair_grads = sample_backward(
        queries_one, pairs_all, key_live, log_totals, attended_grad, block_features, score_scale
    )
    packed_grad = (
        jnp.concatenate([query_grads[:, :, None], pair_grads], 2)
        .astype(jnp.bfloat16)
        .reshape(flat_rows, 3 * D)
    )
    in_one_grad = contract_rows(normed_one.reshape(flat_rows, D), packed_grad)
    normed_grad = times_transpose(packed_grad, in_one).reshape(local_rows, features, D)
    hidden_grad, gain_one_grad = norm_backward(hidden_in, gain_one, normed_grad)
    cells_grad = (grad_one + hidden_grad)[None]
    sample_shard = reduce_grads(gain_one_grad, in_one_grad, out_one_grad)
    sample_state = lamb_prepare(sample_shard, sample_block, sample_first, sample_second, 3 * D)
    totals = lax.psum(
        jnp.concatenate([sample_state[4], feature_state[4], mlp_state[4]], 0), ("task", "samp")
    )
    norm_pairs = jnp.sqrt(totals)
    trust_ratio = norm_pairs[:, 0] / (norm_pairs[:, 1] + EPS_ADAM)
    sample_master = lamb_finish(sample_block, sample_state, trust_ratio[0:3])
    feature_master = lamb_finish(feature_block, feature_state, trust_ratio[3:6])
    mlp_master = lamb_finish(mlp_block, mlp_state, trust_ratio[6:9])
    return (
        layer_out,
        cells_grad,
        sample_shard,
        sample_state[0],
        sample_state[1],
        sample_master,
        sample_master.astype(jnp.bfloat16),
        feature_shard,
        feature_state[0],
        feature_state[1],
        feature_master,
        feature_master.astype(jnp.bfloat16),
        mlp_shard,
        mlp_state[0],
        mlp_state[1],
        mlp_master,
        mlp_master.astype(jnp.bfloat16),
        norm_pairs,
    )


D = 512
MESH = pl.DeviceIdType.MESH
BF = jnp.bfloat16
F32 = jnp.float32
NEG = -1e30


def mult(value, factor):
    return value if isinstance(value, int) else pl.multiple_of(value, factor)


def repeat(lo, hi, body, ways):
    def step(i, _):
        for k in range(ways):
            body(lo + i * ways + k)
        return 0

    lax.fori_loop(0, (hi - lo) // ways, step, 0)


def nt(left, right):
    return lax.dot_general(left, right, (((1,), (1,)), ((), ())), preferred_element_type=F32)


def nn(left, right):
    return lax.dot_general(left, right, (((1,), (0,)), ((), ())), preferred_element_type=F32)


def here():
    return lax.axis_index("task"), lax.axis_index("samp")


def peers(t, s):
    return [(jnp.bitwise_xor(t, e), s) for e in range(1, 8)] + [(t, jnp.bitwise_xor(s, e)) for e in (1, 2, 3)]


def enter(t, s):
    barrier = pltpu.get_barrier_semaphore()
    for peer in peers(t, s):
        pl.semaphore_signal(barrier, inc=1, device_id=peer, device_id_type=MESH)
    return barrier


def send(src, dst, ssem, rsem, peer):
    copy = pltpu.make_async_remote_copy(
        src_ref=src, dst_ref=dst, send_sem=ssem, recv_sem=rsem, device_id=peer, device_id_type=MESH
    )
    copy.start()
    return copy


class Gather:
    def __init__(self, buf, ssem, rsem, t, s):
        self.buf, self.t, self.s = buf, t, s
        half = buf.shape[2] // 2
        self.ha, self.hb, self.all = pl.ds(0, half), pl.ds(half, half), pl.ds(0, 2 * half)
        self.rows = pl.ds(0, buf.shape[1])
        self.ssem, self.rsem = ssem, rsem
        self.moves = []
        self.tx, self.ty = jnp.bitwise_xor(t, 2), jnp.bitwise_xor(t, 4)
        self.txy, self.tc = jnp.bitwise_xor(t, 6), jnp.bitwise_xor(t, 1)
        self.hops, self.sent = {}, {k: {} for k in ("x", "y", "c", "xy", "yx", "cx", "cy")}

    def z(self, key):
        return jnp.bitwise_xor(self.s, key)

    def go(self, slots, cols, peer):
        view = self.buf.at[slots, self.rows, cols]
        i = len(self.moves)
        copy = send(view, view, self.ssem.at[i], self.rsem.at[i], peer)
        self.moves.append(copy)
        return copy

    def pass_on(self, kind, key, t, cols, to):
        self.sent[kind][key] = self.go(pl.ds(4 * t + self.z(key), 1), cols, (to, self.s))

    def spread(self, key):
        self.pass_on("x", key, self.t, self.all, self.tx)
        self.pass_on("y", key, self.t, self.all, self.ty)
        self.pass_on("c", key, self.t, self.all, self.tc)

    def hop(self, key, slot, to):
        self.hops[key] = self.go(pl.ds(4 * self.t + self.z(slot), 1), self.all, (self.t, self.z(to)))

    def start_z(self):
        self.hop(2, 0, 2)
        self.hop(1, 0, 1)

    def zin(self, *keys):
        for key in keys:
            self.hops[key].wait_recv()
            if key == 2:
                self.hop(3, 2, 1)
            self.spread(key)

    def near(self, *keys):
        for key in keys:
            self.sent["x"][key].wait_recv()
            self.pass_on("xy", key, self.tx, self.ha, self.ty)
            self.pass_on("cx", key, self.tx, self.all, self.tc)
            self.sent["y"][key].wait_recv()
            self.pass_on("yx", key, self.ty, self.hb, self.tx)
            self.pass_on("cy", key, self.ty, self.all, self.tc)

    def far(self):
        for kind in ("xy", "yx"):
            for copy in self.sent[kind].values():
                copy.wait_recv()
        self.last = self.go(pl.ds(4 * self.txy, 4), self.all, (self.tc, self.s))

    def end(self):
        for kind in ("c", "cx", "cy"):
            for copy in self.sent[kind].values():
                copy.wait_recv()
        self.last.wait_recv()

    def drain(self):
        for copy in self.moves:
            copy.wait_send()


def realign(m_ref, sh_ref, d, rows, out_ref, out_at, roll_to, split=False):
    whole = 4 * rows
    total = whole + 8
    q, p = d // 8, d % 8
    lane = lax.broadcasted_iota(jnp.int32, (total, 128), 1)
    roll_to[0:8, :] = jnp.zeros((8, 128), F32)
    for i in range(whole // 8):
        sh_ref[8 * i : 8 * i + 8, :] = m_ref[pl.ds(1024 * i, 1024)].reshape(8, 128)
    sh_ref[whole:total, :] = jnp.zeros((8, 128), F32)
    sh_ref[whole : whole + 1, 0:16] = m_ref[pl.ds(128 * whole, 16)].reshape(1, 16)
    rolled = pltpu.roll(sh_ref[0:total, :], 16 * p, 1)
    roll_to[8 : 8 + total, :] = rolled
    sh_ref[0:8, :] = jnp.zeros((8, 128), F32)
    sh_ref[8 : 8 + total, :] = jnp.where(lane < 16 * p, roll_to[7 : 7 + total, :], rolled)
    firsts = []

    def straight():
        for b in range(4):
            cols = slice(128 * b, 128 * b + 128)
            out_ref[out_at, 0:rows, cols] = sh_ref[pl.ds(12 - q + b, rows, stride=4), :].astype(BF)

    def by_piece():
        for b in range(4):
            cols = slice(128 * b, 128 * b + 128)
            for j in range(4):
                piece = sh_ref[pl.ds(12 - q + b + 4 * j, rows // 4, stride=16), :]
                out_ref[out_at, rows // 4 * j : rows // 4 * (j + 1), cols] = piece.astype(BF)

    if split:
        pl.when(d < 16)(by_piece)
        pl.when(d >= 16)(straight)
    else:
        straight()
    for b in range(4):
        firsts.append(sh_ref[pl.ds(8 - q + b, 1), :])
    return jnp.concatenate(firsts, 1)


def spread(buf, firsts, kind, rows, lo, hi, put):
    tail = lax.broadcasted_iota(jnp.int32, (8, D), 0) == 7

    def body(i):
        nxt = jnp.minimum(i + 1, 31)
        row = firsts[nxt, :, D * kind : D * kind + D]
        block = buf[i, 0:rows, :].astype(F32)
        last = block[rows - 8 : rows, :] + jnp.where(tail & (i < 31), row, 0.0)
        put(i - lo, block[0 : rows - 8, :], last)

    repeat(lo, hi, body, 4 if rows == 64 else 2)


def put_f32(dst, rows):
    def put(i, head, last):
        for b in range(4):
            cols = slice(128 * b, 128 * b + 128)
            dst[b, pl.ds(mult(i * rows, rows), rows - 8), :] = head[:, cols]
            dst[b, pl.ds(mult(i * rows + rows - 8, 8), 8), :] = last[:, cols]

    return put


def put_bf(dst, rows):
    def put(i, head, last):
        dst[pl.ds(mult(i * rows, rows), rows), :] = jnp.concatenate([head, last], 0).astype(BF)

    return put


def split_columns(wide, ways, dst):
    def body(i):
        for j in range(ways):
            for b in range(4):
                piece = wide[b, pl.ds(64 * ways * i + j, 64, stride=ways), :]
                dst[j, pl.ds(mult(64 * i, 64), 64), 128 * b : 128 * b + 128] = piece.astype(BF)

    repeat(0, 8, body, 2)


def halves():
    lane = lax.broadcasted_iota(jnp.int32, (128, 128), 1)
    return lane < 64


def two_heads(x, one, two):
    return jnp.concatenate([x * one, x * two], 0)


def soft(scores, axis):
    e = [jnp.exp(x - jnp.max(x, axis, keepdims=True)) for x in scores]
    return [x * (1.0 / jnp.sum(x, axis, keepdims=True)) for x in e]


def attend_chunk(qkv, c, live, out):
    left = halves()
    one = jnp.where(left, 0.125, 0.0).astype(BF)
    two = jnp.where(left, 0.0, 0.125).astype(BF)
    rows = pl.ds(mult(c * 128, 128), 128)

    def body(h, _):
        cols = [pl.ds(128 * i, 128) for i in range(4)]
        scores = [jnp.where(live, nt(two_heads(qkv[0, rows, w], one, two), qkv[1, :, w]), NEG) for w in cols]
        prob = [p.astype(BF) for p in soft(scores, 1)]
        outs = [nn(p, qkv[2, :, w]) for p, w in zip(prob, cols)]
        for o, w in zip(outs, cols):
            o = jnp.where(left, o[0:128], o[128:256]).astype(BF)
            for g in range(4):
                out[g, :, w] = o[32 * g : 32 * g + 32]
        return 0

    body(0, 0)


def edges(d, entries, width):
    begin = d * entries
    return D - begin, D + D * width - begin


def segment(k, ends):
    return (k >= ends[0]).astype(jnp.int32) + (k >= ends[1]).astype(jnp.int32)


def lamb_step(g, m, f, s):
    fn = 0.5 * f + 0.5 * g
    sn = 0.5 * s + 0.5 * g * g
    return fn, sn, fn / (jnp.sqrt(sn) + 1e-6)


def flat_index(rows=32):
    lane = lax.broadcasted_iota(jnp.int32, (rows, 128), 1)
    return lax.broadcasted_iota(jnp.int32, (rows, 128), 0) * 128 + lane


def fold(x):
    return x.reshape(-1, 8, 128).sum(0)


def squares(sh, m, f, s, sums, d, width, b, lo, hi):
    entries = m.shape[0]
    ends = edges(d, entries, width)
    index = flat_index()

    def body(i, acc):
        at = pl.ds(mult(i * 4096, 4096), 4096)
        old = m[at].reshape(32, 128)
        _, _, r = lamb_step(sh[pl.ds(mult(i * 32, 32), 32), :], old, f[at].reshape(32, 128), s[at].reshape(32, 128))
        part = segment(index + i * 4096, ends)
        out = []
        for n, value in enumerate((old * old, r * r)):
            for k in range(3):
                out.append(acc[3 * n + k] + fold(jnp.where(part == k, value, 0.0)))
        return tuple(out)

    acc = lax.fori_loop(lo, hi, body, (jnp.zeros((8, 128), F32),) * 6)
    for n in range(2):
        for k in range(3):
            row = 16 * n + 3 * b + k
            sums[row : row + 1, :] += jnp.sum(acc[3 * n + k], 0, keepdims=True)


def squares_tail(sh, m, f, s, sums, d, width, b):
    entries = m.shape[0]
    base = entries - 16
    ends = edges(d, entries, width)
    at = pl.ds(base, 16)
    old = m[at].reshape(1, 16)
    row = base // 128
    _, _, r = lamb_step(sh[row : row + 1, 0:16], old, f[at].reshape(1, 16), s[at].reshape(1, 16))
    part = segment(lax.broadcasted_iota(jnp.int32, (1, 16), 1) + base, ends)
    for n, value in enumerate((old * old, r * r)):
        for k in range(3):
            row = 16 * n + 3 * b + k
            sums[row : row + 1, 0:16] += jnp.where(part == k, value, 0.0)


def update(sh, m, f, s, grad, fout, sout, mout, wout, ratio, d, width, b):
    entries = m.shape[0]
    whole = entries // 8192
    ends = edges(d, entries, width)
    half = [0.5 * ratio[3 * b + k : 3 * b + k + 1, :] for k in range(3)]

    def put(at, g, part, shape):
        old = m[at].reshape(shape)
        fn, sn, r = lamb_step(g, old, f[at].reshape(shape), s[at].reshape(shape))
        factor = jnp.where(part == 0, half[0], jnp.where(part == 1, half[1], half[2]))
        new = (old - factor * r).reshape(-1)
        grad[at] = g.reshape(-1)
        fout[at] = fn.reshape(-1)
        sout[at] = sn.reshape(-1)
        mout[at] = new
        wout[at] = new.astype(BF)

    index = flat_index(64)

    def body(i, _):
        at = pl.ds(mult(i * 8192, 8192), 8192)
        put(at, sh[pl.ds(mult(i * 64, 64), 64), :], segment(index + i * 8192, ends), (64, 128))
        return 0

    lax.fori_loop(0, whole, body, 0)
    part = segment(lax.broadcasted_iota(jnp.int32, (1, 16), 1) + whole * 8192, ends)
    put(pl.ds(whole * 8192, 16), sh[64 * whole : 64 * whole + 1, 0:16], part, (1, 16))


def diagonal(rows):
    lane = lax.broadcasted_iota(jnp.int32, (32, 128), 1)
    return lane == lax.broadcasted_iota(jnp.int32, (32, 128), 0)


def sum_all(sums, ts, zs, ssem, rsem, t, s, meanwhile):
    column = jnp.sum(sums[...], 1, keepdims=True)
    ts[t] = jnp.broadcast_to(jnp.sum(jnp.where(diagonal(32), column, 0.0), 0, keepdims=True), (8, 128))
    plane = [
        send(ts.at[t], ts.at[t], ssem.at[e - 1], rsem.at[e - 1], (jnp.bitwise_xor(t, e), s)) for e in range(1, 8)
    ]
    meanwhile()
    for copy in plane:
        copy.wait_recv()
    zs[s] = ((ts[0] + ts[1]) + (ts[2] + ts[3])) + ((ts[4] + ts[5]) + (ts[6] + ts[7]))
    last = [
        send(zs.at[s], zs.at[s], ssem.at[6 + e], rsem.at[6 + e], (t, jnp.bitwise_xor(s, e))) for e in (1, 2, 3)
    ]
    for copy in last:
        copy.wait_recv()
    return (zs[0] + zs[1]) + (zs[2] + zs[3]), plane + last


def by_sample(x, out):
    for g in range(4):
        out[32 * g : 32 * g + 32, :, :] = jnp.transpose(x[g].astype(F32), (1, 0, 2)).astype(out.dtype)


def kernel_e(*refs):
    ins, outs, vin, vout, sin, sout = refs[:15], refs[15:33], refs[33:48], refs[48:66], refs[66], refs[67]
    t, s = here()
    d = 4 * t + s
    loads = [pltpu.make_async_copy(a, b, sin.at[i]) for i, (a, b) in enumerate(zip(ins, vin))]
    stores = [pltpu.make_async_copy(a, b, sout.at[i]) for i, (a, b) in enumerate(zip(vout, outs))]
    order = [0, 1, 4, 5, 6, 2, 7, 8, 9, 3, 10, 11, 12, 13, 14]
    for i in order:
        loads[i].start()
    loads[0].wait()
    norms = jnp.sqrt(vin[0][0:1, :])
    vout[15][0:1, :] = norms[:, 0:9]
    vout[15][1:2, :] = pltpu.roll(norms, 112, 1)[:, 0:9]
    stores[15].start()
    norm = jnp.sum(jnp.where(diagonal(32), norms, 0.0), 1, keepdims=True)
    ratio = norm[0:9] / (norm[16:25] + 1e-6)
    for b in range(3):
        used = [1 + b, 4 + 3 * b, 5 + 3 * b, 6 + 3 * b]
        for i in used:
            loads[i].wait()
        width = 4 * D if b == 2 else 3 * D
        update(*[vin[i] for i in used], *vout[5 * b : 5 * b + 5], ratio, d, width, b)
        for i in range(5 * b, 5 * b + 5):
            stores[i].start()
    for i in (13, 14):
        loads[i].wait()
        by_sample(vin[i], vout[i + 3])
        stores[i + 3].start()
    for copy in stores:
        copy.wait()


def call_e(total, shards, args, lout, cgrad):
    sds = jax.ShapeDtypeStruct
    hb = pl.BlockSpec(memory_space=pl.ANY)
    shapes = []
    for m in args[0::3]:
        n = m.shape
        shapes += [sds(n, F32)] * 4 + [sds(n, BF)]
    shapes += [sds((2, 9), F32), sds((128, 4, D), BF), sds((128, 4, D), F32)]
    given = (total, *shards, *args, lout, cgrad)
    return pl.pallas_call(
        kernel_e,
        name="kernel_e",
        out_shape=tuple(shapes),
        in_specs=[hb] * 15,
        out_specs=(hb,) * 18,
        scratch_shapes=[pltpu.VMEM(x.shape, x.dtype) for x in (*given, *shapes)]
        + [pltpu.SemaphoreType.DMA((15,)), pltpu.SemaphoreType.DMA((18,))],
        compiler_params=pltpu.CompilerParams(vmem_limit_bytes=63 << 20),
    )(*given)


def backward_heads(h, qkv, do, live, dqkv, kt, dkv):
    left = halves()
    one, two = jnp.where(left, 1.0, 0.0).astype(BF), jnp.where(left, 0.0, 1.0).astype(BF)
    cols = pl.ds(mult(h * 128, 128), 128)
    kt[...] = jnp.transpose(qkv[1, :, cols])
    top_lane = lax.broadcasted_iota(jnp.int32, (128, 128), 0) < 64

    def chunk(n, _):
        each = [0, 1, 2, 3]
        rows = [pl.ds(c * 128, 128) for c in each]
        qm = [two_heads(qkv[0, r, cols] * jnp.asarray(0.125, BF), one, two) for r in rows]
        gm = [two_heads(do[c, :, :, cols].reshape(128, 128), one, two) for c in each]
        prob = soft([jnp.where(live, nt(qkv[1, :, cols], q), NEG) for q in qm], 0)
        pg = [nt(qkv[2, :, cols], g) for g in gm]
        sg = [(p * (x - jnp.sum(p * x, 0, keepdims=True))).astype(BF) for p, x in zip(prob, pg)]
        dqkv[1, :, cols] = (nn(sg[0], qm[0]) + nn(sg[1], qm[1]) + nn(sg[2], qm[2]) + nn(sg[3], qm[3])).astype(BF)
        pb = [p.astype(BF) for p in prob]
        dqkv[2, :, cols] = (nn(pb[0], gm[0]) + nn(pb[1], gm[1]) + nn(pb[2], gm[2]) + nn(pb[3], gm[3])).astype(BF)
        for r, x in zip(rows, sg):
            dqt = nn(kt[...], x)
            dq = jnp.transpose(jnp.where(top_lane, dqt[:, 0:128], dqt[:, 128:256])) * 0.125
            dqkv[0, r, cols] = dq.astype(BF)
        return 0

    chunk(0, 0)


def turn(x):
    return jnp.transpose(x)


def stats(h):
    x = h - jnp.mean(h, 1, keepdims=True)
    rstd = lax.rsqrt(jnp.mean(x * x, 1, keepdims=True) + 1e-5)
    return x * rstd, rstd


def norm_grad(h, da, gain):
    x, rstd = stats(h)
    dgain = jnp.sum(da * x, 0, keepdims=True)
    dx = da * gain
    dh = rstd * (dx - jnp.mean(dx, 1, keepdims=True) - x * jnp.mean(dx * x, 1, keepdims=True))
    return dh, dgain


def block(g):
    return pl.ds(mult(g * 128, 128), 128)


def feature_mask(fcnt, axis):
    shape = (256, 128) if axis else (128, 256)
    query = lax.broadcasted_iota(jnp.int32, shape, 1 - axis)
    key = lax.broadcasted_iota(jnp.int32, shape, axis)
    return (query % 32 == key % 32) & (key // 32 < fcnt)


def feature_forward(qkv, o2, fcnt, half):
    left = halves()
    one = jnp.where(left, 0.125, 0.0).astype(BF)
    two = jnp.where(left, 0.0, 0.125).astype(BF)
    ok = feature_mask(fcnt, 1)
    cols = [slice(128 * h, 128 * h + 128) for h in range(4)]

    def body(n, _):
        rows = block(n)
        scores = [
            jnp.where(ok, nt(two_heads(qkv[0, rows, c], one, two), qkv[1, rows, c]), NEG) for c in cols
        ]
        prob = [p.astype(BF) for p in soft(scores, 1)]
        out = [nn(p, qkv[2, rows, c]) for p, c in zip(prob, cols)]
        for o, c in zip(out, cols):
            o2[rows, c] = jnp.where(left, o[0:128], o[128:256]).astype(BF)
        return 0

    lax.fori_loop(2 * half, 2 * half + 2, body, 0)


def feature_backward(qkv, do, dqkv, fcnt, half):
    left = halves()
    one, two = jnp.where(left, 1.0, 0.0).astype(BF), jnp.where(left, 0.0, 1.0).astype(BF)
    ok = feature_mask(fcnt, 0)
    top_lane = lax.broadcasted_iota(jnp.int32, (128, 128), 0) < 64
    cols = [slice(128 * h, 128 * h + 128) for h in range(4)]

    def body(n, _):
        rows = block(n)
        qm = [two_heads(qkv[0, rows, c] * jnp.asarray(0.125, BF), one, two) for c in cols]
        gm = [two_heads(do[rows, c], one, two) for c in cols]
        prob = soft([jnp.where(ok, nt(qkv[1, rows, c], q), NEG) for c, q in zip(cols, qm)], 0)
        pg = [nt(qkv[2, rows, c], g) for c, g in zip(cols, gm)]
        sg = [(p * (x - jnp.sum(p * x, 0, keepdims=True))).astype(BF) for p, x in zip(prob, pg)]
        dqt = [nn(turn(qkv[1, rows, c]), x) for c, x in zip(cols, sg)]
        dk = [nn(x, q).astype(BF) for x, q in zip(sg, qm)]
        dv = [nn(p.astype(BF), g).astype(BF) for p, g in zip(prob, gm)]
        dq = [turn(jnp.where(top_lane, x[:, 0:128], x[:, 128:256])) * 0.125 for x in dqt]
        for i, c in enumerate(cols):
            dqkv[0, rows, c] = dq[i].astype(BF)
            dqkv[1, rows, c] = dk[i]
            dqkv[2, rows, c] = dv[i]
        return 0

    lax.fori_loop(2 * half, 2 * half + 2, body, 0)


def four_blocks(body, init=0):
    for r in range(4):
        init = body(r, init)
    return init


def two_blocks(half, body, init=0):
    for r in (2 * half, 2 * half + 1):
        init = body(r, init)
    return init


def flat(x):
    return x.reshape(128, D)


def cube(x):
    return x.reshape(4, 32, D)


def narrow_to(wide, part, slots, rows):
    def body(i):
        at = pl.ds(mult(i * rows, rows), rows)
        for b in range(4):
            part[i, :, 128 * b : 128 * b + 128] = wide[b, at, :].astype(BF)

    repeat(0, slots, body, 2)


def store_wide(wide, j, ways, value):
    for b in range(4):
        wide[b, pl.ds(j, value.shape[0], stride=ways), :] = value[:, 128 * b : 128 * b + 128]


def mlp(a3, a3t, g, h2, wup, wdn, h3, da, zb, dub, u, dz, p3, after):
    def act(rows):
        x = u[rows, :]
        cdf = 0.5 * (1.0 + lax.erf(x * 0.7071067811865476))
        zb[rows, :] = (x * cdf).astype(BF)
        slope = cdf + x * (0.3989422804014327 * jnp.exp(-0.5 * x * x))
        dub[rows, :] = (slope * dz[rows, :].astype(F32)).astype(BF)

    h3[...] = h2[...]
    da[...] = jnp.zeros((512, D), F32)

    def body(j, _):
        u[...] = nn(a3[...], wup[j])
        dz[...] = nt(g[...], wdn[j]).astype(BF)
        for n in range(2):
            rows = slice(256 * n, 256 * n + 256)
            act(rows)
            h3[rows, :] += nn(zb[rows, :], wdn[j])
            da[rows, :] += nt(dub[rows, :], wup[j])
        up = nn(a3t[...], dub[...]).astype(BF)
        for i in range(16):
            p3[i, pl.ds(mult(32 * j, 32), 32), :] = up[32 * i : 32 * i + 32]
        dw = nn(turn(zb[...]), g[...]).astype(BF)
        for i in range(4):
            p3[16 + 4 * j + i] = dw[128 * i : 128 * i + 128]
        after(j)
        return 0

    lax.fori_loop(0, 4, body, 0)


def middle_forward(half, s, cells, top, o1, wo1, w2, wo2, gains, scnt, fcnt, h1, h2, a2, qkv, o2, a3, g):
    gain2, gain3 = gains[1:2, :], gains[2:3, :]
    every = pl.ds(256 * half, 256)
    h1[every, :] = nn(o1[2 * half : 2 * half + 2].reshape(256, D), wo1[...])

    def first(r, _):
        rows = block(r)
        h = h1[rows, :] + flat(cells[r].astype(F32))
        h1[rows, :] = h
        x, _ = stats(h)
        a2[rows, :] = (x * gain2).astype(BF)
        n = lax.broadcasted_iota(jnp.int32, (128, 1), 0)
        live = (n // 32 < fcnt) & (128 * s + 32 * r + n % 32 < scnt)
        g[rows, :] = jnp.where(live, flat(top[r].astype(F32)), 0.0).astype(BF)
        return 0

    two_blocks(half, first)
    for j in range(3):
        qkv[j, every, :] = nn(a2[every, :], w2[j]).astype(BF)
    feature_forward(qkv, o2, fcnt, half)
    h2[every, :] = h1[every, :] + nn(o2[every, :], wo2[...])

    def second(r, _):
        rows = block(r)
        x, _ = stats(h2[rows, :])
        a3[rows, :] = (x * gain3).astype(BF)
        return 0

    two_blocks(half, second)


def layer_output(s, h3, lout, scnt, fcnt):
    def last(r, _):
        n = lax.broadcasted_iota(jnp.int32, (128, 1), 0)
        live = (n // 32 < fcnt) & (128 * s + 32 * r + n % 32 < scnt)
        lout[r] = cube(jnp.where(live, h3[block(r), :], 0.0).astype(BF))
        return 0

    four_blocks(last)


def feature_grads(half, wo1, w2, wo2, gains, fcnt, h1, h2, qkv, g, da, b2, b1, do, dqkv, do1, gr, dg2, dg3):
    gain2, gain3 = gains[1:2, :], gains[2:3, :]
    every = pl.ds(256 * half, 256)

    def third(r, dg):
        rows = block(r)
        dh, part = norm_grad(h2[rows, :], da[rows, :], gain3)
        total = g[rows, :].astype(F32) + dh
        gr[r] = cube(total)
        b2[rows, :] = total.astype(BF)
        return dg + part

    dg3 = two_blocks(half, third, dg3)
    do[every, :] = nt(b2[every, :], wo2[...]).astype(BF)
    feature_backward(qkv, do, dqkv, fcnt, half)
    da[every, :] = nt(dqkv[0, every, :], w2[0]) + nt(dqkv[1, every, :], w2[1]) + nt(dqkv[2, every, :], w2[2])

    def fourth(r, dg):
        rows = block(r)
        dh, part = norm_grad(h1[rows, :], da[rows, :], gain2)
        total = flat(gr[r]) + dh
        gr[r] = cube(total)
        b1[rows, :] = total.astype(BF)
        return dg + part

    dg2 = two_blocks(half, fourth, dg2)
    do1[2 * half : 2 * half + 2] = nt(b1[every, :], wo1[...]).astype(BF).reshape(2, 4, 32, D)
    return dg2, dg3


def feature_weights(o1, a2, o2, b2, b1, dqkv, wide, p2, dwo1):
    def weights(j, _):
        store_wide(wide, j, 3, nn(turn(a2[...]), dqkv[j]))
        return 0

    lax.fori_loop(0, 3, weights, 0)
    narrow_to(wide, p2, 24, 64)
    dw = nn(turn(o2[...]), b2[...]).astype(BF)
    for i in range(8):
        p2[24 + i] = dw[64 * i : 64 * i + 64]
    dwo1[...] = nn(turn(o1[...].reshape(512, D)), b1[...]).astype(BF)


class Reduce:
    def __init__(self, part, r1, ry, rx, ry2, rx2, rz, ssem, rsem, t, s, chunk=None):
        self.part, self.r1 = part, r1
        self.ry, self.rx, self.ry2, self.rx2, self.rz = ry, rx, ry2, rx2, rz
        rows, half = part.shape[1], part.shape[2] // 2
        if chunk is None:
            every = pl.ds(0, rows)
            self.ha, self.hb, self.all = [(every, pl.ds(o, n)) for o, n in ((0, half), (half, half), (0, 2 * half))]
        else:
            cols, half = pl.ds(128 * chunk, 128), rows // 2
            self.ha, self.hb, self.all = [(pl.ds(o, n), cols) for o, n in ((0, half), (half, half), (0, rows))]
        self.ssem, self.rsem, self.t, self.s = ssem, rsem, t, s
        self.copies = []

    def go(self, src, dst, peer):
        i = len(self.copies)
        copy = send(src, dst, self.ssem.at[i], self.rsem.at[i], peer)
        self.copies.append(copy)
        return copy

    def xor(self, e):
        return jnp.bitwise_xor(self.t, e)

    def group(self, e, box, t=None):
        t = self.t if t is None else t
        return self.part.at[pl.ds(4 * jnp.bitwise_xor(t, 2 * e), 4), *box]

    def core_copy(self, e):
        tc = self.xor(1)
        return pltpu.make_async_remote_copy(
            src_ref=self.group(e, self.all, tc), dst_ref=self.r1.at[e], send_sem=self.ssem.at[e],
            recv_sem=self.rsem.at[e], device_id=(tc, self.s), device_id_type=MESH,
        )

    def core(self, start=True):
        self.c = {e: self.core_copy(e) for e in (2, 3, 1, 0)}
        for copy in self.c.values():
            if start:
                copy.start()
            self.copies.append(copy)

    def add(self, e, box, got):
        base = 4 * self.xor(2 * e)
        for j in range(4):
            own = self.part[base + j, *box].astype(F32)
            self.part[base + j, *box] = (own + got[j].astype(F32)).astype(self.part.dtype)

    def one(self):
        ty, tx, s = self.xor(4), self.xor(2), self.s
        self.y, self.x = {}, {}
        for e in (2, 3, 1, 0):
            self.c[e].wait_recv()
            self.add(e, self.all, self.r1.at[e])
            if e in (2, 3):
                self.y[e - 2] = self.go(self.group(e, self.ha), self.ry.at[e - 2], (ty, s))
            if e in (3, 1):
                self.x[e // 2] = self.go(self.group(e, self.hb), self.rx.at[e // 2], (tx, s))

    def two(self):
        ty, tx, s = self.xor(4), self.xor(2), self.s
        self.y[1].wait_recv()
        self.add(1, self.ha, self.ry.at[1])
        self.x2 = self.go(self.group(1, self.ha), self.rx2, (tx, s))
        self.x[1].wait_recv()
        self.add(2, self.hb, self.rx.at[1])
        self.y2 = self.go(self.group(2, self.hb), self.ry2, (ty, s))
        self.y[0].wait_recv()
        self.add(0, self.ha, self.ry.at[0])
        self.x[0].wait_recv()
        self.add(0, self.hb, self.rx.at[0])

    def three(self):
        self.x2.wait_recv()
        self.add(0, self.ha, self.rx2)
        self.y2.wait_recv()
        self.add(0, self.hb, self.ry2)
        self.z = [self.z_send(1, 0), self.z_send(3, 1)]

    def z_send(self, slot, into):
        t, s = self.t, self.s
        to = jnp.bitwise_xor(s, 2 if into == 2 else 1)
        return self.go(self.part.at[4 * t + jnp.bitwise_xor(s, slot), *self.all], self.rz.at[into], (t, to))

    def four(self):
        self.z[1].wait_recv()
        mine = 4 * self.t + jnp.bitwise_xor(self.s, 2)
        own = self.part[mine, *self.all].astype(F32)
        self.part[mine, *self.all] = (own + self.rz[1, :, :].astype(F32)).astype(self.part.dtype)
        self.z.append(self.z_send(2, 2))

    def result(self):
        self.z[0].wait_recv()
        self.z[2].wait_recv()
        own = self.part[4 * self.t + self.s, *self.all].astype(F32)
        return own + self.rz[0, :, :].astype(F32) + self.rz[2, :, :].astype(F32)

    def drain(self):
        for copy in self.copies:
            copy.wait_send()


def edge_rows(part, edges, kind, lo=0, size=D):
    rows = part.shape[1]

    for i in range(1, 32):
        row = part[i - 1, rows - 16 : rows, lo : lo + size].astype(F32)[15:16, :]
        edges[i, :, D * kind + lo : D * kind + lo + size] = row


def by_feature(x, out):
    for g in range(4):
        out[g] = jnp.transpose(x[32 * g : 32 * g + 32, :, :].astype(F32), (1, 0, 2)).astype(BF)


def to_rows(main, fl):
    rows = main.shape[0]
    for b in range(4):
        fl[pl.ds(4 + b, rows, stride=4), :] = main[:, 128 * b : 128 * b + 128]


def first_row(row, fl):
    for b in range(4):
        fl[b : b + 1, :] = row[:, 128 * b : 128 * b + 128]


def shifted(fl, d, total):
    q, p = d // 8, d % 8
    back = (128 - 16 * p) % 128
    lane = lax.broadcasted_iota(jnp.int32, (total, 128), 1)
    low = pltpu.roll(fl[pl.ds(q, total), :], back, 1)
    high = pltpu.roll(fl[pl.ds(q + 1, total), :], back, 1)
    return jnp.where(lane < 128 - 16 * p, low, high)


def to_shard(fl, rows, d, out_ref):
    total = out_ref.shape[0]
    fl[4 + 4 * rows : total + 8, :] = jnp.zeros((total + 4 - 4 * rows, 128), F32)
    out_ref[...] = shifted(fl, d, total)


def top_shard(fl, d, out_ref):
    out_ref[0:8, :] = shifted(fl, d, 8)


def early_core(red, j):
    tc = red.xor(1)

    def piece(group, rows):
        e = jnp.bitwise_xor(tc, group) // 2
        pltpu.make_async_remote_copy(
            src_ref=red.part.at[pl.ds(4 * group, 4), rows], dst_ref=red.r1.at[e, :, rows], send_sem=red.ssem.at[e],
            recv_sem=red.rsem.at[e], device_id=(tc, red.s), device_id_type=MESH,
        ).start()

    for k in (0, 2):
        piece(jnp.bitwise_xor(tc % 4, k), pl.ds(mult(32 * j, 32), 32))

    @pl.when(j % 2 == tc % 2)
    def _():
        piece(4 + j, pl.ds(0, 128))


class Refs:
    def __init__(self, names, refs):
        for name, ref in zip(names, refs, strict=True):
            setattr(self, name, ref)


def reduce_names(n):
    return [k + n for k in ("r1", "ry", "rx", "ry2", "rx2", "rz")]


def reduce_scratch(rows, width=D, kind=BF):
    half = width // 2
    return [
        pltpu.VMEM((4, 4, rows, width), kind), pltpu.VMEM((2, 4, rows, half), kind),
        pltpu.VMEM((2, 4, rows, half), kind), pltpu.VMEM((4, rows, half), kind), pltpu.VMEM((4, rows, half), kind),
        pltpu.VMEM((3, rows, width), kind),
    ]


def chunk_scratch(rows):
    half = rows // 2
    shapes = [(4, 4, rows), (2, 4, half), (2, 4, half), (4, half), (4, half), (3, rows)]
    return [pltpu.VMEM((*shape, 128), BF) for shape in shapes]


PARAMS = ["m1", "f1", "s1", "m2", "f2", "s2", "m3", "f3", "s3"]
WIDE = pltpu.VMEM((D, D), F32)
NARROW = pltpu.VMEM((D, D), BF)
THREE = pltpu.VMEM((3, D, D), BF)
FOUR = pltpu.VMEM((4, D, D), BF)
TILE = pltpu.VMEM((4, 4, 32, D), BF)
DMA = pltpu.SemaphoreType.DMA
SCRATCH = {
    "cells_in": pltpu.VMEM((128, 4, D), BF), "top_in": pltpu.VMEM((128, 4, D), BF),
    **{k + n: pltpu.VMEM((size,), F32) for n, size in (("1", 32784), ("2", 32784), ("3", 65552)) for k in "mfs"},
    "lout": TILE, "cgrad": pltpu.VMEM((4, 4, 32, D), F32), "sh1": pltpu.VMEM((264, 128), F32),
    "sh2": pltpu.VMEM((264, 128), F32), "sh3": pltpu.VMEM((520, 128), F32), "total": pltpu.VMEM((8, 128), F32),
    "ls": DMA((11,)), "os": DMA((6,)),
    "g1": pltpu.VMEM((32, 64, D), BF), "ge": pltpu.VMEM((32, 1, 3 * D), F32), "g2": pltpu.VMEM((32, 64, D), BF), "g3": pltpu.VMEM((32, 128, D), BF),
    "wide": pltpu.VMEM((4, 4 * D, 128), F32), "sh": pltpu.VMEM((536, 128), F32), "ro": pltpu.VMEM((536, 128), F32),
    "w1": THREE, "wo1": NARROW, "w2": THREE, "wo2": NARROW, "wup": FOUR, "wdn": FOUR,
    "gains": pltpu.VMEM((8, D), F32), "dgain": pltpu.VMEM((8, D), F32),
    "cells": TILE, "top": TILE, "cf": TILE, "a1": NARROW, "qkv1": THREE, "o1c": pltpu.VMEM((3, 4, 32, D), BF), "o1": TILE,
    "h1": WIDE, "h2": WIDE, "a2": NARROW, "qkv2": THREE, "o2": NARROW, "a3": NARROW, "at": NARROW, "g": NARROW,
    "h3": WIDE, "da": WIDE, "zb": NARROW, "dub": NARROW, "u": WIDE, "dz": NARROW, "b": NARROW, "b1": NARROW, "do2": NARROW,
    "dqkv": THREE, "gr": pltpu.VMEM((4, 4, 32, D), F32), "do1": TILE, "do": TILE, "dwo1": NARROW,
    "kt": pltpu.VMEM((128, D), BF), "dkv": pltpu.VMEM((2, D, 128), F32), "dhs": TILE, "dhr": TILE,
    **{k: v for h in range(4) for k, v in zip(reduce_names(f"a{h}"), chunk_scratch(64))},
    **dict(zip(reduce_names("b"), reduce_scratch(64))),
    **dict(zip(reduce_names("c"), reduce_scratch(128))),
    **dict(zip(reduce_names("d"), reduce_scratch(1, 3 * D, F32))),
    "fl1": pltpu.VMEM((272, 128), F32), "fl2": pltpu.VMEM((272, 128), F32), "fl3": pltpu.VMEM((528, 128), F32),
    "sums": pltpu.VMEM((32, 128), F32), "ts": pltpu.VMEM((8, 8, 128), F32), "zs": pltpu.VMEM((4, 8, 128), F32),
    "gs": DMA((4, 32)), "gq": DMA((4, 32)), "rs": DMA((7, 16)), "rq": DMA((7, 16)),
    "as1": DMA((3,)), "aq1": DMA((3,)), "as2": DMA((6,)), "aq2": DMA((6,)),
    "as3": DMA((6,)), "aq3": DMA((6,)), "as4": DMA((3,)), "aq4": DMA((3,)), "ns": DMA((10,)), "nq": DMA((10,)),
}
LOADED = ["m1", "cells_in", "m2", "m3", "top_in", "f3", "s3", "f2", "s2", "f1", "s1"]
INPUTS = ["scnt", "fcnt", "cells_any", "top_any"] + [k + "_any" for k in PARAMS]
STORED = ["lout", "cgrad", "sh1", "sh2", "sh3", "total"]
OUTPUTS = [k + "_any" for k in STORED]


def kernel_m(*refs):
    r = Refs(INPUTS + OUTPUTS + list(SCRATCH), refs)
    t, s = here()
    d = 4 * t + s
    scnt, fcnt = r.scnt[0], r.fcnt[0]
    barrier = enter(t, s)
    loads, stores = {}, []
    for i, name in enumerate(LOADED):
        source = name.replace("_in", "") + "_any"
        loads[name] = pltpu.make_async_copy(getattr(r, source), getattr(r, name), r.ls.at[i])
        loads[name].start()

    def store(name):
        i = STORED.index(name)
        copy = pltpu.make_async_copy(getattr(r, name), getattr(r, name + "_any"), r.os.at[i])
        copy.start()
        stores.append(copy)

    def params(n):
        loads["f" + n].wait()
        loads["s" + n].wait()

    loads["m1"].wait()
    ga, gb, gc, ge = [
        Gather(buf, r.gs.at[i], r.gq.at[i], t, s) for i, buf in enumerate((r.g1, r.g2, r.g3, r.ge))
    ]
    first1 = realign(r.m1, r.sh, d, 64, r.g1, d, r.ro)
    pl.semaphore_wait(barrier, 10)
    ga.start_z()
    ga.spread(0)
    loads["m2"].wait()
    loads["m3"].wait()
    first2 = realign(r.m2, r.sh, d, 64, r.g2, d, r.ro)
    first3 = realign(r.m3, r.sh, d, 128, r.g3, d, r.ro, True)
    r.ge[d] = jnp.concatenate([first1, first2, first3], 1).astype(BF).astype(F32)
    ge.start_z()
    ge.spread(0)
    gb.start_z()
    gb.spread(0)
    loads["cells_in"].wait()
    by_feature(r.cells_in, r.cells)
    r.cf[s] = r.cells[:, s, :, :]
    for one in (ge, ga):
        one.near(0)
        one.zin(2, 1)
    for one in (ge, ga):
        one.near(2, 1)
        one.zin(3)
    gc.start_z()
    gc.spread(0)
    moves = [
        send(r.cells.at[:, (s + k) % 4], r.cf.at[s], r.as1.at[k - 1], r.aq1.at[k - 1], (t, (s + k) % 4))
        for k in (1, 2, 3)
    ]
    for one in (ge, ga):
        one.near(3)
    loads["top_in"].wait()
    by_feature(r.top_in, r.top)
    for one in (ge, ga):
        one.far()
    for one in (gb, gc):
        one.near(0)
        one.zin(2)
    gb.zin(1)
    ge.end()
    ga.end()
    gb.near(2)
    gb.zin(3)
    gc.zin(1)
    gb.near(1)
    spread(r.g1, r.ge, 0, 64, 0, 24, put_f32(r.wide, 64))
    split_columns(r.wide, 3, r.w1)
    spread(r.g1, r.ge, 0, 64, 24, 32, put_bf(r.wo1, 64))
    for copy in moves:
        copy.wait_recv()
    for k in range(3):
        r.gains[k : k + 1, :] = r.ge[0, :, D * k : D * k + D]
    gain1 = r.gains[0:1, :]

    def norm(i, _):
        x, _ = stats(r.cf[i].astype(F32).reshape(128, D))
        r.a1[block(i), :] = (x * gain1).astype(BF)
        return 0

    four_blocks(norm)

    def project(j, _):
        r.qkv1[j] = nn(r.a1[...], r.w1[j]).astype(BF)
        return 0

    lax.fori_loop(0, 3, project, 0)
    live = lax.broadcasted_iota(jnp.int32, (1, 512), 1) < scnt
    gb.near(3)
    gc.near(2)
    gc.zin(3)
    backs = ([], [])

    def give_back(k, half):
        two = pl.ds(2 * half, 2)
        at = 3 * half + k - 1
        peer = (t, (s + k) % 4)
        backs[half].append(send(r.o1c.at[k - 1, two], r.o1.at[two, s], r.as2.at[at], r.aq2.at[at], peer))

    for k in (2, 1, 3, 0):
        if k:
            attend_chunk(r.qkv1, (s + k) % 4, live, r.o1c.at[k - 1])
            give_back(k, 0)
        else:
            for j in (2, 1, 3):
                give_back(j, 1)
            attend_chunk(r.qkv1, s, live, r.o1.at[:, s])
        if k == 1:
            gb.far()
            gc.near(1)
    gb.end()
    spread(r.g2, r.ge, 1, 64, 0, 24, put_f32(r.wide, 64))
    split_columns(r.wide, 3, r.w2)
    spread(r.g2, r.ge, 1, 64, 24, 32, put_bf(r.wo2, 64))
    gc.near(3)
    for half in range(2):
        for copy in backs[half]:
            copy.wait_recv()
        middle_forward(
            half, s, r.cells, r.top, r.o1, r.wo1, r.w2, r.wo2, r.gains, scnt, fcnt, r.h1, r.h2, r.a2, r.qkv2, r.o2,
            r.a3, r.g,
        )
        if half == 0:
            gc.far()
    r.at[...] = turn(r.a3[...])
    gc.end()

    def put_up(i, head, last):
        block = jnp.concatenate([head, last], 0).astype(BF)
        for j in range(4):
            r.wup[j, pl.ds(mult(i * 32, 32), 32), :] = block[32 * j : 32 * j + 32]

    spread(r.g3, r.ge, 2, 128, 0, 16, put_up)

    def put_down(i, head, last):
        r.wdn[i // 4, pl.ds(mult((i % 4) * 128, 128), 128), :] = jnp.concatenate([head, last], 0).astype(BF)

    spread(r.g3, r.ge, 2, 128, 16, 32, put_down)
    for one in (ga, gb, gc, ge):
        one.drain()
    def reducer(n, part, i, chunk=None):
        bufs = [getattr(r, k) for k in reduce_names(n)]
        return Reduce(part, *bufs, r.rs.at[i], r.rq.at[i], t, s, chunk)

    sb, sc, sd = reducer("b", r.g2, 0), reducer("c", r.g3, 1), reducer("d", r.ge, 2)
    sa = [reducer(f"a{h}", r.g1, 3 + h, h) for h in range(4)]
    mlp(r.a3, r.at, r.g, r.h2, r.wup, r.wdn, r.h3, r.da, r.zb, r.dub, r.u, r.dz, r.g3, lambda j: early_core(sc, j))
    edge_rows(r.g3, r.ge, 2)

    sc.core(False)
    layer_output(s, r.h3, r.lout, scnt, fcnt)
    store("lout")
    dg2 = dg3 = jnp.zeros((1, D), F32)
    moves2 = []
    for half in range(2):
        if half:
            sc.one()
        dg2, dg3 = feature_grads(
            half, r.wo1, r.w2, r.wo2, r.gains, fcnt, r.h1, r.h2, r.qkv2, r.g, r.da, r.b, r.b1, r.do2, r.dqkv, r.do1,
            r.gr, dg2, dg3,
        )
        two = pl.ds(2 * half, 2)
        for k in (1, 2, 3):
            at, f = 3 * half + k - 1, (s + k) % 4
            moves2.append(send(r.do1.at[two, f], r.do.at[s, two], r.as3.at[at], r.aq3.at[at], (t, f)))
    n = lax.broadcasted_iota(jnp.int32, (8, D), 0)
    r.dgain[...] = jnp.where(n == 1, dg2, jnp.where(n == 2, dg3, 0.0))
    feature_weights(r.o1, r.a2, r.o2, r.b, r.b1, r.dqkv, r.wide, r.g2, r.dwo1)
    edge_rows(r.g2, r.ge, 1)
    r.do[s] = r.do1[:, s, :, :]
    sb.core()
    r.at[...] = turn(r.a1[...])
    sb.one()
    for copy in moves2:
        copy.wait_recv()
    live = lax.broadcasted_iota(jnp.int32, (512, 1), 0) < scnt

    for i in range(8):
        r.g1[24 + i] = r.dwo1[64 * i : 64 * i + 64, :]

    def heads(h):
        backward_heads(h, r.qkv1, r.do, live, r.dqkv, r.kt, r.dkv)
        cols = slice(128 * h, 128 * h + 128)
        for j in range(3):
            r.wide[h, pl.ds(j, D, stride=3), :] = nn(r.at[...], r.dqkv[j, :, cols])

        def narrow(i):
            r.g1[i, :, cols] = r.wide[h, pl.ds(mult(i * 64, 64), 64), :].astype(BF)

        repeat(0, 24, narrow, 4)
        edge_rows(r.g1, r.ge, 0, 128 * h, 128)
        sa[h].core()

    heads(0)
    sc.two()
    heads(1)
    sa[0].one()
    sb.two()
    heads(2)
    sa[1].one()
    sa[0].two()
    heads(3)
    sc.three()
    r.da[...] = nt(r.dqkv[0], r.w1[0]) + nt(r.dqkv[1], r.w1[1]) + nt(r.dqkv[2], r.w1[2])
    sa[2].one()
    sa[1].two()
    sb.three()

    def norm_back(i, dg):
        dh, part = norm_grad(r.cf[i].astype(F32).reshape(128, D), r.da[block(i), :], gain1)
        r.dhs[i] = dh.astype(BF).reshape(4, 32, D)
        return dg + part

    dg = four_blocks(norm_back, jnp.zeros((1, D), F32))
    r.ge[0] = jnp.concatenate([dg, r.dgain[1:2, :], r.dgain[2:3, :]], 1)
    sd.core()
    sa[3].one()
    sa[0].three()
    sc.four()
    sa[2].two()
    sa[1].three()
    sd.one()
    sa[0].four()
    sa[3].two()
    sa[2].three()
    sa[1].four()
    sd.two()
    sb.four()
    sa[3].three()
    sa[2].four()
    sd.three()
    homes = [
        send(r.dhs.at[(s + k) % 4], r.dhr.at[:, s], r.as4.at[k - 1], r.aq4.at[k - 1], (t, (s + k) % 4))
        for k in (1, 2, 3)
    ]
    r.sums[...] = jnp.zeros((32, 128), F32)
    for fl in (r.fl2, r.fl3):
        fl[0:4, :] = jnp.zeros((4, 128), F32)
    main = sc.result()

    @pl.when(d < 16)
    def _():
        for j in range(4):
            for b in range(4):
                piece = main[32 * j : 32 * j + 32, 128 * b : 128 * b + 128]
                r.fl3[pl.ds(4 + b + 4 * j, 32, stride=16), :] = piece

    @pl.when(d >= 16)
    def _():
        to_rows(main, r.fl3)

    to_shard(r.fl3, 128, d, r.sh3)
    params("3")
    squares(r.sh3, r.m3, r.f3, r.s3, r.sums, d, 4 * D, 2, 1, 16)
    squares_tail(r.sh3, r.m3, r.f3, r.s3, r.sums, d, 4 * D, 2)
    sa[3].four()
    sd.four()
    to_rows(sb.result(), r.fl2)
    to_shard(r.fl2, 64, d, r.sh2)
    params("2")
    squares(r.sh2, r.m2, r.f2, r.s2, r.sums, d, 3 * D, 1, 1, 8)
    squares_tail(r.sh2, r.m2, r.f2, r.s2, r.sums, d, 3 * D, 1)
    for h in range(4):
        r.fl1[pl.ds(4 + h, 64, stride=4), :] = sa[h].result()
    first = sd.result()
    for k, fl in enumerate((r.fl1, r.fl2, r.fl3)):
        first_row(first[:, D * k : D * k + D], fl)
    to_shard(r.fl1, 64, d, r.sh1)
    top_shard(r.fl2, d, r.sh2)
    top_shard(r.fl3, d, r.sh3)
    for name in ("sh1", "sh2", "sh3"):
        store(name)
    params("1")
    squares(r.sh1, r.m1, r.f1, r.s1, r.sums, d, 3 * D, 0, 0, 8)
    squares_tail(r.sh1, r.m1, r.f1, r.s1, r.sums, d, 3 * D, 0)
    squares(r.sh2, r.m2, r.f2, r.s2, r.sums, d, 3 * D, 1, 0, 1)
    squares(r.sh3, r.m3, r.f3, r.s3, r.sums, d, 4 * D, 2, 0, 1)

    def finish_input():
        r.cgrad[:, s, :, :] = r.gr[:, s, :, :] + r.dhs[s].astype(F32)
        for k in (1, 2, 3):
            homes[k - 1].wait_recv()
            f = (s + 4 - k) % 4
            r.cgrad[:, f, :, :] = r.gr[:, f, :, :] + r.dhr[:, f, :, :].astype(F32)
        store("cgrad")

    r.total[...], adds = sum_all(r.sums, r.ts, r.zs, r.ns, r.nq, t, s, finish_input)
    store("total")
    for one in (*sa, sb, sc, sd):
        one.drain()
    for copy in moves + backs[0] + backs[1] + moves2 + homes + adds:
        copy.wait_send()
    for copy in stores:
        copy.wait()


def call_m(scnt, fcnt, cells, top, params, name="kernel_m"):
    sds = jax.ShapeDtypeStruct
    hb = pl.BlockSpec(memory_space=pl.ANY)
    sm = pl.BlockSpec(memory_space=pltpu.SMEM)
    return pl.pallas_call(
        kernel_m,
        name=name,
        out_shape=(
            sds((4, 4, 32, D), BF), sds((4, 4, 32, D), F32), sds((264, 128), F32), sds((264, 128), F32),
            sds((520, 128), F32), sds((8, 128), F32),
        ),
        in_specs=[sm, sm] + [hb] * 11,
        out_specs=(hb,) * 6,
        scratch_shapes=list(SCRATCH.values()),
        compiler_params=pltpu.CompilerParams(collective_id=1, has_side_effects=True, vmem_limit_bytes=63 << 20),
    )(scnt, fcnt, cells, top, *params)


def fast_device(cells, out_grad, scnt, fcnt, b1, f1, s1, b2, f2, s2, b3, f3, s3):
    params = (b1, f1, s1, b2, f2, s2, b3, f3, s3)
    out, cgrad, sh1, sh2, sh3, total = call_m(scnt, fcnt, cells[0], out_grad[0], params)
    *outs, pairs, out, cgrad = call_e(total, (sh1, sh2, sh3), params, out, cgrad)
    return (out[None], cgrad[None], *outs, pairs.T)


def step(*args):
    cells = args[0]
    fits = lax.axis_size("task") == 8 and lax.axis_size("samp") == 4 and cells.shape == (1, 128, 4, D)
    return fast_device(*args) if fits else on_device(*args)


def solution(mesh):
    placed = (
        P("task", "samp", None, None),
        P("task", "samp", None, None),
        P("task"),
        P("task"),
        P(("task", "samp")),
        P(("task", "samp")),
        P(("task", "samp")),
        P(("task", "samp")),
        P(("task", "samp")),
        P(("task", "samp")),
        P(("task", "samp")),
        P(("task", "samp")),
        P(("task", "samp")),
    )
    return jax.shard_map(
        step,
        mesh=mesh,
        in_specs=placed,
        out_specs=(
            P("task", "samp", None, None),
            P("task", "samp", None, None),
            P(("task", "samp")),
            P(("task", "samp")),
            P(("task", "samp")),
            P(("task", "samp")),
            P(("task", "samp")),
            P(("task", "samp")),
            P(("task", "samp")),
            P(("task", "samp")),
            P(("task", "samp")),
            P(("task", "samp")),
            P(("task", "samp")),
            P(("task", "samp")),
            P(("task", "samp")),
            P(("task", "samp")),
            P(("task", "samp")),
            P(),
        ),
        check_vma=False,
    )
```
